32 devices in a mesh: dp: 8 (over z, x), seq: 4 (over y, core).
Axes of the slice: x: 2, y: 2, z: 4, core: 2. Of those that a mesh axis runs over, the one named last changes fastest.
Arguments:
- tokens: bfloat16 [16, 1024, 768], P('dp', 'seq'), may hold values from -6 to 6
- cotangent: bfloat16 [16, 1024, 768], P('dp', 'seq'), may hold values from -6 to 6
- prefix: int32 [16], P('dp'), may hold values from 102 to 512
- ln1_gain: bfloat16 [768], P(('dp', 'seq')), may hold values from 0.5 to 1.5
- ln1_bias: bfloat16 [768], P(('dp', 'seq')), may hold values from -1.25 to 1.25
- w_qkv: bfloat16 [768, 2304], P(('dp', 'seq')), may hold values from -0.21875 to 0.21875
- b_qkv: bfloat16 [2304], P(('dp', 'seq')), may hold values from -1.75 to 1.75
- w_out: bfloat16 [768, 768], P(('dp', 'seq')), may hold values from -4 to 4
- b_out: bfloat16 [768], P(('dp', 'seq')), may hold values from -1.75 to 1.75
- ln2_gain: bfloat16 [768], P(('dp', 'seq')), may hold values from 0.5 to 1.5
- ln2_bias: bfloat16 [768], P(('dp', 'seq')), may hold values from -1.25 to 1.25
- w_up: bfloat16 [768, 3072], P(('dp', 'seq')), may hold values from -0.21875 to 0.21875
- b_up: bfloat16 [3072], P(('dp', 'seq')), may hold values from -1.75 to 1.75
- w_down: bfloat16 [3072, 768], P(('dp', 'seq')), may hold values from -0.109375 to 0.109375
- b_down: bfloat16 [768], P(('dp', 'seq')), may hold values from -1.75 to 1.75
Outputs:
- block_out: bfloat16 [16, 1024, 768], P('dp', 'seq')
- grad_tokens: bfloat16 [16, 1024, 768], P('dp', 'seq')
- grad_ln1_gain: float32 [768], P(('dp', 'seq'))
- grad_ln1_bias: float32 [768], P(('dp', 'seq'))
- grad_w_qkv: float32 [768, 2304], P(('dp', 'seq'))
- grad_b_qkv: float32 [2304], P(('dp', 'seq'))
- grad_w_out: float32 [768, 768], P(('dp', 'seq'))
- grad_b_out: float32 [768], P(('dp', 'seq'))
- grad_ln2_gain: float32 [768], P(('dp', 'seq'))
- grad_ln2_bias: float32 [768], P(('dp', 'seq'))
- grad_w_up: float32 [768, 3072], P(('dp', 'seq'))
- grad_b_up: float32 [3072], P(('dp', 'seq'))
- grad_w_down: float32 [3072, 768], P(('dp', 'seq'))
- grad_b_down: float32 [768], P(('dp', 'seq'))
The draws below stay inside these ranges and needn't reach their ends.
Inputs may be any that keep to these rules, and one draw needn't show every extreme that they name: Every prefix length is an integer within the range stated in the table.
All inputs are finite; a program needn't handle non-finite values.
Results may differ from the reference program's by a relative error of at most 0.014.
The reference program's roundings to bfloat16 on the way count: a program that leaves them out, or rounds other values in their place, can miss the bound.
Values may be sent and summed in bfloat16 or wider, within the bound.
A program may use at most 256 MiB of HBM per device.

```python
from functools import partial
import jax
import jax.numpy as jnp
from jax import lax

D = 768
HEADS = 12
HEAD_DIM = 64
FF = 3072
LENGTH = 1024
SEQS = 16


def touch_ends(values, own_key, low, largest):
    shape = values.shape
    place = [jax.random.randint(jax.random.fold_in(own_key, axis), (), 0, shape[axis]) for axis in range(len(shape))]
    values = values.at[tuple(place)].set(low)
    longest = shape.index(max(shape))
    place[longest] = (place[longest] + 1) % shape[longest]
    return values.at[tuple(place)].set(largest)


def block_scale(rng, dims, split, least, top_value):
    loudness = 1.0
    for axis_at, shards_of in split:
        draws = jax.random.uniform(jax.random.fold_in(jax.random.fold_in(rng, 6), axis_at), (shards_of,), jnp.float32, least / len(split), top_value / len(split))
        loudness = loudness * jnp.repeat(jnp.exp(draws), dims[axis_at] // shards_of).reshape((-1,) + (1,) * (len(dims) - 1 - axis_at))
    return loudness


def scatter_about(rng, extent, scale, most, cuts=(), held_as=jnp.bfloat16):
    level = block_scale(rng, extent, cuts, -0.22, 0.18) if cuts else 1.0
    drawn = jax.random.normal(rng, extent, jnp.float32) * scale * level
    return jnp.minimum(jnp.maximum(drawn, -most), most).astype(held_as)


def setup_inputs(seed: int = 0) -> dict:
    arg_keys = jax.random.split(jax.random.key(seed), 16)
    return {
        "tokens": scatter_about(arg_keys[0], (SEQS, LENGTH, D), 1.0, 6.0, ((0, 8), (1, 4))),
        "cotangent": scatter_about(arg_keys[1], (SEQS, LENGTH, D), 1.0, 6.0, ((0, 8), (1, 4))),
        "prefix": touch_ends(jax.random.randint(arg_keys[2], (SEQS,), LENGTH // 10, LENGTH // 2 + 1), jax.random.fold_in(arg_keys[2], 1), LENGTH // 10, (LENGTH // 2 + 1) - 1).astype(jnp.int32),
        "ln1_gain": jnp.clip(1.0 + 0.1 * jax.random.normal(arg_keys[3], (D,), jnp.float32), 0.5, 1.5).astype(jnp.bfloat16),
        "ln1_bias": scatter_about(arg_keys[4], (D,), 0.2, 1.25, ((0, 32),)),
        "w_qkv": scatter_about(arg_keys[5], (D, 3 * D), D ** -0.5, 0.21875, ((0, 32),)),
        "b_qkv": scatter_about(arg_keys[6], (3 * D,), 0.3, 1.75, ((0, 32),)),
        "w_out": scatter_about(arg_keys[7], (D, D), (max(1, 3 * D // LENGTH)) ** -0.5, 4.0, ((0, 32),)),
        "b_out": scatter_about(arg_keys[8], (D,), 0.3, 1.75, ((0, 32),)),
        "ln2_gain": jnp.clip(1.0 + 0.1 * jax.random.normal(arg_keys[9], (D,), jnp.float32), 0.5, 1.5).astype(jnp.bfloat16),
        "ln2_bias": scatter_about(arg_keys[10], (D,), 0.2, 1.25, ((0, 32),)),
        "w_up": scatter_about(arg_keys[11], (D, FF), D ** -0.5, 0.21875, ((0, 32),)),
        "b_up": scatter_about(arg_keys[12], (FF,), 0.3, 1.75, ((0, 32),)),
        "w_down": scatter_about(arg_keys[13], (FF, D), FF ** -0.5, 0.109375, ((0, 32),)),
        "b_down": scatter_about(arg_keys[14], (D,), 0.3, 1.75, ((0, 32),)),
    }


@jax.custom_vjp
def low(v):
    return lax.optimization_barrier(v.astype(jnp.bfloat16)).astype(jnp.float32)

@jax.custom_vjp
def low_back(v):
    return v

def low_keep(v):
    return (low(v), None)

def low_pass(kept, grad):
    return (grad,)

def back_keep(v):
    return (v, None)

def back_low(kept, grad):
    return (low(grad),)
low.defvjp(low_keep, low_pass)
low_back.defvjp(back_keep, back_low)
norm_eps = 1e-05

def matmul(left, right):
    return jnp.dot(left, right, precision=lax.Precision.HIGHEST, preferred_element_type=jnp.float32)

def layer_norm(features, gain, shift):
    centre = features - lax.optimization_barrier(jnp.mean(features, axis=-1, keepdims=True))
    spread = lax.optimization_barrier(jnp.mean(centre * centre, axis=-1, keepdims=True))
    return centre * lax.rsqrt(spread + norm_eps) * gain + shift

def head_attention(prefix_len, heads_in):
    query_rows, key_rows, value_rows = heads_in
    places = jnp.arange(LENGTH, dtype=jnp.int32)
    visible = (places[None, :] <= places[:, None]) | (places[None, :] < prefix_len)
    scores = low_back(matmul(query_rows, key_rows.T) * HEAD_DIM ** (-0.5))
    magnitude = jnp.where(visible, jnp.abs(scores), 0.0)
    ceiling = lax.optimization_barrier(jnp.max(magnitude, axis=1, keepdims=True))
    exponent = jnp.where(visible, jnp.exp(magnitude - ceiling), 0.0)
    weights = low(jnp.sign(scores) * exponent)
    return matmul(weights, value_rows) / lax.optimization_barrier(jnp.sum(exponent, axis=1, keepdims=True))

def heads_first(section):
    return low(low_back(section)).reshape(LENGTH, HEADS, HEAD_DIM).transpose(1, 0, 2)

def layer_block(params, sequence, prefix_len):
    gain_one, shift_one, w_qkv, b_qkv, w_out, b_out, gain_two, shift_two, w_up, b_up, w_down, b_down = params
    normed_one = low(layer_norm(sequence, gain_one, shift_one))
    projected = matmul(normed_one, w_qkv) + b_qkv
    head_inputs = (heads_first(projected[:, :D]), heads_first(projected[:, D:2 * D]), heads_first(projected[:, 2 * D:]))
    attended = lax.map(jax.checkpoint(partial(head_attention, prefix_len)), head_inputs)
    attended = attended.transpose(1, 0, 2).reshape(LENGTH, D)
    branch_one = low_back(matmul(low(low_back(attended)), w_out) + b_out)
    residual_mid = sequence + branch_one
    normed_two = low(layer_norm(residual_mid, gain_two, shift_two))
    hidden = low(jax.nn.gelu(low_back(matmul(normed_two, w_up) + b_up), approximate=True))
    branch_two = low_back(matmul(hidden, w_down) + b_down)
    return residual_mid + branch_two

def reference(tokens, cotangent, prefix, ln1_gain, ln1_bias, w_qkv, b_qkv, w_out, b_out, ln2_gain, ln2_bias, w_up, b_up, w_down, b_down):
    params = (ln1_gain.astype(jnp.float32), ln1_bias.astype(jnp.float32), w_qkv.astype(jnp.float32), b_qkv.astype(jnp.float32), w_out.astype(jnp.float32), b_out.astype(jnp.float32), ln2_gain.astype(jnp.float32), ln2_bias.astype(jnp.float32), w_up.astype(jnp.float32), b_up.astype(jnp.float32), w_down.astype(jnp.float32), b_down.astype(jnp.float32))

    def whole(weights_in, inputs_all):

        def one_sequence(element):
            return layer_block(weights_in, element[0], element[1])
        return lax.map(jax.checkpoint(one_sequence), (inputs_all, prefix))
    result, pullback = jax.vjp(whole, params, tokens.astype(jnp.float32))
    grads, grad_inputs = pullback(cotangent.astype(jnp.float32))
    return (result.astype(jnp.bfloat16), grad_inputs.astype(jnp.bfloat16), grads[0], grads[1], grads[2], grads[3], grads[4], grads[5], grads[6], grads[7], grads[8], grads[9], grads[10], grads[11])
```

```python
import functools
import numpy as np
import jax
import jax.numpy as jnp
from jax import lax
from jax.experimental import pallas as pl
from jax.experimental.pallas import tpu as pltpu
from jax.sharding import PartitionSpec as P


HEADS = 12
HEAD_DIM = 64
MB = 2

F32 = jnp.float32
BF = jnp.bfloat16
EPS = 1e-05
MESH = pl.DeviceIdType.MESH
NEG = -1e30
ANY = pl.BlockSpec(memory_space=pl.ANY)
VM = pl.BlockSpec(memory_space=pltpu.VMEM)
SM = pl.BlockSpec(memory_space=pltpu.SMEM)
WIDTHS = (24, 24, 72, 24, 24, 24, 96, 24)


def places():
    dp = lax.axis_index("dp")
    sq = lax.axis_index("seq")
    return dp // 2, dp % 2, sq // 2, sq % 2


def device(z, x, y, c):
    return (z * 2 + x, y * 2 + c)


def spread_row(gathered, index, width):
    total = 32 * width
    owner = lax.broadcasted_iota(jnp.int32, (32, 256), 0)
    place = lax.broadcasted_iota(jnp.int32, (32, 256), 1)
    pick = jnp.where(place == owner * 8 + index, 1.0, 0.0).astype(BF)
    mine = jnp.dot(pick, gathered, preferred_element_type=F32).astype(BF)
    column = lax.broadcasted_iota(jnp.int32, (1, total), 1).astype(F32)
    row_of = jnp.floor((column + 0.5) * (1.0 / width))
    rest = (column - row_of * width).astype(jnp.int32)
    row_of = row_of.astype(jnp.int32)
    spread = jnp.where(lax.broadcasted_iota(jnp.int32, (128, total), 0) == rest, 1.0, 0.0).astype(BF)
    full = jnp.dot(mine, spread, preferred_element_type=F32)
    keep = lax.broadcasted_iota(jnp.int32, (32, total), 0) == row_of
    return jnp.sum(jnp.where(keep, full, 0.0), axis=0, keepdims=True)


def forward_kernel(
    prefix, tok, cot, vec_s, wq_s, wo_s, wu_s, wd_s,
    wq, wo, wu, wd, gv, cots, attl_out, xs, n1t_out, qs_out, qst_out, k_out, v_out, att_out, lt_out, vrows,
    tok_all, gvm, wqm, vt, attl, n1, ssem, rsem, lsem,
):
    z, x, y, c = places()
    x2, y2, c2 = 1 - x, 1 - y, 1 - c
    px, py, pc = device(z, x2, y, c), device(z, x, y2, c), device(z, x, y, c2)
    zs = [lax.rem(z + d, 4) for d in (1, 2, 3)]
    pz = [device(zz, x, y, c) for zz in zs]

    sent = []
    counts = [0, 0]

    def remote(src, dst, dev):
        i = counts[0]
        counts[0] += 1
        copy = pltpu.make_async_remote_copy(
            src_ref=src, dst_ref=dst, send_sem=ssem.at[i], recv_sem=rsem.at[i],
            device_id=dev, device_id_type=MESH)
        copy.start()
        sent.append(copy)
        return copy

    def local(src, dst):
        i = counts[1]
        counts[1] += 1
        copy = pltpu.make_async_copy(src, dst, lsem.at[i])
        copy.start()
        return copy

    def arrive(copies):
        for copy in copies:
            copy.wait_recv()

    def landed(copies):
        for copy in copies:
            copy.wait()

    barrier = pltpu.get_barrier_semaphore()
    for dev in [px, py, pc] + pz:
        pl.semaphore_signal(barrier, inc=1, device_id=dev, device_id_type=MESH)
    pl.semaphore_wait(barrier, 6)

    width = 768
    third = 384

    def shard(xx, yy, cc):
        return pl.ds(pl.multiple_of(((xx * 2 + yy) * 2 + cc) * 24, 8), 24)

    own_vec = [local(vec_s, gv.at[z, x, y, c])]
    vec_c = [remote(vec_s, gv.at[z, x, y, c], pc)]
    tok_y = [remote(tok.at[y2], tok_all.at[y, c], py)]
    own_tok = [local(tok.at[y], tok_all.at[y, c])]
    own_wq, wq_c = [], []
    for kind in range(3):
        there = pl.ds(kind * third, third)
        mine_cols = pl.ds(pl.multiple_of(kind * width + c * third, 128), third)
        peer_cols = pl.ds(pl.multiple_of(kind * width + c2 * third, 128), third)
        own_wq.append(local(wq_s.at[:, mine_cols], wq.at[z, shard(x, y, c), there]))
        wq_c.append(remote(wq_s.at[:, peer_cols], wq.at[z, shard(x, y, c), there], pc))
    own_w = [local(s, w.at[z, x, y, c]) for s, w in ((wo_s, wo), (wu_s, wu), (wd_s, wd))]
    own_cot = [local(cot.at[y], cots.at[y])]

    landed(own_vec)
    arrive(vec_c)
    vec_z = [remote(gv.at[z, x, y], gv.at[z, x, y], dev) for dev in pz]
    landed(own_wq)
    arrive(wq_c)
    both = pl.ds(pl.multiple_of((x * 2 + y) * 48, 16), 48)
    wq_z = [remote(wq.at[z, both], wq.at[z, both], dev) for dev in pz]
    landed(own_tok)
    arrive(tok_y)
    own_xs = local(tok_all.at[:, c], xs)
    tok_c = [remote(tok_all.at[:, c], tok_all.at[:, c], pc)]
    arrive(vec_z)
    vec_x = [remote(gv.at[:, x, y], gv.at[:, x, y], px)]
    arrive(vec_x)
    vec_y = [remote(gv.at[:, :, y], gv.at[:, :, y], py)]
    arrive(tok_c)
    arrive(vec_y)
    gcopy = local(gv, gvm)
    gcopy.wait()
    table = gvm[...].reshape(256, 128)
    for index, wide in enumerate(WIDTHS):
        vrows[index : index + 1, 0 : 32 * wide] = spread_row(table, index, wide)
    gain = vrows[0:1, 0:width]
    shift = vrows[1:2, 0:width]

    def norm_block(b, carry):
        yy, cc = b // 2, lax.rem(b, 2)
        rows = tok_all[yy, cc].astype(F32)
        centre = rows - jnp.mean(rows, axis=-1, keepdims=True)
        spread = jnp.mean(centre * centre, axis=-1, keepdims=True)
        normed = (centre * lax.rsqrt(spread + EPS) * gain + shift).astype(BF)
        rows_at = pl.ds(pl.multiple_of(b * 256, 256), 256)
        n1[rows_at, :] = normed
        n1t_out[:, rows_at] = normed.astype(F32).T.astype(BF)
        return carry

    lax.fori_loop(0, 4, norm_block, 0)

    arrive(wq_z)
    wq_1 = [remote(wq.at[:, shard(x, y, 0)], wq.at[:, shard(x, y, 0)], px),
            remote(wq.at[:, shard(x, y, 1)], wq.at[:, shard(x, y, 1)], py)]
    landed(own_w)
    wo_z = [remote(wo_s, wo.at[z, x, y, c], dev) for dev in pz]
    wu_z = [remote(wu_s, wu.at[z, x, y, c], dev) for dev in pz]

    def spread_1(w):
        half = w.shape[5] // 2
        return [remote(w.at[:, x, y, c, :, 0:half], w.at[:, x, y, c, :, 0:half], px),
                remote(w.at[:, x, y, c, :, half:], w.at[:, x, y, c, :, half:], py)]

    def spread_2(w):
        half = w.shape[5] // 2
        return [remote(w.at[:, :, y, c, :, 0:half], w.at[:, :, y, c, :, 0:half], py),
                remote(w.at[:, x, :, c, :, half:], w.at[:, x, :, c, :, half:], px)]

    def spread_3(w):
        return [remote(w.at[:, :, :, c], w.at[:, :, :, c], pc)]

    arrive(wq_1)
    wq_2 = [remote(wq.at[:, shard(i, y, 0)], wq.at[:, shard(i, y, 0)], py) for i in range(2)]
    wq_2 += [remote(wq.at[:, shard(x, i, 1)], wq.at[:, shard(x, i, 1)], px) for i in range(2)]
    wd_z = [remote(wd_s, wd.at[z, x, y, c], dev) for dev in pz]
    arrive(wq_2)
    arrive(wo_z)
    wo_1 = spread_1(wo)
    arrive(wu_z)
    wu_1 = spread_1(wu)
    gather_q = local(wq.reshape(width, 3 * third), wqm)
    gather_q.wait()

    def project(b, carry):
        rows = pl.ds(pl.multiple_of(b * 256, 256), 256)
        block = n1[rows, :]
        parts = []
        for kind in range(3):
            bias = vrows[2:3, pl.ds(pl.multiple_of(kind * width + c * third, 128), third)]
            value = jnp.dot(block, wqm[:, kind * third : (kind + 1) * third], preferred_element_type=F32)
            parts.append((value + bias).astype(BF))
        qs = (parts[0].astype(F32) * 0.125)
        qs_out[rows, :] = qs.astype(BF)
        qst_out[:, rows] = qs.T.astype(BF)
        k_out[rows, :] = parts[1]
        v_out[rows, :] = parts[2]
        vt[:, rows] = parts[2].astype(F32).T.astype(BF)
        return carry

    lax.fori_loop(0, 4, project, 0)

    limit = prefix[y] - 1
    sub = lax.broadcasted_iota(jnp.int32, (128, 256), 0)

    def attend(block):
        rows = min(4, max(block + 1, 2)) * 256
        qcols = pl.ds(block * 256, 256)

        def unit(u, carry):
            cols = pl.ds(pl.multiple_of(u * 128, 128), 128)
            keys = k_out[0:rows, cols]
            queries = qst_out[cols, qcols]
            qpos = block * 256 + lax.broadcasted_iota(jnp.int32, (1, 256), 1)
            bound = jnp.maximum(qpos, limit)
            seen = lax.broadcasted_iota(jnp.int32, (rows, 256), 0) <= bound
            for half in range(2):
                chosen = jnp.where(sub // 64 == half, queries, jnp.zeros_like(queries))
                scores = jnp.dot(keys, chosen, preferred_element_type=F32)
                size = jnp.where(seen, jnp.abs(scores), NEG)
                top = jnp.max(size, axis=0, keepdims=True)
                exponent = jnp.exp(size - top)
                total = jnp.sum(exponent, axis=0, keepdims=True)
                weights = jnp.where(scores > 0, exponent, jnp.where(scores < 0, -exponent, 0.0)).astype(BF)
                values = vt[pl.ds(pl.multiple_of(u * 128 + half * 64, 64), 64), 0:rows]
                result = jnp.dot(values, weights, preferred_element_type=F32) / total
                att_out[pl.ds(pl.multiple_of(u * 128 + half * 64, 64), 64), qcols] = result
                lt_out[pl.ds(u * 2 + half, 1), qcols] = top + jnp.log(total)
            both = att_out[cols, qcols]
            attl[block // 2, block % 2, :, cols] = both.T.astype(BF)
            return carry

        lax.fori_loop(0, 3, unit, 0)

    lt_out[...] = jnp.zeros_like(lt_out)
    attend(3)
    arrive(wo_1)
    wo_2 = spread_2(wo)
    arrive(wu_1)
    wu_2 = spread_2(wu)
    arrive(wd_z)
    wd_1 = spread_1(wd)
    cot_y = [remote(cot.at[y2], cots.at[y], py)]
    attend(2)
    arrive(wo_2)
    wo_3 = spread_3(wo)
    attend(1)
    attend(0)
    mine_cols = pl.ds(pl.multiple_of(c * third, 128), third)
    own_att = local(attl.at[:, c], attl_out.at[:, :, mine_cols])
    att_c = [remote(attl.at[:, c2], attl_out.at[:, :, mine_cols], pc)]
    arrive(wu_2)
    wu_3 = spread_3(wu)
    arrive(wd_1)
    wd_2 = spread_2(wd)
    arrive(wd_2)
    wd_3 = spread_3(wd)
    own_att.wait()
    own_xs.wait()
    landed(own_cot)
    arrive(att_c + cot_y + wo_3 + wu_3 + wd_3)
    for copy in sent:
        copy.wait_send()


N_REMOTE = 64
N_LOCAL = 24


def forward_call(prefix, tok, cot, vec_s, wq_s, wo_s, wu_s, wd_s):
    sds = jax.ShapeDtypeStruct
    out_shape = (
        sds((4, 192, 1152), BF), sds((4, 2, 2, 2, 24, 768), BF), sds((4, 2, 2, 2, 24, 3072), BF),
        sds((4, 2, 2, 2, 96, 768), BF), sds((4, 2, 2, 2, 8, 128), BF), sds((2, 256, 768), BF), sds((2, 256, 768), BF), sds((2, 256, 768), BF),
        sds((768, 1024), BF), sds((1024, 384), BF), sds((384, 1024), BF), sds((1024, 384), BF), sds((1024, 384), BF),
        sds((384, 1024), F32), sds((8, 1024), F32), sds((8, 3072), F32),
    )
    return pl.pallas_call(
        forward_kernel,
        out_shape=out_shape,
        in_specs=[SM] + [ANY] * 7,
        out_specs=(ANY,) * 8 + (VM,) * 8,
        scratch_shapes=[
            pltpu.VMEM((2, 2, 256, 768), BF), pltpu.VMEM((4, 2, 2, 2, 8, 128), BF), pltpu.VMEM((768, 1152), BF),
            pltpu.VMEM((384, 1024), BF), pltpu.VMEM((2, 2, 256, 384), BF), pltpu.VMEM((1024, 768), BF),
            pltpu.SemaphoreType.DMA((N_REMOTE,)), pltpu.SemaphoreType.DMA((N_REMOTE,)),
            pltpu.SemaphoreType.DMA((N_LOCAL,)),
        ],
        compiler_params=pltpu.CompilerParams(
            collective_id=0, has_side_effects=True, vmem_limit_bytes=56 * 2**20),
    )(prefix, tok, cot, vec_s, wq_s, wo_s, wu_s, wd_s)


def pack_vectors(vectors):
    return jnp.stack([jnp.pad(v, (0, 128 - v.shape[0])) for v in vectors])


def collect_rows(vector, wide):
    total = 32 * wide
    column = lax.broadcasted_iota(jnp.int32, (1, total), 1).astype(F32)
    row_of = jnp.floor((column + 0.5) * (1.0 / wide))
    rest = (column - row_of * wide).astype(jnp.int32)
    row_of = row_of.astype(jnp.int32)
    gather = jnp.where(lax.broadcasted_iota(jnp.int32, (128, total), 0) == rest, 1.0, 0.0).astype(BF)
    keep = lax.broadcasted_iota(jnp.int32, (32, total), 0) == row_of
    high = vector.astype(BF).astype(F32)
    low = vector - high
    dims = (((1,), (1,)), ((), ()))
    out = None
    for part in (high, low):
        placed = jnp.where(keep, part, 0.0).astype(BF)
        term = lax.dot_general(placed, gather, dims, preferred_element_type=F32)
        out = term if out is None else out + term
    return out


def add_into(ref, at, other):
    ref[at] = (ref[at].astype(F32) + other.astype(F32)).astype(BF)


def backward_kernel(
    prefix, gd, gu, go, bo, ga, wq, n1t, xs, gmid, qs, qst, k, v, att, lt, vrows,
    vb_out, vg2, vb2, vb_up, vb_down,
    out_bo, out_gt, out_q, out_o, out_u, out_d, out_vec,
    ld, lu, lo, r0d, r0u, r0o, r1ad, r1bd, r1au, r1bu, r1ao, r1bo, r2ad, r2bd, r2au, r2bu, r2ao, r2bo, r3d, r3u, r3o,
    ga_all, gt, kt, dk, dv, gp, gpu, qbuf, qr1a, qr1b, qr2a, qr2b, qr3, qsend, qrecv,
    wqm, n1m, gmm, part_send, part_own, part_recv, gtb, vsum, vbq, vtab, vr0, vr1, vr2, vr3,
    ssem, rsem, lsem,
):
    z, x, y, c = places()
    x2, y2, c2 = 1 - x, 1 - y, 1 - c
    px, py, pc = device(z, x2, y, c), device(z, x, y2, c), device(z, x, y, c2)
    zs = [lax.rem(z + d, 4) for d in (1, 2, 3)]
    pz = [device(zz, x, y, c) for zz in zs]
    third = 384
    width = 768

    def remote(i, src, dst, dev):
        return pltpu.make_async_remote_copy(
            src_ref=src, dst_ref=dst, send_sem=ssem.at[i], recv_sem=rsem.at[i],
            device_id=dev, device_id_type=MESH)

    ids = [0]

    def fresh(count=1):
        first = ids[0]
        ids[0] += count
        return first

    def start(copies):
        for copy in copies:
            copy.start()

    def arrive(copies):
        for copy in copies:
            copy.wait_recv()

    def gone(copies):
        for copy in copies:
            copy.wait_send()

    barrier = pltpu.get_barrier_semaphore()
    for dev in [px, py, pc] + pz:
        pl.semaphore_signal(barrier, inc=1, device_id=dev, device_id_type=MESH)
    pl.semaphore_wait(barrier, 6)

    locals_used = [0]

    def local(src, dst):
        i = locals_used[0]
        locals_used[0] += 1
        return pltpu.make_async_copy(src, dst, lsem.at[i])

    mine_cols = pl.ds(pl.multiple_of(c * third, 128), third)
    peer_cols = pl.ds(pl.multiple_of(c2 * third, 128), third)
    ga_own = local(ga.at[:, :, mine_cols], ga_all.at[:, c])
    ga_own.start()
    ga_c = [remote(fresh(), ga.at[:, :, peer_cols], ga_all.at[:, c], pc)]
    start(ga_c)
    bo_own = local(bo.at[y], out_bo.at[y])
    bo_own.start()
    bo_y = [remote(fresh(), bo.at[y2], out_bo.at[y], py)]
    start(bo_y)

    class Scatter:
        def __init__(self, grad, held, r0, r1a, r1b, r2a, r2b, r3, out):
            half = out.shape[1] // 2
            self.half, self.held, self.out = half, held, out
            self.r0, self.r1a, self.r1b, self.r2a, self.r2b, self.r3 = r0, r1a, r1b, r2a, r2b, r3
            self.mine = local(grad.at[:, :, :, c], held)
            self.c0 = [remote(fresh(), grad.at[:, :, :, c2], r0, pc)]
            self.c1 = [remote(fresh(), held.at[:, :, y2, :, 0:half], r1a, py),
                       remote(fresh(), held.at[:, x2, :, :, half:], r1b, px)]
            self.c2 = [remote(fresh(), held.at[:, x2, y, :, 0:half], r2a, px),
                       remote(fresh(), held.at[:, x, y2, :, half:], r2b, py)]
            self.c3 = [remote(fresh(), held.at[zs[d], x, y], r3.at[d], pz[d]) for d in range(3)]

        def s0(self):
            self.mine.start()
            start(self.c0)

        def s1(self):
            self.mine.wait()
            arrive(self.c0)

            def add(i, carry):
                zz, xx, yy = i // 4, lax.rem(i // 2, 2), lax.rem(i, 2)
                add_into(self.held, (zz, xx, yy), self.r0[zz, xx, yy])
                return carry

            lax.fori_loop(0, 16, add, 0)
            start(self.c1)

        def s2(self):
            arrive(self.c1)

            def add(i, carry):
                zz, other = i // 2, lax.rem(i, 2)
                add_into(self.held, (zz, other, y, slice(None), slice(0, self.half)), self.r1a[zz, other])
                add_into(self.held, (zz, x, other, slice(None), slice(self.half, None)), self.r1b[zz, other])
                return carry

            lax.fori_loop(0, 8, add, 0)
            start(self.c2)

        def s3(self):
            arrive(self.c2)

            def add(zz, carry):
                add_into(self.held, (zz, x, y, slice(None), slice(0, self.half)), self.r2a[zz])
                add_into(self.held, (zz, x, y, slice(None), slice(self.half, None)), self.r2b[zz])
                return carry

            lax.fori_loop(0, 4, add, 0)
            start(self.c3)

        def s4(self):
            arrive(self.c3)
            self.out[...] = (self.held[z, x, y].astype(F32) + self.r3[0].astype(F32)
                             + self.r3[1].astype(F32) + self.r3[2].astype(F32))

        def sends(self):
            return self.c0 + self.c1 + self.c2 + self.c3

    down = Scatter(gd, ld, r0d, r1ad, r1bd, r2ad, r2bd, r3d, out_d)
    up = Scatter(gu, lu, r0u, r1au, r1bu, r2au, r2bu, r3u, out_u)
    outp = Scatter(go, lo, r0o, r1ao, r1bo, r2ao, r2bo, r3o, out_o)
    down.s0()
    up.s0()
    outp.s0()
    late = [local(wq, wqm), local(n1t, n1m), local(gmid, gmm)]
    start(late)

    q1a, q1b, q2a, q2b = fresh(3), fresh(3), fresh(3), fresh(3)
    q3 = [fresh(3) for d in range(3)]
    q4 = fresh(3)

    class QScatter:
        def __init__(self, u):
            self.u = u
            buf = qbuf.at[u]
            self.buf = buf
            self.c1 = [remote(q1a + u, buf.at[:, :, y2, 0], qr1a.at[u], py),
                       remote(q1b + u, buf.at[:, x2, :, 1], qr1b.at[u], px)]
            self.c2 = [remote(q2a + u, buf.at[:, x2, y, 0], qr2a.at[u], px),
                       remote(q2b + u, buf.at[:, x, y2, 1], qr2b.at[u], py)]
            self.c3 = [remote(q3[d] + u, buf.at[zs[d], x, y], qr3.at[u, d], pz[d]) for d in range(3)]
            self.c4 = [remote(q4 + u, qsend.at[u], qrecv.at[u], pc)]

        def s1(self):
            start(self.c1)

        def s2(self):
            u = self.u
            arrive(self.c1)

            def add(i, carry):
                zz, other = i // 2, lax.rem(i, 2)
                add_into(qbuf, (u, zz, other, y, 0), qr1a[u, zz, other])
                add_into(qbuf, (u, zz, x, other, 1), qr1b[u, zz, other])
                return carry

            lax.fori_loop(0, 8, add, 0)
            start(self.c2)

        def s3(self):
            u = self.u
            arrive(self.c2)

            def add(zz, carry):
                add_into(qbuf, (u, zz, x, y, 0), qr2a[u, zz])
                add_into(qbuf, (u, zz, x, y, 1), qr2b[u, zz])
                return carry

            lax.fori_loop(0, 4, add, 0)
            start(self.c3)

        def total(self, cs):
            u = self.u
            return (qbuf[u, z, x, y, cs].astype(F32) + qr3[u, 0, cs].astype(F32)
                    + qr3[u, 1, cs].astype(F32) + qr3[u, 2, cs].astype(F32))

        def put(self, value, core):
            for kind in range(3):
                cols = pl.ds(pl.multiple_of(kind * width + core * third + self.u * 128, 128), 128)
                out_q[:, cols] = value[:, kind * 128 : (kind + 1) * 128]

        def s4(self):
            arrive(self.c3)
            qsend[self.u] = self.total(c2)
            start(self.c4)
            self.put(self.total(c), c)

        def s5(self):
            arrive(self.c4)
            self.put(qrecv[self.u], c2)

        def sends(self):
            return self.c1 + self.c2 + self.c3 + self.c4

    queue = [QScatter(u) for u in range(3)]
    slots = {
        (0, 3): [down.s1], (0, 2): [up.s1], (0, 1): [outp.s1], (0, 0): [down.s2],
        (1, 3): [], (1, 2): [up.s2], (1, 1): [outp.s2, down.s3], (1, 0): [up.s3],
        (2, 3): [queue[0].s2, outp.s3], (2, 2): [down.s4], (2, 1): [queue[0].s3], (2, 0): [],
    }

    ga_own.wait()
    arrive(ga_c)
    limit = prefix[y] - 1
    sub = lax.broadcasted_iota(jnp.int32, (128, 256), 0)
    lane = lax.broadcasted_iota(jnp.int32, (256, 128), 1)
    vbq[...] = jnp.zeros_like(vbq)

    def unit(u, carry):
        cols = pl.ds(pl.multiple_of(u * 128, 128), 128)
        for b in range(4):
            rows = slice(b * 256, (b + 1) * 256)
            gt[:, rows] = ga_all[b // 2, b % 2, :, cols].astype(F32).T.astype(BF)
            kt[:, rows] = k[rows, cols].astype(F32).T.astype(BF)
        dk[...] = jnp.zeros_like(dk)
        dv[...] = jnp.zeros_like(dv)
        for block in (3, 2, 1, 0):
            rows = min(4, max(block + 1, 2)) * 256
            qrange = slice(block * 256, (block + 1) * 256)
            keys = k[0:rows, cols]
            values = v[0:rows, cols]
            queries_t = qst[cols, qrange]
            grads_t = gt[:, qrange]
            queries = qs[qrange, cols]
            grads = ga_all[block // 2, block % 2, :, cols]
            qpos = block * 256 + lax.broadcasted_iota(jnp.int32, (1, 256), 1)
            bound = jnp.maximum(qpos, limit)
            seen = lax.broadcasted_iota(jnp.int32, (rows, 256), 0) <= bound
            prod = grads_t.astype(F32) * att[cols, qrange]
            dqs, dks, dvs = [], None, None
            for half in range(2):
                part = slice(half * 64, half * 64 + 64)
                in_sub = sub // 64 == half
                in_lane = lane // 64 == half
                delta = jnp.sum(prod[part], axis=0, keepdims=True)
                total = lt[pl.ds(u * 2 + half, 1), qrange]
                zero = jnp.zeros((), BF)
                scores = jnp.dot(keys, jnp.where(in_sub, queries_t, zero), preferred_element_type=F32)
                pull = jnp.dot(values, jnp.where(in_sub, grads_t, zero), preferred_element_type=F32)
                share = jnp.exp(jnp.where(seen, jnp.abs(scores) - total, NEG))
                signed = jnp.where(scores > 0, share, jnp.where(scores < 0, -share, 0.0))
                grad_scores = (share * pull - signed * delta).astype(BF)
                signed = signed.astype(BF)
                dvt = jnp.dot(signed, jnp.where(in_lane, grads, zero), preferred_element_type=F32)
                dkt = jnp.dot(grad_scores, jnp.where(in_lane, queries, zero), preferred_element_type=F32)
                dvs = dvt if dvs is None else dvs + dvt
                dks = dkt if dks is None else dks + dkt
                dqs.append(jnp.dot(kt[part, 0:rows], grad_scores, preferred_element_type=F32))
            dk[0:rows, :] += dks
            dv[0:rows, :] += dvs
            gpu[qrange, 0:128] = (jnp.concatenate(dqs, axis=0).T * 0.125).astype(BF)
            for which in range(3):
                if slots[which, block]:
                    @pl.when(u == which)
                    def _():
                        for step in slots[which, block]:
                            step()
        gpu[:, 128:256] = dk[...].astype(BF)
        gpu[:, 256:384] = dv[...].astype(BF)
        sums = jnp.sum(gpu[...].astype(F32), axis=0, keepdims=True)
        for kind in range(3):
            part = slice(kind * 128, (kind + 1) * 128)
            vbq[0:1, pl.ds(pl.multiple_of(kind * width + c * third + u * 128, 128), 128)] = sums[:, part]
            gp[:, pl.ds(pl.multiple_of(kind * third + u * 128, 128), 128)] = gpu[:, part]

        @pl.when(u == 0)
        def _():
            late[1].wait()

        def weights(i, inner):
            zz, xx = i // 2, lax.rem(i, 2)
            block = jnp.dot(n1m[pl.ds(pl.multiple_of(i * 96, 32), 96), :], gpu[...], preferred_element_type=F32)
            for j in range(4):
                qbuf[u, zz, xx, j // 2, j % 2] = block[j * 24 : (j + 1) * 24].astype(BF)
            return inner

        lax.fori_loop(0, 8, weights, 0)
        QScatter(u).s1()
        return carry

    lax.fori_loop(0, 3, unit, 0)

    late[0].wait()
    late[2].wait()
    dims = (((1,), (1,)), ((), ()))

    def back_rows(b):
        return lax.dot_general(gp[pl.ds(pl.multiple_of(b * 256, 256), 256), :], wqm[...], dims,
                               preferred_element_type=F32)

    def back_peer(yy, carry):
        part_send[yy] = back_rows(yy * 2 + c2)
        return carry

    lax.fori_loop(0, 2, back_peer, 0)
    part_c = [remote(fresh(), part_send, part_recv, pc)]
    start(part_c)
    queue[1].s2()

    def back_own(yy, carry):
        part_own[yy] = back_rows(yy * 2 + c)
        return carry

    lax.fori_loop(0, 2, back_own, 0)
    queue[2].s2()
    up.s4()
    outp.s4()
    queue[0].s4()
    gain = vrows[0:1, 0:width]
    vsum[...] = jnp.zeros_like(vsum)
    arrive(part_c)

    def norm_back(yy, carry):
        rows = xs[yy].astype(F32)
        centre = rows - jnp.mean(rows, axis=-1, keepdims=True)
        scale = lax.rsqrt(jnp.mean(centre * centre, axis=-1, keepdims=True) + EPS)
        unit_rows = centre * scale
        grad = part_own[yy] + part_recv[yy]
        vsum[0:1, :] += jnp.sum(grad * unit_rows, axis=0, keepdims=True)
        vsum[1:2, :] += jnp.sum(grad, axis=0, keepdims=True)
        grad = grad * gain
        inner = (grad - jnp.mean(grad, axis=-1, keepdims=True)
                 - unit_rows * jnp.mean(grad * unit_rows, axis=-1, keepdims=True))
        gtb[yy] = (gmm[yy] + scale * inner).astype(BF)
        return carry

    lax.fori_loop(0, 2, norm_back, 0)
    gt_own = local(gtb.at[y], out_gt.at[y])
    gt_own.start()
    gt_y = [remote(fresh(), gtb.at[y2], out_gt.at[y], py)]
    start(gt_y)
    queue[1].s3()
    vectors = (vsum[0:1, :], vsum[1:2, :], vbq[...], vb_out[...], vg2[...], vb2[...], vb_up[...], vb_down[...])
    for index, wide in enumerate(WIDTHS):
        vtab[pl.ds(index, 32, stride=8), :] = collect_rows(vectors[index], wide)
    table = vtab.reshape(4, 2, 2, 2, 8, 128)
    v0 = [remote(fresh(), table.at[:, :, :, c2], vr0, pc)]
    v1 = [remote(fresh(), table.at[:, :, y2, c], vr1, py)]
    v2 = [remote(fresh(), table.at[:, x2, y, c], vr2, px)]
    v3 = [remote(fresh(), table.at[zs[d], x, y, c], vr3.at[d], pz[d]) for d in range(3)]

    def tile(zz, xx, yy):
        return pl.ds(pl.multiple_of((((zz * 2 + xx) * 2 + yy) * 2 + c) * 8, 8), 8)

    start(v0)
    queue[2].s3()
    arrive(v0)

    def add_core(i, carry):
        zz, xx, yy = i // 4, lax.rem(i // 2, 2), lax.rem(i, 2)
        vtab[tile(zz, xx, yy), :] += vr0[zz, xx, yy]
        return carry

    lax.fori_loop(0, 16, add_core, 0)
    start(v1)
    queue[1].s4()
    queue[0].s5()
    arrive(v1)

    def add_y(i, carry):
        vtab[tile(i // 2, lax.rem(i, 2), y), :] += vr1[i // 2, lax.rem(i, 2)]
        return carry

    lax.fori_loop(0, 8, add_y, 0)
    start(v2)
    queue[2].s4()
    arrive(v2)

    def add_x(zz, carry):
        vtab[tile(zz, x, y), :] += vr2[zz]
        return carry

    lax.fori_loop(0, 4, add_x, 0)
    start(v3)
    queue[1].s5()
    queue[2].s5()
    arrive(v3)
    out_vec[...] = vtab[tile(z, x, y), :] + vr3[0] + vr3[1] + vr3[2]
    gt_own.wait()
    bo_own.wait()
    arrive(gt_y + bo_y)
    gone(ga_c + bo_y + down.sends() + up.sends() + outp.sends() + part_c + gt_y + v0 + v1 + v2 + v3)
    for u in range(3):
        gone(queue[u].sends())


def backward_call(*operands):
    sds = jax.ShapeDtypeStruct
    vmem = pltpu.VMEM
    dma = pltpu.SemaphoreType.DMA
    out_shape = (
        sds((2, 256, 768), BF), sds((2, 256, 768), BF), sds((24, 2304), F32), sds((24, 768), F32),
        sds((24, 3072), F32), sds((96, 768), F32), sds((8, 128), F32),
    )
    shapes = ((96, 768), (24, 3072), (24, 768))
    scratch = [vmem((4, 2, 2) + s, BF) for s in shapes] + [vmem((4, 2, 2) + s, BF) for s in shapes]
    for rows, columns in shapes:
        scratch += [vmem((4, 2, rows, columns // 2), BF)] * 2
    for rows, columns in shapes:
        scratch += [vmem((4, rows, columns // 2), BF)] * 2
    scratch += [vmem((3,) + s, BF) for s in shapes]
    scratch += [
        vmem((2, 2, 256, 384), BF), vmem((128, 1024), BF), vmem((128, 1024), BF), vmem((1024, 128), F32),
        vmem((1024, 128), F32), vmem((1024, 1152), BF), vmem((1024, 384), BF), vmem((3, 4, 2, 2, 2, 24, 384), BF),
        vmem((3, 4, 2, 24, 384), BF), vmem((3, 4, 2, 24, 384), BF), vmem((3, 4, 24, 384), BF), vmem((3, 4, 24, 384), BF),
        vmem((3, 3, 2, 24, 384), BF), vmem((3, 24, 384), F32), vmem((3, 24, 384), F32),
        vmem((768, 1152), BF), vmem((768, 1024), BF), vmem((2, 256, 768), F32), vmem((2, 256, 768), F32),
        vmem((2, 256, 768), F32), vmem((2, 256, 768), F32), vmem((2, 256, 768), BF), vmem((2, 768), F32),
        vmem((1, 2304), F32), vmem((256, 128), F32), vmem((4, 2, 2, 8, 128), F32), vmem((4, 2, 8, 128), F32),
        vmem((4, 8, 128), F32), vmem((3, 8, 128), F32),
        dma((96,)), dma((96,)), dma((16,)),
    ]
    return pl.pallas_call(
        backward_kernel,
        out_shape=out_shape,
        in_specs=[SM] + [ANY] * 7 + [VM, ANY] + [VM] * 7 + [VM] * 5,
        out_specs=(ANY, ANY) + (VM,) * 5,
        scratch_shapes=scratch,
        compiler_params=pltpu.CompilerParams(
            collective_id=1, has_side_effects=True, vmem_limit_bytes=60 * 2**20),
    )(*operands)


def middle(wo, wu, wd, cots, attl, xs, vrows):
    width = xs.shape[-1]
    w_out = wo.reshape(width, width)
    w_up = wu.reshape(width, -1)
    w_down = wd.reshape(-1, width)
    hidden_units = w_up.shape[1]
    b_out, gain_two, shift_two = vrows[3, :width], vrows[4, :width], vrows[5, :width]
    b_up, b_down = vrows[6, :hidden_units], vrows[7, :width]
    residual_in = xs.reshape(-1, width).astype(F32)
    attended_low = attl.reshape(-1, width)
    grad_branch = cots.reshape(-1, width)
    residual_mid = residual_in + jnp.dot(attended_low, w_out, preferred_element_type=F32) + b_out
    normed_two, norm_two_pull = jax.vjp(layer_norm, residual_mid, gain_two, shift_two)
    normed_two = normed_two.astype(BF)
    pre_gelu = jnp.dot(normed_two, w_up, preferred_element_type=F32) + b_up
    hidden, gelu_pull = jax.vjp(gelu_tanh, pre_gelu)
    hidden = hidden.astype(BF)
    block_out = (residual_mid + jnp.dot(hidden, w_down, preferred_element_type=F32) + b_down).astype(BF)
    g_down = jnp.einsum("rf,rd->fd", hidden, grad_branch, preferred_element_type=F32).astype(BF)
    v_down = jnp.sum(grad_branch, axis=0, dtype=F32)
    grad_hidden = jnp.einsum("rd,fd->rf", grad_branch, w_down, preferred_element_type=F32)
    grad_pre = gelu_pull(grad_hidden)[0].astype(BF)
    g_up = jnp.einsum("rd,rf->df", normed_two, grad_pre, preferred_element_type=F32).astype(BF)
    v_up = jnp.sum(grad_pre, axis=0, dtype=F32)
    grad_normed_two = jnp.einsum("rf,df->rd", grad_pre, w_up, preferred_element_type=F32)
    grad_mid, v_gain, v_shift = norm_two_pull(grad_normed_two)
    grad_mid = grad_mid + grad_branch.astype(F32)
    grad_attn = grad_mid.astype(BF)
    g_out = jnp.einsum("rd,re->de", attended_low, grad_attn, preferred_element_type=F32).astype(BF)
    v_out = jnp.sum(grad_attn, axis=0, dtype=F32)
    grad_attended = jnp.einsum("re,de->rd", grad_attn, w_out, preferred_element_type=F32).astype(BF)
    return (
        g_down.reshape(wd.shape), g_up.reshape(wu.shape), g_out.reshape(wo.shape), block_out.reshape(xs.shape),
        grad_attended.reshape(xs.shape), grad_mid.reshape(xs.shape),
        (v_out[None], v_gain[None], v_shift[None], v_up[None], v_down[None]),
    )


def body(
    tokens, cotangent, prefix, ln1_gain, ln1_bias, w_qkv, b_qkv, w_out, b_out,
    ln2_gain, ln2_bias, w_up, b_up, w_down, b_down,
):
    vec = pack_vectors((ln1_gain, ln1_bias, b_qkv, b_out, ln2_gain, ln2_bias, b_up, b_down))
    (wq, wo, wu, wd, _, cots, attl, xs, n1t, qs, qst, k, v, att, lt, vrows) = forward_call(
        prefix, tokens, cotangent, vec, w_qkv, w_out, w_up, w_down)
    g_down, g_up, g_out, bo, ga, gmid, small = middle(wo, wu, wd, cots, attl, xs, vrows)
    block_out, grad_tokens, gq, go, gu, gd, gvec = backward_call(
        prefix, g_down, g_up, g_out, bo, ga, wq.reshape(-1, wq.shape[-1]), n1t, xs, gmid, qs, qst, k, v, att, lt, vrows, *small)
    rows = [gvec[i, :wide] for i, wide in enumerate(WIDTHS)]
    return (
        block_out, grad_tokens, rows[0], rows[1], gq, rows[2], go, rows[3], rows[4], rows[5], gu, rows[6], gd, rows[7],
    )


def fits(mesh):
    return dict(mesh.shape) == {"dp": 8, "seq": 4}


norm_eps = 1e-05
block_rows = 512


def layer_norm(features, gain, shift):
    centre = features - jnp.mean(features, axis=-1, keepdims=True)
    spread = jnp.mean(centre * centre, axis=-1, keepdims=True)
    return centre * lax.rsqrt(spread + norm_eps) * gain + shift


def gelu_tanh(values):
    return jax.nn.gelu(values, approximate=True)


def in_blocks(update, running, pieces):
    length = pieces[0].shape[1]
    blocks = length // block_rows
    blocked_pieces = tuple(
        (
            jnp.swapaxes(
                member.reshape((member.shape[0], blocks, block_rows) + member.shape[2:]), 0, 1
            )
            for member in pieces
        )
    )

    def advance(carried, element):
        return (update(carried, element[0], element[1] * block_rows), None)

    running, unused = lax.scan(
        advance, running, (blocked_pieces, jnp.arange(blocks, dtype=jnp.int32))
    )
    return running


def to_heads(flat_rows):
    return flat_rows.reshape(flat_rows.shape[0], flat_rows.shape[1], HEADS, HEAD_DIM)


def visible_mask(query_places, key_places, prefix_len):
    earlier = key_places[None, None, :] <= query_places[None, :, None]
    in_prefix = key_places[None, None, :] < prefix_len[:, None, None]
    return (earlier | in_prefix)[:, :, None, :]


def head_scores(query_heads, key_flat):
    return jnp.einsum(
        "bqhd,bkhd->bqhk", query_heads, to_heads(key_flat), preferred_element_type=jnp.float32
    ) * HEAD_DIM ** (-0.5)


def attend(query_heads, key_flat, value_flat, prefix_len):
    local_len = query_heads.shape[1]
    query_places = lax.axis_index("seq") * local_len + jnp.arange(local_len, dtype=jnp.int32)
    starting = (
        jnp.zeros(query_heads.shape, jnp.float32),
        jnp.zeros(query_heads.shape[:3], jnp.float32),
        jnp.zeros(query_heads.shape[:3], jnp.float32),
    )

    def update(running, pieces, offset):
        weighted, normaliser, ceiling = running
        key_piece, value_piece = pieces
        key_places = offset + jnp.arange(key_piece.shape[1], dtype=jnp.int32)
        scores = head_scores(query_heads, key_piece)
        visible = visible_mask(query_places, key_places, prefix_len)
        magnitude = jnp.where(visible, jnp.abs(scores), 0.0)
        new_ceiling = jnp.maximum(ceiling, jnp.max(magnitude, axis=-1))
        exponent = jnp.where(visible, jnp.exp(magnitude - new_ceiling[..., None]), 0.0)
        factor = jnp.exp(ceiling - new_ceiling)
        weights = (jnp.sign(scores) * exponent).astype(jnp.bfloat16)
        weighted = weighted * factor[..., None] + jnp.einsum(
            "bqhk,bkhd->bqhd", weights, to_heads(value_piece), preferred_element_type=jnp.float32
        )
        normaliser = normaliser * factor + jnp.sum(exponent, axis=-1)
        return (weighted, normaliser, new_ceiling)

    weighted, normaliser, ceiling = in_blocks(
        update,
        starting,
        (
            lax.all_gather(key_flat, "seq", axis=1, tiled=True),
            lax.all_gather(value_flat, "seq", axis=1, tiled=True),
        ),
    )
    return (weighted / normaliser[..., None], ceiling + jnp.log(normaliser))


def grad_terms(
    query_heads,
    grad_heads,
    key_flat,
    value_flat,
    log_total,
    delta_sum,
    query_places,
    key_places,
    prefix_len,
):
    scores = head_scores(query_heads, key_flat)
    sign_of = jnp.sign(scores)
    visible = visible_mask(query_places, key_places, prefix_len)
    shares = jnp.where(visible, jnp.exp(jnp.abs(scores) - log_total[..., None]), 0.0)
    grad_weights = jnp.einsum(
        "bqhd,bkhd->bqhk", grad_heads, to_heads(value_flat), preferred_element_type=jnp.float32
    )
    grad_scores = (shares * (grad_weights - sign_of * delta_sum[..., None])).astype(jnp.bfloat16)
    return ((sign_of * shares).astype(jnp.bfloat16), grad_scores)


def query_term(grad_scores, key_flat):
    return jnp.einsum(
        "bqhk,bkhd->bqhd", grad_scores, to_heads(key_flat), preferred_element_type=jnp.float32
    ) * HEAD_DIM ** (-0.5)


def key_value_terms(query_heads, grad_heads, shares_low, grad_scores):
    key_term = jnp.einsum(
        "bqhk,bqhd->bkhd", grad_scores, query_heads, preferred_element_type=jnp.float32
    ) * HEAD_DIM ** (-0.5)
    value_term = jnp.einsum(
        "bqhk,bqhd->bkhd", shares_low, grad_heads, preferred_element_type=jnp.float32
    )
    flat_shape = (key_term.shape[0], key_term.shape[1], key_term.shape[2] * key_term.shape[3])
    return jnp.concatenate([key_term.reshape(flat_shape), value_term.reshape(flat_shape)], axis=-1)


def attend_back(query_heads, key_flat, value_flat, grad_heads, log_total, delta_sum, prefix_len):
    seq_block, local_len = (query_heads.shape[0], query_heads.shape[1])
    width = key_flat.shape[2]
    local_places = lax.axis_index("seq") * local_len + jnp.arange(local_len, dtype=jnp.int32)
    starting = (
        jnp.zeros(query_heads.shape, jnp.float32),
        jnp.zeros((seq_block, lax.axis_size("seq") * local_len, 2 * width), jnp.float32),
    )

    def update_both(running, pieces, offset):
        grad_query, grad_keys = running
        key_piece, value_piece = pieces
        piece_len = key_piece.shape[1]
        key_places = offset + jnp.arange(piece_len, dtype=jnp.int32)
        shares_low, grad_scores = grad_terms(
            query_heads,
            grad_heads,
            key_piece,
            value_piece,
            log_total,
            delta_sum,
            local_places,
            key_places,
            prefix_len,
        )
        grad_query = grad_query + query_term(grad_scores, key_piece)
        current = lax.dynamic_slice_in_dim(grad_keys, offset, piece_len, 1)
        updated = current + key_value_terms(query_heads, grad_heads, shares_low, grad_scores)
        return (grad_query, lax.dynamic_update_slice_in_dim(grad_keys, updated, offset, 1))

    grad_query, grad_keys = in_blocks(
        update_both,
        starting,
        (
            lax.all_gather(key_flat, "seq", axis=1, tiled=True),
            lax.all_gather(value_flat, "seq", axis=1, tiled=True),
        ),
    )
    key_local = lax.psum_scatter(
        grad_keys.astype(jnp.bfloat16), "seq", scatter_dimension=1, tiled=True
    ).astype(jnp.float32)
    return (grad_query, key_local)


def forward_block(weights_in, token_part, prefix_len):
    (
        gain_one,
        shift_one,
        w_qkv,
        b_qkv,
        w_out,
        b_out,
        gain_two,
        shift_two,
        w_up,
        b_up,
        w_down,
        b_down,
    ) = weights_in
    seq_block, local_len, width = token_part.shape
    residual_in = token_part.reshape(-1, width).astype(jnp.float32)
    normed_one = layer_norm(
        residual_in, gain_one.astype(jnp.float32), shift_one.astype(jnp.float32)
    ).astype(jnp.bfloat16)
    projected = jnp.dot(normed_one, w_qkv, preferred_element_type=jnp.float32) + b_qkv.astype(
        jnp.float32
    )
    query_heads = (
        projected[:, :width].astype(jnp.bfloat16).reshape(seq_block, local_len, HEADS, HEAD_DIM)
    )
    key_flat = (
        projected[:, width : 2 * width].astype(jnp.bfloat16).reshape(seq_block, local_len, width)
    )
    value_flat = projected[:, 2 * width :].astype(jnp.bfloat16).reshape(seq_block, local_len, width)
    attended, log_total = attend(query_heads, key_flat, value_flat, prefix_len)
    attended_low = attended.reshape(-1, width).astype(jnp.bfloat16)
    residual_mid = (
        residual_in
        + jnp.dot(attended_low, w_out, preferred_element_type=jnp.float32)
        + b_out.astype(jnp.float32)
    )
    normed_two = layer_norm(
        residual_mid, gain_two.astype(jnp.float32), shift_two.astype(jnp.float32)
    ).astype(jnp.bfloat16)
    pre_gelu = jnp.dot(normed_two, w_up, preferred_element_type=jnp.float32) + b_up.astype(
        jnp.float32
    )
    hidden = gelu_tanh(pre_gelu).astype(jnp.bfloat16)
    result = (
        residual_mid
        + jnp.dot(hidden, w_down, preferred_element_type=jnp.float32)
        + b_down.astype(jnp.float32)
    )
    saved = (
        residual_in,
        normed_one,
        query_heads,
        key_flat,
        value_flat,
        attended,
        log_total,
        attended_low,
        residual_mid,
        normed_two,
        pre_gelu,
        hidden,
    )
    return (result.astype(jnp.bfloat16).reshape(token_part.shape), saved)


def backward_block(weights_in, saved, grad_part, prefix_len):
    (
        gain_one,
        shift_one,
        w_qkv,
        b_qkv,
        w_out,
        b_out,
        gain_two,
        shift_two,
        w_up,
        b_up,
        w_down,
        b_down,
    ) = weights_in
    (
        residual_in,
        normed_one,
        query_heads,
        key_flat,
        value_flat,
        attended,
        log_total,
        attended_low,
        residual_mid,
        normed_two,
        pre_gelu,
        hidden,
    ) = saved
    seq_block, local_len, width = grad_part.shape
    grad_result = grad_part.reshape(-1, width).astype(jnp.float32)
    grad_branch = grad_part.reshape(-1, width)
    grads_down = jnp.einsum("rf,rd->fd", hidden, grad_branch, preferred_element_type=jnp.float32)
    bias_down = jnp.sum(grad_branch, axis=0, dtype=jnp.float32)
    grad_hidden = jnp.einsum("rd,fd->rf", grad_branch, w_down, preferred_element_type=jnp.float32)
    gelu_pull = jax.vjp(gelu_tanh, pre_gelu)[1]
    grad_pre = gelu_pull(grad_hidden)[0].astype(jnp.bfloat16)
    grads_up = jnp.einsum("rd,rf->df", normed_two, grad_pre, preferred_element_type=jnp.float32)
    bias_up = jnp.sum(grad_pre, axis=0, dtype=jnp.float32)
    grad_normed_two = jnp.einsum("rf,df->rd", grad_pre, w_up, preferred_element_type=jnp.float32)
    norm_two_pull = jax.vjp(
        layer_norm, residual_mid, gain_two.astype(jnp.float32), shift_two.astype(jnp.float32)
    )[1]
    grad_mid, grads_gain_two, grads_shift_two = norm_two_pull(grad_normed_two)
    grad_mid = grad_mid + grad_result
    grad_attn = grad_mid.astype(jnp.bfloat16)
    grads_out = jnp.einsum("rd,re->de", attended_low, grad_attn, preferred_element_type=jnp.float32)
    bias_out = jnp.sum(grad_attn, axis=0, dtype=jnp.float32)
    grad_heads = (
        jnp.einsum("re,de->rd", grad_attn, w_out, preferred_element_type=jnp.float32)
        .astype(jnp.bfloat16)
        .reshape(seq_block, local_len, HEADS, HEAD_DIM)
    )
    delta_sum = jnp.sum(grad_heads.astype(jnp.float32) * attended, axis=-1)
    grad_query, key_local = attend_back(
        query_heads, key_flat, value_flat, grad_heads, log_total, delta_sum, prefix_len
    )
    grad_proj = jnp.concatenate(
        [grad_query.reshape(-1, width), key_local.reshape(-1, 2 * width)], axis=1
    ).astype(jnp.bfloat16)
    grads_qkv = jnp.einsum("rd,re->de", normed_one, grad_proj, preferred_element_type=jnp.float32)
    bias_qkv = jnp.sum(grad_proj, axis=0, dtype=jnp.float32)
    grad_normed_one = jnp.einsum("re,de->rd", grad_proj, w_qkv, preferred_element_type=jnp.float32)
    norm_one_pull = jax.vjp(
        layer_norm, residual_in, gain_one.astype(jnp.float32), shift_one.astype(jnp.float32)
    )[1]
    grad_in, grads_gain_one, grads_shift_one = norm_one_pull(grad_normed_one)
    grad_in = grad_in + grad_mid
    weight_grads = (
        grads_gain_one,
        grads_shift_one,
        grads_qkv,
        bias_qkv,
        grads_out,
        bias_out,
        grads_gain_two,
        grads_shift_two,
        grads_up,
        bias_up,
        grads_down,
        bias_down,
    )
    return (grad_in.astype(jnp.bfloat16).reshape(grad_part.shape), weight_grads)


def general_body(
    tokens,
    cotangent,
    prefix,
    ln1_gain,
    ln1_bias,
    w_qkv,
    b_qkv,
    w_out,
    b_out,
    ln2_gain,
    ln2_bias,
    w_up,
    b_up,
    w_down,
    b_down,
):
    shards = (
        ln1_gain,
        ln1_bias,
        w_qkv,
        b_qkv,
        w_out,
        b_out,
        ln2_gain,
        ln2_bias,
        w_up,
        b_up,
        w_down,
        b_down,
    )
    spread_count = lax.axis_size(("dp", "seq"))
    totals = tuple(
        (
            jnp.zeros((member.shape[0] * spread_count,) + member.shape[1:], jnp.float32)
            for member in shards
        )
    )
    seq_block = tokens.shape[0] // MB
    outputs = []
    grad_inputs = []
    for batch_index in range(MB):
        first_row = batch_index * seq_block
        token_part = tokens[first_row : first_row + seq_block]
        cotangent_part = cotangent[first_row : first_row + seq_block]
        prefix_part = prefix[first_row : first_row + seq_block]
        forward_weights = (
            lax.all_gather(shards[0], ("dp", "seq"), axis=0, tiled=True),
            lax.all_gather(shards[1], ("dp", "seq"), axis=0, tiled=True),
            lax.all_gather(shards[2], ("dp", "seq"), axis=0, tiled=True),
            lax.all_gather(shards[3], ("dp", "seq"), axis=0, tiled=True),
            lax.all_gather(shards[4], ("dp", "seq"), axis=0, tiled=True),
            lax.all_gather(shards[5], ("dp", "seq"), axis=0, tiled=True),
            lax.all_gather(shards[6], ("dp", "seq"), axis=0, tiled=True),
            lax.all_gather(shards[7], ("dp", "seq"), axis=0, tiled=True),
            lax.all_gather(shards[8], ("dp", "seq"), axis=0, tiled=True),
            lax.all_gather(shards[9], ("dp", "seq"), axis=0, tiled=True),
            lax.all_gather(shards[10], ("dp", "seq"), axis=0, tiled=True),
            lax.all_gather(shards[11], ("dp", "seq"), axis=0, tiled=True),
        )
        result, saved = forward_block(forward_weights, token_part, prefix_part)
        back_weights = (
            lax.all_gather(shards[0], ("dp", "seq"), axis=0, tiled=True),
            lax.all_gather(shards[1], ("dp", "seq"), axis=0, tiled=True),
            lax.all_gather(shards[2], ("dp", "seq"), axis=0, tiled=True),
            lax.all_gather(shards[3], ("dp", "seq"), axis=0, tiled=True),
            lax.all_gather(shards[4], ("dp", "seq"), axis=0, tiled=True),
            lax.all_gather(shards[5], ("dp", "seq"), axis=0, tiled=True),
            lax.all_gather(shards[6], ("dp", "seq"), axis=0, tiled=True),
            lax.all_gather(shards[7], ("dp", "seq"), axis=0, tiled=True),
            lax.all_gather(shards[8], ("dp", "seq"), axis=0, tiled=True),
            lax.all_gather(shards[9], ("dp", "seq"), axis=0, tiled=True),
            lax.all_gather(shards[10], ("dp", "seq"), axis=0, tiled=True),
            lax.all_gather(shards[11], ("dp", "seq"), axis=0, tiled=True),
        )
        grad_piece, weight_grads = backward_block(back_weights, saved, cotangent_part, prefix_part)
        totals = tuple(
            (running_sum + new_term for running_sum, new_term in zip(totals, weight_grads))
        )
        outputs.append(result)
        grad_inputs.append(grad_piece)
    reduced = (
        lax.psum_scatter(totals[0], ("dp", "seq"), scatter_dimension=0, tiled=True),
        lax.psum_scatter(totals[1], ("dp", "seq"), scatter_dimension=0, tiled=True),
        lax.psum_scatter(totals[2], ("dp", "seq"), scatter_dimension=0, tiled=True),
        lax.psum_scatter(totals[3], ("dp", "seq"), scatter_dimension=0, tiled=True),
        lax.psum_scatter(totals[4], ("dp", "seq"), scatter_dimension=0, tiled=True),
        lax.psum_scatter(totals[5], ("dp", "seq"), scatter_dimension=0, tiled=True),
        lax.psum_scatter(totals[6], ("dp", "seq"), scatter_dimension=0, tiled=True),
        lax.psum_scatter(totals[7], ("dp", "seq"), scatter_dimension=0, tiled=True),
        lax.psum_scatter(totals[8], ("dp", "seq"), scatter_dimension=0, tiled=True),
        lax.psum_scatter(totals[9], ("dp", "seq"), scatter_dimension=0, tiled=True),
        lax.psum_scatter(totals[10], ("dp", "seq"), scatter_dimension=0, tiled=True),
        lax.psum_scatter(totals[11], ("dp", "seq"), scatter_dimension=0, tiled=True),
    )
    return (
        jnp.concatenate(outputs, axis=0),
        jnp.concatenate(grad_inputs, axis=0),
        reduced[0],
        reduced[1],
        reduced[2],
        reduced[3],
        reduced[4],
        reduced[5],
        reduced[6],
        reduced[7],
        reduced[8],
        reduced[9],
        reduced[10],
        reduced[11],
    )


def solution(mesh):
    in_specs = (
        P("dp", "seq", None),
        P("dp", "seq", None),
        P("dp"),
        P(("dp", "seq")),
        P(("dp", "seq")),
        P(("dp", "seq"), None),
        P(("dp", "seq")),
        P(("dp", "seq"), None),
        P(("dp", "seq")),
        P(("dp", "seq")),
        P(("dp", "seq")),
        P(("dp", "seq"), None),
        P(("dp", "seq")),
        P(("dp", "seq"), None),
        P(("dp", "seq")),
    )
    out_specs = (
        P("dp", "seq", None),
        P("dp", "seq", None),
        P(("dp", "seq")),
        P(("dp", "seq")),
        P(("dp", "seq"), None),
        P(("dp", "seq")),
        P(("dp", "seq"), None),
        P(("dp", "seq")),
        P(("dp", "seq")),
        P(("dp", "seq")),
        P(("dp", "seq"), None),
        P(("dp", "seq")),
        P(("dp", "seq"), None),
        P(("dp", "seq")),
    )
    chosen = body if fits(mesh) else general_body
    return jax.shard_map(chosen, mesh=mesh, in_specs=in_specs, out_specs=out_specs, check_vma=False)
```

```python
import jax
import jax.numpy as jnp
from jax import lax
from jax.experimental import pallas as pl
from jax.experimental.pallas import tpu as pltpu
from jax.sharding import PartitionSpec as P

HEADS = 12
HEAD_DIM = 64
MB = 2

F32 = jnp.float32
BF = jnp.bfloat16
EPS = 1e-05
MESH = pl.DeviceIdType.MESH
NEG = -1e30
ANY = pl.BlockSpec(memory_space=pl.ANY)
VM = pl.BlockSpec(memory_space=pltpu.VMEM)
SM = pl.BlockSpec(memory_space=pltpu.SMEM)
WIDTHS = (24, 24, 72, 24, 24, 24, 96, 24)
D = 768
FF = 3072
THIRD = 384
LAST = (((1,), (1,)), ((), ()))
FIRST = (((0,), (0,)), ((), ()))
ALL = slice(None)
REMOTES = 128
LOCALS = 64


def places():
    dp = lax.axis_index("dp")
    sq = lax.axis_index("seq")
    return dp // 2, dp % 2, sq // 2, sq % 2


def device(z, x, y, c):
    return (z * 2 + x, y * 2 + c)


def owner_of(wide):
    column = lax.broadcasted_iota(jnp.int32, (1, 32 * wide), 1).astype(F32)
    owner = jnp.floor((column + 0.5) * (1.0 / wide))
    return owner.astype(jnp.int32), (column - owner * wide).astype(jnp.int32)


def spread_row(gathered, index, wide):
    total = 32 * wide
    row = lax.broadcasted_iota(jnp.int32, (32, 256), 0)
    place = lax.broadcasted_iota(jnp.int32, (32, 256), 1)
    pick = jnp.where(place == row * 8 + index, 1.0, 0.0).astype(BF)
    mine = jnp.dot(pick, gathered, preferred_element_type=F32).astype(BF)
    owner, rest = owner_of(wide)
    spread = jnp.where(lax.broadcasted_iota(jnp.int32, (128, total), 0) == rest, 1.0, 0.0).astype(BF)
    full = jnp.dot(mine, spread, preferred_element_type=F32)
    keep = lax.broadcasted_iota(jnp.int32, (32, total), 0) == owner
    return jnp.sum(jnp.where(keep, full, 0.0), axis=0, keepdims=True)


def collect_rows(vector, wide):
    total = 32 * wide
    owner, rest = owner_of(wide)
    gather = jnp.where(lax.broadcasted_iota(jnp.int32, (128, total), 0) == rest, 1.0, 0.0).astype(BF)
    keep = lax.broadcasted_iota(jnp.int32, (32, total), 0) == owner
    high = vector.astype(BF).astype(F32)
    out = None
    for part in (high, vector - high):
        placed = jnp.where(keep, part, 0.0).astype(BF)
        term = lax.dot_general(placed, gather, LAST, preferred_element_type=F32)
        out = term if out is None else out + term
    return out


def add_into(ref, at, other):
    ref[at] = (ref[at].astype(F32) + other.astype(F32)).astype(BF)


def start(copies):
    for copy in copies:
        copy.start()


def arrive(copies):
    for copy in copies:
        copy.wait_recv()


def landed(copies):
    for copy in copies:
        copy.wait()


def lanes(first, count=128):
    return pl.ds(pl.multiple_of(first, 128), count)


def rows_at(first, count, step=256):
    return pl.ds(pl.multiple_of(first, step), count)


class Links:
    def __init__(self, ssem, rsem, lsem):
        self.ssem, self.rsem, self.lsem = ssem, rsem, lsem
        self.remotes = self.locals = 0
        self.sent = []
        z, x, y, c = places()
        self.z, self.x, self.y, self.c = z, x, y, c
        self.x2, self.y2, self.c2 = 1 - x, 1 - y, 1 - c
        self.px, self.py, self.pc = device(z, 1 - x, y, c), device(z, x, 1 - y, c), device(z, x, y, 1 - c)
        self.zs = [lax.rem(z + d, 4) for d in (1, 2, 3)]
        self.pz = [device(zz, x, y, c) for zz in self.zs]

    def fresh(self, count=1):
        first = self.remotes
        self.remotes += count
        return first

    def remote(self, src, dst, dev, at=None):
        i = self.fresh() if at is None else at
        copy = pltpu.make_async_remote_copy(
            src_ref=src, dst_ref=dst, send_sem=self.ssem.at[i], recv_sem=self.rsem.at[i],
            device_id=dev, device_id_type=MESH)
        if at is None:
            self.sent.append(copy)
        return copy

    def local(self, src, dst):
        i = self.locals
        self.locals += 1
        return pltpu.make_async_copy(src, dst, self.lsem.at[i])

    def greet(self):
        barrier = pltpu.get_barrier_semaphore()
        for dev in [self.px, self.py, self.pc] + self.pz:
            pl.semaphore_signal(barrier, inc=1, device_id=dev, device_id_type=MESH)
        pl.semaphore_wait(barrier, 6)


class Gather:
    def __init__(self, links, shard, full, cut, kinds=None):
        k = links
        self.k, self.full, self.kinds = k, full, kinds
        rows = shard.shape[0]
        own = pl.ds(pl.multiple_of(k.c * rows, 8), rows)
        mine = full if kinds else full.at[k.c]
        theirs = full if kinds else full.at[k.c2]
        half = full.shape[-1]
        z, x, y = k.z, k.x, k.y
        if kinds:
            self.own, self.c0 = [], []
            for kind in range(kinds):
                there = pl.ds(kind * THIRD, THIRD)
                self.own.append(k.local(shard.at[:, lanes(kind * D + k.c * THIRD, THIRD)], mine.at[z, x, y, own, there]))
                self.c0.append(k.remote(shard.at[:, lanes(kind * D + k.c2 * THIRD, THIRD)],
                                        theirs.at[z, x, y, own, there], k.pc))
        else:
            self.own = [k.local(shard.at[:, lanes(k.c * half, half)], mine.at[z, x, y, own])]
            self.c0 = [k.remote(shard.at[:, lanes(k.c2 * half, half)], theirs.at[z, x, y, own], k.pc)]
        self.c1 = [k.remote(mine.at[z, x, y], mine.at[z, x, y], dev) for dev in k.pz]
        a, b = slice(0, cut), slice(cut, None)
        self.c2 = [k.remote(mine.at[:, x, y, :, a], mine.at[:, x, y, :, a], k.px),
                   k.remote(mine.at[:, x, y, :, b], mine.at[:, x, y, :, b], k.py)]
        self.c3 = [k.remote(mine.at[:, :, y, :, a], mine.at[:, :, y, :, a], k.py),
                   k.remote(mine.at[:, x, :, :, b], mine.at[:, x, :, :, b], k.px)]
        self.c4 = [] if kinds else [k.remote(full.at[k.c], full.at[k.c], k.pc)]

    def s0(self):
        start(self.own)
        start(self.c0)

    def s1(self):
        landed(self.own)
        arrive(self.c0)
        start(self.c1)

    def s2(self):
        arrive(self.c1)
        start(self.c2)

    def s3(self):
        arrive(self.c2)
        start(self.c3)

    def s4(self):
        arrive(self.c3)
        start(self.c4)

    def done(self):
        arrive(self.c4)


class Scatter:
    def __init__(self, links, grad, r0, r1a, r1b, r2a, r2b, r3, tot, fin, put, cut, base=None, whole=True):
        k = links
        self.k, self.grad, self.whole, self.put = k, grad, whole, put
        self.r0, self.r1a, self.r1b, self.r2a, self.r2b, self.r3, self.tot, self.fin = r0, r1a, r1b, r2a, r2b, r3, tot, fin
        self.mine = grad.at[k.c] if whole else grad
        self.a = (ALL, slice(0, cut))
        self.b = (ALL, slice(cut, None))
        x, y, x2, y2 = k.x, k.y, k.x2, k.y2
        at = iter([None] * 10 if base is None else base)
        mine = self.mine
        self.c0 = [k.remote(grad.at[k.c2], r0, k.pc, next(at))] if whole else []
        self.c1 = [k.remote(mine.at[(ALL, ALL, y2) + self.a], r1a, k.py, next(at)),
                   k.remote(mine.at[(ALL, x2, ALL) + self.b], r1b, k.px, next(at))]
        self.c2 = [k.remote(mine.at[(ALL, x2, y) + self.a], r2a, k.px, next(at)),
                   k.remote(mine.at[(ALL, x, y2) + self.b], r2b, k.py, next(at))]
        self.c3 = [k.remote(mine.at[k.zs[d], x, y], r3.at[d], k.pz[d], next(at)) for d in range(3)]
        self.c4 = [k.remote(tot.at[k.c2], fin, k.pc, next(at))]

    def at(self, place):
        return ((self.k.c,) if self.whole else ()) + place

    def s0(self):
        start(self.c0)

    def s1(self):
        if self.whole:
            arrive(self.c0)

            def add(i, carry):
                where = (i // 4, lax.rem(i // 2, 2), lax.rem(i, 2))
                add_into(self.grad, self.at(where), self.r0[where])
                return carry

            lax.fori_loop(0, 16, add, 0)
        start(self.c1)

    def s2(self):
        arrive(self.c1)
        k = self.k

        def add(i, carry):
            zz, other = i // 2, lax.rem(i, 2)
            add_into(self.grad, self.at((zz, other, k.y) + self.a), self.r1a[zz, other])
            add_into(self.grad, self.at((zz, k.x, other) + self.b), self.r1b[zz, other])
            return carry

        lax.fori_loop(0, 8, add, 0)
        start(self.c2)

    def s3(self):
        arrive(self.c2)
        k = self.k

        def add(zz, carry):
            add_into(self.grad, self.at((zz, k.x, k.y) + self.a), self.r2a[zz])
            add_into(self.grad, self.at((zz, k.x, k.y) + self.b), self.r2b[zz])
            return carry

        lax.fori_loop(0, 4, add, 0)
        start(self.c3)

    def s4(self):
        arrive(self.c3)
        k = self.k
        total = self.mine[k.z, k.x, k.y].astype(F32)
        for d in range(3):
            total = total + self.r3[d].astype(F32)
        rows = total.shape[0] // 2
        self.tot[0] = total[:rows]
        self.tot[1] = total[rows:]
        start(self.c4)
        self.put(self.tot[k.c], k.c)

    def s5(self):
        arrive(self.c4)
        self.put(self.fin[...], self.k.c2)

    def gone(self):
        for copy in self.c0 + self.c1 + self.c2 + self.c3 + self.c4:
            copy.wait_send()


def gelu_parts(value):
    rate = 0.7978845608028654
    bent = jnp.tanh(rate * (value + 0.044715 * (value * value * value)))
    result = 0.5 * value * (1.0 + bent)
    slope = 0.5 * (1.0 + bent) + 0.5 * value * (1.0 - bent * bent) * (rate * (1.0 + 0.134145 * (value * value)))
    return result, slope


def unit_rows(rows):
    centre = rows - jnp.mean(rows, axis=-1, keepdims=True)
    scale = lax.rsqrt(jnp.mean(centre * centre, axis=-1, keepdims=True) + EPS)
    return centre * scale, scale


def norm_back(grad, normed, scale):
    return scale * (grad - jnp.mean(grad, axis=-1, keepdims=True)
                    - normed * jnp.mean(grad * normed, axis=-1, keepdims=True))


def layer_kernel(
    prefix, tok, cot, vec_s, wq_s, wo_s, wu_s, wd_s,
    out_bo, out_gt, out_q, out_o, out_u, out_d, out_vec,
    wq, wo, wu, wd, gv, k_qs, k_qst, k_k, k_v, k_att, k_n1t,
    gvm, tok_all, vrows, wom, al_send, al, cotm, ga_send, ga_all, fa, fb, fc, fr, lt,
    gd, gu, go, gq,
    r0d, r0u, r0o, r1ad, r1bd, r1au, r1bu, r1ao, r1bo, r2ad, r2bd, r2au, r2bu, r2ao, r2bo, r3d, r3u, r3o,
    td, tu, to, fd, fu, fo,
    q1a, q1b, q2a, q2b, q3, tq, fq,
    vs, vbq, vup, vtab, vr0, vr1, vr2, vr3,
    ssem, rsem, lsem,
):
    k = Links(ssem, rsem, lsem)
    bo, gtb = al, cotm
    z, x, y, c, x2, y2, c2 = k.z, k.x, k.y, k.c, k.x2, k.y2, k.c2
    k.greet()
    vmem = pltpu.VMEM

    gather_q = Gather(k, wq_s, wq, 512, 3)
    gather_o = Gather(k, wo_s, wo, 256)
    gather_u = Gather(k, wu_s, wu, 768)
    gather_d = Gather(k, wd_s, wd, 128)
    own_vec = k.local(vec_s, gv.at[z, x, y, c])
    vec_c = k.remote(vec_s, gv.at[z, x, y, c], k.pc)
    own_vec.start()
    vec_c.start()
    own_tok = k.local(tok.at[y], tok_all.at[y, c])
    tok_y = k.remote(tok.at[y2], tok_all.at[y, c], k.py)
    own_tok.start()
    tok_y.start()
    gather_q.s0()
    own_cot = k.local(cot.at[y], cotm.at[y])
    cot_y = k.remote(cot.at[y2], cotm.at[y], k.py)
    own_vec.wait()
    vec_c.wait_recv()
    vec_z = [k.remote(gv.at[z, x, y], gv.at[z, x, y], dev) for dev in k.pz]
    start(vec_z)
    gather_q.s1()
    gather_o.s0()
    gather_u.s0()
    gather_d.s0()
    own_tok.wait()
    tok_y.wait_recv()
    tok_c = k.remote(tok_all.at[:, c], tok_all.at[:, c], k.pc)
    tok_c.start()
    own_cot.start()
    cot_y.start()
    arrive(vec_z)
    vec_x = k.remote(gv.at[:, x, y], gv.at[:, x, y], k.px)
    vec_x.start()
    vec_x.wait_recv()
    vec_y = k.remote(gv.at[:, :, y], gv.at[:, :, y], k.py)
    vec_y.start()
    tok_c.wait_recv()
    vec_y.wait_recv()
    table = k.local(gv, gvm)
    table.start()
    table.wait()
    table = gvm[...].reshape(256, 128)
    for index, wide in enumerate(WIDTHS):
        vrows[index : index + 1, 0 : 32 * wide] = spread_row(table, index, wide)

    mine_cols = lanes(c * THIRD, THIRD)
    peer_cols = lanes(c2 * THIRD, THIRD)
    al_own = k.local(al_send.at[:, c], al.at[:, :, mine_cols])
    al_c = k.remote(al_send.at[:, c2], al.at[:, :, mine_cols], k.pc)
    limit = prefix[y] - 1
    sub = lax.broadcasted_iota(jnp.int32, (128, 256), 0)

    def forward(n1, n1t, vt, qs, qst, keys_ref, values_ref, att, wqm):
        gain = vrows[0:1, 0:D]
        shift = vrows[1:2, 0:D]

        def norm_block(b, carry):
            normed, _ = unit_rows(tok_all[b // 2, lax.rem(b, 2)].astype(F32))
            normed = (normed * gain + shift).astype(BF)
            at = rows_at(b * 256, 256)
            n1[at, :] = normed
            n1t[:, at] = normed.astype(F32).T.astype(BF)
            return carry

        lax.fori_loop(0, 4, norm_block, 0)
        keep_n1t = k.local(n1t, k_n1t)
        keep_n1t.start()
        gather_q.s2()
        gather_o.s1()
        gather_u.s1()
        gather_q.s3()
        gather_o.s2()
        gather_q.s4()
        load_q = k.local(wq.reshape(D, 3 * THIRD), wqm)
        load_q.start()
        load_q.wait()

        def project(b, carry):
            rows = rows_at(b * 256, 256)
            block = n1[rows, :]
            parts = []
            for kind in range(3):
                bias = vrows[2:3, lanes(kind * D + c * THIRD, THIRD)]
                value = jnp.dot(block, wqm[:, kind * THIRD : (kind + 1) * THIRD], preferred_element_type=F32)
                parts.append((value + bias).astype(BF))
            queries = parts[0].astype(F32) * 0.125
            qs[rows, :] = queries.astype(BF)
            qst[:, rows] = queries.T.astype(BF)
            keys_ref[rows, :] = parts[1]
            values_ref[rows, :] = parts[2]
            vt[:, rows] = parts[2].astype(F32).T.astype(BF)
            return carry

        lax.fori_loop(0, 4, project, 0)
        keep = [k.local(qs, k_qs), k.local(qst, k_qst), k.local(keys_ref, k_k), k.local(values_ref, k_v)]
        start(keep)
        gather_u.s2()
        gather_d.s1()

        def attend(block):
            rows = min(4, max(block + 1, 2)) * 256
            qcols = pl.ds(block * 256, 256)

            def unit(u, carry):
                cols = lanes(u * 128)
                keys = keys_ref[0:rows, cols]
                queries = qst[cols, qcols]
                qpos = block * 256 + lax.broadcasted_iota(jnp.int32, (1, 256), 1)
                seen = lax.broadcasted_iota(jnp.int32, (rows, 256), 0) <= jnp.maximum(qpos, limit)
                for half in range(2):
                    chosen = jnp.where(sub // 64 == half, queries, jnp.zeros_like(queries))
                    scores = jnp.dot(keys, chosen, preferred_element_type=F32)
                    size = jnp.where(seen, jnp.abs(scores), NEG)
                    top = jnp.max(size, axis=0, keepdims=True)
                    exponent = jnp.exp(size - top)
                    total = jnp.sum(exponent, axis=0, keepdims=True)
                    weights = jnp.where(scores > 0, exponent, jnp.where(scores < 0, -exponent, 0.0)).astype(BF)
                    at = pl.ds(pl.multiple_of(u * 128 + half * 64, 64), 64)
                    att[at, qcols] = jnp.dot(vt[at, 0:rows], weights, preferred_element_type=F32) / total
                    lt[pl.ds(u * 2 + half, 1), qcols] = top + jnp.log(total)
                al_send[block // 2, block % 2, :, cols] = att[cols, qcols].T.astype(BF)
                return carry

            lax.fori_loop(0, 3, unit, 0)

        attend(3)
        gather_o.s3()
        attend(2)
        gather_u.s3()
        attend(1)
        gather_o.s4()
        attend(0)
        al_own.start()
        al_c.start()
        keep_att = k.local(att, k_att)
        keep_att.start()
        gather_o.done()
        load_o = k.local(wo.reshape(2, D, THIRD), wom)
        load_o.start()
        gather_d.s2()
        al_own.wait()
        al_c.wait_recv()
        load_o.wait()
        landed(keep + [keep_n1t, keep_att])

    pl.run_scoped(
        forward, vmem((1024, D), BF), vmem((D, 1024), BF), vmem((THIRD, 1024), BF), vmem((1024, THIRD), BF),
        vmem((THIRD, 1024), BF), vmem((1024, THIRD), BF), vmem((1024, THIRD), BF), vmem((THIRD, 1024), F32), vmem((D, 1152), BF))

    def put_to(out, half):
        def put(value, core):
            out[:, lanes(core * half, half)] = value
        return put

    down = Scatter(k, gd, r0d, r1ad, r1bd, r2ad, r2bd, r3d, td, fd, put_to(out_d, THIRD), 128)
    up = Scatter(k, gu, r0u, r1au, r1bu, r2au, r2bu, r3u, tu, fu, put_to(out_u, 1536), 768)
    outp = Scatter(k, go, r0o, r1ao, r1bo, r2ao, r2bo, r3o, to, fo, put_to(out_o, THIRD), 256)

    def middle(wbuf, wdb, hid, slope, n2, n2t, alt, gpc):
        b_out, gain, shift = vrows[3:4, 0:D], vrows[4:5, 0:D], vrows[5:6, 0:D]

        def begin(yy, carry):
            rows = rows_at(yy * 256, 256)
            branch = jnp.concatenate([jnp.dot(al[yy], wom[h], preferred_element_type=F32) for h in range(2)], axis=1)
            residual = tok_all[yy, c].astype(F32) + branch + b_out
            fa[yy] = residual
            normed, _ = unit_rows(residual)
            normed = (normed * gain + shift).astype(BF)
            n2[rows, :] = normed
            n2t[:, rows] = normed.astype(F32).T.astype(BF)
            alt[:, rows] = al[yy].astype(F32).T.astype(BF)
            return carry

        lax.fori_loop(0, 2, begin, 0)
        own_cot.wait()
        cot_y.wait_recv()

        wu2 = wu.reshape(2, D, 1536)
        wd2 = wd.reshape(2, FF, THIRD)

        def chunk(j, first, second):
            h = first if j < 2 else second
            return h, j % 2

        def up_load(j, slot, order):
            h, part = chunk(j, *order)
            return k.local(wu2.at[h, :, part * D : (part + 1) * D], wbuf.at[slot])

        def down_load(j, slot, order):
            h, part = chunk(j, *order)
            return k.local(wd2.at[:, rows_at(h * 1536 + part * D, D), :], wdb.at[slot])

        forth = (c, c2)
        gather_u.s4()
        loads = [up_load(j, j % 2, forth) for j in range(4)]
        loads[0].start()
        for j in range(4):
            if j == 1:
                gather_u.done()
            if j < 3:
                loads[j + 1].start()
            loads[j].wait()
            h, part = chunk(j, *forth)
            cols = lanes(h * 1536 + part * D, D)

            def ahead(yy, carry):
                rows = rows_at(yy * 256, 256)
                value = jnp.dot(n2[rows, :], wbuf[j % 2], preferred_element_type=F32) + vrows[6:7, cols]
                result, bend = gelu_parts(value)
                hid[rows, cols] = result.astype(BF)
                slope[rows, cols] = bend
                return carry

            lax.fori_loop(0, 2, ahead, 0)
        gather_d.s3()

        vs[7:8, :] = jnp.sum(cotm[0].astype(F32), axis=0, keepdims=True) + jnp.sum(
            cotm[1].astype(F32), axis=0, keepdims=True)

        def down_grad(i, carry):
            total = jnp.zeros((THIRD, D), F32)
            for yy in range(2):
                total += lax.dot_general(hid[yy * 256 : (yy + 1) * 256, lanes(i * THIRD, THIRD)], cotm[yy], FIRST,
                                         preferred_element_type=F32)
            zz, xx = i // 2, lax.rem(i, 2)
            for yy in range(2):
                for h in range(2):
                    gd[h, zz, xx, yy] = total[yy * 192 : (yy + 1) * 192, h * THIRD : (h + 1) * THIRD].astype(BF)
            return carry

        lax.fori_loop(0, 8, down_grad, 0)
        down.s0()
        fb[...] = jnp.zeros_like(fb)
        fc[...] = jnp.zeros_like(fc)
        vup[...] = jnp.zeros_like(vup)
        gather_d.s4()
        back = (c2, c)
        again = [up_load(j, j % 2, back) for j in range(4)]
        lower = [down_load(j, j % 2, back) for j in range(4)]
        again[0].start()
        down.s1()
        gather_d.done()
        lower[0].start()
        for j in range(4):
            slot = j % 2
            if j < 3:
                again[j + 1].start()
                lower[j + 1].start()
            again[j].wait()
            lower[j].wait()
            h, part = chunk(j, *back)
            cols = lanes(h * 1536 + part * D, D)

            def behind(yy, carry):
                rows = rows_at(yy * 256, 256)
                units = hid[rows, cols]
                grad = None
                for side in range(2):
                    there = slice(side * THIRD, (side + 1) * THIRD)
                    fc[yy, :, there] += jnp.dot(units, wdb[slot, side], preferred_element_type=F32)
                    term = lax.dot_general(cotm[yy, :, there], wdb[slot, side], LAST, preferred_element_type=F32)
                    grad = term if grad is None else grad + term
                grad = (grad * slope[rows, cols]).astype(BF)
                gpc[rows, :] = grad
                vup[0:1, cols] += jnp.sum(grad.astype(F32), axis=0, keepdims=True)
                fb[yy] += lax.dot_general(grad, wbuf[slot], LAST, preferred_element_type=F32)
                return carry

            lax.fori_loop(0, 2, behind, 0)

            def up_grad(zz, carry):
                total = jnp.dot(n2t[rows_at(zz * 192, 192, 64), :], gpc[...], preferred_element_type=F32)
                for i in range(4):
                    gu[h, zz, i // 2, i % 2, :, part * D : (part + 1) * D] = total[i * 48 : (i + 1) * 48].astype(BF)
                return carry

            lax.fori_loop(0, 4, up_grad, 0)
            if j == 1:
                up.s0()
        bo[...] = (fa[...] + fc[...] + vrows[7:8, 0:D].reshape(1, 1, D)).astype(BF)
        up.s1()

        vs[3:6, :] = jnp.zeros((3, D), F32)

        def mid_back(yy, carry):
            rows = rows_at(yy * 256, 256)
            normed, scale = unit_rows(fa[yy])
            grad = fb[yy]
            vs[4:5, :] += jnp.sum(grad * normed, axis=0, keepdims=True)
            vs[5:6, :] += jnp.sum(grad, axis=0, keepdims=True)
            total = cotm[yy].astype(F32) + norm_back(grad * gain, normed, scale)
            fa[yy] = total
            low = total.astype(BF)
            vs[3:4, :] += jnp.sum(low.astype(F32), axis=0, keepdims=True)
            gpc[rows, :] = low
            heads = None
            for side in range(2):
                term = lax.dot_general(low[:, side * THIRD : (side + 1) * THIRD], wom[side], LAST,
                                       preferred_element_type=F32)
                heads = term if heads is None else heads + term
            ga_send[yy] = heads.astype(BF)
            ga_all[yy, c] = ga_send[yy, :, mine_cols]
            return carry

        lax.fori_loop(0, 2, mid_back, 0)
        ga_c.start()

        def out_grad(zz, carry):
            total = jnp.dot(alt[rows_at(zz * 192, 192, 64), :], gpc[...], preferred_element_type=F32)
            for i in range(4):
                for h in range(2):
                    go[h, zz, i // 2, i % 2] = total[i * 48 : (i + 1) * 48, h * THIRD : (h + 1) * THIRD].astype(BF)
            return carry

        lax.fori_loop(0, 4, out_grad, 0)
        outp.s0()

    ga_c = k.remote(ga_send.at[:, :, peer_cols], ga_all.at[:, c], k.pc)
    pl.run_scoped(
        middle, vmem((2, D, D), BF), vmem((2, 2, D, THIRD), BF), vmem((512, FF), BF), vmem((512, FF), F32),
        vmem((512, D), BF), vmem((D, 512), BF), vmem((D, 512), BF), vmem((512, D), BF))

    bo_own = k.local(bo.at[y], out_bo.at[y])
    bo_y = k.remote(bo.at[y2], out_bo.at[y], k.py)
    bo_own.start()
    bo_y.start()

    def put_q(u):
        def put(value, core):
            for kind in range(3):
                out_q[:, lanes(kind * D + core * THIRD + u * 128)] = value[:, kind * 128 : (kind + 1) * 128]
        return put

    bases = [k.fresh(3) for _ in range(8)]

    def query_scatter(u):
        return Scatter(k, gq.at[u], None, q1a.at[u], q1b.at[u], q2a.at[u], q2b.at[u], q3.at[u], tq.at[u], fq.at[u],
                       put_q(u), 128, base=[b + u for b in bases], whole=False)

    queue = [query_scatter(u) for u in range(3)]

    def backward(qs, qst, keys_ref, values_ref, att, n1t, gt, kt, dk, dv, gp, gpu, wqm):
        loads = [k.local(k_qs, qs), k.local(k_qst, qst), k.local(k_k, keys_ref), k.local(k_v, values_ref),
                 k.local(k_att, att), k.local(k_n1t, n1t), k.local(wq.reshape(D, 3 * THIRD), wqm)]
        start(loads)
        ga_c.wait_recv()
        landed(loads)
        lane = lax.broadcasted_iota(jnp.int32, (256, 128), 1)
        vbq[...] = jnp.zeros_like(vbq)
        slots = {
            (0, 3): [down.s2, outp.s1], (0, 2): [], (0, 1): [down.s3], (0, 0): [up.s2],
            (1, 3): [], (1, 2): [outp.s2], (1, 1): [up.s3], (1, 0): [down.s4, outp.s3],
            (2, 3): [queue[0].s2], (2, 2): [down.s5], (2, 1): [queue[0].s3, up.s4], (2, 0): [outp.s4],
        }

        def unit(u, carry):
            cols = lanes(u * 128)
            for b in range(4):
                rows = slice(b * 256, (b + 1) * 256)
                gt[:, rows] = ga_all[b // 2, b % 2, :, cols].astype(F32).T.astype(BF)
                kt[:, rows] = keys_ref[rows, cols].astype(F32).T.astype(BF)
            dk[...] = jnp.zeros_like(dk)
            dv[...] = jnp.zeros_like(dv)
            for block in (3, 2, 1, 0):
                rows = min(4, max(block + 1, 2)) * 256
                qrange = slice(block * 256, (block + 1) * 256)
                keys = keys_ref[0:rows, cols]
                values = values_ref[0:rows, cols]
                queries_t = qst[cols, qrange]
                grads_t = gt[:, qrange]
                queries = qs[qrange, cols]
                grads = ga_all[block // 2, block % 2, :, cols]
                qpos = block * 256 + lax.broadcasted_iota(jnp.int32, (1, 256), 1)
                seen = lax.broadcasted_iota(jnp.int32, (rows, 256), 0) <= jnp.maximum(qpos, limit)
                prod = grads_t.astype(F32) * att[cols, qrange]
                dqs, dks, dvs = [], None, None
                for half in range(2):
                    part = slice(half * 64, half * 64 + 64)
                    in_sub = sub // 64 == half
                    in_lane = lane // 64 == half
                    delta = jnp.sum(prod[part], axis=0, keepdims=True)
                    total = lt[pl.ds(u * 2 + half, 1), qrange]
                    zero = jnp.zeros((), BF)
                    scores = jnp.dot(keys, jnp.where(in_sub, queries_t, zero), preferred_element_type=F32)
                    pull = jnp.dot(values, jnp.where(in_sub, grads_t, zero), preferred_element_type=F32)
                    share = jnp.exp(jnp.where(seen, jnp.abs(scores) - total, NEG))
                    signed = jnp.where(scores > 0, share, jnp.where(scores < 0, -share, 0.0))
                    grad_scores = (share * pull - signed * delta).astype(BF)
                    signed = signed.astype(BF)
                    dvt = jnp.dot(signed, jnp.where(in_lane, grads, zero), preferred_element_type=F32)
                    dkt = jnp.dot(grad_scores, jnp.where(in_lane, queries, zero), preferred_element_type=F32)
                    dvs = dvt if dvs is None else dvs + dvt
                    dks = dkt if dks is None else dks + dkt
                    dqs.append(jnp.dot(kt[part, 0:rows], grad_scores, preferred_element_type=F32))
                dk[0:rows, :] += dks
                dv[0:rows, :] += dvs
                gpu[qrange, 0:128] = (jnp.concatenate(dqs, axis=0).T * 0.125).astype(BF)
                for which in range(3):
                    if slots[which, block]:
                        @pl.when(u == which)
                        def _():
                            for step in slots[which, block]:
                                step()
            gpu[:, 128:256] = dk[...].astype(BF)
            gpu[:, 256:384] = dv[...].astype(BF)
            sums = jnp.sum(gpu[...].astype(F32), axis=0, keepdims=True)
            for kind in range(3):
                part = slice(kind * 128, (kind + 1) * 128)
                vbq[0:1, lanes(kind * D + c * THIRD + u * 128)] = sums[:, part]
                gp[:, lanes(kind * THIRD + u * 128)] = gpu[:, part]

            def weights(zz, inner):
                block = jnp.dot(n1t[rows_at(zz * 192, 192, 64), :], gpu[...], preferred_element_type=F32)
                for i in range(4):
                    gq[u, zz, i // 2, i % 2] = block[i * 48 : (i + 1) * 48].astype(BF)
                return inner

            lax.fori_loop(0, 4, weights, 0)
            for which in range(3):
                @pl.when(u == which)
                def _():
                    queue[which].s1()
            return carry

        lax.fori_loop(0, 3, unit, 0)

        def back_rows(b):
            return lax.dot_general(gp[rows_at(b * 256, 256), :], wqm[...], LAST, preferred_element_type=F32)

        def back_peer(yy, carry):
            fb[yy] = back_rows(yy * 2 + c2)
            return carry

        lax.fori_loop(0, 2, back_peer, 0)
        part_c.start()
        queue[1].s2()

        def back_own(yy, carry):
            fc[yy] = back_rows(yy * 2 + c)
            return carry

        lax.fori_loop(0, 2, back_own, 0)
        queue[2].s2()
        queue[0].s4()

    part_c = k.remote(fb, fr, k.pc)
    pl.run_scoped(
        backward, vmem((1024, THIRD), BF), vmem((THIRD, 1024), BF), vmem((1024, THIRD), BF), vmem((1024, THIRD), BF),
        vmem((THIRD, 1024), F32), vmem((D, 1024), BF), vmem((128, 1024), BF), vmem((128, 1024), BF),
        vmem((1024, 128), F32), vmem((1024, 128), F32), vmem((1024, 3 * THIRD), BF), vmem((1024, THIRD), BF),
        vmem((D, 1152), BF))

    gain = vrows[0:1, 0:D]
    vs[0:2, :] = jnp.zeros((2, D), F32)
    part_c.wait_recv()

    def last_back(yy, carry):
        normed, scale = unit_rows(tok_all[yy, c].astype(F32))
        grad = fc[yy] + fr[yy]
        vs[0:1, :] += jnp.sum(grad * normed, axis=0, keepdims=True)
        vs[1:2, :] += jnp.sum(grad, axis=0, keepdims=True)
        gtb[yy] = (fa[yy] + norm_back(grad * gain, normed, scale)).astype(BF)
        return carry

    lax.fori_loop(0, 2, last_back, 0)
    gt_own = k.local(gtb.at[y], out_gt.at[y])
    gt_y = k.remote(gtb.at[y2], out_gt.at[y], k.py)
    gt_own.start()
    gt_y.start()
    queue[1].s3()
    for index, wide in enumerate(WIDTHS):
        if index == 2:
            row = vbq[...]
        elif index == 6:
            row = vup[...]
        else:
            row = vs[index : index + 1, :]
        vtab[pl.ds(index, 32, stride=8), :] = collect_rows(row, wide)
    table = vtab.reshape(4, 2, 2, 2, 8, 128)
    v0 = k.remote(table.at[:, :, :, c2], vr0, k.pc)
    v1 = k.remote(table.at[:, :, y2, c], vr1, k.py)
    v2 = k.remote(table.at[:, x2, y, c], vr2, k.px)
    v3 = [k.remote(table.at[k.zs[d], x, y, c], vr3.at[d], k.pz[d]) for d in range(3)]

    def tile(zz, xx, yy):
        return rows_at((((zz * 2 + xx) * 2 + yy) * 2 + c) * 8, 8, 8)

    v0.start()
    queue[2].s3()
    up.s5()
    outp.s5()
    v0.wait_recv()

    def add_core(i, carry):
        zz, xx, yy = i // 4, lax.rem(i // 2, 2), lax.rem(i, 2)
        vtab[tile(zz, xx, yy), :] += vr0[zz, xx, yy]
        return carry

    lax.fori_loop(0, 16, add_core, 0)
    v1.start()
    queue[1].s4()
    queue[0].s5()
    v1.wait_recv()

    def add_y(i, carry):
        vtab[tile(i // 2, lax.rem(i, 2), y), :] += vr1[i // 2, lax.rem(i, 2)]
        return carry

    lax.fori_loop(0, 8, add_y, 0)
    v2.start()
    queue[2].s4()
    v2.wait_recv()

    def add_x(zz, carry):
        vtab[tile(zz, x, y), :] += vr2[zz]
        return carry

    lax.fori_loop(0, 4, add_x, 0)
    start(v3)
    queue[1].s5()
    queue[2].s5()
    arrive(v3)
    out_vec[...] = vtab[tile(z, x, y), :] + vr3[0] + vr3[1] + vr3[2]
    landed([gt_own, bo_own])
    arrive([gt_y, bo_y])
    for copy in k.sent:
        copy.wait_send()
    for scatter in queue:
        scatter.gone()


def layer_call(*operands):
    sds = jax.ShapeDtypeStruct
    vmem = pltpu.VMEM
    dma = pltpu.SemaphoreType.DMA
    results = (
        sds((2, 256, D), BF), sds((2, 256, D), BF), sds((24, 3 * D), F32), sds((24, D), F32), sds((24, FF), F32),
        sds((96, D), F32), sds((8, 128), F32),
    )
    held = (
        sds((4, 2, 2, 48, 1152), BF), sds((2, 4, 2, 2, 48, 384), BF), sds((2, 4, 2, 2, 48, 1536), BF),
        sds((2, 4, 2, 2, 192, 384), BF), sds((4, 2, 2, 2, 8, 128), BF), sds((1024, THIRD), BF), sds((THIRD, 1024), BF),
        sds((1024, THIRD), BF), sds((1024, THIRD), BF), sds((THIRD, 1024), F32), sds((D, 1024), BF),
    )
    scratch = [
        vmem((4, 2, 2, 2, 8, 128), BF), vmem((2, 2, 256, D), BF), vmem((8, FF), F32),
        vmem((2, D, THIRD), BF), vmem((2, 2, 256, THIRD), BF), vmem((2, 256, D), BF), vmem((2, 256, D), BF),
        vmem((2, 256, D), BF), vmem((2, 2, 256, THIRD), BF), vmem((2, 256, D), F32), vmem((2, 256, D), F32),
        vmem((2, 256, D), F32), vmem((2, 256, D), F32), vmem((8, 1024), F32),
    ]
    kinds = ((192, 384, 128), (48, 1536, 768), (48, 384, 256))
    scratch += [vmem((2, 4, 2, 2, r, n), BF) for r, n, _ in kinds] + [vmem((3, 4, 2, 2, 48, 384), BF)]
    scratch += [vmem((4, 2, 2, r, n), BF) for r, n, _ in kinds]
    for r, n, cut in kinds:
        scratch += [vmem((4, 2, r, cut), BF), vmem((4, 2, r, n - cut), BF)]
    for r, n, cut in kinds:
        scratch += [vmem((4, r, cut), BF), vmem((4, r, n - cut), BF)]
    scratch += [vmem((3, r, n), BF) for r, n, _ in kinds]
    scratch += [vmem((2, r // 2, n), F32) for r, n, _ in kinds]
    scratch += [vmem((r // 2, n), F32) for r, n, _ in kinds]
    scratch += [
        vmem((3, 4, 2, 48, 128), BF), vmem((3, 4, 2, 48, 256), BF), vmem((3, 4, 48, 128), BF), vmem((3, 4, 48, 256), BF),
        vmem((3, 3, 48, 384), BF), vmem((3, 2, 24, 384), F32), vmem((3, 24, 384), F32),
        vmem((8, D), F32), vmem((1, 3 * D), F32), vmem((1, FF), F32), vmem((256, 128), F32), vmem((4, 2, 2, 8, 128), F32),
        vmem((4, 2, 8, 128), F32), vmem((4, 8, 128), F32), vmem((3, 8, 128), F32),
        dma((REMOTES,)), dma((REMOTES,)), dma((LOCALS,)),
    ]
    return pl.pallas_call(
        layer_kernel,
        out_shape=results + held,
        in_specs=[SM] + [ANY] * 7,
        out_specs=(ANY, ANY) + (VM,) * 5 + (ANY,) * len(held),
        scratch_shapes=scratch,
        compiler_params=pltpu.CompilerParams(
            collective_id=0, has_side_effects=True, vmem_limit_bytes=63 * 2**20),
    )(*operands)[: len(results)]


def pack_vectors(vectors):
    return jnp.stack([jnp.pad(v, (0, 128 - v.shape[0])) for v in vectors])


def body(
    tokens, cotangent, prefix, ln1_gain, ln1_bias, w_qkv, b_qkv, w_out, b_out,
    ln2_gain, ln2_bias, w_up, b_up, w_down, b_down,
):
    vec = pack_vectors((ln1_gain, ln1_bias, b_qkv, b_out, ln2_gain, ln2_bias, b_up, b_down))
    block_out, grad_tokens, gq, go, gu, gd, gvec = layer_call(
        prefix, tokens, cotangent, vec, w_qkv, w_out, w_up, w_down)
    rows = [gvec[i, :wide] for i, wide in enumerate(WIDTHS)]
    return (
        block_out, grad_tokens, rows[0], rows[1], gq, rows[2], go, rows[3], rows[4], rows[5], gu, rows[6], gd, rows[7],
    )


def fits(mesh):
    return dict(mesh.shape) == {"dp": 8, "seq": 4}


norm_eps = 1e-05
block_rows = 512


def layer_norm(features, gain, shift):
    centre = features - jnp.mean(features, axis=-1, keepdims=True)
    spread = jnp.mean(centre * centre, axis=-1, keepdims=True)
    return centre * lax.rsqrt(spread + norm_eps) * gain + shift


def gelu_tanh(values):
    return jax.nn.gelu(values, approximate=True)


def in_blocks(update, running, pieces):
    length = pieces[0].shape[1]
    blocks = length // block_rows
    blocked_pieces = tuple(
        (
            jnp.swapaxes(
                member.reshape((member.shape[0], blocks, block_rows) + member.shape[2:]), 0, 1
            )
            for member in pieces
        )
    )

    def advance(carried, element):
        return (update(carried, element[0], element[1] * block_rows), None)

    running, unused = lax.scan(
        advance, running, (blocked_pieces, jnp.arange(blocks, dtype=jnp.int32))
    )
    return running


def to_heads(flat_rows):
    return flat_rows.reshape(flat_rows.shape[0], flat_rows.shape[1], HEADS, HEAD_DIM)


def visible_mask(query_places, key_places, prefix_len):
    earlier = key_places[None, None, :] <= query_places[None, :, None]
    in_prefix = key_places[None, None, :] < prefix_len[:, None, None]
    return (earlier | in_prefix)[:, :, None, :]


def head_scores(query_heads, key_flat):
    return jnp.einsum(
        "bqhd,bkhd->bqhk", query_heads, to_heads(key_flat), preferred_element_type=jnp.float32
    ) * HEAD_DIM ** (-0.5)


def attend(query_heads, key_flat, value_flat, prefix_len):
    local_len = query_heads.shape[1]
    query_places = lax.axis_index("seq") * local_len + jnp.arange(local_len, dtype=jnp.int32)
    starting = (
        jnp.zeros(query_heads.shape, jnp.float32),
        jnp.zeros(query_heads.shape[:3], jnp.float32),
        jnp.zeros(query_heads.shape[:3], jnp.float32),
    )

    def update(running, pieces, offset):
        weighted, normaliser, ceiling = running
        key_piece, value_piece = pieces
        key_places = offset + jnp.arange(key_piece.shape[1], dtype=jnp.int32)
        scores = head_scores(query_heads, key_piece)
        visible = visible_mask(query_places, key_places, prefix_len)
        magnitude = jnp.where(visible, jnp.abs(scores), 0.0)
        new_ceiling = jnp.maximum(ceiling, jnp.max(magnitude, axis=-1))
        exponent = jnp.where(visible, jnp.exp(magnitude - new_ceiling[..., None]), 0.0)
        factor = jnp.exp(ceiling - new_ceiling)
        weights = (jnp.sign(scores) * exponent).astype(jnp.bfloat16)
        weighted = weighted * factor[..., None] + jnp.einsum(
            "bqhk,bkhd->bqhd", weights, to_heads(value_piece), preferred_element_type=jnp.float32
        )
        normaliser = normaliser * factor + jnp.sum(exponent, axis=-1)
        return (weighted, normaliser, new_ceiling)

    weighted, normaliser, ceiling = in_blocks(
        update,
        starting,
        (
            lax.all_gather(key_flat, "seq", axis=1, tiled=True),
            lax.all_gather(value_flat, "seq", axis=1, tiled=True),
        ),
    )
    return (weighted / normaliser[..., None], ceiling + jnp.log(normaliser))


def grad_terms(
    query_heads,
    grad_heads,
    key_flat,
    value_flat,
    log_total,
    delta_sum,
    query_places,
    key_places,
    prefix_len,
):
    scores = head_scores(query_heads, key_flat)
    sign_of = jnp.sign(scores)
    visible = visible_mask(query_places, key_places, prefix_len)
    shares = jnp.where(visible, jnp.exp(jnp.abs(scores) - log_total[..., None]), 0.0)
    grad_weights = jnp.einsum(
        "bqhd,bkhd->bqhk", grad_heads, to_heads(value_flat), preferred_element_type=jnp.float32
    )
    grad_scores = (shares * (grad_weights - sign_of * delta_sum[..., None])).astype(jnp.bfloat16)
    return ((sign_of * shares).astype(jnp.bfloat16), grad_scores)


def query_term(grad_scores, key_flat):
    return jnp.einsum(
        "bqhk,bkhd->bqhd", grad_scores, to_heads(key_flat), preferred_element_type=jnp.float32
    ) * HEAD_DIM ** (-0.5)


def key_value_terms(query_heads, grad_heads, shares_low, grad_scores):
    key_term = jnp.einsum(
        "bqhk,bqhd->bkhd", grad_scores, query_heads, preferred_element_type=jnp.float32
    ) * HEAD_DIM ** (-0.5)
    value_term = jnp.einsum(
        "bqhk,bqhd->bkhd", shares_low, grad_heads, preferred_element_type=jnp.float32
    )
    flat_shape = (key_term.shape[0], key_term.shape[1], key_term.shape[2] * key_term.shape[3])
    return jnp.concatenate([key_term.reshape(flat_shape), value_term.reshape(flat_shape)], axis=-1)


def attend_back(query_heads, key_flat, value_flat, grad_heads, log_total, delta_sum, prefix_len):
    seq_block, local_len = (query_heads.shape[0], query_heads.shape[1])
    width = key_flat.shape[2]
    local_places = lax.axis_index("seq") * local_len + jnp.arange(local_len, dtype=jnp.int32)
    starting = (
        jnp.zeros(query_heads.shape, jnp.float32),
        jnp.zeros((seq_block, lax.axis_size("seq") * local_len, 2 * width), jnp.float32),
    )

    def update_both(running, pieces, offset):
        grad_query, grad_keys = running
        key_piece, value_piece = pieces
        piece_len = key_piece.shape[1]
        key_places = offset + jnp.arange(piece_len, dtype=jnp.int32)
        shares_low, grad_scores = grad_terms(
            query_heads,
            grad_heads,
            key_piece,
            value_piece,
            log_total,
            delta_sum,
            local_places,
            key_places,
            prefix_len,
        )
        grad_query = grad_query + query_term(grad_scores, key_piece)
        current = lax.dynamic_slice_in_dim(grad_keys, offset, piece_len, 1)
        updated = current + key_value_terms(query_heads, grad_heads, shares_low, grad_scores)
        return (grad_query, lax.dynamic_update_slice_in_dim(grad_keys, updated, offset, 1))

    grad_query, grad_keys = in_blocks(
        update_both,
        starting,
        (
            lax.all_gather(key_flat, "seq", axis=1, tiled=True),
            lax.all_gather(value_flat, "seq", axis=1, tiled=True),
        ),
    )
    key_local = lax.psum_scatter(
        grad_keys.astype(jnp.bfloat16), "seq", scatter_dimension=1, tiled=True
    ).astype(jnp.float32)
    return (grad_query, key_local)


def forward_block(weights_in, token_part, prefix_len):
    (
        gain_one,
        shift_one,
        w_qkv,
        b_qkv,
        w_out,
        b_out,
        gain_two,
        shift_two,
        w_up,
        b_up,
        w_down,
        b_down,
    ) = weights_in
    seq_block, local_len, width = token_part.shape
    residual_in = token_part.reshape(-1, width).astype(jnp.float32)
    normed_one = layer_norm(
        residual_in, gain_one.astype(jnp.float32), shift_one.astype(jnp.float32)
    ).astype(jnp.bfloat16)
    projected = jnp.dot(normed_one, w_qkv, preferred_element_type=jnp.float32) + b_qkv.astype(
        jnp.float32
    )
    query_heads = (
        projected[:, :width].astype(jnp.bfloat16).reshape(seq_block, local_len, HEADS, HEAD_DIM)
    )
    key_flat = (
        projected[:, width : 2 * width].astype(jnp.bfloat16).reshape(seq_block, local_len, width)
    )
    value_flat = projected[:, 2 * width :].astype(jnp.bfloat16).reshape(seq_block, local_len, width)
    attended, log_total = attend(query_heads, key_flat, value_flat, prefix_len)
    attended_low = attended.reshape(-1, width).astype(jnp.bfloat16)
    residual_mid = (
        residual_in
        + jnp.dot(attended_low, w_out, preferred_element_type=jnp.float32)
        + b_out.astype(jnp.float32)
    )
    normed_two = layer_norm(
        residual_mid, gain_two.astype(jnp.float32), shift_two.astype(jnp.float32)
    ).astype(jnp.bfloat16)
    pre_gelu = jnp.dot(normed_two, w_up, preferred_element_type=jnp.float32) + b_up.astype(
        jnp.float32
    )
    hidden = gelu_tanh(pre_gelu).astype(jnp.bfloat16)
    result = (
        residual_mid
        + jnp.dot(hidden, w_down, preferred_element_type=jnp.float32)
        + b_down.astype(jnp.float32)
    )
    saved = (
        residual_in,
        normed_one,
        query_heads,
        key_flat,
        value_flat,
        attended,
        log_total,
        attended_low,
        residual_mid,
        normed_two,
        pre_gelu,
        hidden,
    )
    return (result.astype(jnp.bfloat16).reshape(token_part.shape), saved)


def backward_block(weights_in, saved, grad_part, prefix_len):
    (
        gain_one,
        shift_one,
        w_qkv,
        b_qkv,
        w_out,
        b_out,
        gain_two,
        shift_two,
        w_up,
        b_up,
        w_down,
        b_down,
    ) = weights_in
    (
        residual_in,
        normed_one,
        query_heads,
        key_flat,
        value_flat,
        attended,
        log_total,
        attended_low,
        residual_mid,
        normed_two,
        pre_gelu,
        hidden,
    ) = saved
    seq_block, local_len, width = grad_part.shape
    grad_result = grad_part.reshape(-1, width).astype(jnp.float32)
    grad_branch = grad_part.reshape(-1, width)
    grads_down = jnp.einsum("rf,rd->fd", hidden, grad_branch, preferred_element_type=jnp.float32)
    bias_down = jnp.sum(grad_branch, axis=0, dtype=jnp.float32)
    grad_hidden = jnp.einsum("rd,fd->rf", grad_branch, w_down, preferred_element_type=jnp.float32)
    gelu_pull = jax.vjp(gelu_tanh, pre_gelu)[1]
    grad_pre = gelu_pull(grad_hidden)[0].astype(jnp.bfloat16)
    grads_up = jnp.einsum("rd,rf->df", normed_two, grad_pre, preferred_element_type=jnp.float32)
    bias_up = jnp.sum(grad_pre, axis=0, dtype=jnp.float32)
    grad_normed_two = jnp.einsum("rf,df->rd", grad_pre, w_up, preferred_element_type=jnp.float32)
    norm_two_pull = jax.vjp(
        layer_norm, residual_mid, gain_two.astype(jnp.float32), shift_two.astype(jnp.float32)
    )[1]
    grad_mid, grads_gain_two, grads_shift_two = norm_two_pull(grad_normed_two)
    grad_mid = grad_mid + grad_result
    grad_attn = grad_mid.astype(jnp.bfloat16)
    grads_out = jnp.einsum("rd,re->de", attended_low, grad_attn, preferred_element_type=jnp.float32)
    bias_out = jnp.sum(grad_attn, axis=0, dtype=jnp.float32)
    grad_heads = (
        jnp.einsum("re,de->rd", grad_attn, w_out, preferred_element_type=jnp.float32)
        .astype(jnp.bfloat16)
        .reshape(seq_block, local_len, HEADS, HEAD_DIM)
    )
    delta_sum = jnp.sum(grad_heads.astype(jnp.float32) * attended, axis=-1)
    grad_query, key_local = attend_back(
        query_heads, key_flat, value_flat, grad_heads, log_total, delta_sum, prefix_len
    )
    grad_proj = jnp.concatenate(
        [grad_query.reshape(-1, width), key_local.reshape(-1, 2 * width)], axis=1
    ).astype(jnp.bfloat16)
    grads_qkv = jnp.einsum("rd,re->de", normed_one, grad_proj, preferred_element_type=jnp.float32)
    bias_qkv = jnp.sum(grad_proj, axis=0, dtype=jnp.float32)
    grad_normed_one = jnp.einsum("re,de->rd", grad_proj, w_qkv, preferred_element_type=jnp.float32)
    norm_one_pull = jax.vjp(
        layer_norm, residual_in, gain_one.astype(jnp.float32), shift_one.astype(jnp.float32)
    )[1]
    grad_in, grads_gain_one, grads_shift_one = norm_one_pull(grad_normed_one)
    grad_in = grad_in + grad_mid
    weight_grads = (
        grads_gain_one,
        grads_shift_one,
        grads_qkv,
        bias_qkv,
        grads_out,
        bias_out,
        grads_gain_two,
        grads_shift_two,
        grads_up,
        bias_up,
        grads_down,
        bias_down,
    )
    return (grad_in.astype(jnp.bfloat16).reshape(grad_part.shape), weight_grads)


def general_body(
    tokens,
    cotangent,
    prefix,
    ln1_gain,
    ln1_bias,
    w_qkv,
    b_qkv,
    w_out,
    b_out,
    ln2_gain,
    ln2_bias,
    w_up,
    b_up,
    w_down,
    b_down,
):
    shards = (
        ln1_gain,
        ln1_bias,
        w_qkv,
        b_qkv,
        w_out,
        b_out,
        ln2_gain,
        ln2_bias,
        w_up,
        b_up,
        w_down,
        b_down,
    )
    spread_count = lax.axis_size(("dp", "seq"))
    totals = tuple(
        (
            jnp.zeros((member.shape[0] * spread_count,) + member.shape[1:], jnp.float32)
            for member in shards
        )
    )
    seq_block = tokens.shape[0] // MB
    outputs = []
    grad_inputs = []
    for batch_index in range(MB):
        first_row = batch_index * seq_block
        token_part = tokens[first_row : first_row + seq_block]
        cotangent_part = cotangent[first_row : first_row + seq_block]
        prefix_part = prefix[first_row : first_row + seq_block]
        forward_weights = (
            lax.all_gather(shards[0], ("dp", "seq"), axis=0, tiled=True),
            lax.all_gather(shards[1], ("dp", "seq"), axis=0, tiled=True),
            lax.all_gather(shards[2], ("dp", "seq"), axis=0, tiled=True),
            lax.all_gather(shards[3], ("dp", "seq"), axis=0, tiled=True),
            lax.all_gather(shards[4], ("dp", "seq"), axis=0, tiled=True),
            lax.all_gather(shards[5], ("dp", "seq"), axis=0, tiled=True),
            lax.all_gather(shards[6], ("dp", "seq"), axis=0, tiled=True),
            lax.all_gather(shards[7], ("dp", "seq"), axis=0, tiled=True),
            lax.all_gather(shards[8], ("dp", "seq"), axis=0, tiled=True),
            lax.all_gather(shards[9], ("dp", "seq"), axis=0, tiled=True),
            lax.all_gather(shards[10], ("dp", "seq"), axis=0, tiled=True),
            lax.all_gather(shards[11], ("dp", "seq"), axis=0, tiled=True),
        )
        result, saved = forward_block(forward_weights, token_part, prefix_part)
        back_weights = (
            lax.all_gather(shards[0], ("dp", "seq"), axis=0, tiled=True),
            lax.all_gather(shards[1], ("dp", "seq"), axis=0, tiled=True),
            lax.all_gather(shards[2], ("dp", "seq"), axis=0, tiled=True),
            lax.all_gather(shards[3], ("dp", "seq"), axis=0, tiled=True),
            lax.all_gather(shards[4], ("dp", "seq"), axis=0, tiled=True),
            lax.all_gather(shards[5], ("dp", "seq"), axis=0, tiled=True),
            lax.all_gather(shards[6], ("dp", "seq"), axis=0, tiled=True),
            lax.all_gather(shards[7], ("dp", "seq"), axis=0, tiled=True),
            lax.all_gather(shards[8], ("dp", "seq"), axis=0, tiled=True),
            lax.all_gather(shards[9], ("dp", "seq"), axis=0, tiled=True),
            lax.all_gather(shards[10], ("dp", "seq"), axis=0, tiled=True),
            lax.all_gather(shards[11], ("dp", "seq"), axis=0, tiled=True),
        )
        grad_piece, weight_grads = backward_block(back_weights, saved, cotangent_part, prefix_part)
        totals = tuple(
            (running_sum + new_term for running_sum, new_term in zip(totals, weight_grads))
        )
        outputs.append(result)
        grad_inputs.append(grad_piece)
    reduced = (
        lax.psum_scatter(totals[0], ("dp", "seq"), scatter_dimension=0, tiled=True),
        lax.psum_scatter(totals[1], ("dp", "seq"), scatter_dimension=0, tiled=True),
        lax.psum_scatter(totals[2], ("dp", "seq"), scatter_dimension=0, tiled=True),
        lax.psum_scatter(totals[3], ("dp", "seq"), scatter_dimension=0, tiled=True),
        lax.psum_scatter(totals[4], ("dp", "seq"), scatter_dimension=0, tiled=True),
        lax.psum_scatter(totals[5], ("dp", "seq"), scatter_dimension=0, tiled=True),
        lax.psum_scatter(totals[6], ("dp", "seq"), scatter_dimension=0, tiled=True),
        lax.psum_scatter(totals[7], ("dp", "seq"), scatter_dimension=0, tiled=True),
        lax.psum_scatter(totals[8], ("dp", "seq"), scatter_dimension=0, tiled=True),
        lax.psum_scatter(totals[9], ("dp", "seq"), scatter_dimension=0, tiled=True),
        lax.psum_scatter(totals[10], ("dp", "seq"), scatter_dimension=0, tiled=True),
        lax.psum_scatter(totals[11], ("dp", "seq"), scatter_dimension=0, tiled=True),
    )
    return (
        jnp.concatenate(outputs, axis=0),
        jnp.concatenate(grad_inputs, axis=0),
        reduced[0],
        reduced[1],
        reduced[2],
        reduced[3],
        reduced[4],
        reduced[5],
        reduced[6],
        reduced[7],
        reduced[8],
        reduced[9],
        reduced[10],
        reduced[11],
    )


def solution(mesh):
    in_specs = (
        P("dp", "seq", None),
        P("dp", "seq", None),
        P("dp"),
        P(("dp", "seq")),
        P(("dp", "seq")),
        P(("dp", "seq"), None),
        P(("dp", "seq")),
        P(("dp", "seq"), None),
        P(("dp", "seq")),
        P(("dp", "seq")),
        P(("dp", "seq")),
        P(("dp", "seq"), None),
        P(("dp", "seq")),
        P(("dp", "seq"), None),
        P(("dp", "seq")),
    )
    out_specs = (
        P("dp", "seq", None),
        P("dp", "seq", None),
        P(("dp", "seq")),
        P(("dp", "seq")),
        P(("dp", "seq"), None),
        P(("dp", "seq")),
        P(("dp", "seq"), None),
        P(("dp", "seq")),
        P(("dp", "seq")),
        P(("dp", "seq")),
        P(("dp", "seq"), None),
        P(("dp", "seq")),
        P(("dp", "seq"), None),
        P(("dp", "seq")),
    )
    chosen = body if fits(mesh) else general_body
    return jax.shard_map(chosen, mesh=mesh, in_specs=in_specs, out_specs=out_specs, check_vma=False)
```

```python
import functools

import jax
import jax.numpy as jnp
from jax import lax
from jax.experimental import pallas as pl
from jax.experimental.pallas import tpu as pltpu
from jax.sharding import PartitionSpec as P

HEADS = 12
HEAD_DIM = 64
MB = 2

F32 = jnp.float32
BF = jnp.bfloat16
EPS = 1e-05
MESH = pl.DeviceIdType.MESH
NEG = -1e30
ANY = pl.BlockSpec(memory_space=pl.ANY)
VM = pl.BlockSpec(memory_space=pltpu.VMEM)
SM = pl.BlockSpec(memory_space=pltpu.SMEM)
WIDTHS = (24, 24, 72, 24, 24, 24, 96, 24)
D = 768
FF = 3072
THIRD = 384
LAST = (((1,), (1,)), ((), ()))
FIRST = (((0,), (0,)), ((), ()))
ALL = slice(None)
REMOTES = 128
LOCALS = 64


def places():
    dp = lax.axis_index("dp")
    sq = lax.axis_index("seq")
    return dp // 2, dp % 2, sq // 2, sq % 2


def device(z, x, y, c):
    return (z * 2 + x, y * 2 + c)


def owner_of(wide):
    column = lax.broadcasted_iota(jnp.int32, (1, 32 * wide), 1).astype(F32)
    owner = jnp.floor((column + 0.5) * (1.0 / wide))
    return owner.astype(jnp.int32), (column - owner * wide).astype(jnp.int32)


def spread_row(gathered, index, wide):
    total = 32 * wide
    row = lax.broadcasted_iota(jnp.int32, (32, 256), 0)
    place = lax.broadcasted_iota(jnp.int32, (32, 256), 1)
    pick = jnp.where(place == row * 8 + index, 1.0, 0.0).astype(BF)
    mine = jnp.dot(pick, gathered, preferred_element_type=F32).astype(BF)
    owner, rest = owner_of(wide)
    spread = jnp.where(lax.broadcasted_iota(jnp.int32, (128, total), 0) == rest, 1.0, 0.0).astype(BF)
    full = jnp.dot(mine, spread, preferred_element_type=F32)
    keep = lax.broadcasted_iota(jnp.int32, (32, total), 0) == owner
    return jnp.sum(jnp.where(keep, full, 0.0), axis=0, keepdims=True)


def collect_rows(vector, wide):
    total = 32 * wide
    owner, rest = owner_of(wide)
    gather = jnp.where(lax.broadcasted_iota(jnp.int32, (128, total), 0) == rest, 1.0, 0.0).astype(BF)
    keep = lax.broadcasted_iota(jnp.int32, (32, total), 0) == owner
    high = vector.astype(BF).astype(F32)
    out = None
    for part in (high, vector - high):
        placed = jnp.where(keep, part, 0.0).astype(BF)
        term = lax.dot_general(placed, gather, LAST, preferred_element_type=F32)
        out = term if out is None else out + term
    return out


def add_into(ref, at, other):
    ref[at] = (ref[at].astype(F32) + other.astype(F32)).astype(BF)


def start(copies):
    for copy in copies:
        copy.start()


def arrive(copies):
    for copy in copies:
        copy.wait_recv()


def landed(copies):
    for copy in copies:
        copy.wait()


def lanes(first, count=128):
    return pl.ds(pl.multiple_of(first, 128), count)


def rows_at(first, count, step=256):
    return pl.ds(pl.multiple_of(first, step), count)


class Links:
    def __init__(self, ssem, rsem, lsem):
        self.ssem, self.rsem, self.lsem = ssem, rsem, lsem
        self.remotes = self.locals = 0
        self.sent = []
        z, x, y, c = places()
        self.z, self.x, self.y, self.c = z, x, y, c
        self.x2, self.y2, self.c2 = 1 - x, 1 - y, 1 - c
        self.px, self.py, self.pc = device(z, 1 - x, y, c), device(z, x, 1 - y, c), device(z, x, y, 1 - c)
        self.zs = [lax.rem(z + d, 4) for d in (1, 2, 3)]
        self.pz = [device(zz, x, y, c) for zz in self.zs]

    def fresh(self, count=1):
        first = self.remotes
        self.remotes += count
        return first

    def remote(self, src, dst, dev, at=None):
        i = self.fresh() if at is None else at
        copy = pltpu.make_async_remote_copy(
            src_ref=src, dst_ref=dst, send_sem=self.ssem.at[i], recv_sem=self.rsem.at[i],
            device_id=dev, device_id_type=MESH)
        if at is None:
            self.sent.append(copy)
        return copy

    def local(self, src, dst):
        i = self.locals
        self.locals += 1
        return pltpu.make_async_copy(src, dst, self.lsem.at[i])

    def greet(self):
        barrier = pltpu.get_barrier_semaphore()
        for dev in [self.px, self.py, self.pc] + self.pz:
            pl.semaphore_signal(barrier, inc=1, device_id=dev, device_id_type=MESH)

    def greeted(self):
        pl.semaphore_wait(pltpu.get_barrier_semaphore(), 6)


class Gather:
    def __init__(self, links, own, other, mine, theirs, cut, full=None):
        k = links
        rows = own.shape[0]
        at = pl.ds(pl.multiple_of(k.c * rows, 8), rows)
        z, x, y = k.z, k.x, k.y
        self.own = [k.local(own, mine.at[z, x, y, at])]
        self.c0 = [k.remote(other, theirs.at[z, x, y, at], k.pc)]
        self.c1 = [k.remote(mine.at[z, x, y], mine.at[z, x, y], dev) for dev in k.pz]
        a, b = slice(0, cut), slice(cut, None)
        self.c2 = [k.remote(mine.at[:, x, y, :, a], mine.at[:, x, y, :, a], k.px),
                   k.remote(mine.at[:, x, y, :, b], mine.at[:, x, y, :, b], k.py)]
        self.c3 = [k.remote(mine.at[:, :, y, :, a], mine.at[:, :, y, :, a], k.py),
                   k.remote(mine.at[:, x, :, :, b], mine.at[:, x, :, :, b], k.px)]
        self.c4 = [] if full is None else [k.remote(full.at[k.c], full.at[k.c], k.pc)]

    def s0(self):
        start(self.c0)

    def s1(self):
        landed(self.own)
        arrive(self.c0)
        start(self.c1)

    def s2(self):
        arrive(self.c1)
        start(self.c2)

    def s3(self):
        arrive(self.c2)
        start(self.c3)

    def s4(self):
        arrive(self.c3)
        start(self.c4)

    def done(self):
        arrive(self.c4)


class Scatter:
    def __init__(self, links, grad, r0, r1a, r1b, r2a, r2b, r3, tot, fin, put, cut, base=None, whole=True):
        k = links
        self.k, self.grad, self.whole, self.put = k, grad, whole, put
        self.r0, self.r1a, self.r1b, self.r2a, self.r2b, self.r3, self.tot, self.fin = r0, r1a, r1b, r2a, r2b, r3, tot, fin
        self.mine = grad.at[k.c] if whole else grad
        self.a = (ALL, slice(0, cut))
        self.b = (ALL, slice(cut, None))
        x, y, x2, y2 = k.x, k.y, k.x2, k.y2
        at = iter([None] * 10 if base is None else base)
        mine = self.mine
        self.c0 = [k.remote(grad.at[k.c2], r0, k.pc, next(at))] if whole else []
        self.c1 = [k.remote(mine.at[(ALL, ALL, y2) + self.a], r1a, k.py, next(at)),
                   k.remote(mine.at[(ALL, x2, ALL) + self.b], r1b, k.px, next(at))]
        self.c2 = [k.remote(mine.at[(ALL, x2, y) + self.a], r2a, k.px, next(at)),
                   k.remote(mine.at[(ALL, x, y2) + self.b], r2b, k.py, next(at))]
        self.c3 = [k.remote(mine.at[k.zs[d], x, y], r3.at[d], k.pz[d], next(at)) for d in range(3)]
        self.c4 = [k.remote(tot.at[k.c2], fin, k.pc, next(at))]

    def at(self, place):
        return ((self.k.c,) if self.whole else ()) + place

    def s0(self):
        start(self.c0)

    def s1(self):
        if self.whole:
            arrive(self.c0)

            def add(i, carry):
                where = (i // 4, lax.rem(i // 2, 2), lax.rem(i, 2))
                add_into(self.grad, self.at(where), self.r0[where])
                return carry

            lax.fori_loop(0, 16, add, 0)
        start(self.c1)

    def s2(self):
        arrive(self.c1)
        k = self.k

        def add(i, carry):
            zz, other = i // 2, lax.rem(i, 2)
            add_into(self.grad, self.at((zz, other, k.y) + self.a), self.r1a[zz, other])
            add_into(self.grad, self.at((zz, k.x, other) + self.b), self.r1b[zz, other])
            return carry

        lax.fori_loop(0, 8, add, 0)
        start(self.c2)

    def s3(self):
        arrive(self.c2)
        k = self.k

        def add(zz, carry):
            add_into(self.grad, self.at((zz, k.x, k.y) + self.a), self.r2a[zz])
            add_into(self.grad, self.at((zz, k.x, k.y) + self.b), self.r2b[zz])
            return carry

        lax.fori_loop(0, 4, add, 0)
        start(self.c3)

    def s4(self):
        arrive(self.c3)
        k = self.k
        total = self.mine[k.z, k.x, k.y].astype(F32)
        for d in range(3):
            total = total + self.r3[d].astype(F32)
        rows = total.shape[0] // 2
        self.tot[0] = total[:rows]
        self.tot[1] = total[rows:]
        start(self.c4)
        self.put(self.tot[k.c], k.c)

    def s5(self):
        arrive(self.c4)
        self.put(self.fin[...], self.k.c2)

    def gone(self):
        for copy in self.c0 + self.c1 + self.c2 + self.c3 + self.c4:
            copy.wait_send()


def gelu_parts(value):
    rate = 0.7978845608028654
    bent = jnp.tanh(rate * (value + 0.044715 * (value * value * value)))
    result = 0.5 * value * (1.0 + bent)
    slope = 0.5 * (1.0 + bent) + 0.5 * value * (1.0 - bent * bent) * (rate * (1.0 + 0.134145 * (value * value)))
    return result, slope


def unit_rows(rows):
    centre = rows - jnp.mean(rows, axis=-1, keepdims=True)
    scale = lax.rsqrt(jnp.mean(centre * centre, axis=-1, keepdims=True) + EPS)
    return centre * scale, scale


def norm_back(grad, normed, scale):
    return scale * (grad - jnp.mean(grad, axis=-1, keepdims=True)
                    - normed * jnp.mean(grad * normed, axis=-1, keepdims=True))


def layer_kernel(
    prefix, tok, cot, v0_s, v1_s, v2_s, v3_s, v4_s, v5_s, v6_s, v7_s, wq_s, wo_s, wu_s, wd_s,
    out_bo, out_gt, out_q, out_o, out_u, out_d, out_vec,
    wq, wo, wu, wd, gv, k_qs, k_qst, k_k, k_v, k_att, k_n1t,
    vec_s, wq_p, gvm, tok_all, vrows, wom, al_send, al, cotm, ga_send, ga_all, fa, fb, fc, fr, lt,
    gd, gu, go, gq,
    r0d, r0u, r0o, r1ad, r1bd, r1au, r1bu, r1ao, r1bo, r2ad, r2bd, r2au, r2bu, r2ao, r2bo, r3d, r3u, r3o,
    td, tu, to, fd, fu, fo,
    q1a, q1b, q2a, q2b, q3, tq, fq,
    vs, vbq, vup, vtab, vr0, vr1, vr2, vr3,
    ssem, rsem, lsem,
):
    k = Links(ssem, rsem, lsem)
    bo, gtb = al, cotm
    z, x, y, c, x2, y2, c2 = k.z, k.x, k.y, k.c, k.x2, k.y2, k.c2
    k.greet()
    vmem = pltpu.VMEM

    vec_s[...] = jnp.zeros_like(vec_s)
    for index, (wide, ref) in enumerate(zip(WIDTHS, (v0_s, v1_s, v2_s, v3_s, v4_s, v5_s, v6_s, v7_s))):
        vec_s[index : index + 1, 0:wide] = ref[...].astype(F32).reshape(1, wide)
    for core in range(2):
        for u in range(3):
            for kind in range(3):
                first = kind * D + core * THIRD + u * 128
                wq_p[core, u, :, kind * 128 : (kind + 1) * 128] = wq_s[:, first : first + 128]
    cuts = (128, 256, 128)
    gather_q = [Gather(k, wq_p.at[c, u], wq_p.at[c2, u], wq.at[u], wq.at[u], cuts[u]) for u in range(3)]

    def halves(shard, full, cut):
        half = full.shape[-1]
        return Gather(k, shard.at[:, lanes(c * half, half)], shard.at[:, lanes(c2 * half, half)], full.at[c], full.at[c2],
                      cut, full)

    gather_o = halves(wo_s, wo, 256)
    gather_u = halves(wu_s, wu, 768)
    gather_d = halves(wd_s, wd, 128)
    own_vec = k.local(vec_s, gv.at[z, x, y, c])
    own_tok = k.local(tok.at[y], tok_all.at[y, c])
    own_cot = k.local(cot.at[y], cotm.at[y])
    own_vec.start()
    start(gather_q[0].own)
    own_tok.start()
    start(gather_q[1].own + gather_q[2].own + gather_o.own + gather_u.own + gather_d.own)
    own_cot.start()
    k.greeted()

    vec_c = k.remote(vec_s, gv.at[z, x, y, c], k.pc)
    tok_y = k.remote(tok.at[y2], tok_all.at[y, c], k.py)
    cot_y = k.remote(cot.at[y2], cotm.at[y], k.py)
    gather_q[0].s0()
    vec_c.start()
    tok_y.start()
    for gather in (gather_q[1], gather_q[2], gather_o, gather_u, gather_d):
        gather.s0()
    gather_q[0].s1()
    own_vec.wait()
    vec_c.wait_recv()
    vec_z = [k.remote(gv.at[z, x, y], gv.at[z, x, y], dev) for dev in k.pz]
    start(vec_z)
    gather_q[1].s1()
    own_tok.wait()
    arrive(vec_z)
    vec_x = k.remote(gv.at[:, x, y], gv.at[:, x, y], k.px)
    vec_x.start()
    gather_q[0].s2()
    gather_q[2].s1()
    tok_y.wait_recv()
    tok_c = k.remote(tok_all.at[:, c], tok_all.at[:, c], k.pc)
    tok_c.start()
    cot_y.start()
    vec_x.wait_recv()
    vec_y = k.remote(gv.at[:, :, y], gv.at[:, :, y], k.py)
    vec_y.start()
    gather_q[1].s2()
    gather_o.s1()
    gather_q[0].s3()
    gather_q[2].s2()
    gather_u.s1()
    vec_y.wait_recv()
    table = k.local(gv, gvm)
    table.start()
    table.wait()
    table = gvm[...].reshape(256, 128).astype(BF)
    for index, wide in enumerate(WIDTHS):
        vrows[index : index + 1, 0 : 32 * wide] = spread_row(table, index, wide)
    tok_c.wait_recv()

    mine_cols = lanes(c * THIRD, THIRD)
    peer_cols = lanes(c2 * THIRD, THIRD)
    al_own = k.local(al_send.at[:, c], al.at[:, :, mine_cols])
    al_c = k.remote(al_send.at[:, c2], al.at[:, :, mine_cols], k.pc)
    limit = prefix[y] - 1
    sub = lax.broadcasted_iota(jnp.int32, (128, 256), 0)
    wq3 = wq.reshape(3, D, THIRD)

    def forward(n1, n1t, vt, qs, qst, keys_ref, values_ref, att, wqm):
        gain = vrows[0:1, 0:D]
        shift = vrows[1:2, 0:D]

        def norm_block(b, carry):
            normed, _ = unit_rows(tok_all[b // 2, lax.rem(b, 2)].astype(F32))
            normed = (normed * gain + shift).astype(BF)
            at = rows_at(b * 256, 256)
            n1[at, :] = normed
            n1t[:, at] = normed.astype(F32).T.astype(BF)
            return carry

        lax.fori_loop(0, 4, norm_block, 0)
        keep = [k.local(n1t, k_n1t), k.local(qs, k_qs), k.local(qst, k_qst), k.local(keys_ref, k_k),
                k.local(values_ref, k_v), k.local(att, k_att)]
        keep[0].start()
        gather_q[1].s3()
        load_q = [k.local(wq3.at[u], wqm.at[u]) for u in range(3)]
        load_o = k.local(wo.reshape(2, D, THIRD), wom)

        def head(u):
            gather_q[u].s4()
            load_q[u].start()
            load_q[u].wait()

        slots = {
            (0, 3): [gather_q[2].s3, gather_o.s2], (0, 2): [gather_u.s2, gather_d.s1], (0, 1): [gather_o.s3], (0, 0): [],
            (1, 3): [], (1, 2): [gather_u.s3], (1, 1): [gather_o.s4, gather_d.s2], (1, 0): [],
            (2, 3): [], (2, 2): [gather_o.done, load_o.start], (2, 1): [], (2, 0): [],
        }

        def unit(u, carry):
            cols = lanes(u * 128)
            for which in range(3):
                @pl.when(u == which)
                def _():
                    head(which)

            def project(b, inner):
                rows = rows_at(b * 256, 256)
                value = jnp.dot(n1[rows, :], wqm[u], preferred_element_type=F32)
                parts = []
                for kind in range(3):
                    bias = vrows[2:3, lanes(kind * D + c * THIRD + u * 128)]
                    parts.append((value[:, kind * 128 : (kind + 1) * 128] + bias).astype(BF))
                queries = parts[0].astype(F32) * 0.125
                qs[rows, cols] = queries.astype(BF)
                qst[cols, rows] = queries.T.astype(BF)
                keys_ref[rows, cols] = parts[1]
                values_ref[rows, cols] = parts[2]
                vt[cols, rows] = parts[2].astype(F32).T.astype(BF)
                return inner

            lax.fori_loop(0, 4, project, 0)
            for block in (3, 2, 1, 0):
                attend(u, block)
                for which in range(3):
                    if slots[which, block]:
                        @pl.when(u == which)
                        def _():
                            for step in slots[which, block]:
                                step()
            return carry

        def attend(u, block):
            rows = min(4, max(block + 1, 2)) * 256
            qcols = slice(block * 256, (block + 1) * 256)
            cols = lanes(u * 128)
            keys = keys_ref[0:rows, cols]
            queries = qst[cols, qcols]
            qpos = block * 256 + lax.broadcasted_iota(jnp.int32, (1, 256), 1)
            seen = lax.broadcasted_iota(jnp.int32, (rows, 256), 0) <= jnp.maximum(qpos, limit)
            for half in range(2):
                chosen = jnp.where(sub // 64 == half, queries, jnp.zeros_like(queries))
                scores = jnp.dot(keys, chosen, preferred_element_type=F32)
                size = jnp.where(seen, jnp.abs(scores), NEG)
                top = jnp.max(size, axis=0, keepdims=True)
                exponent = jnp.exp(size - top)
                total = jnp.sum(exponent, axis=0, keepdims=True)
                weights = jnp.where(scores > 0, exponent, jnp.where(scores < 0, -exponent, 0.0)).astype(BF)
                at = pl.ds(pl.multiple_of(u * 128 + half * 64, 64), 64)
                att[at, qcols] = jnp.dot(vt[at, 0:rows], weights, preferred_element_type=F32) / total
                lt[pl.ds(u * 2 + half, 1), qcols] = top + jnp.log(total)
            al_send[block // 2, block % 2, :, cols] = att[cols, qcols].T.astype(BF)

        lax.fori_loop(0, 3, unit, 0)
        al_own.start()
        al_c.start()
        start(keep[1:])
        gather_u.s4()
        gather_d.s3()
        load_o.wait()
        al_own.wait()
        al_c.wait_recv()
        landed(keep)

    pl.run_scoped(
        forward, vmem((1024, D), BF), vmem((D, 1024), BF), vmem((THIRD, 1024), BF), vmem((1024, THIRD), BF),
        vmem((THIRD, 1024), BF), vmem((1024, THIRD), BF), vmem((1024, THIRD), BF), vmem((THIRD, 1024), F32),
        vmem((3, D, THIRD), BF))

    def put_to(out, half):
        def put(value, core):
            out[:, lanes(core * half, half)] = value
        return put

    down = Scatter(k, gd, r0d, r1ad, r1bd, r2ad, r2bd, r3d, td, fd, put_to(out_d, THIRD), 128)
    up = Scatter(k, gu, r0u, r1au, r1bu, r2au, r2bu, r3u, tu, fu, put_to(out_u, 1536), 768)
    outp = Scatter(k, go, r0o, r1ao, r1bo, r2ao, r2bo, r3o, to, fo, put_to(out_o, THIRD), 256)

    def feed(wbuf, wdb, hid, slope, n2, n2t, alt, gpc):
        b_out, gain, shift = vrows[3:4, 0:D], vrows[4:5, 0:D], vrows[5:6, 0:D]

        def begin(yy, carry):
            rows = rows_at(yy * 256, 256)
            branch = jnp.concatenate([jnp.dot(al[yy], wom[h], preferred_element_type=F32) for h in range(2)], axis=1)
            residual = tok_all[yy, c].astype(F32) + branch + b_out
            fa[yy] = residual
            normed, _ = unit_rows(residual)
            normed = (normed * gain + shift).astype(BF)
            n2[rows, :] = normed
            n2t[:, rows] = normed.astype(F32).T.astype(BF)
            alt[:, rows] = al[yy].astype(F32).T.astype(BF)
            return carry

        lax.fori_loop(0, 2, begin, 0)
        own_cot.wait()
        cot_y.wait_recv()

        wu2 = wu.reshape(2, D, 1536)
        wd2 = wd.reshape(2, FF, THIRD)

        def chunk(j, first, second):
            h = first if j < 2 else second
            return h, j % 2

        def up_load(j, slot, order):
            h, part = chunk(j, *order)
            return k.local(wu2.at[h, :, part * D : (part + 1) * D], wbuf.at[slot])

        def down_load(j, slot, order):
            h, part = chunk(j, *order)
            return k.local(wd2.at[:, rows_at(h * 1536 + part * D, D), :], wdb.at[slot])

        forth = (c, c2)
        loads = [up_load(j, j % 2, forth) for j in range(4)]
        loads[0].start()
        for j in range(4):
            if j == 1:
                gather_u.done()
            if j < 3:
                loads[j + 1].start()
            loads[j].wait()
            h, part = chunk(j, *forth)
            cols = lanes(h * 1536 + part * D, D)

            def ahead(yy, carry):
                rows = rows_at(yy * 256, 256)
                value = jnp.dot(n2[rows, :], wbuf[j % 2], preferred_element_type=F32) + vrows[6:7, cols]
                result, bend = gelu_parts(value)
                hid[rows, cols] = result.astype(BF)
                slope[rows, cols] = bend
                return carry

            lax.fori_loop(0, 2, ahead, 0)
        vs[7:8, :] = jnp.sum(cotm[0].astype(F32), axis=0, keepdims=True) + jnp.sum(
            cotm[1].astype(F32), axis=0, keepdims=True)

        def down_grad(i, carry):
            total = jnp.zeros((THIRD, D), F32)
            for yy in range(2):
                total += lax.dot_general(hid[yy * 256 : (yy + 1) * 256, lanes(i * THIRD, THIRD)], cotm[yy], FIRST,
                                         preferred_element_type=F32)
            zz, xx = i // 2, lax.rem(i, 2)
            for yy in range(2):
                for h in range(2):
                    gd[h, zz, xx, yy] = total[yy * 192 : (yy + 1) * 192, h * THIRD : (h + 1) * THIRD].astype(BF)
            return carry

        lax.fori_loop(0, 8, down_grad, 0)
        down.s0()
        fb[...] = jnp.zeros_like(fb)
        fc[...] = jnp.zeros_like(fc)
        vup[...] = jnp.zeros_like(vup)
        gather_d.s4()
        back = (c2, c)
        again = [up_load(j, j % 2, back) for j in range(4)]
        lower = [down_load(j, j % 2, back) for j in range(4)]
        again[0].start()
        down.s1()
        gather_d.done()
        lower[0].start()
        for j in range(4):
            slot = j % 2
            if j < 3:
                again[j + 1].start()
                lower[j + 1].start()
            again[j].wait()
            lower[j].wait()
            h, part = chunk(j, *back)
            cols = lanes(h * 1536 + part * D, D)

            def behind(yy, carry):
                rows = rows_at(yy * 256, 256)
                units = hid[rows, cols]
                grad = None
                for side in range(2):
                    there = slice(side * THIRD, (side + 1) * THIRD)
                    fc[yy, :, there] += jnp.dot(units, wdb[slot, side], preferred_element_type=F32)
                    term = lax.dot_general(cotm[yy, :, there], wdb[slot, side], LAST, preferred_element_type=F32)
                    grad = term if grad is None else grad + term
                grad = (grad * slope[rows, cols]).astype(BF)
                gpc[rows, :] = grad
                vup[0:1, cols] += jnp.sum(grad.astype(F32), axis=0, keepdims=True)
                fb[yy] += lax.dot_general(grad, wbuf[slot], LAST, preferred_element_type=F32)
                return carry

            lax.fori_loop(0, 2, behind, 0)

            def up_grad(zz, carry):
                total = jnp.dot(n2t[rows_at(zz * 192, 192, 64), :], gpc[...], preferred_element_type=F32)
                for i in range(4):
                    gu[h, zz, i // 2, i % 2, :, part * D : (part + 1) * D] = total[i * 48 : (i + 1) * 48].astype(BF)
                return carry

            lax.fori_loop(0, 4, up_grad, 0)
            if j == 1:
                up.s0()
            if j == 2:
                down.s2()
        bo[...] = (fa[...] + fc[...] + vrows[7:8, 0:D].reshape(1, 1, D)).astype(BF)
        up.s1()

    ga_c = k.remote(ga_send.at[:, :, peer_cols], ga_all.at[:, c], k.pc)
    def turn(alt, gpc):
        gain = vrows[4:5, 0:D]
        vs[3:6, :] = jnp.zeros((3, D), F32)

        def mid_back(yy, carry):
            rows = rows_at(yy * 256, 256)
            normed, scale = unit_rows(fa[yy])
            grad = fb[yy]
            vs[4:5, :] += jnp.sum(grad * normed, axis=0, keepdims=True)
            vs[5:6, :] += jnp.sum(grad, axis=0, keepdims=True)
            total = cotm[yy].astype(F32) + norm_back(grad * gain, normed, scale)
            fa[yy] = total
            low = total.astype(BF)
            vs[3:4, :] += jnp.sum(low.astype(F32), axis=0, keepdims=True)
            gpc[rows, :] = low
            heads = None
            for side in range(2):
                term = lax.dot_general(low[:, side * THIRD : (side + 1) * THIRD], wom[side], LAST,
                                       preferred_element_type=F32)
                heads = term if heads is None else heads + term
            ga_send[yy] = heads.astype(BF)
            ga_all[yy, c] = ga_send[yy, :, mine_cols]
            return carry

        lax.fori_loop(0, 2, mid_back, 0)
        ga_c.start()

        def out_grad(zz, carry):
            total = jnp.dot(alt[rows_at(zz * 192, 192, 64), :], gpc[...], preferred_element_type=F32)
            for i in range(4):
                for h in range(2):
                    go[h, zz, i // 2, i % 2] = total[i * 48 : (i + 1) * 48, h * THIRD : (h + 1) * THIRD].astype(BF)
            return carry

        lax.fori_loop(0, 4, out_grad, 0)
        outp.s0()

    def put_q(u):
        def put(value, core):
            for kind in range(3):
                out_q[:, lanes(kind * D + core * THIRD + u * 128)] = value[:, kind * 128 : (kind + 1) * 128]
        return put

    bases = [k.fresh(3) for _ in range(8)]

    def query_scatter(u):
        return Scatter(k, gq.at[u], None, q1a.at[u], q1b.at[u], q2a.at[u], q2b.at[u], q3.at[u], tq.at[u], fq.at[u],
                       put_q(u), 128, base=[b + u for b in bases], whole=False)

    queue = [query_scatter(u) for u in range(3)]
    bo_own = k.local(bo.at[y], out_bo.at[y])
    bo_y = k.remote(bo.at[y2], out_bo.at[y], k.py)

    def send_out():
        bo_own.start()
        bo_y.start()

    def backward(alt, gpc, qs, qst, keys_ref, values_ref, att, n1t, gt, kt, dk, dv, gpu, wqm):
        loads = [k.local(k_qs, qs), k.local(k_qst, qst), k.local(k_k, keys_ref), k.local(k_v, values_ref),
                 k.local(k_att, att), k.local(k_n1t, n1t), k.local(wq3, wqm)]
        start(loads)
        turn(alt, gpc)
        fb[...] = jnp.zeros_like(fb)
        fc[...] = jnp.zeros_like(fc)
        ga_c.wait_recv()
        landed(loads)
        lane = lax.broadcasted_iota(jnp.int32, (256, 128), 1)
        vbq[...] = jnp.zeros_like(vbq)
        slots = {
            (0, 3): [outp.s1, down.s3], (0, 2): [], (0, 1): [up.s2], (0, 0): [send_out],
            (1, 3): [outp.s2], (1, 2): [down.s4], (1, 1): [up.s3], (1, 0): [outp.s3, down.s5],
            (2, 3): [queue[0].s2], (2, 2): [], (2, 1): [queue[0].s3], (2, 0): [outp.s4],
        }

        def unit(u, carry):
            cols = lanes(u * 128)
            for b in range(4):
                rows = slice(b * 256, (b + 1) * 256)
                gt[:, rows] = ga_all[b // 2, b % 2, :, cols].astype(F32).T.astype(BF)
                kt[:, rows] = keys_ref[rows, cols].astype(F32).T.astype(BF)
            dk[...] = jnp.zeros_like(dk)
            dv[...] = jnp.zeros_like(dv)
            for block in (3, 2, 1, 0):
                rows = min(4, max(block + 1, 2)) * 256
                qrange = slice(block * 256, (block + 1) * 256)
                keys = keys_ref[0:rows, cols]
                values = values_ref[0:rows, cols]
                queries_t = qst[cols, qrange]
                grads_t = gt[:, qrange]
                queries = qs[qrange, cols]
                grads = ga_all[block // 2, block % 2, :, cols]
                qpos = block * 256 + lax.broadcasted_iota(jnp.int32, (1, 256), 1)
                seen = lax.broadcasted_iota(jnp.int32, (rows, 256), 0) <= jnp.maximum(qpos, limit)
                prod = grads_t.astype(F32) * att[cols, qrange]
                dqs, dks, dvs = [], None, None
                for half in range(2):
                    part = slice(half * 64, half * 64 + 64)
                    in_sub = sub // 64 == half
                    in_lane = lane // 64 == half
                    delta = jnp.sum(prod[part], axis=0, keepdims=True)
                    total = lt[pl.ds(u * 2 + half, 1), qrange]
                    zero = jnp.zeros((), BF)
                    scores = jnp.dot(keys, jnp.where(in_sub, queries_t, zero), preferred_element_type=F32)
                    pull = jnp.dot(values, jnp.where(in_sub, grads_t, zero), preferred_element_type=F32)
                    share = jnp.exp(jnp.where(seen, jnp.abs(scores) - total, NEG))
                    signed = jnp.where(scores > 0, share, jnp.where(scores < 0, -share, 0.0))
                    grad_scores = (share * pull - signed * delta).astype(BF)
                    signed = signed.astype(BF)
                    dvt = jnp.dot(signed, jnp.where(in_lane, grads, zero), preferred_element_type=F32)
                    dkt = jnp.dot(grad_scores, jnp.where(in_lane, queries, zero), preferred_element_type=F32)
                    dvs = dvt if dvs is None else dvs + dvt
                    dks = dkt if dks is None else dks + dkt
                    dqs.append(jnp.dot(kt[part, 0:rows], grad_scores, preferred_element_type=F32))
                dk[0:rows, :] += dks
                dv[0:rows, :] += dvs
                gpu[qrange, 0:128] = (jnp.concatenate(dqs, axis=0).T * 0.125).astype(BF)
                for which in range(3):
                    if slots[which, block]:
                        @pl.when(u == which)
                        def _():
                            for step in slots[which, block]:
                                step()
            gpu[:, 128:256] = dk[...].astype(BF)
            gpu[:, 256:384] = dv[...].astype(BF)
            sums = jnp.sum(gpu[...].astype(F32), axis=0, keepdims=True)
            for kind in range(3):
                part = slice(kind * 128, (kind + 1) * 128)
                vbq[0:1, lanes(kind * D + c * THIRD + u * 128)] = sums[:, part]

            def weights(zz, inner):
                block = jnp.dot(n1t[rows_at(zz * 192, 192, 64), :], gpu[...], preferred_element_type=F32)
                for i in range(4):
                    gq[u, zz, i // 2, i % 2] = block[i * 48 : (i + 1) * 48].astype(BF)
                return inner

            lax.fori_loop(0, 4, weights, 0)
            for which in range(3):
                @pl.when(u == which)
                def _():
                    queue[which].s1()

            def back_rows(b):
                return lax.dot_general(gpu[rows_at(b * 256, 256), :], wqm[u], LAST, preferred_element_type=F32)

            def back_peer(yy, inner):
                fb[yy] += back_rows(yy * 2 + c2)
                return inner

            def back_own(yy, inner):
                fc[yy] += back_rows(yy * 2 + c)
                return inner

            lax.fori_loop(0, 2, back_peer, 0)

            @pl.when(u == 2)
            def _():
                part_c.start()

            lax.fori_loop(0, 2, back_own, 0)
            return carry

        lax.fori_loop(0, 3, unit, 0)

    part_c = k.remote(fb, fr, k.pc)

    def both(alt, gpc):
        pl.run_scoped(
            functools.partial(feed, alt=alt, gpc=gpc), vmem((2, D, D), BF), vmem((2, 2, D, THIRD), BF),
            vmem((512, FF), BF), vmem((512, FF), F32), vmem((512, D), BF), vmem((D, 512), BF))
        pl.run_scoped(
            functools.partial(backward, alt, gpc), vmem((1024, THIRD), BF), vmem((THIRD, 1024), BF), vmem((1024, THIRD), BF),
            vmem((1024, THIRD), BF), vmem((THIRD, 1024), F32), vmem((D, 1024), BF), vmem((128, 1024), BF),
            vmem((128, 1024), BF), vmem((1024, 128), F32), vmem((1024, 128), F32), vmem((1024, THIRD), BF),
            vmem((3, D, THIRD), BF))

    pl.run_scoped(both, vmem((D, 512), BF), vmem((512, D), BF))

    queue[1].s2()
    gain = vrows[0:1, 0:D]
    vs[0:2, :] = jnp.zeros((2, D), F32)

    def sums(core, ref):
        def add(yy, carry):
            normed, _ = unit_rows(tok_all[yy, core].astype(F32))
            grad = ref[yy]
            vs[0:1, :] += jnp.sum(grad * normed, axis=0, keepdims=True)
            vs[1:2, :] += jnp.sum(grad, axis=0, keepdims=True)
            return carry

        lax.fori_loop(0, 2, add, 0)

    sums(c2, fb)
    sums(c, fc)
    for index, wide in enumerate(WIDTHS):
        row = vbq[...] if index == 2 else vup[...] if index == 6 else vs[index : index + 1, :]
        vtab[pl.ds(index, 32, stride=8), :] = collect_rows(row, wide)
    table = vtab.reshape(4, 2, 2, 2, 8, 128)
    v0 = k.remote(table.at[:, :, :, c2], vr0, k.pc)
    v1 = k.remote(table.at[:, :, y2, c], vr1, k.py)
    v2 = k.remote(table.at[:, x2, y, c], vr2, k.px)
    v3 = [k.remote(table.at[k.zs[d], x, y, c], vr3.at[d], k.pz[d]) for d in range(3)]

    def tile(zz, xx, yy):
        return rows_at((((zz * 2 + xx) * 2 + yy) * 2 + c) * 8, 8, 8)

    v0.start()
    queue[2].s2()
    part_c.wait_recv()

    def last_back(yy):
        normed, scale = unit_rows(tok_all[yy, c].astype(F32))
        grad = fc[yy] + fr[yy]
        gtb[yy] = (fa[yy] + norm_back(grad * gain, normed, scale)).astype(BF)

    gt_own = k.local(gtb.at[y], out_gt.at[y])
    gt_y = k.remote(gtb.at[y2], out_gt.at[y], k.py)
    last_back(y2)
    gt_y.start()
    last_back(y)
    gt_own.start()
    v0.wait_recv()

    def add_core(i, carry):
        zz, xx, yy = i // 4, lax.rem(i // 2, 2), lax.rem(i, 2)
        vtab[tile(zz, xx, yy), :] += vr0[zz, xx, yy]
        return carry

    lax.fori_loop(0, 16, add_core, 0)
    v1.start()
    queue[1].s3()
    queue[2].s3()
    up.s4()
    queue[0].s4()
    v1.wait_recv()

    def add_y(i, carry):
        vtab[tile(i // 2, lax.rem(i, 2), y), :] += vr1[i // 2, lax.rem(i, 2)]
        return carry

    lax.fori_loop(0, 8, add_y, 0)
    v2.start()
    outp.s5()
    queue[1].s4()
    v2.wait_recv()

    def add_x(zz, carry):
        vtab[tile(zz, x, y), :] += vr2[zz]
        return carry

    lax.fori_loop(0, 4, add_x, 0)
    start(v3)
    queue[2].s4()
    up.s5()
    queue[0].s5()
    queue[1].s5()
    queue[2].s5()
    arrive(v3)
    out_vec[...] = vtab[tile(z, x, y), :] + vr3[0] + vr3[1] + vr3[2]
    landed([gt_own, bo_own])
    arrive([gt_y, bo_y])
    for copy in k.sent:
        copy.wait_send()
    for scatter in queue:
        scatter.gone()


def layer_call(*operands):
    sds = jax.ShapeDtypeStruct
    vmem = pltpu.VMEM
    dma = pltpu.SemaphoreType.DMA
    results = (
        sds((2, 256, D), BF), sds((2, 256, D), BF), sds((24, 3 * D), F32), sds((24, D), F32), sds((24, FF), F32),
        sds((96, D), F32), sds((8, 128), F32),
    )
    held = (
        sds((3, 4, 2, 2, 48, 384), BF), sds((2, 4, 2, 2, 48, 384), BF), sds((2, 4, 2, 2, 48, 1536), BF),
        sds((2, 4, 2, 2, 192, 384), BF), sds((4, 2, 2, 2, 8, 128), F32), sds((1024, THIRD), BF), sds((THIRD, 1024), BF),
        sds((1024, THIRD), BF), sds((1024, THIRD), BF), sds((THIRD, 1024), F32), sds((D, 1024), BF),
    )
    scratch = [
        vmem((8, 128), F32), vmem((2, 3, 24, THIRD), BF), vmem((4, 2, 2, 2, 8, 128), F32), vmem((2, 2, 256, D), BF), vmem((8, FF), F32),
        vmem((2, D, THIRD), BF), vmem((2, 2, 256, THIRD), BF), vmem((2, 256, D), BF), vmem((2, 256, D), BF),
        vmem((2, 256, D), BF), vmem((2, 2, 256, THIRD), BF), vmem((2, 256, D), F32), vmem((2, 256, D), F32),
        vmem((2, 256, D), F32), vmem((2, 256, D), F32), vmem((8, 1024), F32),
    ]
    kinds = ((192, 384, 128), (48, 1536, 768), (48, 384, 256))
    scratch += [vmem((2, 4, 2, 2, r, n), BF) for r, n, _ in kinds] + [vmem((3, 4, 2, 2, 48, 384), BF)]
    scratch += [vmem((4, 2, 2, r, n), BF) for r, n, _ in kinds]
    for r, n, cut in kinds:
        scratch += [vmem((4, 2, r, cut), BF), vmem((4, 2, r, n - cut), BF)]
    for r, n, cut in kinds:
        scratch += [vmem((4, r, cut), BF), vmem((4, r, n - cut), BF)]
    scratch += [vmem((3, r, n), BF) for r, n, _ in kinds]
    scratch += [vmem((2, r // 2, n), F32) for r, n, _ in kinds]
    scratch += [vmem((r // 2, n), F32) for r, n, _ in kinds]
    scratch += [
        vmem((3, 4, 2, 48, 128), BF), vmem((3, 4, 2, 48, 256), BF), vmem((3, 4, 48, 128), BF), vmem((3, 4, 48, 256), BF),
        vmem((3, 3, 48, 384), BF), vmem((3, 2, 24, 384), F32), vmem((3, 24, 384), F32),
        vmem((8, D), F32), vmem((1, 3 * D), F32), vmem((1, FF), F32), vmem((256, 128), F32), vmem((4, 2, 2, 8, 128), F32),
        vmem((4, 2, 8, 128), F32), vmem((4, 8, 128), F32), vmem((3, 8, 128), F32),
        dma((REMOTES,)), dma((REMOTES,)), dma((LOCALS,)),
    ]
    return pl.pallas_call(
        layer_kernel,
        out_shape=results + held,
        in_specs=[SM] + [ANY] * 2 + [VM] * 12,
        out_specs=(ANY, ANY) + (VM,) * 5 + (ANY,) * len(held),
        scratch_shapes=scratch,
        compiler_params=pltpu.CompilerParams(
            collective_id=0, has_side_effects=True, vmem_limit_bytes=63 * 2**20),
    )(*operands)[: len(results)]


def finish_kernel(bo, gt, gq, go, gu, gd, gvec, *out):
    for source, result in zip((bo, gt, gq, go, gu, gd), out[:6]):
        result[...] = source[...]
    for index, wide in enumerate(WIDTHS):
        out[6 + index][...] = gvec[index, 0:wide]


def finish_call(*operands):
    sds = jax.ShapeDtypeStruct
    shapes = tuple(sds(o.shape, o.dtype) for o in operands[:6]) + tuple(sds((wide,), F32) for wide in WIDTHS)
    return pl.pallas_call(
        finish_kernel, out_shape=shapes, in_specs=[VM] * 7, out_specs=(VM,) * 14,
        compiler_params=pltpu.CompilerParams(vmem_limit_bytes=32 * 2**20),
    )(*operands)


def body(
    tokens, cotangent, prefix, ln1_gain, ln1_bias, w_qkv, b_qkv, w_out, b_out,
    ln2_gain, ln2_bias, w_up, b_up, w_down, b_down,
):
    results = layer_call(
        prefix, tokens, cotangent, ln1_gain, ln1_bias, b_qkv, b_out, ln2_gain, ln2_bias, b_up, b_down,
        w_qkv, w_out, w_up, w_down)
    block_out, grad_tokens, gq, go, gu, gd, *rows = finish_call(*results)
    return (
        block_out, grad_tokens, rows[0], rows[1], gq, rows[2], go, rows[3], rows[4], rows[5], gu, rows[6], gd, rows[7],
    )


def fits(mesh):
    return dict(mesh.shape) == {"dp": 8, "seq": 4}


norm_eps = 1e-05
block_rows = 512


def layer_norm(features, gain, shift):
    centre = features - jnp.mean(features, axis=-1, keepdims=True)
    spread = jnp.mean(centre * centre, axis=-1, keepdims=True)
    return centre * lax.rsqrt(spread + norm_eps) * gain + shift


def gelu_tanh(values):
    return jax.nn.gelu(values, approximate=True)


def in_blocks(update, running, pieces):
    length = pieces[0].shape[1]
    blocks = length // block_rows
    blocked_pieces = tuple(
        (
            jnp.swapaxes(
                member.reshape((member.shape[0], blocks, block_rows) + member.shape[2:]), 0, 1
            )
            for member in pieces
        )
    )

    def advance(carried, element):
        return (update(carried, element[0], element[1] * block_rows), None)

    running, unused = lax.scan(
        advance, running, (blocked_pieces, jnp.arange(blocks, dtype=jnp.int32))
    )
    return running


def to_heads(flat_rows):
    return flat_rows.reshape(flat_rows.shape[0], flat_rows.shape[1], HEADS, HEAD_DIM)


def visible_mask(query_places, key_places, prefix_len):
    earlier = key_places[None, None, :] <= query_places[None, :, None]
    in_prefix = key_places[None, None, :] < prefix_len[:, None, None]
    return (earlier | in_prefix)[:, :, None, :]


def head_scores(query_heads, key_flat):
    return jnp.einsum(
        "bqhd,bkhd->bqhk", query_heads, to_heads(key_flat), preferred_element_type=jnp.float32
    ) * HEAD_DIM ** (-0.5)


def attend(query_heads, key_flat, value_flat, prefix_len):
    local_len = query_heads.shape[1]
    query_places = lax.axis_index("seq") * local_len + jnp.arange(local_len, dtype=jnp.int32)
    starting = (
        jnp.zeros(query_heads.shape, jnp.float32),
        jnp.zeros(query_heads.shape[:3], jnp.float32),
        jnp.zeros(query_heads.shape[:3], jnp.float32),
    )

    def update(running, pieces, offset):
        weighted, normaliser, ceiling = running
        key_piece, value_piece = pieces
        key_places = offset + jnp.arange(key_piece.shape[1], dtype=jnp.int32)
        scores = head_scores(query_heads, key_piece)
        visible = visible_mask(query_places, key_places, prefix_len)
        magnitude = jnp.where(visible, jnp.abs(scores), 0.0)
        new_ceiling = jnp.maximum(ceiling, jnp.max(magnitude, axis=-1))
        exponent = jnp.where(visible, jnp.exp(magnitude - new_ceiling[..., None]), 0.0)
        factor = jnp.exp(ceiling - new_ceiling)
        weights = (jnp.sign(scores) * exponent).astype(jnp.bfloat16)
        weighted = weighted * factor[..., None] + jnp.einsum(
            "bqhk,bkhd->bqhd", weights, to_heads(value_piece), preferred_element_type=jnp.float32
        )
        normaliser = normaliser * factor + jnp.sum(exponent, axis=-1)
        return (weighted, normaliser, new_ceiling)

    weighted, normaliser, ceiling = in_blocks(
        update,
        starting,
        (
            lax.all_gather(key_flat, "seq", axis=1, tiled=True),
            lax.all_gather(value_flat, "seq", axis=1, tiled=True),
        ),
    )
    return (weighted / normaliser[..., None], ceiling + jnp.log(normaliser))


def grad_terms(
    query_heads,
    grad_heads,
    key_flat,
    value_flat,
    log_total,
    delta_sum,
    query_places,
    key_places,
    prefix_len,
):
    scores = head_scores(query_heads, key_flat)
    sign_of = jnp.sign(scores)
    visible = visible_mask(query_places, key_places, prefix_len)
    shares = jnp.where(visible, jnp.exp(jnp.abs(scores) - log_total[..., None]), 0.0)
    grad_weights = jnp.einsum(
        "bqhd,bkhd->bqhk", grad_heads, to_heads(value_flat), preferred_element_type=jnp.float32
    )
    grad_scores = (shares * (grad_weights - sign_of * delta_sum[..., None])).astype(jnp.bfloat16)
    return ((sign_of * shares).astype(jnp.bfloat16), grad_scores)


def query_term(grad_scores, key_flat):
    return jnp.einsum(
        "bqhk,bkhd->bqhd", grad_scores, to_heads(key_flat), preferred_element_type=jnp.float32
    ) * HEAD_DIM ** (-0.5)


def key_value_terms(query_heads, grad_heads, shares_low, grad_scores):
    key_term = jnp.einsum(
        "bqhk,bqhd->bkhd", grad_scores, query_heads, preferred_element_type=jnp.float32
    ) * HEAD_DIM ** (-0.5)
    value_term = jnp.einsum(
        "bqhk,bqhd->bkhd", shares_low, grad_heads, preferred_element_type=jnp.float32
    )
    flat_shape = (key_term.shape[0], key_term.shape[1], key_term.shape[2] * key_term.shape[3])
    return jnp.concatenate([key_term.reshape(flat_shape), value_term.reshape(flat_shape)], axis=-1)


def attend_back(query_heads, key_flat, value_flat, grad_heads, log_total, delta_sum, prefix_len):
    seq_block, local_len = (query_heads.shape[0], query_heads.shape[1])
    width = key_flat.shape[2]
    local_places = lax.axis_index("seq") * local_len + jnp.arange(local_len, dtype=jnp.int32)
    starting = (
        jnp.zeros(query_heads.shape, jnp.float32),
        jnp.zeros((seq_block, lax.axis_size("seq") * local_len, 2 * width), jnp.float32),
    )

    def update_both(running, pieces, offset):
        grad_query, grad_keys = running
        key_piece, value_piece = pieces
        piece_len = key_piece.shape[1]
        key_places = offset + jnp.arange(piece_len, dtype=jnp.int32)
        shares_low, grad_scores = grad_terms(
            query_heads,
            grad_heads,
            key_piece,
            value_piece,
            log_total,
            delta_sum,
            local_places,
            key_places,
            prefix_len,
        )
        grad_query = grad_query + query_term(grad_scores, key_piece)
        current = lax.dynamic_slice_in_dim(grad_keys, offset, piece_len, 1)
        updated = current + key_value_terms(query_heads, grad_heads, shares_low, grad_scores)
        return (grad_query, lax.dynamic_update_slice_in_dim(grad_keys, updated, offset, 1))

    grad_query, grad_keys = in_blocks(
        update_both,
        starting,
        (
            lax.all_gather(key_flat, "seq", axis=1, tiled=True),
            lax.all_gather(value_flat, "seq", axis=1, tiled=True),
        ),
    )
    key_local = lax.psum_scatter(
        grad_keys.astype(jnp.bfloat16), "seq", scatter_dimension=1, tiled=True
    ).astype(jnp.float32)
    return (grad_query, key_local)


def forward_block(weights_in, token_part, prefix_len):
    (
        gain_one,
        shift_one,
        w_qkv,
        b_qkv,
        w_out,
        b_out,
        gain_two,
        shift_two,
        w_up,
        b_up,
        w_down,
        b_down,
    ) = weights_in
    seq_block, local_len, width = token_part.shape
    residual_in = token_part.reshape(-1, width).astype(jnp.float32)
    normed_one = layer_norm(
        residual_in, gain_one.astype(jnp.float32), shift_one.astype(jnp.float32)
    ).astype(jnp.bfloat16)
    projected = jnp.dot(normed_one, w_qkv, preferred_element_type=jnp.float32) + b_qkv.astype(
        jnp.float32
    )
    query_heads = (
        projected[:, :width].astype(jnp.bfloat16).reshape(seq_block, local_len, HEADS, HEAD_DIM)
    )
    key_flat = (
        projected[:, width : 2 * width].astype(jnp.bfloat16).reshape(seq_block, local_len, width)
    )
    value_flat = projected[:, 2 * width :].astype(jnp.bfloat16).reshape(seq_block, local_len, width)
    attended, log_total = attend(query_heads, key_flat, value_flat, prefix_len)
    attended_low = attended.reshape(-1, width).astype(jnp.bfloat16)
    residual_mid = (
        residual_in
        + jnp.dot(attended_low, w_out, preferred_element_type=jnp.float32)
        + b_out.astype(jnp.float32)
    )
    normed_two = layer_norm(
        residual_mid, gain_two.astype(jnp.float32), shift_two.astype(jnp.float32)
    ).astype(jnp.bfloat16)
    pre_gelu = jnp.dot(normed_two, w_up, preferred_element_type=jnp.float32) + b_up.astype(
        jnp.float32
    )
    hidden = gelu_tanh(pre_gelu).astype(jnp.bfloat16)
    result = (
        residual_mid
        + jnp.dot(hidden, w_down, preferred_element_type=jnp.float32)
        + b_down.astype(jnp.float32)
    )
    saved = (
        residual_in,
        normed_one,
        query_heads,
        key_flat,
        value_flat,
        attended,
        log_total,
        attended_low,
        residual_mid,
        normed_two,
        pre_gelu,
        hidden,
    )
    return (result.astype(jnp.bfloat16).reshape(token_part.shape), saved)


def backward_block(weights_in, saved, grad_part, prefix_len):
    (
        gain_one,
        shift_one,
        w_qkv,
        b_qkv,
        w_out,
        b_out,
        gain_two,
        shift_two,
        w_up,
        b_up,
        w_down,
        b_down,
    ) = weights_in
    (
        residual_in,
        normed_one,
        query_heads,
        key_flat,
        value_flat,
        attended,
        log_total,
        attended_low,
        residual_mid,
        normed_two,
        pre_gelu,
        hidden,
    ) = saved
    seq_block, local_len, width = grad_part.shape
    grad_result = grad_part.reshape(-1, width).astype(jnp.float32)
    grad_branch = grad_part.reshape(-1, width)
    grads_down = jnp.einsum("rf,rd->fd", hidden, grad_branch, preferred_element_type=jnp.float32)
    bias_down = jnp.sum(grad_branch, axis=0, dtype=jnp.float32)
    grad_hidden = jnp.einsum("rd,fd->rf", grad_branch, w_down, preferred_element_type=jnp.float32)
    gelu_pull = jax.vjp(gelu_tanh, pre_gelu)[1]
    grad_pre = gelu_pull(grad_hidden)[0].astype(jnp.bfloat16)
    grads_up = jnp.einsum("rd,rf->df", normed_two, grad_pre, preferred_element_type=jnp.float32)
    bias_up = jnp.sum(grad_pre, axis=0, dtype=jnp.float32)
    grad_normed_two = jnp.einsum("rf,df->rd", grad_pre, w_up, preferred_element_type=jnp.float32)
    norm_two_pull = jax.vjp(
        layer_norm, residual_mid, gain_two.astype(jnp.float32), shift_two.astype(jnp.float32)
    )[1]
    grad_mid, grads_gain_two, grads_shift_two = norm_two_pull(grad_normed_two)
    grad_mid = grad_mid + grad_result
    grad_attn = grad_mid.astype(jnp.bfloat16)
    grads_out = jnp.einsum("rd,re->de", attended_low, grad_attn, preferred_element_type=jnp.float32)
    bias_out = jnp.sum(grad_attn, axis=0, dtype=jnp.float32)
    grad_heads = (
        jnp.einsum("re,de->rd", grad_attn, w_out, preferred_element_type=jnp.float32)
        .astype(jnp.bfloat16)
        .reshape(seq_block, local_len, HEADS, HEAD_DIM)
    )
    delta_sum = jnp.sum(grad_heads.astype(jnp.float32) * attended, axis=-1)
    grad_query, key_local = attend_back(
        query_heads, key_flat, value_flat, grad_heads, log_total, delta_sum, prefix_len
    )
    grad_proj = jnp.concatenate(
        [grad_query.reshape(-1, width), key_local.reshape(-1, 2 * width)], axis=1
    ).astype(jnp.bfloat16)
    grads_qkv = jnp.einsum("rd,re->de", normed_one, grad_proj, preferred_element_type=jnp.float32)
    bias_qkv = jnp.sum(grad_proj, axis=0, dtype=jnp.float32)
    grad_normed_one = jnp.einsum("re,de->rd", grad_proj, w_qkv, preferred_element_type=jnp.float32)
    norm_one_pull = jax.vjp(
        layer_norm, residual_in, gain_one.astype(jnp.float32), shift_one.astype(jnp.float32)
    )[1]
    grad_in, grads_gain_one, grads_shift_one = norm_one_pull(grad_normed_one)
    grad_in = grad_in + grad_mid
    weight_grads = (
        grads_gain_one,
        grads_shift_one,
        grads_qkv,
        bias_qkv,
        grads_out,
        bias_out,
        grads_gain_two,
        grads_shift_two,
        grads_up,
        bias_up,
        grads_down,
        bias_down,
    )
    return (grad_in.astype(jnp.bfloat16).reshape(grad_part.shape), weight_grads)


def general_body(
    tokens,
    cotangent,
    prefix,
    ln1_gain,
    ln1_bias,
    w_qkv,
    b_qkv,
    w_out,
    b_out,
    ln2_gain,
    ln2_bias,
    w_up,
    b_up,
    w_down,
    b_down,
):
    shards = (
        ln1_gain,
        ln1_bias,
        w_qkv,
        b_qkv,
        w_out,
        b_out,
        ln2_gain,
        ln2_bias,
        w_up,
        b_up,
        w_down,
        b_down,
    )
    spread_count = lax.axis_size(("dp", "seq"))
    totals = tuple(
        (
            jnp.zeros((member.shape[0] * spread_count,) + member.shape[1:], jnp.float32)
            for member in shards
        )
    )
    seq_block = tokens.shape[0] // MB
    outputs = []
    grad_inputs = []
    for batch_index in range(MB):
        first_row = batch_index * seq_block
        token_part = tokens[first_row : first_row + seq_block]
        cotangent_part = cotangent[first_row : first_row + seq_block]
        prefix_part = prefix[first_row : first_row + seq_block]
        forward_weights = (
            lax.all_gather(shards[0], ("dp", "seq"), axis=0, tiled=True),
            lax.all_gather(shards[1], ("dp", "seq"), axis=0, tiled=True),
            lax.all_gather(shards[2], ("dp", "seq"), axis=0, tiled=True),
            lax.all_gather(shards[3], ("dp", "seq"), axis=0, tiled=True),
            lax.all_gather(shards[4], ("dp", "seq"), axis=0, tiled=True),
            lax.all_gather(shards[5], ("dp", "seq"), axis=0, tiled=True),
            lax.all_gather(shards[6], ("dp", "seq"), axis=0, tiled=True),
            lax.all_gather(shards[7], ("dp", "seq"), axis=0, tiled=True),
            lax.all_gather(shards[8], ("dp", "seq"), axis=0, tiled=True),
            lax.all_gather(shards[9], ("dp", "seq"), axis=0, tiled=True),
            lax.all_gather(shards[10], ("dp", "seq"), axis=0, tiled=True),
            lax.all_gather(shards[11], ("dp", "seq"), axis=0, tiled=True),
        )
        result, saved = forward_block(forward_weights, token_part, prefix_part)
        back_weights = (
            lax.all_gather(shards[0], ("dp", "seq"), axis=0, tiled=True),
            lax.all_gather(shards[1], ("dp", "seq"), axis=0, tiled=True),
            lax.all_gather(shards[2], ("dp", "seq"), axis=0, tiled=True),
            lax.all_gather(shards[3], ("dp", "seq"), axis=0, tiled=True),
            lax.all_gather(shards[4], ("dp", "seq"), axis=0, tiled=True),
            lax.all_gather(shards[5], ("dp", "seq"), axis=0, tiled=True),
            lax.all_gather(shards[6], ("dp", "seq"), axis=0, tiled=True),
            lax.all_gather(shards[7], ("dp", "seq"), axis=0, tiled=True),
            lax.all_gather(shards[8], ("dp", "seq"), axis=0, tiled=True),
            lax.all_gather(shards[9], ("dp", "seq"), axis=0, tiled=True),
            lax.all_gather(shards[10], ("dp", "seq"), axis=0, tiled=True),
            lax.all_gather(shards[11], ("dp", "seq"), axis=0, tiled=True),
        )
        grad_piece, weight_grads = backward_block(back_weights, saved, cotangent_part, prefix_part)
        totals = tuple(
            (running_sum + new_term for running_sum, new_term in zip(totals, weight_grads))
        )
        outputs.append(result)
        grad_inputs.append(grad_piece)
    reduced = (
        lax.psum_scatter(totals[0], ("dp", "seq"), scatter_dimension=0, tiled=True),
        lax.psum_scatter(totals[1], ("dp", "seq"), scatter_dimension=0, tiled=True),
        lax.psum_scatter(totals[2], ("dp", "seq"), scatter_dimension=0, tiled=True),
        lax.psum_scatter(totals[3], ("dp", "seq"), scatter_dimension=0, tiled=True),
        lax.psum_scatter(totals[4], ("dp", "seq"), scatter_dimension=0, tiled=True),
        lax.psum_scatter(totals[5], ("dp", "seq"), scatter_dimension=0, tiled=True),
        lax.psum_scatter(totals[6], ("dp", "seq"), scatter_dimension=0, tiled=True),
        lax.psum_scatter(totals[7], ("dp", "seq"), scatter_dimension=0, tiled=True),
        lax.psum_scatter(totals[8], ("dp", "seq"), scatter_dimension=0, tiled=True),
        lax.psum_scatter(totals[9], ("dp", "seq"), scatter_dimension=0, tiled=True),
        lax.psum_scatter(totals[10], ("dp", "seq"), scatter_dimension=0, tiled=True),
        lax.psum_scatter(totals[11], ("dp", "seq"), scatter_dimension=0, tiled=True),
    )
    return (
        jnp.concatenate(outputs, axis=0),
        jnp.concatenate(grad_inputs, axis=0),
        reduced[0],
        reduced[1],
        reduced[2],
        reduced[3],
        reduced[4],
        reduced[5],
        reduced[6],
        reduced[7],
        reduced[8],
        reduced[9],
        reduced[10],
        reduced[11],
    )


def solution(mesh):
    in_specs = (
        P("dp", "seq", None),
        P("dp", "seq", None),
        P("dp"),
        P(("dp", "seq")),
        P(("dp", "seq")),
        P(("dp", "seq"), None),
        P(("dp", "seq")),
        P(("dp", "seq"), None),
        P(("dp", "seq")),
        P(("dp", "seq")),
        P(("dp", "seq")),
        P(("dp", "seq"), None),
        P(("dp", "seq")),
        P(("dp", "seq"), None),
        P(("dp", "seq")),
    )
    out_specs = (
        P("dp", "seq", None),
        P("dp", "seq", None),
        P(("dp", "seq")),
        P(("dp", "seq")),
        P(("dp", "seq"), None),
        P(("dp", "seq")),
        P(("dp", "seq"), None),
        P(("dp", "seq")),
        P(("dp", "seq")),
        P(("dp", "seq")),
        P(("dp", "seq"), None),
        P(("dp", "seq")),
        P(("dp", "seq"), None),
        P(("dp", "seq")),
    )
    chosen = body if fits(mesh) else general_body
    return jax.shard_map(chosen, mesh=mesh, in_specs=in_specs, out_specs=out_specs, check_vma=False)
```

```python
import functools

import jax
import jax.numpy as jnp
from jax import lax
from jax.experimental import pallas as pl
from jax.experimental.pallas import tpu as pltpu
from jax.sharding import PartitionSpec as P

HEADS = 12
HEAD_DIM = 64
MB = 2

F32 = jnp.float32
BF = jnp.bfloat16
EPS = 1e-05
MESH = pl.DeviceIdType.MESH
NEG = -1e30
ANY = pl.BlockSpec(memory_space=pl.ANY)
VM = pl.BlockSpec(memory_space=pltpu.VMEM)
SM = pl.BlockSpec(memory_space=pltpu.SMEM)
WIDTHS = (24, 24, 72, 24, 24, 24, 96, 24)
D = 768
FF = 3072
THIRD = 384
LAST = (((1,), (1,)), ((), ()))
FIRST = (((0,), (0,)), ((), ()))
ALL = slice(None)
REMOTES = 160
LOCALS = 64


def places():
    dp = lax.axis_index("dp")
    sq = lax.axis_index("seq")
    return dp // 2, dp % 2, sq // 2, sq % 2


def device(z, x, y, c):
    return (z * 2 + x, y * 2 + c)


def owner_of(wide):
    column = lax.broadcasted_iota(jnp.int32, (1, 32 * wide), 1).astype(F32)
    owner = jnp.floor((column + 0.5) * (1.0 / wide))
    return owner.astype(jnp.int32), (column - owner * wide).astype(jnp.int32)


def spread_row(gathered, index, wide):
    total = 32 * wide
    row = lax.broadcasted_iota(jnp.int32, (32, 256), 0)
    place = lax.broadcasted_iota(jnp.int32, (32, 256), 1)
    pick = jnp.where(place == row * 8 + index, 1.0, 0.0).astype(BF)
    mine = jnp.dot(pick, gathered, preferred_element_type=F32).astype(BF)
    owner, rest = owner_of(wide)
    spread = jnp.where(lax.broadcasted_iota(jnp.int32, (128, total), 0) == rest, 1.0, 0.0).astype(BF)
    full = jnp.dot(mine, spread, preferred_element_type=F32)
    keep = lax.broadcasted_iota(jnp.int32, (32, total), 0) == owner
    return jnp.sum(jnp.where(keep, full, 0.0), axis=0, keepdims=True)


def collect_rows(vector, wide):
    total = 32 * wide
    owner, rest = owner_of(wide)
    gather = jnp.where(lax.broadcasted_iota(jnp.int32, (128, total), 0) == rest, 1.0, 0.0).astype(BF)
    keep = lax.broadcasted_iota(jnp.int32, (32, total), 0) == owner
    high = vector.astype(BF).astype(F32)
    out = None
    for part in (high, vector - high):
        placed = jnp.where(keep, part, 0.0).astype(BF)
        term = lax.dot_general(placed, gather, LAST, preferred_element_type=F32)
        out = term if out is None else out + term
    return out


def add_into(ref, at, other):
    ref[at] = (ref[at].astype(F32) + other.astype(F32)).astype(BF)


def start(copies):
    for copy in copies:
        copy.start()


def arrive(copies):
    for copy in copies:
        copy.wait_recv()


def landed(copies):
    for copy in copies:
        copy.wait()


def lanes(first, count=128):
    return pl.ds(pl.multiple_of(first, 128), count)


def rows_at(first, count, step=256):
    return pl.ds(pl.multiple_of(first, step), count)


class Links:
    def __init__(self, ssem, rsem, lsem):
        self.ssem, self.rsem, self.lsem = ssem, rsem, lsem
        self.remotes = self.locals = 0
        self.sent = []
        z, x, y, c = places()
        self.z, self.x, self.y, self.c = z, x, y, c
        self.x2, self.y2, self.c2 = 1 - x, 1 - y, 1 - c
        self.px, self.py, self.pc = device(z, 1 - x, y, c), device(z, x, 1 - y, c), device(z, x, y, 1 - c)
        self.zs = [lax.rem(z + d, 4) for d in (1, 2, 3)]
        self.pz = [device(zz, x, y, c) for zz in self.zs]

    def fresh(self, count=1):
        first = self.remotes
        self.remotes += count
        return first

    def remote(self, src, dst, dev, at=None):
        i = self.fresh() if at is None else at
        copy = pltpu.make_async_remote_copy(
            src_ref=src, dst_ref=dst, send_sem=self.ssem.at[i], recv_sem=self.rsem.at[i],
            device_id=dev, device_id_type=MESH)
        if at is None:
            self.sent.append(copy)
        return copy

    def local(self, src, dst):
        i = self.locals
        self.locals += 1
        return pltpu.make_async_copy(src, dst, self.lsem.at[i])

    def greet(self):
        barrier = pltpu.get_barrier_semaphore()
        for dev in [self.px, self.py, self.pc] + self.pz:
            pl.semaphore_signal(barrier, inc=1, device_id=dev, device_id_type=MESH)

    def greeted(self):
        pl.semaphore_wait(pltpu.get_barrier_semaphore(), 6)


class Gather:
    def __init__(self, links, own, other, mine, theirs, cut, whole=True):
        k = links
        rows = own.shape[0]
        at = pl.ds(pl.multiple_of(k.c * rows, 8), rows)
        z, x, y = k.z, k.x, k.y
        self.own = [k.local(own, mine.at[z, x, y, at])]
        self.c0 = [k.remote(other, theirs.at[z, x, y, at], k.pc)]
        self.c1 = [k.remote(mine.at[z, x, y], mine.at[z, x, y], dev) for dev in k.pz]
        a, b = slice(0, cut), slice(cut, None)
        self.c2 = [k.remote(mine.at[:, x, y, :, a], mine.at[:, x, y, :, a], k.px),
                   k.remote(mine.at[:, x, y, :, b], mine.at[:, x, y, :, b], k.py)]
        self.c3 = [k.remote(mine.at[:, :, y, :, a], mine.at[:, :, y, :, a], k.py),
                   k.remote(mine.at[:, x, :, :, b], mine.at[:, x, :, :, b], k.px)]
        self.c4 = [k.remote(mine, mine, k.pc)] if whole else []

    def s0(self):
        start(self.c0)

    def s1(self):
        landed(self.own)
        arrive(self.c0)
        start(self.c1)

    def s2(self):
        arrive(self.c1)
        start(self.c2)

    def s3(self):
        arrive(self.c2)
        start(self.c3)

    def s4(self):
        arrive(self.c3)
        start(self.c4)

    def done(self):
        arrive(self.c4)


class Scatter:
    def __init__(self, links, grad, prefix, other, r0, r1a, r1b, r2a, r2b, r3, tot, fin, put, cut, base=None):
        k = links
        self.k, self.grad, self.prefix, self.put = k, grad, prefix, put
        self.r0, self.r1a, self.r1b, self.r2a, self.r2b, self.r3, self.tot, self.fin = r0, r1a, r1b, r2a, r2b, r3, tot, fin
        self.whole = other is not None
        mine = self.mine = grad.at[prefix] if prefix else grad
        self.a = (ALL, slice(0, cut))
        self.b = (ALL, slice(cut, None))
        x, y, x2, y2 = k.x, k.y, k.x2, k.y2
        at = iter([None] * 10 if base is None else base)
        self.c0 = [k.remote(grad.at[other], r0, k.pc, next(at))] if self.whole else []
        self.c1 = [k.remote(mine.at[(ALL, ALL, y2) + self.a], r1a, k.py, next(at)),
                   k.remote(mine.at[(ALL, x2, ALL) + self.b], r1b, k.px, next(at))]
        self.c2 = [k.remote(mine.at[(ALL, x2, y) + self.a], r2a, k.px, next(at)),
                   k.remote(mine.at[(ALL, x, y2) + self.b], r2b, k.py, next(at))]
        self.c3 = [k.remote(mine.at[k.zs[d], x, y], r3.at[d], k.pz[d], next(at)) for d in range(3)]
        self.c4 = [k.remote(tot.at[k.c2], fin, k.pc, next(at))]

    def at(self, place):
        return self.prefix + place

    def s0(self):
        start(self.c0)

    def s1(self):
        if self.whole:
            arrive(self.c0)

            def add(i, carry):
                where = (i // 4, lax.rem(i // 2, 2), lax.rem(i, 2))
                add_into(self.grad, self.at(where), self.r0[where])
                return carry

            lax.fori_loop(0, 16, add, 0)
        start(self.c1)

    def s2(self):
        arrive(self.c1)
        k = self.k

        def add(i, carry):
            zz, other = i // 2, lax.rem(i, 2)
            add_into(self.grad, self.at((zz, other, k.y) + self.a), self.r1a[zz, other])
            add_into(self.grad, self.at((zz, k.x, other) + self.b), self.r1b[zz, other])
            return carry

        lax.fori_loop(0, 8, add, 0)
        start(self.c2)

    def s3(self):
        arrive(self.c2)
        k = self.k

        def add(zz, carry):
            add_into(self.grad, self.at((zz, k.x, k.y) + self.a), self.r2a[zz])
            add_into(self.grad, self.at((zz, k.x, k.y) + self.b), self.r2b[zz])
            return carry

        lax.fori_loop(0, 4, add, 0)
        start(self.c3)

    def s4(self):
        arrive(self.c3)
        k = self.k
        total = self.mine[k.z, k.x, k.y].astype(F32)
        for d in range(3):
            total = total + self.r3[d].astype(F32)
        rows = total.shape[0] // 2
        self.tot[0] = total[:rows]
        self.tot[1] = total[rows:]
        start(self.c4)
        self.put(self.tot[k.c], k.c)

    def s5(self):
        arrive(self.c4)
        self.put(self.fin[...], self.k.c2)

    def gone(self):
        for copy in self.c0 + self.c1 + self.c2 + self.c3 + self.c4:
            copy.wait_send()


def masked(size, seen, low):
    last = jnp.where(seen, size[low:], NEG)
    return last if low == 0 else jnp.concatenate([size[:low], last], axis=0)


def gelu_parts(value):
    rate = 0.7978845608028654
    bent = jnp.tanh(rate * (value + 0.044715 * (value * value * value)))
    result = 0.5 * value * (1.0 + bent)
    slope = 0.5 * (1.0 + bent) + 0.5 * value * (1.0 - bent * bent) * (rate * (1.0 + 0.134145 * (value * value)))
    return result, slope


def unit_rows(rows):
    centre = rows - jnp.mean(rows, axis=-1, keepdims=True)
    scale = lax.rsqrt(jnp.mean(centre * centre, axis=-1, keepdims=True) + EPS)
    return centre * scale, scale


def norm_back(grad, normed, scale):
    return scale * (grad - jnp.mean(grad, axis=-1, keepdims=True)
                    - normed * jnp.mean(grad * normed, axis=-1, keepdims=True))


def layer_kernel(
    prefix, tok, cot, v0_s, v1_s, v2_s, v3_s, v4_s, v5_s, v6_s, v7_s, wq_s, wo_s, wu_s, wd_s,
    out_bo, out_gt, out_q, out_o, out_u, out_d, out_vec,
    wq, wo, wu, wd, gv, k_qs, k_qst, k_k, k_v, k_att, k_n1t,
    vec_s, wq_p, gvm, tok_all, vrows, wom, al_send, al, cotm, ga_send, ga_all, fa, fb, fc, fr, lt,
    gd, gu, go, gq,
    r0d, r0u, r0o, r1ad, r1bd, r1au, r1bu, r1av, r1bv, r1ao, r1bo, r2ad, r2bd, r2au, r2bu, r2av, r2bv, r2ao, r2bo, r3d, r3u, r3o,
    td, tu, to, fd, fu, fo,
    q1a, q1b, q2a, q2b, q3, tq, fq,
    vs, vbq, vup, vtab, vr0, vr1, vr2, vr3,
    ssem, rsem, lsem,
):
    k = Links(ssem, rsem, lsem)
    bo, gtb = al, cotm
    z, x, y, c, x2, y2, c2 = k.z, k.x, k.y, k.c, k.x2, k.y2, k.c2
    k.greet()
    vmem = pltpu.VMEM

    vec_s[...] = jnp.zeros_like(vec_s)
    for index, (wide, ref) in enumerate(zip(WIDTHS, (v0_s, v1_s, v2_s, v3_s, v4_s, v5_s, v6_s, v7_s))):
        vec_s[index : index + 1, 0:wide] = ref[...].astype(F32).reshape(1, wide)
    for core in range(2):
        for u in range(3):
            for kind in range(3):
                first = kind * D + core * THIRD + u * 128
                wq_p[core, u, :, kind * 128 : (kind + 1) * 128] = wq_s[:, first : first + 128]
    gather_q = [Gather(k, wq_p.at[c, u], wq_p.at[c2, u], wq.at[u], wq.at[u], 128, False) for u in range(3)]

    def halves(shard, full, cut):
        half = full.shape[-1]
        return Gather(k, shard.at[:, lanes(c * half, half)], shard.at[:, lanes(c2 * half, half)], full.at[c], full.at[c2], cut)

    gather_o = halves(wo_s, wo, 128)
    gather_d = halves(wd_s, wd, 128)
    gather_u = [Gather(k, wu_s.at[:, lanes(c * 1536 + part * D, D)], wu_s.at[:, lanes(c2 * 1536 + part * D, D)],
                       wu.at[c, part], wu.at[c2, part], 256 - 128 * part) for part in range(2)]
    own_vec = k.local(vec_s, gv.at[z, x, y, c])
    own_tok = k.local(tok.at[y], tok_all.at[y, c])
    own_cot = k.local(cot.at[y], cotm.at[y])
    own_vec.start()
    start(gather_q[0].own)
    own_tok.start()
    others = [gather_q[1], gather_q[2], gather_o] + gather_u + [gather_d]
    for gather in others:
        start(gather.own)
    own_cot.start()
    k.greeted()

    vec_c = k.remote(vec_s, gv.at[z, x, y, c], k.pc)
    tok_y = k.remote(tok.at[y2], tok_all.at[y, c], k.py)
    cot_y = k.remote(cot.at[y2], cotm.at[y], k.py)
    vec_c.start()
    gather_q[0].s0()
    tok_y.start()
    for gather in others:
        gather.s0()
    own_vec.wait()
    vec_c.wait_recv()
    vec_z = [k.remote(gv.at[z, x, y], gv.at[z, x, y], dev) for dev in k.pz]
    start(vec_z)
    gather_q[0].s1()
    gather_q[1].s1()
    own_tok.wait()
    arrive(vec_z)
    vec_x = k.remote(gv.at[:, x, y], gv.at[:, x, y], k.px)
    vec_x.start()
    gather_q[0].s2()
    gather_q[2].s1()
    vec_x.wait_recv()
    vec_y = k.remote(gv.at[:, :, y], gv.at[:, :, y], k.py)
    vec_y.start()
    gather_q[1].s2()
    gather_o.s1()
    gather_q[0].s3()
    tok_y.wait_recv()
    tok_c = k.remote(tok_all.at[:, c], tok_all.at[:, c], k.pc)
    tok_c.start()
    gather_q[2].s2()
    gather_u[0].s1()
    vec_y.wait_recv()
    table = k.local(gv, gvm)
    table.start()
    table.wait()
    table = gvm[...].reshape(256, 128).astype(BF)
    for index, wide in enumerate(WIDTHS):
        vrows[index : index + 1, 0 : 32 * wide] = spread_row(table, index, wide)
    gather_q[1].s3()
    tok_c.wait_recv()

    mine_cols = lanes(c * THIRD, THIRD)
    peer_cols = lanes(c2 * THIRD, THIRD)
    al_own = k.local(al_send.at[:, c], al.at[:, :, mine_cols])
    al_c = k.remote(al_send.at[:, c2], al.at[:, :, mine_cols], k.pc)
    limit = prefix[y] - 1
    sub = lax.broadcasted_iota(jnp.int32, (128, 256), 0)
    wq3 = wq.reshape(3, D, THIRD)

    def forward(n1, n1t, vt, qs, qst, keys_ref, values_ref, att, wqm):
        gain = vrows[0:1, 0:D]
        shift = vrows[1:2, 0:D]

        def norm_block(b, carry):
            normed, _ = unit_rows(tok_all[b // 2, lax.rem(b, 2)].astype(F32))
            normed = (normed * gain + shift).astype(BF)
            at = rows_at(b * 256, 256)
            n1[at, :] = normed
            n1t[:, at] = normed.astype(F32).T.astype(BF)
            return carry

        lax.fori_loop(0, 4, norm_block, 0)
        keep = [k.local(n1t, k_n1t), k.local(qs, k_qs), k.local(qst, k_qst), k.local(keys_ref, k_k),
                k.local(values_ref, k_v), k.local(att, k_att)]
        keep[0].start()
        load_q = [k.local(wq3.at[u], wqm.at[u]) for u in range(3)]
        load_o = k.local(wo.reshape(2, D, THIRD), wom)

        def head(u):
            gather_q[u].s4()
            load_q[u].start()
            load_q[u].wait()

        slots = {
            (0, 3): [gather_q[2].s3, gather_o.s2, gather_u[1].s1], (0, 2): [gather_u[0].s2],
            (0, 1): [gather_o.s3, gather_d.s1], (0, 0): [gather_u[1].s2],
            (1, 3): [gather_u[0].s3], (1, 2): [gather_o.s4], (1, 1): [gather_d.s2], (1, 0): [gather_u[1].s3],
            (2, 3): [gather_o.done, load_o.start, gather_u[0].s4], (2, 2): [cot_y.start], (2, 1): [gather_d.s3], (2, 0): [],
        }

        def unit(u, carry):
            cols = lanes(u * 128)
            for which in range(3):
                @pl.when(u == which)
                def _():
                    head(which)

            def project(b, inner):
                rows = rows_at(b * 512, 512)
                value = jnp.dot(n1[rows, :], wqm[u], preferred_element_type=F32)
                parts = []
                for kind in range(3):
                    bias = vrows[2:3, lanes(kind * D + c * THIRD + u * 128)]
                    parts.append((value[:, kind * 128 : (kind + 1) * 128] + bias).astype(BF))
                queries = parts[0].astype(F32) * 0.125
                qs[rows, cols] = queries.astype(BF)
                qst[cols, rows] = queries.T.astype(BF)
                keys_ref[rows, cols] = parts[1]
                values_ref[rows, cols] = parts[2]
                vt[cols, rows] = parts[2].astype(F32).T.astype(BF)
                return inner

            lax.fori_loop(0, 2, project, 0)
            for block in (3, 2, 1, 0):
                attend(u, block)
                for which in range(3):
                    if slots[which, block]:
                        @pl.when(u == which)
                        def _():
                            for step in slots[which, block]:
                                step()
            return carry

        def attend(u, block):
            rows = min(4, max(block + 1, 2)) * 256
            qcols = slice(block * 256, (block + 1) * 256)
            cols = lanes(u * 128)
            keys = keys_ref[0:rows, cols]
            queries = qst[cols, qcols]
            qpos = block * 256 + lax.broadcasted_iota(jnp.int32, (1, 256), 1)
            low = block * 256
            seen = low + lax.broadcasted_iota(jnp.int32, (rows - low, 256), 0) <= jnp.maximum(qpos, limit)
            for half in range(2):
                chosen = jnp.where(sub // 64 == half, queries, jnp.zeros_like(queries))
                scores = jnp.dot(keys, chosen, preferred_element_type=F32)
                size = jnp.abs(scores)
                size = masked(size, seen, low)
                top = jnp.max(size, axis=0, keepdims=True)
                exponent = jnp.exp(size - top)
                total = jnp.sum(exponent, axis=0, keepdims=True)
                weights = jnp.where(scores > 0, exponent, jnp.where(scores < 0, -exponent, 0.0)).astype(BF)
                at = pl.ds(pl.multiple_of(u * 128 + half * 64, 64), 64)
                att[at, qcols] = jnp.dot(vt[at, 0:rows], weights, preferred_element_type=F32) / total
                lt[pl.ds(u * 2 + half, 1), qcols] = top + jnp.log(total)
            al_send[block // 2, block % 2, :, cols] = att[cols, qcols].T.astype(BF)

        lax.fori_loop(0, 3, unit, 0)
        al_own.start()
        al_c.start()
        start(keep[1:])
        load_o.wait()
        al_own.wait()
        al_c.wait_recv()
        landed(keep)

    pl.run_scoped(
        forward, vmem((1024, D), BF), vmem((D, 1024), BF), vmem((THIRD, 1024), BF), vmem((1024, THIRD), BF),
        vmem((THIRD, 1024), BF), vmem((1024, THIRD), BF), vmem((1024, THIRD), BF), vmem((THIRD, 1024), F32),
        vmem((3, D, THIRD), BF))

    def put_to(out, half):
        def put(value, core):
            out[:, lanes(core * half, half)] = value
        return put

    down = Scatter(k, gd, (c,), c2, r0d, r1ad, r1bd, r2ad, r2bd, r3d, td, fd, put_to(out_d, THIRD), 128)

    def put_up(part):
        def put(value, core):
            out_u[:, lanes(core * 1536 + part * D, D)] = value
        return put

    up = [Scatter(k, gu, (c, part), (c2, part), r0u.at[part], (r1au, r1av)[part], (r1bu, r1bv)[part], (r2au, r2av)[part],
                  (r2bu, r2bv)[part], r3u.at[part], tu.at[part], fu.at[part], put_up(part), 256 - 128 * part)
          for part in range(2)]
    outp = Scatter(k, go, (c,), c2, r0o, r1ao, r1bo, r2ao, r2bo, r3o, to, fo, put_to(out_o, THIRD), 128)

    def feed(wbuf, wdb, hid, slope, n2, n2t, alt, gpc):
        b_out, gain, shift = vrows[3:4, 0:D], vrows[4:5, 0:D], vrows[5:6, 0:D]

        def begin(yy, carry):
            rows = rows_at(yy * 256, 256)
            branch = jnp.concatenate([jnp.dot(al[yy], wom[h], preferred_element_type=F32) for h in range(2)], axis=1)
            residual = tok_all[yy, c].astype(F32) + branch + b_out
            fa[yy] = residual
            normed, _ = unit_rows(residual)
            normed = (normed * gain + shift).astype(BF)
            n2[rows, :] = normed
            n2t[:, rows] = normed.astype(F32).T.astype(BF)
            alt[:, rows] = al[yy].astype(F32).T.astype(BF)
            return carry

        lax.fori_loop(0, 2, begin, 0)
        own_cot.wait()
        cot_y.wait_recv()

        wu2 = wu.reshape(2, 2, D, D)
        wd2 = wd.reshape(2, FF, THIRD)

        def chunk(j, first, second):
            h = first if j < 2 else second
            return h, j % 2

        def up_load(j, slot, order):
            h, part = chunk(j, *order)
            return k.local(wu2.at[h, part], wbuf.at[slot])

        def down_load(j, slot, order):
            h, part = chunk(j, *order)
            return k.local(wd2.at[:, rows_at(h * 1536 + part * D, D), :], wdb.at[slot])

        forth = (c, c2)
        loads = [up_load(j, j % 2, forth) for j in range(4)]
        loads[0].start()
        gather_u[1].s4()
        for j in range(4):
            loads[j].wait()
            if j == 0:
                loads[1].start()
            if j == 1:
                gather_u[0].done()
                loads[2].start()
            if j == 2:
                gather_u[1].done()
                loads[3].start()
            h, part = chunk(j, *forth)

            def ahead(side, carry):
                there = lanes(side * THIRD, THIRD)
                cols = lanes(h * 1536 + part * D + side * THIRD, THIRD)
                value = jnp.dot(n2[...], wbuf[j % 2, :, there], preferred_element_type=F32) + vrows[6:7, cols]
                result, bend = gelu_parts(value)
                hid[:, cols] = result.astype(BF)
                slope[:, cols] = bend
                return carry

            lax.fori_loop(0, 2, ahead, 0)

        vs[7:8, :] = jnp.sum(cotm[0].astype(F32), axis=0, keepdims=True) + jnp.sum(
            cotm[1].astype(F32), axis=0, keepdims=True)

        def down_grad(i, carry):
            total = lax.dot_general(hid[:, lanes(i * THIRD, THIRD)], cotm[...].reshape(512, D), FIRST,
                                    preferred_element_type=F32)
            zz, xx = i // 2, lax.rem(i, 2)
            for yy in range(2):
                for h in range(2):
                    gd[h, zz, xx, yy] = total[yy * 192 : (yy + 1) * 192, h * THIRD : (h + 1) * THIRD].astype(BF)
            return carry

        lax.fori_loop(0, 8, down_grad, 0)
        down.s0()
        fb[...] = jnp.zeros_like(fb)
        fc[...] = jnp.zeros_like(fc)
        vup[...] = jnp.zeros_like(vup)
        gather_d.s4()
        back = (c2, c)
        again = [up_load(j, j % 2, back) for j in range(4)]
        lower = [down_load(j, j % 2, back) for j in range(4)]
        again[0].start()
        down.s1()
        gather_d.done()
        lower[0].start()
        for j in range(4):
            slot = j % 2
            if j < 3:
                again[j + 1].start()
                lower[j + 1].start()
            again[j].wait()
            lower[j].wait()
            h, part = chunk(j, *back)
            first = h * 1536 + part * D

            def behind(side, carry):
                there = lanes(side * THIRD, THIRD)
                cols = lanes(first + side * THIRD, THIRD)
                units = hid[:, lanes(first, D)]
                fc[:, :, there] += jnp.dot(units, wdb[slot, side], preferred_element_type=F32).reshape(2, 256, THIRD)
                grad = None
                for other in range(2):
                    term = lax.dot_general(
                        cotm[:, :, other * THIRD : (other + 1) * THIRD].reshape(512, THIRD), wdb[slot, other, there, :],
                        LAST, preferred_element_type=F32)
                    grad = term if grad is None else grad + term
                grad = (grad * slope[:, cols]).astype(BF)
                gpc[:, there] = grad
                vup[0:1, cols] += jnp.sum(grad.astype(F32), axis=0, keepdims=True)
                return carry

            lax.fori_loop(0, 2, behind, 0)

            def normed_grad(side, carry):
                there = lanes(side * THIRD, THIRD)
                term = lax.dot_general(gpc[...], wbuf[slot, there, :], LAST, preferred_element_type=F32)
                fb[:, :, there] += term.reshape(2, 256, THIRD)
                return carry

            lax.fori_loop(0, 2, normed_grad, 0)

            def up_grad(zz, carry):
                total = jnp.dot(n2t[rows_at(zz * THIRD, THIRD, 128), :], gpc[...], preferred_element_type=F32)
                for i in range(8):
                    gu[h, part, zz * 2 + i // 4, i // 2 % 2, i % 2] = total[i * 48 : (i + 1) * 48].astype(BF)
                return carry

            lax.fori_loop(0, 2, up_grad, 0)
            if j < 2:
                up[j].s0()
            if j == 2:
                up[0].s1()
                down.s2()
        bo[...] = (fa[...] + fc[...] + vrows[7:8, 0:D].reshape(1, 1, D)).astype(BF)
        up[1].s1()

    ga_c = k.remote(ga_send.at[:, :, peer_cols], ga_all.at[:, c], k.pc)
    def turn(alt, gpc):
        gain = vrows[4:5, 0:D]
        vs[3:6, :] = jnp.zeros((3, D), F32)

        def mid_back(yy, carry):
            rows = rows_at(yy * 256, 256)
            normed, scale = unit_rows(fa[yy])
            grad = fb[yy]
            vs[4:5, :] += jnp.sum(grad * normed, axis=0, keepdims=True)
            vs[5:6, :] += jnp.sum(grad, axis=0, keepdims=True)
            total = cotm[yy].astype(F32) + norm_back(grad * gain, normed, scale)
            fa[yy] = total
            low = total.astype(BF)
            vs[3:4, :] += jnp.sum(low.astype(F32), axis=0, keepdims=True)
            gpc[rows, :] = low
            heads = None
            for side in range(2):
                term = lax.dot_general(low[:, side * THIRD : (side + 1) * THIRD], wom[side], LAST,
                                       preferred_element_type=F32)
                heads = term if heads is None else heads + term
            ga_send[yy] = heads.astype(BF)
            ga_all[yy, c] = ga_send[yy, :, mine_cols]
            return carry

        lax.fori_loop(0, 2, mid_back, 0)
        ga_c.start()

        def out_grad(zz, carry):
            total = jnp.dot(alt[rows_at(zz * THIRD, THIRD, 128), :], gpc[...], preferred_element_type=F32)
            for i in range(8):
                for h in range(2):
                    go[h, zz * 2 + i // 4, i // 2 % 2, i % 2] = total[i * 48 : (i + 1) * 48, h * THIRD : (h + 1) * THIRD].astype(BF)
            return carry

        lax.fori_loop(0, 2, out_grad, 0)
        outp.s0()

    def put_q(u):
        def put(value, core):
            for kind in range(3):
                out_q[:, lanes(kind * D + core * THIRD + u * 128)] = value[:, kind * 128 : (kind + 1) * 128]
        return put

    bases = [k.fresh(3) for _ in range(8)]

    def query_scatter(u):
        return Scatter(k, gq.at[u], (), None, None, q1a.at[u], q1b.at[u], q2a.at[u], q2b.at[u], q3.at[u], tq.at[u], fq.at[u],
                       put_q(u), 128, base=[b + u for b in bases])

    queue = [query_scatter(u) for u in range(3)]
    bo_own = k.local(bo.at[y], out_bo.at[y])
    bo_y = k.remote(bo.at[y2], out_bo.at[y], k.py)

    def send_out():
        bo_own.start()
        bo_y.start()

    def backward(alt, gpc, qs, qst, keys_ref, values_ref, att, n1t, gt, kt, dk, dv, gpu, wqm):
        loads = [k.local(k_qs, qs), k.local(k_qst, qst), k.local(k_k, keys_ref), k.local(k_v, values_ref),
                 k.local(k_att, att), k.local(k_n1t, n1t), k.local(wq3, wqm)]
        start(loads)
        turn(alt, gpc)
        fb[...] = jnp.zeros_like(fb)
        fc[...] = jnp.zeros_like(fc)
        ga_c.wait_recv()
        landed(loads)
        lane = lax.broadcasted_iota(jnp.int32, (256, 128), 1)
        vbq[...] = jnp.zeros_like(vbq)
        slots = {
            (0, 3): [outp.s1, down.s3], (0, 2): [], (0, 1): [up[0].s2], (0, 0): [send_out, up[1].s2],
            (1, 3): [outp.s2], (1, 2): [down.s4], (1, 1): [up[0].s3], (1, 0): [up[1].s3, down.s5],
            (2, 3): [queue[0].s2], (2, 2): [outp.s3], (2, 1): [queue[0].s3], (2, 0): [up[0].s4],
        }

        def unit(u, carry):
            cols = lanes(u * 128)
            for b in range(4):
                rows = slice(b * 256, (b + 1) * 256)
                gt[:, rows] = ga_all[b // 2, b % 2, :, cols].astype(F32).T.astype(BF)
                kt[:, rows] = keys_ref[rows, cols].astype(F32).T.astype(BF)
            dk[...] = jnp.zeros_like(dk)
            dv[...] = jnp.zeros_like(dv)
            for block in (3, 2, 1, 0):
                rows = min(4, max(block + 1, 2)) * 256
                qrange = slice(block * 256, (block + 1) * 256)
                keys = keys_ref[0:rows, cols]
                values = values_ref[0:rows, cols]
                queries_t = qst[cols, qrange]
                grads_t = gt[:, qrange]
                queries = qs[qrange, cols]
                grads = ga_all[block // 2, block % 2, :, cols]
                qpos = block * 256 + lax.broadcasted_iota(jnp.int32, (1, 256), 1)
                low = block * 256
                seen = low + lax.broadcasted_iota(jnp.int32, (rows - low, 256), 0) <= jnp.maximum(qpos, limit)
                prod = grads_t.astype(F32) * att[cols, qrange]
                dqs, dks, dvs = [], None, None
                for half in range(2):
                    part = slice(half * 64, half * 64 + 64)
                    in_sub = sub // 64 == half
                    in_lane = lane // 64 == half
                    delta = jnp.sum(prod[part], axis=0, keepdims=True)
                    total = lt[pl.ds(u * 2 + half, 1), qrange]
                    zero = jnp.zeros((), BF)
                    scores = jnp.dot(keys, jnp.where(in_sub, queries_t, zero), preferred_element_type=F32)
                    pull = jnp.dot(values, jnp.where(in_sub, grads_t, zero), preferred_element_type=F32)
                    share = jnp.exp(masked(jnp.abs(scores) - total, seen, low))
                    signed = jnp.where(scores > 0, share, jnp.where(scores < 0, -share, 0.0))
                    grad_scores = (share * pull - signed * delta).astype(BF)
                    signed = signed.astype(BF)
                    dvt = jnp.dot(signed, jnp.where(in_lane, grads, zero), preferred_element_type=F32)
                    dkt = jnp.dot(grad_scores, jnp.where(in_lane, queries, zero), preferred_element_type=F32)
                    dvs = dvt if dvs is None else dvs + dvt
                    dks = dkt if dks is None else dks + dkt
                    dqs.append(jnp.dot(kt[part, 0:rows], grad_scores, preferred_element_type=F32))
                dk[0:rows, :] += dks
                dv[0:rows, :] += dvs
                gpu[qrange, 0:128] = (jnp.concatenate(dqs, axis=0).T * 0.125).astype(BF)
                for which in range(3):
                    if slots[which, block]:
                        @pl.when(u == which)
                        def _():
                            for step in slots[which, block]:
                                step()
            gpu[:, 128:256] = dk[...].astype(BF)
            gpu[:, 256:384] = dv[...].astype(BF)
            sums = jnp.sum(gpu[...].astype(F32), axis=0, keepdims=True)
            for kind in range(3):
                part = slice(kind * 128, (kind + 1) * 128)
                vbq[0:1, lanes(kind * D + c * THIRD + u * 128)] = sums[:, part]

            def weights(zz, inner):
                block = jnp.dot(n1t[rows_at(zz * THIRD, THIRD, 128), :], gpu[...], preferred_element_type=F32)
                for i in range(8):
                    gq[u, zz * 2 + i // 4, i // 2 % 2, i % 2] = block[i * 48 : (i + 1) * 48].astype(BF)
                return inner

            lax.fori_loop(0, 2, weights, 0)
            for which in range(3):
                @pl.when(u == which)
                def _():
                    queue[which].s1()

            def back_rows(b):
                return lax.dot_general(gpu[rows_at(b * 256, 256), :], wqm[u], LAST, preferred_element_type=F32)

            def back_peer(yy, inner):
                fb[yy] += back_rows(yy * 2 + c2)
                return inner

            def back_own(yy, inner):
                fc[yy] += back_rows(yy * 2 + c)
                return inner

            lax.fori_loop(0, 2, back_peer, 0)

            @pl.when(u == 2)
            def _():
                part_c.start()

            lax.fori_loop(0, 2, back_own, 0)
            return carry

        lax.fori_loop(0, 3, unit, 0)

    part_c = k.remote(fb, fr, k.pc)

    def both(alt, gpc):
        pl.run_scoped(
            functools.partial(feed, alt=alt, gpc=gpc), vmem((2, D, D), BF), vmem((2, 2, D, THIRD), BF),
            vmem((512, FF), BF), vmem((512, FF), F32), vmem((512, D), BF), vmem((D, 512), BF))
        pl.run_scoped(
            functools.partial(backward, alt, gpc), vmem((1024, THIRD), BF), vmem((THIRD, 1024), BF), vmem((1024, THIRD), BF),
            vmem((1024, THIRD), BF), vmem((THIRD, 1024), F32), vmem((D, 1024), BF), vmem((128, 1024), BF),
            vmem((128, 1024), BF), vmem((1024, 128), F32), vmem((1024, 128), F32), vmem((1024, THIRD), BF),
            vmem((3, D, THIRD), BF))

    pl.run_scoped(both, vmem((D, 512), BF), vmem((512, D), BF))

    gain = vrows[0:1, 0:D]
    vs[0:2, :] = jnp.zeros((2, D), F32)

    def sums(core, ref):
        def add(yy, carry):
            normed, _ = unit_rows(tok_all[yy, core].astype(F32))
            grad = ref[yy]
            vs[0:1, :] += jnp.sum(grad * normed, axis=0, keepdims=True)
            vs[1:2, :] += jnp.sum(grad, axis=0, keepdims=True)
            return carry

        lax.fori_loop(0, 2, add, 0)

    sums(c2, fb)
    sums(c, fc)
    for index, wide in enumerate(WIDTHS):
        row = vbq[...] if index == 2 else vup[...] if index == 6 else vs[index : index + 1, :]
        vtab[pl.ds(index, 32, stride=8), :] = collect_rows(row, wide)
    table = vtab.reshape(4, 2, 2, 2, 8, 128)
    v0 = k.remote(table.at[:, :, :, c2], vr0, k.pc)
    v1 = k.remote(table.at[:, :, y2, c], vr1, k.py)
    v2 = k.remote(table.at[:, x2, y, c], vr2, k.px)
    v3 = [k.remote(table.at[k.zs[d], x, y, c], vr3.at[d], k.pz[d]) for d in range(3)]

    def tile(zz, xx, yy):
        return rows_at((((zz * 2 + xx) * 2 + yy) * 2 + c) * 8, 8, 8)

    v0.start()
    part_c.wait_recv()

    def last_back(yy):
        normed, scale = unit_rows(tok_all[yy, c].astype(F32))
        grad = fc[yy] + fr[yy]
        gtb[yy] = (fa[yy] + norm_back(grad * gain, normed, scale)).astype(BF)

    gt_own = k.local(gtb.at[y], out_gt.at[y])
    gt_y = k.remote(gtb.at[y2], out_gt.at[y], k.py)
    last_back(y2)
    gt_y.start()
    last_back(y)
    gt_own.start()
    v0.wait_recv()

    def add_core(i, carry):
        zz, xx, yy = i // 4, lax.rem(i // 2, 2), lax.rem(i, 2)
        vtab[tile(zz, xx, yy), :] += vr0[zz, xx, yy]
        return carry

    lax.fori_loop(0, 16, add_core, 0)
    v1.start()
    queue[1].s2()
    queue[2].s2()
    queue[0].s4()
    v1.wait_recv()

    def add_y(i, carry):
        vtab[tile(i // 2, lax.rem(i, 2), y), :] += vr1[i // 2, lax.rem(i, 2)]
        return carry

    lax.fori_loop(0, 8, add_y, 0)
    v2.start()
    queue[1].s3()
    queue[2].s3()
    v2.wait_recv()

    def add_x(zz, carry):
        vtab[tile(zz, x, y), :] += vr2[zz]
        return carry

    lax.fori_loop(0, 4, add_x, 0)
    start(v3)
    up[1].s4()
    outp.s4()
    queue[1].s4()
    queue[2].s4()
    for scatter in (up[0], up[1], outp, queue[0], queue[1], queue[2]):
        scatter.s5()
    arrive(v3)
    out_vec[...] = vtab[tile(z, x, y), :] + vr3[0] + vr3[1] + vr3[2]
    landed([gt_own, bo_own])
    arrive([gt_y, bo_y])
    for copy in k.sent:
        copy.wait_send()
    for scatter in queue:
        scatter.gone()
    assert k.remotes <= REMOTES and k.locals <= LOCALS


def layer_call(*operands):
    sds = jax.ShapeDtypeStruct
    vmem = pltpu.VMEM
    dma = pltpu.SemaphoreType.DMA
    results = (
        sds((2, 256, D), BF), sds((2, 256, D), BF), sds((24, 3 * D), F32), sds((24, D), F32), sds((24, FF), F32),
        sds((96, D), F32), sds((8, 128), F32),
    )
    held = (
        sds((3, 4, 2, 2, 48, 384), BF), sds((2, 4, 2, 2, 48, 384), BF), sds((2, 2, 4, 2, 2, 48, 768), BF),
        sds((2, 4, 2, 2, 192, 384), BF), sds((4, 2, 2, 2, 8, 128), F32), sds((1024, THIRD), BF), sds((THIRD, 1024), BF),
        sds((1024, THIRD), BF), sds((1024, THIRD), BF), sds((THIRD, 1024), F32), sds((D, 1024), BF),
    )
    scratch = [
        vmem((8, 128), F32), vmem((2, 3, 24, THIRD), BF), vmem((4, 2, 2, 2, 8, 128), F32), vmem((2, 2, 256, D), BF), vmem((8, FF), F32),
        vmem((2, D, THIRD), BF), vmem((2, 2, 256, THIRD), BF), vmem((2, 256, D), BF), vmem((2, 256, D), BF),
        vmem((2, 256, D), BF), vmem((2, 2, 256, THIRD), BF), vmem((2, 256, D), F32), vmem((2, 256, D), F32),
        vmem((2, 256, D), F32), vmem((2, 256, D), F32), vmem((8, 1024), F32),
    ]
    kinds = (((), 192, 384, (128,)), ((2,), 48, 768, (256, 128)), ((), 48, 384, (128,)))
    scratch += [vmem((2,) + p + (4, 2, 2, r, n), BF) for p, r, n, _ in kinds] + [vmem((3, 4, 2, 2, 48, 384), BF)]
    scratch += [vmem(p + (4, 2, 2, r, n), BF) for p, r, n, _ in kinds]
    for lead in ((4, 2), (4,)):
        for _, r, n, cuts in kinds:
            for cut in cuts:
                scratch += [vmem(lead + (r, cut), BF), vmem(lead + (r, n - cut), BF)]
    scratch += [vmem(p + (3, r, n), BF) for p, r, n, _ in kinds]
    scratch += [vmem(p + (2, r // 2, n), F32) for p, r, n, _ in kinds]
    scratch += [vmem(p + (r // 2, n), F32) for p, r, n, _ in kinds]
    scratch += [
        vmem((3, 4, 2, 48, 128), BF), vmem((3, 4, 2, 48, 256), BF), vmem((3, 4, 48, 128), BF), vmem((3, 4, 48, 256), BF),
        vmem((3, 3, 48, 384), BF), vmem((3, 2, 24, 384), F32), vmem((3, 24, 384), F32),
        vmem((8, D), F32), vmem((1, 3 * D), F32), vmem((1, FF), F32), vmem((256, 128), F32), vmem((4, 2, 2, 8, 128), F32),
        vmem((4, 2, 8, 128), F32), vmem((4, 8, 128), F32), vmem((3, 8, 128), F32),
        dma((REMOTES,)), dma((REMOTES,)), dma((LOCALS,)),
    ]
    return pl.pallas_call(
        layer_kernel,
        out_shape=results + held,
        in_specs=[SM] + [ANY] * 2 + [VM] * 12,
        out_specs=(ANY, ANY) + (VM,) * 5 + (ANY,) * len(held),
        scratch_shapes=scratch,
        compiler_params=pltpu.CompilerParams(
            collective_id=0, has_side_effects=True, vmem_limit_bytes=63 * 2**20),
    )(*operands)[: len(results)]


def finish_kernel(*refs):
    sources, results, (table, sems) = refs[:7], refs[7:21], refs[21:]
    copies = [pltpu.make_async_copy(source, result, sems.at[i])
              for i, (source, result) in enumerate(zip(sources, results[:6] + (table,)))]
    start(copies)
    landed(copies)
    for index, wide in enumerate(WIDTHS):
        results[6 + index][...] = table[index, 0:wide]


def finish_call(*operands):
    sds = jax.ShapeDtypeStruct
    shapes = tuple(sds(o.shape, o.dtype) for o in operands[:6]) + tuple(sds((wide,), F32) for wide in WIDTHS)
    return pl.pallas_call(
        finish_kernel, out_shape=shapes, in_specs=[ANY] * 7, out_specs=(VM,) * 14,
        scratch_shapes=[pltpu.VMEM((8, 128), F32), pltpu.SemaphoreType.DMA((7,))],
        compiler_params=pltpu.CompilerParams(vmem_limit_bytes=60 * 2**20),
    )(*operands)


def body(
    tokens, cotangent, prefix, ln1_gain, ln1_bias, w_qkv, b_qkv, w_out, b_out,
    ln2_gain, ln2_bias, w_up, b_up, w_down, b_down,
):
    results = layer_call(
        prefix, tokens, cotangent, ln1_gain, ln1_bias, b_qkv, b_out, ln2_gain, ln2_bias, b_up, b_down,
        w_qkv, w_out, w_up, w_down)
    block_out, grad_tokens, gq, go, gu, gd, *rows = finish_call(*results)
    return (
        block_out, grad_tokens, rows[0], rows[1], gq, rows[2], go, rows[3], rows[4], rows[5], gu, rows[6], gd, rows[7],
    )


def fits(mesh):
    return dict(mesh.shape) == {"dp": 8, "seq": 4}


norm_eps = 1e-05
block_rows = 512


def layer_norm(features, gain, shift):
    centre = features - jnp.mean(features, axis=-1, keepdims=True)
    spread = jnp.mean(centre * centre, axis=-1, keepdims=True)
    return centre * lax.rsqrt(spread + norm_eps) * gain + shift


def gelu_tanh(values):
    return jax.nn.gelu(values, approximate=True)


def in_blocks(update, running, pieces):
    length = pieces[0].shape[1]
    blocks = length // block_rows
    blocked_pieces = tuple(
        (
            jnp.swapaxes(
                member.reshape((member.shape[0], blocks, block_rows) + member.shape[2:]), 0, 1
            )
            for member in pieces
        )
    )

    def advance(carried, element):
        return (update(carried, element[0], element[1] * block_rows), None)

    running, unused = lax.scan(
        advance, running, (blocked_pieces, jnp.arange(blocks, dtype=jnp.int32))
    )
    return running


def to_heads(flat_rows):
    return flat_rows.reshape(flat_rows.shape[0], flat_rows.shape[1], HEADS, HEAD_DIM)


def visible_mask(query_places, key_places, prefix_len):
    earlier = key_places[None, None, :] <= query_places[None, :, None]
    in_prefix = key_places[None, None, :] < prefix_len[:, None, None]
    return (earlier | in_prefix)[:, :, None, :]


def head_scores(query_heads, key_flat):
    return jnp.einsum(
        "bqhd,bkhd->bqhk", query_heads, to_heads(key_flat), preferred_element_type=jnp.float32
    ) * HEAD_DIM ** (-0.5)


def attend(query_heads, key_flat, value_flat, prefix_len):
    local_len = query_heads.shape[1]
    query_places = lax.axis_index("seq") * local_len + jnp.arange(local_len, dtype=jnp.int32)
    starting = (
        jnp.zeros(query_heads.shape, jnp.float32),
        jnp.zeros(query_heads.shape[:3], jnp.float32),
        jnp.zeros(query_heads.shape[:3], jnp.float32),
    )

    def update(running, pieces, offset):
        weighted, normaliser, ceiling = running
        key_piece, value_piece = pieces
        key_places = offset + jnp.arange(key_piece.shape[1], dtype=jnp.int32)
        scores = head_scores(query_heads, key_piece)
        visible = visible_mask(query_places, key_places, prefix_len)
        magnitude = jnp.where(visible, jnp.abs(scores), 0.0)
        new_ceiling = jnp.maximum(ceiling, jnp.max(magnitude, axis=-1))
        exponent = jnp.where(visible, jnp.exp(magnitude - new_ceiling[..., None]), 0.0)
        factor = jnp.exp(ceiling - new_ceiling)
        weights = (jnp.sign(scores) * exponent).astype(jnp.bfloat16)
        weighted = weighted * factor[..., None] + jnp.einsum(
            "bqhk,bkhd->bqhd", weights, to_heads(value_piece), preferred_element_type=jnp.float32
        )
        normaliser = normaliser * factor + jnp.sum(exponent, axis=-1)
        return (weighted, normaliser, new_ceiling)

    weighted, normaliser, ceiling = in_blocks(
        update,
        starting,
        (
            lax.all_gather(key_flat, "seq", axis=1, tiled=True),
            lax.all_gather(value_flat, "seq", axis=1, tiled=True),
        ),
    )
    return (weighted / normaliser[..., None], ceiling + jnp.log(normaliser))


def grad_terms(
    query_heads,
    grad_heads,
    key_flat,
    value_flat,
    log_total,
    delta_sum,
    query_places,
    key_places,
    prefix_len,
):
    scores = head_scores(query_heads, key_flat)
    sign_of = jnp.sign(scores)
    visible = visible_mask(query_places, key_places, prefix_len)
    shares = jnp.where(visible, jnp.exp(jnp.abs(scores) - log_total[..., None]), 0.0)
    grad_weights = jnp.einsum(
        "bqhd,bkhd->bqhk", grad_heads, to_heads(value_flat), preferred_element_type=jnp.float32
    )
    grad_scores = (shares * (grad_weights - sign_of * delta_sum[..., None])).astype(jnp.bfloat16)
    return ((sign_of * shares).astype(jnp.bfloat16), grad_scores)


def query_term(grad_scores, key_flat):
    return jnp.einsum(
        "bqhk,bkhd->bqhd", grad_scores, to_heads(key_flat), preferred_element_type=jnp.float32
    ) * HEAD_DIM ** (-0.5)


def key_value_terms(query_heads, grad_heads, shares_low, grad_scores):
    key_term = jnp.einsum(
        "bqhk,bqhd->bkhd", grad_scores, query_heads, preferred_element_type=jnp.float32
    ) * HEAD_DIM ** (-0.5)
    value_term = jnp.einsum(
        "bqhk,bqhd->bkhd", shares_low, grad_heads, preferred_element_type=jnp.float32
    )
    flat_shape = (key_term.shape[0], key_term.shape[1], key_term.shape[2] * key_term.shape[3])
    return jnp.concatenate([key_term.reshape(flat_shape), value_term.reshape(flat_shape)], axis=-1)


def attend_back(query_heads, key_flat, value_flat, grad_heads, log_total, delta_sum, prefix_len):
    seq_block, local_len = (query_heads.shape[0], query_heads.shape[1])
    width = key_flat.shape[2]
    local_places = lax.axis_index("seq") * local_len + jnp.arange(local_len, dtype=jnp.int32)
    starting = (
        jnp.zeros(query_heads.shape, jnp.float32),
        jnp.zeros((seq_block, lax.axis_size("seq") * local_len, 2 * width), jnp.float32),
    )

    def update_both(running, pieces, offset):
        grad_query, grad_keys = running
        key_piece, value_piece = pieces
        piece_len = key_piece.shape[1]
        key_places = offset + jnp.arange(piece_len, dtype=jnp.int32)
        shares_low, grad_scores = grad_terms(
            query_heads,
            grad_heads,
            key_piece,
            value_piece,
            log_total,
            delta_sum,
            local_places,
            key_places,
            prefix_len,
        )
        grad_query = grad_query + query_term(grad_scores, key_piece)
        current = lax.dynamic_slice_in_dim(grad_keys, offset, piece_len, 1)
        updated = current + key_value_terms(query_heads, grad_heads, shares_low, grad_scores)
        return (grad_query, lax.dynamic_update_slice_in_dim(grad_keys, updated, offset, 1))

    grad_query, grad_keys = in_blocks(
        update_both,
        starting,
        (
            lax.all_gather(key_flat, "seq", axis=1, tiled=True),
            lax.all_gather(value_flat, "seq", axis=1, tiled=True),
        ),
    )
    key_local = lax.psum_scatter(
        grad_keys.astype(jnp.bfloat16), "seq", scatter_dimension=1, tiled=True
    ).astype(jnp.float32)
    return (grad_query, key_local)


def forward_block(weights_in, token_part, prefix_len):
    (
        gain_one,
        shift_one,
        w_qkv,
        b_qkv,
        w_out,
        b_out,
        gain_two,
        shift_two,
        w_up,
        b_up,
        w_down,
        b_down,
    ) = weights_in
    seq_block, local_len, width = token_part.shape
    residual_in = token_part.reshape(-1, width).astype(jnp.float32)
    normed_one = layer_norm(
        residual_in, gain_one.astype(jnp.float32), shift_one.astype(jnp.float32)
    ).astype(jnp.bfloat16)
    projected = jnp.dot(normed_one, w_qkv, preferred_element_type=jnp.float32) + b_qkv.astype(
        jnp.float32
    )
    query_heads = (
        projected[:, :width].astype(jnp.bfloat16).reshape(seq_block, local_len, HEADS, HEAD_DIM)
    )
    key_flat = (
        projected[:, width : 2 * width].astype(jnp.bfloat16).reshape(seq_block, local_len, width)
    )
    value_flat = projected[:, 2 * width :].astype(jnp.bfloat16).reshape(seq_block, local_len, width)
    attended, log_total = attend(query_heads, key_flat, value_flat, prefix_len)
    attended_low = attended.reshape(-1, width).astype(jnp.bfloat16)
    residual_mid = (
        residual_in
        + jnp.dot(attended_low, w_out, preferred_element_type=jnp.float32)
        + b_out.astype(jnp.float32)
    )
    normed_two = layer_norm(
        residual_mid, gain_two.astype(jnp.float32), shift_two.astype(jnp.float32)
    ).astype(jnp.bfloat16)
    pre_gelu = jnp.dot(normed_two, w_up, preferred_element_type=jnp.float32) + b_up.astype(
        jnp.float32
    )
    hidden = gelu_tanh(pre_gelu).astype(jnp.bfloat16)
    result = (
        residual_mid
        + jnp.dot(hidden, w_down, preferred_element_type=jnp.float32)
        + b_down.astype(jnp.float32)
    )
    saved = (
        residual_in,
        normed_one,
        query_heads,
        key_flat,
        value_flat,
        attended,
        log_total,
        attended_low,
        residual_mid,
        normed_two,
        pre_gelu,
        hidden,
    )
    return (result.astype(jnp.bfloat16).reshape(token_part.shape), saved)


def backward_block(weights_in, saved, grad_part, prefix_len):
    (
        gain_one,
        shift_one,
        w_qkv,
        b_qkv,
        w_out,
        b_out,
        gain_two,
        shift_two,
        w_up,
        b_up,
        w_down,
        b_down,
    ) = weights_in
    (
        residual_in,
        normed_one,
        query_heads,
        key_flat,
        value_flat,
        attended,
        log_total,
        attended_low,
        residual_mid,
        normed_two,
        pre_gelu,
        hidden,
    ) = saved
    seq_block, local_len, width = grad_part.shape
    grad_result = grad_part.reshape(-1, width).astype(jnp.float32)
    grad_branch = grad_part.reshape(-1, width)
    grads_down = jnp.einsum("rf,rd->fd", hidden, grad_branch, preferred_element_type=jnp.float32)
    bias_down = jnp.sum(grad_branch, axis=0, dtype=jnp.float32)
    grad_hidden = jnp.einsum("rd,fd->rf", grad_branch, w_down, preferred_element_type=jnp.float32)
    gelu_pull = jax.vjp(gelu_tanh, pre_gelu)[1]
    grad_pre = gelu_pull(grad_hidden)[0].astype(jnp.bfloat16)
    grads_up = jnp.einsum("rd,rf->df", normed_two, grad_pre, preferred_element_type=jnp.float32)
    bias_up = jnp.sum(grad_pre, axis=0, dtype=jnp.float32)
    grad_normed_two = jnp.einsum("rf,df->rd", grad_pre, w_up, preferred_element_type=jnp.float32)
    norm_two_pull = jax.vjp(
        layer_norm, residual_mid, gain_two.astype(jnp.float32), shift_two.astype(jnp.float32)
    )[1]
    grad_mid, grads_gain_two, grads_shift_two = norm_two_pull(grad_normed_two)
    grad_mid = grad_mid + grad_result
    grad_attn = grad_mid.astype(jnp.bfloat16)
    grads_out = jnp.einsum("rd,re->de", attended_low, grad_attn, preferred_element_type=jnp.float32)
    bias_out = jnp.sum(grad_attn, axis=0, dtype=jnp.float32)
    grad_heads = (
        jnp.einsum("re,de->rd", grad_attn, w_out, preferred_element_type=jnp.float32)
        .astype(jnp.bfloat16)
        .reshape(seq_block, local_len, HEADS, HEAD_DIM)
    )
    delta_sum = jnp.sum(grad_heads.astype(jnp.float32) * attended, axis=-1)
    grad_query, key_local = attend_back(
        query_heads, key_flat, value_flat, grad_heads, log_total, delta_sum, prefix_len
    )
    grad_proj = jnp.concatenate(
        [grad_query.reshape(-1, width), key_local.reshape(-1, 2 * width)], axis=1
    ).astype(jnp.bfloat16)
    grads_qkv = jnp.einsum("rd,re->de", normed_one, grad_proj, preferred_element_type=jnp.float32)
    bias_qkv = jnp.sum(grad_proj, axis=0, dtype=jnp.float32)
    grad_normed_one = jnp.einsum("re,de->rd", grad_proj, w_qkv, preferred_element_type=jnp.float32)
    norm_one_pull = jax.vjp(
        layer_norm, residual_in, gain_one.astype(jnp.float32), shift_one.astype(jnp.float32)
    )[1]
    grad_in, grads_gain_one, grads_shift_one = norm_one_pull(grad_normed_one)
    grad_in = grad_in + grad_mid
    weight_grads = (
        grads_gain_one,
        grads_shift_one,
        grads_qkv,
        bias_qkv,
        grads_out,
        bias_out,
        grads_gain_two,
        grads_shift_two,
        grads_up,
        bias_up,
        grads_down,
        bias_down,
    )
    return (grad_in.astype(jnp.bfloat16).reshape(grad_part.shape), weight_grads)


def general_body(
    tokens,
    cotangent,
    prefix,
    ln1_gain,
    ln1_bias,
    w_qkv,
    b_qkv,
    w_out,
    b_out,
    ln2_gain,
    ln2_bias,
    w_up,
    b_up,
    w_down,
    b_down,
):
    shards = (
        ln1_gain,
        ln1_bias,
        w_qkv,
        b_qkv,
        w_out,
        b_out,
        ln2_gain,
        ln2_bias,
        w_up,
        b_up,
        w_down,
        b_down,
    )
    spread_count = lax.axis_size(("dp", "seq"))
    totals = tuple(
        (
            jnp.zeros((member.shape[0] * spread_count,) + member.shape[1:], jnp.float32)
            for member in shards
        )
    )
    seq_block = tokens.shape[0] // MB
    outputs = []
    grad_inputs = []
    for batch_index in range(MB):
        first_row = batch_index * seq_block
        token_part = tokens[first_row : first_row + seq_block]
        cotangent_part = cotangent[first_row : first_row + seq_block]
        prefix_part = prefix[first_row : first_row + seq_block]
        forward_weights = (
            lax.all_gather(shards[0], ("dp", "seq"), axis=0, tiled=True),
            lax.all_gather(shards[1], ("dp", "seq"), axis=0, tiled=True),
            lax.all_gather(shards[2], ("dp", "seq"), axis=0, tiled=True),
            lax.all_gather(shards[3], ("dp", "seq"), axis=0, tiled=True),
            lax.all_gather(shards[4], ("dp", "seq"), axis=0, tiled=True),
            lax.all_gather(shards[5], ("dp", "seq"), axis=0, tiled=True),
            lax.all_gather(shards[6], ("dp", "seq"), axis=0, tiled=True),
            lax.all_gather(shards[7], ("dp", "seq"), axis=0, tiled=True),
            lax.all_gather(shards[8], ("dp", "seq"), axis=0, tiled=True),
            lax.all_gather(shards[9], ("dp", "seq"), axis=0, tiled=True),
            lax.all_gather(shards[10], ("dp", "seq"), axis=0, tiled=True),
            lax.all_gather(shards[11], ("dp", "seq"), axis=0, tiled=True),
        )
        result, saved = forward_block(forward_weights, token_part, prefix_part)
        back_weights = (
            lax.all_gather(shards[0], ("dp", "seq"), axis=0, tiled=True),
            lax.all_gather(shards[1], ("dp", "seq"), axis=0, tiled=True),
            lax.all_gather(shards[2], ("dp", "seq"), axis=0, tiled=True),
            lax.all_gather(shards[3], ("dp", "seq"), axis=0, tiled=True),
            lax.all_gather(shards[4], ("dp", "seq"), axis=0, tiled=True),
            lax.all_gather(shards[5], ("dp", "seq"), axis=0, tiled=True),
            lax.all_gather(shards[6], ("dp", "seq"), axis=0, tiled=True),
            lax.all_gather(shards[7], ("dp", "seq"), axis=0, tiled=True),
            lax.all_gather(shards[8], ("dp", "seq"), axis=0, tiled=True),
            lax.all_gather(shards[9], ("dp", "seq"), axis=0, tiled=True),
            lax.all_gather(shards[10], ("dp", "seq"), axis=0, tiled=True),
            lax.all_gather(shards[11], ("dp", "seq"), axis=0, tiled=True),
        )
        grad_piece, weight_grads = backward_block(back_weights, saved, cotangent_part, prefix_part)
        totals = tuple(
            (running_sum + new_term for running_sum, new_term in zip(totals, weight_grads))
        )
        outputs.append(result)
        grad_inputs.append(grad_piece)
    reduced = (
        lax.psum_scatter(totals[0], ("dp", "seq"), scatter_dimension=0, tiled=True),
        lax.psum_scatter(totals[1], ("dp", "seq"), scatter_dimension=0, tiled=True),
        lax.psum_scatter(totals[2], ("dp", "seq"), scatter_dimension=0, tiled=True),
        lax.psum_scatter(totals[3], ("dp", "seq"), scatter_dimension=0, tiled=True),
        lax.psum_scatter(totals[4], ("dp", "seq"), scatter_dimension=0, tiled=True),
        lax.psum_scatter(totals[5], ("dp", "seq"), scatter_dimension=0, tiled=True),
        lax.psum_scatter(totals[6], ("dp", "seq"), scatter_dimension=0, tiled=True),
        lax.psum_scatter(totals[7], ("dp", "seq"), scatter_dimension=0, tiled=True),
        lax.psum_scatter(totals[8], ("dp", "seq"), scatter_dimension=0, tiled=True),
        lax.psum_scatter(totals[9], ("dp", "seq"), scatter_dimension=0, tiled=True),
        lax.psum_scatter(totals[10], ("dp", "seq"), scatter_dimension=0, tiled=True),
        lax.psum_scatter(totals[11], ("dp", "seq"), scatter_dimension=0, tiled=True),
    )
    return (
        jnp.concatenate(outputs, axis=0),
        jnp.concatenate(grad_inputs, axis=0),
        reduced[0],
        reduced[1],
        reduced[2],
        reduced[3],
        reduced[4],
        reduced[5],
        reduced[6],
        reduced[7],
        reduced[8],
        reduced[9],
        reduced[10],
        reduced[11],
    )


def solution(mesh):
    in_specs = (
        P("dp", "seq", None),
        P("dp", "seq", None),
        P("dp"),
        P(("dp", "seq")),
        P(("dp", "seq")),
        P(("dp", "seq"), None),
        P(("dp", "seq")),
        P(("dp", "seq"), None),
        P(("dp", "seq")),
        P(("dp", "seq")),
        P(("dp", "seq")),
        P(("dp", "seq"), None),
        P(("dp", "seq")),
        P(("dp", "seq"), None),
        P(("dp", "seq")),
    )
    out_specs = (
        P("dp", "seq", None),
        P("dp", "seq", None),
        P(("dp", "seq")),
        P(("dp", "seq")),
        P(("dp", "seq"), None),
        P(("dp", "seq")),
        P(("dp", "seq"), None),
        P(("dp", "seq")),
        P(("dp", "seq")),
        P(("dp", "seq")),
        P(("dp", "seq"), None),
        P(("dp", "seq")),
        P(("dp", "seq"), None),
        P(("dp", "seq")),
    )
    chosen = body if fits(mesh) else general_body
    return jax.shard_map(chosen, mesh=mesh, in_specs=in_specs, out_specs=out_specs, check_vma=False)
```

```python
import functools

import jax
import jax.numpy as jnp
from jax import lax
from jax.experimental import pallas as pl
from jax.experimental.pallas import tpu as pltpu
from jax.sharding import PartitionSpec as P

HEADS = 12
HEAD_DIM = 64
MB = 2

F32 = jnp.float32
BF = jnp.bfloat16
EPS = 1e-05
MESH = pl.DeviceIdType.MESH
NEG = -1e30
ANY = pl.BlockSpec(memory_space=pl.ANY)
VM = pl.BlockSpec(memory_space=pltpu.VMEM)
SM = pl.BlockSpec(memory_space=pltpu.SMEM)
WIDTHS = (24, 24, 72, 24, 24, 24, 96, 24)
D = 768
FF = 3072
THIRD = 384
LAST = (((1,), (1,)), ((), ()))
FIRST = (((0,), (0,)), ((), ()))
ALL = slice(None)
REMOTES = 224
LOCALS = 64


def places():
    dp = lax.axis_index("dp")
    sq = lax.axis_index("seq")
    return dp // 2, dp % 2, sq // 2, sq % 2


def device(z, x, y, c):
    return (z * 2 + x, y * 2 + c)


def owner_of(wide):
    column = lax.broadcasted_iota(jnp.int32, (1, 32 * wide), 1).astype(F32)
    owner = jnp.floor((column + 0.5) * (1.0 / wide))
    return owner.astype(jnp.int32), (column - owner * wide).astype(jnp.int32)


def spread_row(gathered, index, wide):
    total = 32 * wide
    row = lax.broadcasted_iota(jnp.int32, (32, 256), 0)
    place = lax.broadcasted_iota(jnp.int32, (32, 256), 1)
    pick = jnp.where(place == row * 8 + index, 1.0, 0.0).astype(BF)
    mine = jnp.dot(pick, gathered, preferred_element_type=F32).astype(BF)
    owner, rest = owner_of(wide)
    spread = jnp.where(lax.broadcasted_iota(jnp.int32, (128, total), 0) == rest, 1.0, 0.0).astype(BF)
    full = jnp.dot(mine, spread, preferred_element_type=F32)
    keep = lax.broadcasted_iota(jnp.int32, (32, total), 0) == owner
    return jnp.sum(jnp.where(keep, full, 0.0), axis=0, keepdims=True)


def collect_rows(vector, wide):
    total = 32 * wide
    owner, rest = owner_of(wide)
    gather = jnp.where(lax.broadcasted_iota(jnp.int32, (128, total), 0) == rest, 1.0, 0.0).astype(BF)
    keep = lax.broadcasted_iota(jnp.int32, (32, total), 0) == owner
    high = vector.astype(BF).astype(F32)
    out = None
    for part in (high, vector - high):
        placed = jnp.where(keep, part, 0.0).astype(BF)
        term = lax.dot_general(placed, gather, LAST, preferred_element_type=F32)
        out = term if out is None else out + term
    return out


def add_into(ref, at, other):
    ref[at] = (ref[at].astype(F32) + other.astype(F32)).astype(BF)


def start(copies):
    for copy in copies:
        copy.start()


def arrive(copies):
    for copy in copies:
        copy.wait_recv()


def landed(copies):
    for copy in copies:
        copy.wait()


def lanes(first, count=128):
    return pl.ds(pl.multiple_of(first, 128), count)


def rows_at(first, count, step=256):
    return pl.ds(pl.multiple_of(first, step), count)


class Cut:
    def __init__(self, rows, columns, a, upto=None, upto_row=None):
        first = slice(0, upto_row or rows)
        end = upto or columns
        self.rows, self.columns = rows, columns
        self.a = (first, slice(0, a))
        self.b = (first, slice(a, end))
        self.ab = (first, slice(0, end))
        self.f = None
        self.axis = 0 if upto_row else 1
        if upto:
            self.f = (slice(0, rows), slice(upto, columns))
        if upto_row:
            self.f = (slice(upto_row, rows), slice(0, columns))

    def shape(self, part):
        return tuple(side.stop - side.start for side in part)


CUTS = {
    "down": Cut(192, 384, 128, upto_row=160), "up0": Cut(48, 768, 256, upto=640), "up1": Cut(48, 768, 128, upto=640),
    "out": Cut(48, 384, 128), "q0": Cut(48, 384, 128), "q1": Cut(48, 384, 128), "q2": Cut(48, 384, 128),
}


class Links:
    def __init__(self, ssem, rsem, lsem):
        self.ssem, self.rsem, self.lsem = ssem, rsem, lsem
        self.remotes = self.locals = 0
        self.sent = []
        z, x, y, c = places()
        self.z, self.x, self.y, self.c = z, x, y, c
        self.x2, self.y2, self.c2 = 1 - x, 1 - y, 1 - c
        self.px, self.py, self.pc = device(z, 1 - x, y, c), device(z, x, 1 - y, c), device(z, x, y, 1 - c)
        self.zs = [lax.rem(z + d, 4) for d in (1, 2, 3)]
        self.pz = [device(zz, x, y, c) for zz in self.zs]

    def remote(self, src, dst, dev):
        i = self.remotes
        self.remotes += 1
        copy = pltpu.make_async_remote_copy(
            src_ref=src, dst_ref=dst, send_sem=self.ssem.at[i], recv_sem=self.rsem.at[i],
            device_id=dev, device_id_type=MESH)
        self.sent.append(copy)
        return copy

    def local(self, src, dst):
        i = self.locals
        self.locals += 1
        return pltpu.make_async_copy(src, dst, self.lsem.at[i])

    def greet(self):
        barrier = pltpu.get_barrier_semaphore()
        for dev in [self.px, self.py, self.pc] + self.pz:
            pl.semaphore_signal(barrier, inc=1, device_id=dev, device_id_type=MESH)

    def greeted(self):
        pl.semaphore_wait(pltpu.get_barrier_semaphore(), 6)


class Gather:
    def __init__(self, links, own, other, mine, theirs, cut, whole=True):
        k = links
        rows = own.shape[0]
        at = pl.ds(pl.multiple_of(k.c * rows, 8), rows)
        z, x, y = k.z, k.x, k.y
        self.own = [k.local(own, mine.at[z, x, y, at])]
        self.c0 = [k.remote(other, theirs.at[z, x, y, at], k.pc)]
        a, b, ab, f = cut.a, cut.b, cut.ab, cut.f

        def send(place, dev):
            return k.remote(mine.at[place], mine.at[place], dev)

        self.c1 = [send((z, x, y) + ab, dev) for dev in k.pz]
        self.c2 = [send((ALL, x, y) + a, k.px), send((ALL, x, y) + b, k.py)]
        self.c3 = [send((ALL, ALL, y) + a, k.py), send((ALL, x, ALL) + b, k.px)]
        if f:
            self.c1.append(send((z, x, y) + f, k.py))
            self.c2.append(send((z, x, ALL) + f, k.px))
            self.c3 += [send((z, ALL, ALL) + f, dev) for dev in k.pz]
        self.c4 = [k.remote(mine, mine, k.pc)] if whole else []

    def s0(self):
        start(self.c0)

    def s1(self):
        landed(self.own)
        arrive(self.c0)
        start(self.c1)

    def s2(self):
        arrive(self.c1)
        start(self.c2)

    def s3(self):
        arrive(self.c2)
        start(self.c3)

    def s4(self):
        arrive(self.c3)
        start(self.c4)

    def done(self):
        arrive(self.c4)


class Scatter:
    @staticmethod
    def buffers(cut, whole):
        block = (cut.rows, cut.columns)
        a, b, ab = cut.shape(cut.a), cut.shape(cut.b), cut.shape(cut.ab)
        low = [(4, 2, 2) + block] if whole else []
        low += [(4, 2) + a, (4, 2) + b, (4,) + a, (4,) + b, (3,) + ab]
        if cut.f:
            f = cut.shape(cut.f)
            low += [(3, 2, 2) + f, (2,) + f, f]
        half = (cut.rows // 2, cut.columns)
        return [pltpu.VMEM(shape, BF) for shape in low] + [pltpu.VMEM((2,) + half, F32), pltpu.VMEM(half, F32)]

    def __init__(self, links, grad, prefix, other, cut, work, put):
        k = links
        self.k, self.grad, self.prefix, self.cut, self.put = k, grad, prefix, cut, put
        self.whole = other is not None
        mine = self.mine = grad.at[prefix]
        if self.whole:
            self.r0 = next(work)
            self.c0 = [k.remote(grad.at[other], self.r0, k.pc)]
        else:
            self.c0 = []
        self.r1a, self.r1b, self.r2a, self.r2b, self.r3 = [next(work) for _ in range(5)]
        z, x, y, x2, y2 = k.z, k.x, k.y, k.x2, k.y2
        a, b, ab, f = cut.a, cut.b, cut.ab, cut.f
        self.c1 = [k.remote(mine.at[(ALL, ALL, y2) + a], self.r1a, k.py), k.remote(mine.at[(ALL, x2, ALL) + b], self.r1b, k.px)]
        self.c2 = [k.remote(mine.at[(ALL, x2, y) + a], self.r2a, k.px), k.remote(mine.at[(ALL, x, y2) + b], self.r2b, k.py)]
        self.c3 = [k.remote(mine.at[(k.zs[d], x, y) + ab], self.r3.at[d], k.pz[d]) for d in range(3)]
        if f:
            self.rf1, self.rf2, self.rf3 = [next(work) for _ in range(3)]
            self.c1 += [k.remote(mine.at[(k.zs[d], ALL, ALL) + f], self.rf1.at[d], k.pz[d]) for d in range(3)]
            self.c2.append(k.remote(mine.at[(z, x2, ALL) + f], self.rf2, k.px))
            self.c3.append(k.remote(mine.at[(z, x, y2) + f], self.rf3, k.py))
        self.tot, self.fin = next(work), next(work)
        self.c4 = [k.remote(self.tot.at[k.c2], self.fin, k.pc)]

    def at(self, place):
        return self.prefix + place

    def s0(self):
        start(self.c0)

    def s1(self):
        if self.whole:
            arrive(self.c0)

            def add(i, carry):
                where = (i // 4, lax.rem(i // 2, 2), lax.rem(i, 2))
                add_into(self.grad, self.at(where), self.r0[where])
                return carry

            lax.fori_loop(0, 16, add, 0)
        start(self.c1)

    def s2(self):
        arrive(self.c1)
        k, cut = self.k, self.cut

        def add(i, carry):
            zz, other = i // 2, lax.rem(i, 2)
            add_into(self.grad, self.at((zz, other, k.y) + cut.a), self.r1a[zz, other])
            add_into(self.grad, self.at((zz, k.x, other) + cut.b), self.r1b[zz, other])
            return carry

        lax.fori_loop(0, 8, add, 0)
        if cut.f:
            def add_f(i, carry):
                xx, yy = i // 2, lax.rem(i, 2)
                three = self.rf1[0, xx, yy].astype(F32) + self.rf1[1, xx, yy].astype(F32) + self.rf1[2, xx, yy].astype(F32)
                add_into(self.grad, self.at((k.z, xx, yy) + cut.f), three)
                return carry

            lax.fori_loop(0, 4, add_f, 0)
        start(self.c2)

    def s3(self):
        arrive(self.c2)
        k, cut = self.k, self.cut

        def add(zz, carry):
            add_into(self.grad, self.at((zz, k.x, k.y) + cut.a), self.r2a[zz])
            add_into(self.grad, self.at((zz, k.x, k.y) + cut.b), self.r2b[zz])
            return carry

        lax.fori_loop(0, 4, add, 0)
        if cut.f:
            for yy in range(2):
                add_into(self.grad, self.at((k.z, k.x, yy) + cut.f), self.rf2[yy])
        start(self.c3)

    def s4(self):
        arrive(self.c3)
        k, cut = self.k, self.cut
        total = self.mine[(k.z, k.x, k.y) + cut.ab].astype(F32)
        for d in range(3):
            total = total + self.r3[d].astype(F32)
        if cut.f:
            rest = self.mine[(k.z, k.x, k.y) + cut.f].astype(F32) + self.rf3[...].astype(F32)
            total = jnp.concatenate([total, rest], axis=cut.axis)
        rows = total.shape[0] // 2
        self.tot[0] = total[:rows]
        self.tot[1] = total[rows:]
        start(self.c4)
        self.put(self.tot[k.c], k.c)

    def s5(self):
        arrive(self.c4)
        self.put(self.fin[...], self.k.c2)


def sign_of(value):
    return jnp.clip(value * 1e38, -1.0, 1.0)


def masked(size, seen, low):
    last = jnp.where(seen, size[low:], NEG)
    return last if low == 0 else jnp.concatenate([size[:low], last], axis=0)


def gelu_parts(value):
    rate = 0.7978845608028654
    bent = jnp.tanh(rate * (value + 0.044715 * (value * value * value)))
    result = 0.5 * value * (1.0 + bent)
    slope = 0.5 * (1.0 + bent) + 0.5 * value * (1.0 - bent * bent) * (rate * (1.0 + 0.134145 * (value * value)))
    return result, slope


def unit_rows(rows):
    centre = rows - jnp.mean(rows, axis=-1, keepdims=True)
    scale = lax.rsqrt(jnp.mean(centre * centre, axis=-1, keepdims=True) + EPS)
    return centre * scale, scale


def norm_back(grad, normed, scale):
    return scale * (grad - jnp.mean(grad, axis=-1, keepdims=True)
                    - normed * jnp.mean(grad * normed, axis=-1, keepdims=True))


def layer_kernel(
    prefix, tok, cot, v0_s, v1_s, v2_s, v3_s, v4_s, v5_s, v6_s, v7_s, wq_s, wo_s, wu_s, wd_s,
    out_bo, out_gt, out_q, out_o, out_u, out_d, out_vec,
    wq, wo, wu, wd, gv, k_qst, k_k, k_v, k_att, k_n1t,
    vec_s, wq_p, gvm, tok_all, vrows, wom, al_send, al, cotm, ga_send, ga_all, fa, fb, fc, fr, lt,
    gd, gu, go, gq,
    vs, vbq, vup, vtab, vr0, vr1, vr2, vr3,
    ssem, rsem, lsem, *work,
):
    k = Links(ssem, rsem, lsem)
    bo, gtb = al, cotm
    work = iter(work)
    z, x, y, c, x2, y2, c2 = k.z, k.x, k.y, k.c, k.x2, k.y2, k.c2
    k.greet()
    vmem = pltpu.VMEM

    vec_s[...] = jnp.zeros_like(vec_s)
    for index, (wide, ref) in enumerate(zip(WIDTHS, (v0_s, v1_s, v2_s, v3_s, v4_s, v5_s, v6_s, v7_s))):
        vec_s[index : index + 1, 0:wide] = ref[...].astype(F32).reshape(1, wide)
    for core in range(2):
        for u in range(3):
            for kind in range(3):
                first = kind * D + core * THIRD + u * 128
                wq_p[core, u, :, kind * 128 : (kind + 1) * 128] = wq_s[:, first : first + 128]
    gather_q = [Gather(k, wq_p.at[c, u], wq_p.at[c2, u], wq.at[u], wq.at[u], CUTS[f"q{u}"], False)
                for u in range(3)]

    def halves(shard, full, cut):
        half = full.shape[-1]
        return Gather(k, shard.at[:, lanes(c * half, half)], shard.at[:, lanes(c2 * half, half)], full.at[c], full.at[c2], cut)

    gather_o = halves(wo_s, wo, CUTS["out"])
    gather_d = halves(wd_s, wd, CUTS["down"])
    gather_u = [Gather(k, wu_s.at[:, lanes(c * 1536 + part * D, D)], wu_s.at[:, lanes(c2 * 1536 + part * D, D)],
                       wu.at[c, part], wu.at[c2, part], CUTS[f"up{part}"]) for part in range(2)]
    own_vec = k.local(vec_s, gv.at[z, x, y, c])
    own_tok = k.local(tok.at[y], tok_all.at[y, c])
    own_cot = k.local(cot.at[y], cotm.at[y])
    own_vec.start()
    start(gather_q[0].own)
    own_tok.start()
    others = [gather_q[1], gather_q[2], gather_o] + gather_u + [gather_d]
    for gather in others:
        start(gather.own)
    own_cot.start()
    k.greeted()

    vec_c = k.remote(vec_s, gv.at[z, x, y, c], k.pc)
    tok_y = k.remote(tok.at[y2], tok_all.at[y, c], k.py)
    cot_y = k.remote(cot.at[y2], cotm.at[y], k.py)
    vec_c.start()
    gather_q[0].s0()
    tok_y.start()
    for gather in others:
        gather.s0()
    own_vec.wait()
    vec_c.wait_recv()
    vec_z = [k.remote(gv.at[z, x, y], gv.at[z, x, y], dev) for dev in k.pz]
    start(vec_z)
    gather_q[0].s1()
    gather_q[1].s1()
    own_tok.wait()
    arrive(vec_z)
    vec_x = k.remote(gv.at[:, x, y], gv.at[:, x, y], k.px)
    vec_x.start()
    gather_q[0].s2()
    gather_q[2].s1()
    vec_x.wait_recv()
    vec_y = k.remote(gv.at[:, :, y], gv.at[:, :, y], k.py)
    vec_y.start()
    gather_q[1].s2()
    gather_o.s1()
    gather_q[0].s3()
    tok_y.wait_recv()
    tok_c = k.remote(tok_all.at[:, c], tok_all.at[:, c], k.pc)
    tok_c.start()
    gather_q[2].s2()
    gather_u[0].s1()
    vec_y.wait_recv()
    table = k.local(gv, gvm)
    table.start()
    table.wait()
    table = gvm[...].reshape(256, 128).astype(BF)
    for index, wide in enumerate(WIDTHS):
        vrows[index : index + 1, 0 : 32 * wide] = spread_row(table, index, wide)
    gather_q[1].s3()
    tok_c.wait_recv()

    mine_cols = lanes(c * THIRD, THIRD)
    peer_cols = lanes(c2 * THIRD, THIRD)
    al_own = k.local(al_send.at[:, c], al.at[:, :, mine_cols])
    al_c = k.remote(al_send.at[:, c2], al.at[:, :, mine_cols], k.pc)
    limit = prefix[y] - 1
    sub = lax.broadcasted_iota(jnp.int32, (128, 256), 0)
    wq3 = wq.reshape(3, D, THIRD)

    def forward(n1, n1t, vt, qst, keys_ref, values_ref, att, wqm):
        gain = vrows[0:1, 0:D]
        shift = vrows[1:2, 0:D]

        def norm_block(b, carry):
            normed, _ = unit_rows(tok_all[b // 2, lax.rem(b, 2)].astype(F32))
            normed = (normed * gain + shift).astype(BF)
            at = rows_at(b * 256, 256)
            n1[at, :] = normed
            n1t[:, at] = normed.astype(F32).T.astype(BF)
            return carry

        lax.fori_loop(0, 4, norm_block, 0)
        keep = [k.local(n1t, k_n1t), k.local(qst, k_qst), k.local(keys_ref, k_k),
                k.local(values_ref, k_v), k.local(att, k_att)]
        keep[0].start()
        load_q = [k.local(wq3.at[u], wqm.at[u]) for u in range(3)]
        load_o = k.local(wo.reshape(2, D, THIRD), wom)

        def head(u):
            gather_q[u].s4()
            load_q[u].start()
            load_q[u].wait()

        slots = {
            (0, 3): [gather_q[2].s3, gather_o.s2, gather_u[1].s1], (0, 2): [gather_u[0].s2],
            (0, 1): [gather_o.s3, gather_d.s1], (0, 0): [gather_u[1].s2],
            (1, 3): [gather_u[0].s3], (1, 2): [gather_o.s4], (1, 1): [gather_d.s2], (1, 0): [gather_u[1].s3],
            (2, 3): [gather_o.done, load_o.start, gather_u[0].s4], (2, 2): [cot_y.start], (2, 1): [gather_d.s3], (2, 0): [],
        }

        def unit(u, carry):
            cols = lanes(u * 128)
            for which in range(3):
                @pl.when(u == which)
                def _():
                    head(which)

            def project(b, inner):
                rows = rows_at(b * 512, 512)
                value = jnp.dot(n1[rows, :], wqm[u], preferred_element_type=F32)
                parts = []
                for kind in range(3):
                    bias = vrows[2:3, lanes(kind * D + c * THIRD + u * 128)]
                    parts.append((value[:, kind * 128 : (kind + 1) * 128] + bias).astype(BF))
                queries = parts[0].astype(F32) * 0.125
                qst[cols, rows] = queries.T.astype(BF)
                keys_ref[rows, cols] = parts[1]
                values_ref[rows, cols] = parts[2]
                vt[cols, rows] = parts[2].astype(F32).T.astype(BF)
                return inner

            lax.fori_loop(0, 2, project, 0)
            for block in (3, 2, 1, 0):
                attend(u, block)
                for which in range(3):
                    if slots[which, block]:
                        @pl.when(u == which)
                        def _():
                            for step in slots[which, block]:
                                step()
            return carry

        def attend(u, block):
            rows = min(4, max(block + 1, 2)) * 256
            qcols = slice(block * 256, (block + 1) * 256)
            cols = lanes(u * 128)
            keys = keys_ref[0:rows, cols]
            queries = qst[cols, qcols]
            qpos = block * 256 + lax.broadcasted_iota(jnp.int32, (1, 256), 1)
            low = block * 256
            seen = low + lax.broadcasted_iota(jnp.int32, (rows - low, 256), 0) <= jnp.maximum(qpos, limit)
            for half in range(2):
                chosen = jnp.where(sub // 64 == half, queries, jnp.zeros_like(queries))
                scores = jnp.dot(keys, chosen, preferred_element_type=F32)
                size = jnp.abs(scores)
                size = masked(size, seen, low)
                top = jnp.max(size, axis=0, keepdims=True)
                exponent = jnp.exp(size - top)
                total = jnp.sum(exponent, axis=0, keepdims=True)
                weights = (sign_of(scores) * exponent).astype(BF)
                at = pl.ds(pl.multiple_of(u * 128 + half * 64, 64), 64)
                att[at, qcols] = jnp.dot(vt[at, 0:rows], weights, preferred_element_type=F32) / total
                lt[pl.ds(u * 2 + half, 1), qcols] = top + jnp.log(total)
            al_send[block // 2, block % 2, :, cols] = att[cols, qcols].T.astype(BF)

        lax.fori_loop(0, 3, unit, 0)
        al_own.start()
        al_c.start()
        start(keep[1:])
        load_o.wait()
        al_own.wait()
        al_c.wait_recv()
        landed(keep)

    pl.run_scoped(
        forward, vmem((1024, D), BF), vmem((D, 1024), BF), vmem((THIRD, 1024), BF),
        vmem((THIRD, 1024), BF), vmem((1024, THIRD), BF), vmem((1024, THIRD), BF), vmem((THIRD, 1024), F32),
        vmem((3, D, THIRD), BF))

    def put_to(out, half):
        def put(value, core):
            out[:, lanes(core * half, half)] = value
        return put

    down = Scatter(k, gd, (c,), (c2,), CUTS["down"], work, put_to(out_d, THIRD))

    def put_up(part):
        def put(value, core):
            out_u[:, lanes(core * 1536 + part * D, D)] = value
        return put

    up = [Scatter(k, gu, (c, part), (c2, part), CUTS[f"up{part}"], work, put_up(part)) for part in range(2)]
    outp = Scatter(k, go, (c,), (c2,), CUTS["out"], work, put_to(out_o, THIRD))

    def feed(wbuf, wdb, hid, slope, n2, n2t, alt, gpc):
        b_out, gain, shift = vrows[3:4, 0:D], vrows[4:5, 0:D], vrows[5:6, 0:D]

        def begin(yy, carry):
            rows = rows_at(yy * 256, 256)
            branch = jnp.concatenate([jnp.dot(al[yy], wom[h], preferred_element_type=F32) for h in range(2)], axis=1)
            residual = tok_all[yy, c].astype(F32) + branch + b_out
            fa[yy] = residual
            normed, _ = unit_rows(residual)
            normed = (normed * gain + shift).astype(BF)
            n2[rows, :] = normed
            n2t[:, rows] = normed.astype(F32).T.astype(BF)
            alt[:, rows] = al[yy].astype(F32).T.astype(BF)
            return carry

        lax.fori_loop(0, 2, begin, 0)
        own_cot.wait()
        cot_y.wait_recv()

        wu2 = wu.reshape(2, 2, D, D)
        wd2 = wd.reshape(2, FF, THIRD)

        def chunk(j, first, second):
            h = first if j < 2 else second
            return h, j % 2

        def up_load(j, slot, order):
            h, part = chunk(j, *order)
            return k.local(wu2.at[h, part], wbuf.at[slot])

        def down_load(j, slot, order):
            h, part = chunk(j, *order)
            rows = rows_at(h * 1536 + part * D, D)
            return [k.local(wd2.at[side, rows, :], wdb.at[slot, :, side * THIRD : (side + 1) * THIRD]) for side in range(2)]

        forth = (c, c2)
        loads = [up_load(j, j % 2, forth) for j in range(4)]
        loads[0].start()
        gather_u[1].s4()
        for j in range(4):
            loads[j].wait()
            if j == 0:
                loads[1].start()
            if j == 1:
                gather_u[0].done()
                loads[2].start()
            if j == 2:
                gather_u[1].done()
                loads[3].start()
            h, part = chunk(j, *forth)

            cols = lanes(h * 1536 + part * D, D)
            value = jnp.dot(n2[...], wbuf[j % 2], preferred_element_type=F32) + vrows[6:7, cols]
            result, bend = gelu_parts(value)
            hid[:, cols] = result.astype(BF)
            slope[:, cols] = bend

        vs[7:8, :] = jnp.sum(cotm[0].astype(F32), axis=0, keepdims=True) + jnp.sum(
            cotm[1].astype(F32), axis=0, keepdims=True)

        def down_grad(i, carry):
            total = lax.dot_general(hid[:, lanes(i * THIRD, THIRD)], cotm[...].reshape(512, D), FIRST,
                                    preferred_element_type=F32)
            zz, xx = i // 2, lax.rem(i, 2)
            for yy in range(2):
                for h in range(2):
                    gd[h, zz, xx, yy] = total[yy * 192 : (yy + 1) * 192, h * THIRD : (h + 1) * THIRD].astype(BF)
            return carry

        lax.fori_loop(0, 8, down_grad, 0)
        down.s0()
        fb[...] = jnp.zeros_like(fb)
        fc[...] = jnp.zeros_like(fc)
        gather_d.s4()
        back = (c2, c)
        again = [up_load(j, j % 2, back) for j in range(4)]
        lower = [down_load(j, j % 2, back) for j in range(4)]
        again[0].start()
        down.s1()
        gather_d.done()
        start(lower[0])
        for j in range(4):
            slot = j % 2
            if j < 3:
                again[j + 1].start()
                start(lower[j + 1])
            again[j].wait()
            landed(lower[j])
            h, part = chunk(j, *back)
            cols = lanes(h * 1536 + part * D, D)
            fc[...] += jnp.dot(hid[:, cols], wdb[slot], preferred_element_type=F32).reshape(2, 256, D)
            grad = lax.dot_general(cotm[...].reshape(512, D), wdb[slot], LAST, preferred_element_type=F32)
            grad = (grad * slope[:, cols]).astype(BF)
            gpc[...] = grad
            vup[0:1, cols] = jnp.sum(grad.astype(F32), axis=0, keepdims=True)
            fb[...] += lax.dot_general(gpc[...], wbuf[slot], LAST, preferred_element_type=F32).reshape(2, 256, D)

            def up_grad(zz, carry):
                total = jnp.dot(n2t[rows_at(zz * THIRD, THIRD, 128), :], gpc[...], preferred_element_type=F32)
                for i in range(8):
                    gu[h, part, zz * 2 + i // 4, i // 2 % 2, i % 2] = total[i * 48 : (i + 1) * 48].astype(BF)
                return carry

            lax.fori_loop(0, 2, up_grad, 0)
            if j < 2:
                up[j].s0()
            if j == 2:
                up[0].s1()
                down.s2()
        bo[...] = (fa[...] + fc[...] + vrows[7:8, 0:D].reshape(1, 1, D)).astype(BF)
        up[1].s1()

    ga_c = k.remote(ga_send.at[:, :, peer_cols], ga_all.at[:, c], k.pc)
    def turn(alt, gpc):
        gain = vrows[4:5, 0:D]
        vs[3:6, :] = jnp.zeros((3, D), F32)

        def mid_back(yy, carry):
            rows = rows_at(yy * 256, 256)
            normed, scale = unit_rows(fa[yy])
            grad = fb[yy]
            vs[4:5, :] += jnp.sum(grad * normed, axis=0, keepdims=True)
            vs[5:6, :] += jnp.sum(grad, axis=0, keepdims=True)
            total = cotm[yy].astype(F32) + norm_back(grad * gain, normed, scale)
            fa[yy] = total
            low = total.astype(BF)
            vs[3:4, :] += jnp.sum(low.astype(F32), axis=0, keepdims=True)
            gpc[rows, :] = low
            heads = None
            for side in range(2):
                term = lax.dot_general(low[:, side * THIRD : (side + 1) * THIRD], wom[side], LAST,
                                       preferred_element_type=F32)
                heads = term if heads is None else heads + term
            ga_send[yy] = heads.astype(BF)
            ga_all[yy, c] = ga_send[yy, :, mine_cols]
            return carry

        lax.fori_loop(0, 2, mid_back, 0)
        ga_c.start()

        def out_grad(zz, carry):
            total = jnp.dot(alt[rows_at(zz * THIRD, THIRD, 128), :], gpc[...], preferred_element_type=F32)
            for i in range(8):
                for h in range(2):
                    go[h, zz * 2 + i // 4, i // 2 % 2, i % 2] = total[i * 48 : (i + 1) * 48, h * THIRD : (h + 1) * THIRD].astype(BF)
            return carry

        lax.fori_loop(0, 2, out_grad, 0)
        outp.s0()

    def put_q(u):
        def put(value, core):
            for kind in range(3):
                out_q[:, lanes(kind * D + core * THIRD + u * 128)] = value[:, kind * 128 : (kind + 1) * 128]
        return put

    queue = [Scatter(k, gq, (u,), None, CUTS[f"q{u}"], work, put_q(u)) for u in range(3)]
    bo_own = k.local(bo.at[y], out_bo.at[y])
    bo_y = k.remote(bo.at[y2], out_bo.at[y], k.py)

    def collect(index):
        row = vbq[...] if index == 2 else vup[...] if index == 6 else vs[index : index + 1, :]
        vtab[pl.ds(index, 32, stride=8), :] = collect_rows(row, WIDTHS[index])

    def early():
        for index in (3, 4, 5, 6, 7):
            collect(index)

    def send_out():
        bo_own.start()
        bo_y.start()

    def backward(alt, gpc, qst, keys_ref, values_ref, att, n1t, gt, kt, dk, dv, gpu, wqm):
        loads = [k.local(k_qst, qst), k.local(k_k, keys_ref), k.local(k_v, values_ref),
                 k.local(k_att, att), k.local(k_n1t, n1t), k.local(wq3, wqm)]
        start(loads)
        turn(alt, gpc)
        fb[...] = jnp.zeros_like(fb)
        fc[...] = jnp.zeros_like(fc)
        ga_c.wait_recv()
        landed(loads)
        vbq[...] = jnp.zeros_like(vbq)
        slots = {
            (0, 3): [outp.s1, down.s3], (0, 2): [], (0, 1): [up[0].s2], (0, 0): [send_out, up[1].s2],
            (1, 3): [outp.s2], (1, 2): [down.s4], (1, 1): [up[0].s3], (1, 0): [up[1].s3, down.s5, early],
            (2, 3): [queue[0].s2], (2, 2): [outp.s3], (2, 1): [queue[0].s3], (2, 0): [up[0].s4],
        }

        def unit(u, carry):
            cols = lanes(u * 128)
            for b in range(4):
                rows = slice(b * 256, (b + 1) * 256)
                gt[:, rows] = ga_all[b // 2, b % 2, :, cols].astype(F32).T.astype(BF)
                kt[:, rows] = keys_ref[rows, cols].astype(F32).T.astype(BF)
            dk[...] = jnp.zeros_like(dk)
            dv[...] = jnp.zeros_like(dv)
            for block in (3, 2, 1, 0):
                rows = min(4, max(block + 1, 2)) * 256
                qrange = slice(block * 256, (block + 1) * 256)
                keys = keys_ref[0:rows, cols]
                values = values_ref[0:rows, cols]
                queries_t = qst[cols, qrange]
                grads_t = gt[:, qrange]
                qpos = block * 256 + lax.broadcasted_iota(jnp.int32, (1, 256), 1)
                low = block * 256
                seen = low + lax.broadcasted_iota(jnp.int32, (rows - low, 256), 0) <= jnp.maximum(qpos, limit)
                prod = grads_t.astype(F32) * att[cols, qrange]
                dqs = []
                for half in range(2):
                    part = slice(half * 64, half * 64 + 64)
                    in_sub = sub // 64 == half
                    delta = jnp.sum(prod[part], axis=0, keepdims=True)
                    total = lt[pl.ds(u * 2 + half, 1), qrange]
                    zero = jnp.zeros((), BF)
                    scores = jnp.dot(keys, jnp.where(in_sub, queries_t, zero), preferred_element_type=F32)
                    pull = jnp.dot(values, jnp.where(in_sub, grads_t, zero), preferred_element_type=F32)
                    share = jnp.exp(masked(jnp.abs(scores) - total, seen, low))
                    signed = sign_of(scores) * share
                    grad_scores = (share * pull - signed * delta).astype(BF)
                    signed = signed.astype(BF)
                    dv[part, 0:rows] += lax.dot_general(grads_t[part], signed, LAST, preferred_element_type=F32)
                    dk[part, 0:rows] += lax.dot_general(queries_t[part], grad_scores, LAST, preferred_element_type=F32)
                    dqs.append(jnp.dot(kt[part, 0:rows], grad_scores, preferred_element_type=F32))
                gpu[qrange, 0:128] = (jnp.concatenate(dqs, axis=0).T * 0.125).astype(BF)
                for which in range(3):
                    if slots[which, block]:
                        @pl.when(u == which)
                        def _():
                            for step in slots[which, block]:
                                step()
            for b in range(4):
                rows = slice(b * 256, (b + 1) * 256)
                gpu[rows, 128:256] = dk[:, rows].T.astype(BF)
                gpu[rows, 256:384] = dv[:, rows].T.astype(BF)
            sums = jnp.sum(gpu[...].astype(F32), axis=0, keepdims=True)
            for kind in range(3):
                part = slice(kind * 128, (kind + 1) * 128)
                vbq[0:1, lanes(kind * D + c * THIRD + u * 128)] = sums[:, part]

            def weights(zz, inner):
                block = jnp.dot(n1t[rows_at(zz * THIRD, THIRD, 128), :], gpu[...], preferred_element_type=F32)
                for i in range(8):
                    gq[u, zz * 2 + i // 4, i // 2 % 2, i % 2] = block[i * 48 : (i + 1) * 48].astype(BF)
                return inner

            lax.fori_loop(0, 2, weights, 0)
            for which in range(3):
                @pl.when(u == which)
                def _():
                    queue[which].s1()

            def back_rows(b):
                return lax.dot_general(gpu[rows_at(b * 256, 256), :], wqm[u], LAST, preferred_element_type=F32)

            def back_peer(yy, inner):
                fb[yy] += back_rows(yy * 2 + c2)
                return inner

            def back_own(yy, inner):
                fc[yy] += back_rows(yy * 2 + c)
                return inner

            lax.fori_loop(0, 2, back_peer, 0)

            @pl.when(u == 2)
            def _():
                part_c.start()

            lax.fori_loop(0, 2, back_own, 0)
            return carry

        lax.fori_loop(0, 3, unit, 0)

    part_c = k.remote(fb, fr, k.pc)

    def both(alt, gpc):
        pl.run_scoped(
            functools.partial(feed, alt=alt, gpc=gpc), vmem((2, D, D), BF), vmem((2, D, D), BF),
            vmem((512, FF), BF), vmem((512, FF), F32), vmem((512, D), BF), vmem((D, 512), BF))
        pl.run_scoped(
            functools.partial(backward, alt, gpc), vmem((THIRD, 1024), BF), vmem((1024, THIRD), BF),
            vmem((1024, THIRD), BF), vmem((THIRD, 1024), F32), vmem((D, 1024), BF), vmem((128, 1024), BF),
            vmem((128, 1024), BF), vmem((128, 1024), F32), vmem((128, 1024), F32), vmem((1024, THIRD), BF),
            vmem((3, D, THIRD), BF))

    pl.run_scoped(both, vmem((D, 512), BF), vmem((512, D), BF))

    gain = vrows[0:1, 0:D]
    vs[0:2, :] = jnp.zeros((2, D), F32)
    part_c.wait_recv()

    def last_back(yy):
        normed, scale = unit_rows(tok_all[yy, c].astype(F32))
        grad = fc[yy] + fr[yy]
        vs[0:1, :] += jnp.sum(grad * normed, axis=0, keepdims=True)
        vs[1:2, :] += jnp.sum(grad, axis=0, keepdims=True)
        gtb[yy] = (fa[yy] + norm_back(grad * gain, normed, scale)).astype(BF)

    gt_own = k.local(gtb.at[y], out_gt.at[y])
    gt_y = k.remote(gtb.at[y2], out_gt.at[y], k.py)
    last_back(y2)
    gt_y.start()
    queue[1].s2()
    last_back(y)
    gt_own.start()
    queue[2].s2()
    for index in range(3):
        collect(index)
    table = vtab.reshape(4, 2, 2, 2, 8, 128)
    v0 = k.remote(table.at[:, :, :, c2], vr0, k.pc)
    v1 = k.remote(table.at[:, :, y2, c], vr1, k.py)
    v2 = k.remote(table.at[:, x2, y, c], vr2, k.px)
    v3 = [k.remote(table.at[k.zs[d], x, y, c], vr3.at[d], k.pz[d]) for d in range(3)]

    def tile(zz, xx, yy):
        return rows_at((((zz * 2 + xx) * 2 + yy) * 2 + c) * 8, 8, 8)

    v0.start()
    queue[1].s3()
    v0.wait_recv()

    def add_core(i, carry):
        zz, xx, yy = i // 4, lax.rem(i // 2, 2), lax.rem(i, 2)
        vtab[tile(zz, xx, yy), :] += vr0[zz, xx, yy]
        return carry

    lax.fori_loop(0, 16, add_core, 0)
    v1.start()
    queue[2].s3()
    queue[0].s4()
    up[1].s4()
    v1.wait_recv()

    def add_y(i, carry):
        vtab[tile(i // 2, lax.rem(i, 2), y), :] += vr1[i // 2, lax.rem(i, 2)]
        return carry

    lax.fori_loop(0, 8, add_y, 0)
    v2.start()
    outp.s4()
    up[0].s5()
    queue[0].s5()
    v2.wait_recv()

    def add_x(zz, carry):
        vtab[tile(zz, x, y), :] += vr2[zz]
        return carry

    lax.fori_loop(0, 4, add_x, 0)
    start(v3)
    queue[1].s4()
    up[1].s5()
    outp.s5()
    queue[2].s4()
    queue[1].s5()
    queue[2].s5()
    arrive(v3)
    out_vec[...] = vtab[tile(z, x, y), :] + vr3[0] + vr3[1] + vr3[2]
    landed([gt_own, bo_own])
    arrive([gt_y, bo_y])
    for copy in k.sent:
        copy.wait_send()
    assert k.remotes <= REMOTES and k.locals <= LOCALS


def layer_call(*operands):
    sds = jax.ShapeDtypeStruct
    vmem = pltpu.VMEM
    dma = pltpu.SemaphoreType.DMA
    results = (
        sds((2, 256, D), BF), sds((2, 256, D), BF), sds((24, 3 * D), F32), sds((24, D), F32), sds((24, FF), F32),
        sds((96, D), F32), sds((8, 128), F32),
    )
    held = (
        sds((3, 4, 2, 2, 48, 384), BF), sds((2, 4, 2, 2, 48, 384), BF), sds((2, 2, 4, 2, 2, 48, 768), BF),
        sds((2, 4, 2, 2, 192, 384), BF), sds((4, 2, 2, 2, 8, 128), F32), sds((THIRD, 1024), BF),
        sds((1024, THIRD), BF), sds((1024, THIRD), BF), sds((THIRD, 1024), F32), sds((D, 1024), BF),
    )
    scratch = [
        vmem((8, 128), F32), vmem((2, 3, 24, THIRD), BF), vmem((4, 2, 2, 2, 8, 128), F32), vmem((2, 2, 256, D), BF), vmem((8, FF), F32),
        vmem((2, D, THIRD), BF), vmem((2, 2, 256, THIRD), BF), vmem((2, 256, D), BF), vmem((2, 256, D), BF),
        vmem((2, 256, D), BF), vmem((2, 2, 256, THIRD), BF), vmem((2, 256, D), F32), vmem((2, 256, D), F32),
        vmem((2, 256, D), F32), vmem((2, 256, D), F32), vmem((8, 1024), F32),
    ]
    scratch += [
        vmem((2, 4, 2, 2, 192, 384), BF), vmem((2, 2, 4, 2, 2, 48, 768), BF), vmem((2, 4, 2, 2, 48, 384), BF),
        vmem((3, 4, 2, 2, 48, 384), BF),
        vmem((8, D), F32), vmem((1, 3 * D), F32), vmem((1, FF), F32), vmem((256, 128), F32), vmem((4, 2, 2, 8, 128), F32),
        vmem((4, 2, 8, 128), F32), vmem((4, 8, 128), F32), vmem((3, 8, 128), F32),
        dma((REMOTES,)), dma((REMOTES,)), dma((LOCALS,)),
    ]
    for name in ("down", "up0", "up1", "out", "q0", "q1", "q2"):
        scratch += Scatter.buffers(CUTS[name], not name.startswith("q"))
    return pl.pallas_call(
        layer_kernel,
        out_shape=results + held,
        in_specs=[SM] + [ANY] * 2 + [VM] * 12,
        out_specs=(ANY, ANY) + (VM,) * 5 + (ANY,) * len(held),
        scratch_shapes=scratch,
        compiler_params=pltpu.CompilerParams(
            collective_id=0, has_side_effects=True, vmem_limit_bytes=63 * 2**20),
    )(*operands)[: len(results)]


def finish_kernel(*refs):
    sources, results, (table, sems) = refs[:7], refs[7:21], refs[21:]
    copies = [pltpu.make_async_copy(source, result, sems.at[i])
              for i, (source, result) in enumerate(zip(sources, results[:6] + (table,)))]
    start(copies)
    landed(copies)
    for index, wide in enumerate(WIDTHS):
        results[6 + index][...] = table[index, 0:wide]


def finish_call(*operands):
    sds = jax.ShapeDtypeStruct
    shapes = tuple(sds(o.shape, o.dtype) for o in operands[:6]) + tuple(sds((wide,), F32) for wide in WIDTHS)
    return pl.pallas_call(
        finish_kernel, out_shape=shapes, in_specs=[ANY] * 7, out_specs=(VM,) * 14,
        scratch_shapes=[pltpu.VMEM((8, 128), F32), pltpu.SemaphoreType.DMA((7,))],
        compiler_params=pltpu.CompilerParams(vmem_limit_bytes=60 * 2**20),
    )(*operands)


def body(
    tokens, cotangent, prefix, ln1_gain, ln1_bias, w_qkv, b_qkv, w_out, b_out,
    ln2_gain, ln2_bias, w_up, b_up, w_down, b_down,
):
    results = layer_call(
        prefix, tokens, cotangent, ln1_gain, ln1_bias, b_qkv, b_out, ln2_gain, ln2_bias, b_up, b_down,
        w_qkv, w_out, w_up, w_down)
    block_out, grad_tokens, gq, go, gu, gd, *rows = finish_call(*results)
    return (
        block_out, grad_tokens, rows[0], rows[1], gq, rows[2], go, rows[3], rows[4], rows[5], gu, rows[6], gd, rows[7],
    )


def fits(mesh):
    return dict(mesh.shape) == {"dp": 8, "seq": 4}


norm_eps = 1e-05
block_rows = 512


def layer_norm(features, gain, shift):
    centre = features - jnp.mean(features, axis=-1, keepdims=True)
    spread = jnp.mean(centre * centre, axis=-1, keepdims=True)
    return centre * lax.rsqrt(spread + norm_eps) * gain + shift


def gelu_tanh(values):
    return jax.nn.gelu(values, approximate=True)


def in_blocks(update, running, pieces):
    length = pieces[0].shape[1]
    blocks = length // block_rows
    blocked_pieces = tuple(
        (
            jnp.swapaxes(
                member.reshape((member.shape[0], blocks, block_rows) + member.shape[2:]), 0, 1
            )
            for member in pieces
        )
    )

    def advance(carried, element):
        return (update(carried, element[0], element[1] * block_rows), None)

    running, unused = lax.scan(
        advance, running, (blocked_pieces, jnp.arange(blocks, dtype=jnp.int32))
    )
    return running


def to_heads(flat_rows):
    return flat_rows.reshape(flat_rows.shape[0], flat_rows.shape[1], HEADS, HEAD_DIM)


def visible_mask(query_places, key_places, prefix_len):
    earlier = key_places[None, None, :] <= query_places[None, :, None]
    in_prefix = key_places[None, None, :] < prefix_len[:, None, None]
    return (earlier | in_prefix)[:, :, None, :]


def head_scores(query_heads, key_flat):
    return jnp.einsum(
        "bqhd,bkhd->bqhk", query_heads, to_heads(key_flat), preferred_element_type=jnp.float32
    ) * HEAD_DIM ** (-0.5)


def attend(query_heads, key_flat, value_flat, prefix_len):
    local_len = query_heads.shape[1]
    query_places = lax.axis_index("seq") * local_len + jnp.arange(local_len, dtype=jnp.int32)
    starting = (
        jnp.zeros(query_heads.shape, jnp.float32),
        jnp.zeros(query_heads.shape[:3], jnp.float32),
        jnp.zeros(query_heads.shape[:3], jnp.float32),
    )

    def update(running, pieces, offset):
        weighted, normaliser, ceiling = running
        key_piece, value_piece = pieces
        key_places = offset + jnp.arange(key_piece.shape[1], dtype=jnp.int32)
        scores = head_scores(query_heads, key_piece)
        visible = visible_mask(query_places, key_places, prefix_len)
        magnitude = jnp.where(visible, jnp.abs(scores), 0.0)
        new_ceiling = jnp.maximum(ceiling, jnp.max(magnitude, axis=-1))
        exponent = jnp.where(visible, jnp.exp(magnitude - new_ceiling[..., None]), 0.0)
        factor = jnp.exp(ceiling - new_ceiling)
        weights = (jnp.sign(scores) * exponent).astype(jnp.bfloat16)
        weighted = weighted * factor[..., None] + jnp.einsum(
            "bqhk,bkhd->bqhd", weights, to_heads(value_piece), preferred_element_type=jnp.float32
        )
        normaliser = normaliser * factor + jnp.sum(exponent, axis=-1)
        return (weighted, normaliser, new_ceiling)

    weighted, normaliser, ceiling = in_blocks(
        update,
        starting,
        (
            lax.all_gather(key_flat, "seq", axis=1, tiled=True),
            lax.all_gather(value_flat, "seq", axis=1, tiled=True),
        ),
    )
    return (weighted / normaliser[..., None], ceiling + jnp.log(normaliser))


def grad_terms(
    query_heads,
    grad_heads,
    key_flat,
    value_flat,
    log_total,
    delta_sum,
    query_places,
    key_places,
    prefix_len,
):
    scores = head_scores(query_heads, key_flat)
    sign_of = jnp.sign(scores)
    visible = visible_mask(query_places, key_places, prefix_len)
    shares = jnp.where(visible, jnp.exp(jnp.abs(scores) - log_total[..., None]), 0.0)
    grad_weights = jnp.einsum(
        "bqhd,bkhd->bqhk", grad_heads, to_heads(value_flat), preferred_element_type=jnp.float32
    )
    grad_scores = (shares * (grad_weights - sign_of * delta_sum[..., None])).astype(jnp.bfloat16)
    return ((sign_of * shares).astype(jnp.bfloat16), grad_scores)


def query_term(grad_scores, key_flat):
    return jnp.einsum(
        "bqhk,bkhd->bqhd", grad_scores, to_heads(key_flat), preferred_element_type=jnp.float32
    ) * HEAD_DIM ** (-0.5)


def key_value_terms(query_heads, grad_heads, shares_low, grad_scores):
    key_term = jnp.einsum(
        "bqhk,bqhd->bkhd", grad_scores, query_heads, preferred_element_type=jnp.float32
    ) * HEAD_DIM ** (-0.5)
    value_term = jnp.einsum(
        "bqhk,bqhd->bkhd", shares_low, grad_heads, preferred_element_type=jnp.float32
    )
    flat_shape = (key_term.shape[0], key_term.shape[1], key_term.shape[2] * key_term.shape[3])
    return jnp.concatenate([key_term.reshape(flat_shape), value_term.reshape(flat_shape)], axis=-1)


def attend_back(query_heads, key_flat, value_flat, grad_heads, log_total, delta_sum, prefix_len):
    seq_block, local_len = (query_heads.shape[0], query_heads.shape[1])
    width = key_flat.shape[2]
    local_places = lax.axis_index("seq") * local_len + jnp.arange(local_len, dtype=jnp.int32)
    starting = (
        jnp.zeros(query_heads.shape, jnp.float32),
        jnp.zeros((seq_block, lax.axis_size("seq") * local_len, 2 * width), jnp.float32),
    )

    def update_both(running, pieces, offset):
        grad_query, grad_keys = running
        key_piece, value_piece = pieces
        piece_len = key_piece.shape[1]
        key_places = offset + jnp.arange(piece_len, dtype=jnp.int32)
        shares_low, grad_scores = grad_terms(
            query_heads,
            grad_heads,
            key_piece,
            value_piece,
            log_total,
            delta_sum,
            local_places,
            key_places,
            prefix_len,
        )
        grad_query = grad_query + query_term(grad_scores, key_piece)
        current = lax.dynamic_slice_in_dim(grad_keys, offset, piece_len, 1)
        updated = current + key_value_terms(query_heads, grad_heads, shares_low, grad_scores)
        return (grad_query, lax.dynamic_update_slice_in_dim(grad_keys, updated, offset, 1))

    grad_query, grad_keys = in_blocks(
        update_both,
        starting,
        (
            lax.all_gather(key_flat, "seq", axis=1, tiled=True),
            lax.all_gather(value_flat, "seq", axis=1, tiled=True),
        ),
    )
    key_local = lax.psum_scatter(
        grad_keys.astype(jnp.bfloat16), "seq", scatter_dimension=1, tiled=True
    ).astype(jnp.float32)
    return (grad_query, key_local)


def forward_block(weights_in, token_part, prefix_len):
    (
        gain_one,
        shift_one,
        w_qkv,
        b_qkv,
        w_out,
        b_out,
        gain_two,
        shift_two,
        w_up,
        b_up,
        w_down,
        b_down,
    ) = weights_in
    seq_block, local_len, width = token_part.shape
    residual_in = token_part.reshape(-1, width).astype(jnp.float32)
    normed_one = layer_norm(
        residual_in, gain_one.astype(jnp.float32), shift_one.astype(jnp.float32)
    ).astype(jnp.bfloat16)
    projected = jnp.dot(normed_one, w_qkv, preferred_element_type=jnp.float32) + b_qkv.astype(
        jnp.float32
    )
    query_heads = (
        projected[:, :width].astype(jnp.bfloat16).reshape(seq_block, local_len, HEADS, HEAD_DIM)
    )
    key_flat = (
        projected[:, width : 2 * width].astype(jnp.bfloat16).reshape(seq_block, local_len, width)
    )
    value_flat = projected[:, 2 * width :].astype(jnp.bfloat16).reshape(seq_block, local_len, width)
    attended, log_total = attend(query_heads, key_flat, value_flat, prefix_len)
    attended_low = attended.reshape(-1, width).astype(jnp.bfloat16)
    residual_mid = (
        residual_in
        + jnp.dot(attended_low, w_out, preferred_element_type=jnp.float32)
        + b_out.astype(jnp.float32)
    )
    normed_two = layer_norm(
        residual_mid, gain_two.astype(jnp.float32), shift_two.astype(jnp.float32)
    ).astype(jnp.bfloat16)
    pre_gelu = jnp.dot(normed_two, w_up, preferred_element_type=jnp.float32) + b_up.astype(
        jnp.float32
    )
    hidden = gelu_tanh(pre_gelu).astype(jnp.bfloat16)
    result = (
        residual_mid
        + jnp.dot(hidden, w_down, preferred_element_type=jnp.float32)
        + b_down.astype(jnp.float32)
    )
    saved = (
        residual_in,
        normed_one,
        query_heads,
        key_flat,
        value_flat,
        attended,
        log_total,
        attended_low,
        residual_mid,
        normed_two,
        pre_gelu,
        hidden,
    )
    return (result.astype(jnp.bfloat16).reshape(token_part.shape), saved)


def backward_block(weights_in, saved, grad_part, prefix_len):
    (
        gain_one,
        shift_one,
        w_qkv,
        b_qkv,
        w_out,
        b_out,
        gain_two,
        shift_two,
        w_up,
        b_up,
        w_down,
        b_down,
    ) = weights_in
    (
        residual_in,
        normed_one,
        query_heads,
        key_flat,
        value_flat,
        attended,
        log_total,
        attended_low,
        residual_mid,
        normed_two,
        pre_gelu,
        hidden,
    ) = saved
    seq_block, local_len, width = grad_part.shape
    grad_result = grad_part.reshape(-1, width).astype(jnp.float32)
    grad_branch = grad_part.reshape(-1, width)
    grads_down = jnp.einsum("rf,rd->fd", hidden, grad_branch, preferred_element_type=jnp.float32)
    bias_down = jnp.sum(grad_branch, axis=0, dtype=jnp.float32)
    grad_hidden = jnp.einsum("rd,fd->rf", grad_branch, w_down, preferred_element_type=jnp.float32)
    gelu_pull = jax.vjp(gelu_tanh, pre_gelu)[1]
    grad_pre = gelu_pull(grad_hidden)[0].astype(jnp.bfloat16)
    grads_up = jnp.einsum("rd,rf->df", normed_two, grad_pre, preferred_element_type=jnp.float32)
    bias_up = jnp.sum(grad_pre, axis=0, dtype=jnp.float32)
    grad_normed_two = jnp.einsum("rf,df->rd", grad_pre, w_up, preferred_element_type=jnp.float32)
    norm_two_pull = jax.vjp(
        layer_norm, residual_mid, gain_two.astype(jnp.float32), shift_two.astype(jnp.float32)
    )[1]
    grad_mid, grads_gain_two, grads_shift_two = norm_two_pull(grad_normed_two)
    grad_mid = grad_mid + grad_result
    grad_attn = grad_mid.astype(jnp.bfloat16)
    grads_out = jnp.einsum("rd,re->de", attended_low, grad_attn, preferred_element_type=jnp.float32)
    bias_out = jnp.sum(grad_attn, axis=0, dtype=jnp.float32)
    grad_heads = (
        jnp.einsum("re,de->rd", grad_attn, w_out, preferred_element_type=jnp.float32)
        .astype(jnp.bfloat16)
        .reshape(seq_block, local_len, HEADS, HEAD_DIM)
    )
    delta_sum = jnp.sum(grad_heads.astype(jnp.float32) * attended, axis=-1)
    grad_query, key_local = attend_back(
        query_heads, key_flat, value_flat, grad_heads, log_total, delta_sum, prefix_len
    )
    grad_proj = jnp.concatenate(
        [grad_query.reshape(-1, width), key_local.reshape(-1, 2 * width)], axis=1
    ).astype(jnp.bfloat16)
    grads_qkv = jnp.einsum("rd,re->de", normed_one, grad_proj, preferred_element_type=jnp.float32)
    bias_qkv = jnp.sum(grad_proj, axis=0, dtype=jnp.float32)
    grad_normed_one = jnp.einsum("re,de->rd", grad_proj, w_qkv, preferred_element_type=jnp.float32)
    norm_one_pull = jax.vjp(
        layer_norm, residual_in, gain_one.astype(jnp.float32), shift_one.astype(jnp.float32)
    )[1]
    grad_in, grads_gain_one, grads_shift_one = norm_one_pull(grad_normed_one)
    grad_in = grad_in + grad_mid
    weight_grads = (
        grads_gain_one,
        grads_shift_one,
        grads_qkv,
        bias_qkv,
        grads_out,
        bias_out,
        grads_gain_two,
        grads_shift_two,
        grads_up,
        bias_up,
        grads_down,
        bias_down,
    )
    return (grad_in.astype(jnp.bfloat16).reshape(grad_part.shape), weight_grads)


def general_body(
    tokens,
    cotangent,
    prefix,
    ln1_gain,
    ln1_bias,
    w_qkv,
    b_qkv,
    w_out,
    b_out,
    ln2_gain,
    ln2_bias,
    w_up,
    b_up,
    w_down,
    b_down,
):
    shards = (
        ln1_gain,
        ln1_bias,
        w_qkv,
        b_qkv,
        w_out,
        b_out,
        ln2_gain,
        ln2_bias,
        w_up,
        b_up,
        w_down,
        b_down,
    )
    spread_count = lax.axis_size(("dp", "seq"))
    totals = tuple(
        (
            jnp.zeros((member.shape[0] * spread_count,) + member.shape[1:], jnp.float32)
            for member in shards
        )
    )
    seq_block = tokens.shape[0] // MB
    outputs = []
    grad_inputs = []
    for batch_index in range(MB):
        first_row = batch_index * seq_block
        token_part = tokens[first_row : first_row + seq_block]
        cotangent_part = cotangent[first_row : first_row + seq_block]
        prefix_part = prefix[first_row : first_row + seq_block]
        forward_weights = (
            lax.all_gather(shards[0], ("dp", "seq"), axis=0, tiled=True),
            lax.all_gather(shards[1], ("dp", "seq"), axis=0, tiled=True),
            lax.all_gather(shards[2], ("dp", "seq"), axis=0, tiled=True),
            lax.all_gather(shards[3], ("dp", "seq"), axis=0, tiled=True),
            lax.all_gather(shards[4], ("dp", "seq"), axis=0, tiled=True),
            lax.all_gather(shards[5], ("dp", "seq"), axis=0, tiled=True),
            lax.all_gather(shards[6], ("dp", "seq"), axis=0, tiled=True),
            lax.all_gather(shards[7], ("dp", "seq"), axis=0, tiled=True),
            lax.all_gather(shards[8], ("dp", "seq"), axis=0, tiled=True),
            lax.all_gather(shards[9], ("dp", "seq"), axis=0, tiled=True),
            lax.all_gather(shards[10], ("dp", "seq"), axis=0, tiled=True),
            lax.all_gather(shards[11], ("dp", "seq"), axis=0, tiled=True),
        )
        result, saved = forward_block(forward_weights, token_part, prefix_part)
        back_weights = (
            lax.all_gather(shards[0], ("dp", "seq"), axis=0, tiled=True),
            lax.all_gather(shards[1], ("dp", "seq"), axis=0, tiled=True),
            lax.all_gather(shards[2], ("dp", "seq"), axis=0, tiled=True),
            lax.all_gather(shards[3], ("dp", "seq"), axis=0, tiled=True),
            lax.all_gather(shards[4], ("dp", "seq"), axis=0, tiled=True),
            lax.all_gather(shards[5], ("dp", "seq"), axis=0, tiled=True),
            lax.all_gather(shards[6], ("dp", "seq"), axis=0, tiled=True),
            lax.all_gather(shards[7], ("dp", "seq"), axis=0, tiled=True),
            lax.all_gather(shards[8], ("dp", "seq"), axis=0, tiled=True),
            lax.all_gather(shards[9], ("dp", "seq"), axis=0, tiled=True),
            lax.all_gather(shards[10], ("dp", "seq"), axis=0, tiled=True),
            lax.all_gather(shards[11], ("dp", "seq"), axis=0, tiled=True),
        )
        grad_piece, weight_grads = backward_block(back_weights, saved, cotangent_part, prefix_part)
        totals = tuple(
            (running_sum + new_term for running_sum, new_term in zip(totals, weight_grads))
        )
        outputs.append(result)
        grad_inputs.append(grad_piece)
    reduced = (
        lax.psum_scatter(totals[0], ("dp", "seq"), scatter_dimension=0, tiled=True),
        lax.psum_scatter(totals[1], ("dp", "seq"), scatter_dimension=0, tiled=True),
        lax.psum_scatter(totals[2], ("dp", "seq"), scatter_dimension=0, tiled=True),
        lax.psum_scatter(totals[3], ("dp", "seq"), scatter_dimension=0, tiled=True),
        lax.psum_scatter(totals[4], ("dp", "seq"), scatter_dimension=0, tiled=True),
        lax.psum_scatter(totals[5], ("dp", "seq"), scatter_dimension=0, tiled=True),
        lax.psum_scatter(totals[6], ("dp", "seq"), scatter_dimension=0, tiled=True),
        lax.psum_scatter(totals[7], ("dp", "seq"), scatter_dimension=0, tiled=True),
        lax.psum_scatter(totals[8], ("dp", "seq"), scatter_dimension=0, tiled=True),
        lax.psum_scatter(totals[9], ("dp", "seq"), scatter_dimension=0, tiled=True),
        lax.psum_scatter(totals[10], ("dp", "seq"), scatter_dimension=0, tiled=True),
        lax.psum_scatter(totals[11], ("dp", "seq"), scatter_dimension=0, tiled=True),
    )
    return (
        jnp.concatenate(outputs, axis=0),
        jnp.concatenate(grad_inputs, axis=0),
        reduced[0],
        reduced[1],
        reduced[2],
        reduced[3],
        reduced[4],
        reduced[5],
        reduced[6],
        reduced[7],
        reduced[8],
        reduced[9],
        reduced[10],
        reduced[11],
    )


def solution(mesh):
    in_specs = (
        P("dp", "seq", None),
        P("dp", "seq", None),
        P("dp"),
        P(("dp", "seq")),
        P(("dp", "seq")),
        P(("dp", "seq"), None),
        P(("dp", "seq")),
        P(("dp", "seq"), None),
        P(("dp", "seq")),
        P(("dp", "seq")),
        P(("dp", "seq")),
        P(("dp", "seq"), None),
        P(("dp", "seq")),
        P(("dp", "seq"), None),
        P(("dp", "seq")),
    )
    out_specs = (
        P("dp", "seq", None),
        P("dp", "seq", None),
        P(("dp", "seq")),
        P(("dp", "seq")),
        P(("dp", "seq"), None),
        P(("dp", "seq")),
        P(("dp", "seq"), None),
        P(("dp", "seq")),
        P(("dp", "seq")),
        P(("dp", "seq")),
        P(("dp", "seq"), None),
        P(("dp", "seq")),
        P(("dp", "seq"), None),
        P(("dp", "seq")),
    )
    chosen = body if fits(mesh) else general_body
    return jax.shard_map(chosen, mesh=mesh, in_specs=in_specs, out_specs=out_specs, check_vma=False)
```

```python
import functools

import jax
import jax.numpy as jnp
from jax import lax
from jax.experimental import pallas as pl
from jax.experimental.pallas import tpu as pltpu
from jax.sharding import PartitionSpec as P

HEADS = 12
HEAD_DIM = 64
MB = 2

F32 = jnp.float32
BF = jnp.bfloat16
EPS = 1e-05
MESH = pl.DeviceIdType.MESH
NEG = -1e30
ANY = pl.BlockSpec(memory_space=pl.ANY)
VM = pl.BlockSpec(memory_space=pltpu.VMEM)
SM = pl.BlockSpec(memory_space=pltpu.SMEM)
WIDTHS = (24, 24, 72, 24, 24, 24, 96, 24)
D = 768
FF = 3072
THIRD = 384
LAST = (((1,), (1,)), ((), ()))
FIRST = (((0,), (0,)), ((), ()))
ALL = slice(None)
REMOTES = 224
LOCALS = 64


def places():
    dp = lax.axis_index("dp")
    sq = lax.axis_index("seq")
    return dp // 2, dp % 2, sq // 2, sq % 2


def device(z, x, y, c):
    return (z * 2 + x, y * 2 + c)


def owner_of(wide):
    column = lax.broadcasted_iota(jnp.int32, (1, 32 * wide), 1).astype(F32)
    owner = jnp.floor((column + 0.5) * (1.0 / wide))
    return owner.astype(jnp.int32), (column - owner * wide).astype(jnp.int32)


def spread_row(gathered, index, wide):
    total = 32 * wide
    row = lax.broadcasted_iota(jnp.int32, (32, 256), 0)
    place = lax.broadcasted_iota(jnp.int32, (32, 256), 1)
    pick = jnp.where(place == row * 8 + index, 1.0, 0.0).astype(BF)
    mine = jnp.dot(pick, gathered, preferred_element_type=F32).astype(BF)
    owner, rest = owner_of(wide)
    spread = jnp.where(lax.broadcasted_iota(jnp.int32, (128, total), 0) == rest, 1.0, 0.0).astype(BF)
    full = jnp.dot(mine, spread, preferred_element_type=F32)
    keep = lax.broadcasted_iota(jnp.int32, (32, total), 0) == owner
    return jnp.sum(jnp.where(keep, full, 0.0), axis=0, keepdims=True)


def collect_rows(vector, wide):
    total = 32 * wide
    owner, rest = owner_of(wide)
    gather = jnp.where(lax.broadcasted_iota(jnp.int32, (128, total), 0) == rest, 1.0, 0.0).astype(BF)
    keep = lax.broadcasted_iota(jnp.int32, (32, total), 0) == owner
    high = vector.astype(BF).astype(F32)
    out = None
    for part in (high, vector - high):
        placed = jnp.where(keep, part, 0.0).astype(BF)
        term = lax.dot_general(placed, gather, LAST, preferred_element_type=F32)
        out = term if out is None else out + term
    return out


def add_into(ref, at, other):
    ref[at] = (ref[at].astype(F32) + other.astype(F32)).astype(BF)


def start(copies):
    for copy in copies:
        copy.start()


def arrive(copies):
    for copy in copies:
        copy.wait_recv()


def landed(copies):
    for copy in copies:
        copy.wait()


def lanes(first, count=128):
    return pl.ds(pl.multiple_of(first, 128), count)


def rows_at(first, count, step=256):
    return pl.ds(pl.multiple_of(first, step), count)


class Cut:
    def __init__(self, rows, columns, a, upto=None, upto_row=None):
        first = slice(0, upto_row or rows)
        end = upto or columns
        self.rows, self.columns = rows, columns
        self.a = (first, slice(0, a))
        self.b = (first, slice(a, end))
        self.ab = (first, slice(0, end))
        self.f = None
        self.axis = 0 if upto_row else 1
        if upto:
            self.f = (slice(0, rows), slice(upto, columns))
        if upto_row:
            self.f = (slice(upto_row, rows), slice(0, columns))

    def shape(self, part):
        return tuple(side.stop - side.start for side in part)


CUTS = {
    "down": Cut(192, 384, 128, upto_row=160), "up0": Cut(48, 768, 256, upto=640), "up1": Cut(48, 768, 128, upto=640),
    "out": Cut(48, 384, 128), "q0": Cut(48, 384, 128), "q1": Cut(48, 384, 128), "q2": Cut(48, 384, 128),
}


class Links:
    def __init__(self, ssem, rsem, lsem):
        self.ssem, self.rsem, self.lsem = ssem, rsem, lsem
        self.remotes = self.locals = 0
        self.sent = []
        z, x, y, c = places()
        self.z, self.x, self.y, self.c = z, x, y, c
        self.x2, self.y2, self.c2 = 1 - x, 1 - y, 1 - c
        self.px, self.py, self.pc = device(z, 1 - x, y, c), device(z, x, 1 - y, c), device(z, x, y, 1 - c)
        self.zs = [lax.rem(z + d, 4) for d in (1, 2, 3)]
        self.pz = [device(zz, x, y, c) for zz in self.zs]

    def remote(self, src, dst, dev):
        i = self.remotes
        self.remotes += 1
        copy = pltpu.make_async_remote_copy(
            src_ref=src, dst_ref=dst, send_sem=self.ssem.at[i], recv_sem=self.rsem.at[i],
            device_id=dev, device_id_type=MESH)
        self.sent.append(copy)
        return copy

    def local(self, src, dst):
        i = self.locals
        self.locals += 1
        return pltpu.make_async_copy(src, dst, self.lsem.at[i])

    def greet(self):
        barrier = pltpu.get_barrier_semaphore()
        for dev in [self.px, self.py, self.pc] + self.pz:
            pl.semaphore_signal(barrier, inc=1, device_id=dev, device_id_type=MESH)

    def greeted(self):
        pl.semaphore_wait(pltpu.get_barrier_semaphore(), 6)


class Gather:
    def __init__(self, links, own, other, mine, theirs, cut, whole=True):
        k = links
        rows = own.shape[0]
        at = pl.ds(pl.multiple_of(k.c * rows, 8), rows)
        z, x, y = k.z, k.x, k.y
        self.own = [k.local(own, mine.at[z, x, y, at])]
        self.c0 = [k.remote(other, theirs.at[z, x, y, at], k.pc)]
        a, b, ab, f = cut.a, cut.b, cut.ab, cut.f

        def send(place, dev):
            return k.remote(mine.at[place], mine.at[place], dev)

        self.c1 = [send((z, x, y) + ab, dev) for dev in k.pz]
        self.c2 = [send((ALL, x, y) + a, k.px), send((ALL, x, y) + b, k.py)]
        self.c3 = [send((ALL, ALL, y) + a, k.py), send((ALL, x, ALL) + b, k.px)]
        if f:
            self.c1.append(send((z, x, y) + f, k.py))
            self.c2.append(send((z, x, ALL) + f, k.px))
            self.c3 += [send((z, ALL, ALL) + f, dev) for dev in k.pz]
        self.c4 = [k.remote(mine, mine, k.pc)] if whole else []

    def s0(self):
        start(self.c0)

    def s1(self):
        landed(self.own)
        arrive(self.c0)
        start(self.c1)

    def s2(self):
        arrive(self.c1)
        start(self.c2)

    def s3(self):
        arrive(self.c2)
        start(self.c3)

    def s4(self):
        arrive(self.c3)
        start(self.c4)

    def done(self):
        arrive(self.c4)


class Scatter:
    @staticmethod
    def buffers(cut, whole):
        block = (cut.rows, cut.columns)
        a, b, ab = cut.shape(cut.a), cut.shape(cut.b), cut.shape(cut.ab)
        low = [(4, 2, 2) + block] if whole else []
        low += [(4, 2) + a, (4, 2) + b, (4,) + a, (4,) + b, (3,) + ab]
        if cut.f:
            f = cut.shape(cut.f)
            low += [(3, 2, 2) + f, (2,) + f, f]
        half = (cut.rows // 2, cut.columns)
        return [pltpu.VMEM(shape, BF) for shape in low] + [pltpu.VMEM((2,) + half, F32), pltpu.VMEM(half, F32)]

    def __init__(self, links, grad, prefix, other, cut, work, put):
        k = links
        self.k, self.grad, self.prefix, self.cut, self.put = k, grad, prefix, cut, put
        self.whole = other is not None
        mine = self.mine = grad.at[prefix]
        if self.whole:
            self.r0 = next(work)
            self.c0 = [k.remote(grad.at[other], self.r0, k.pc)]
        else:
            self.c0 = []
        self.r1a, self.r1b, self.r2a, self.r2b, self.r3 = [next(work) for _ in range(5)]
        z, x, y, x2, y2 = k.z, k.x, k.y, k.x2, k.y2
        a, b, ab, f = cut.a, cut.b, cut.ab, cut.f
        self.c1 = [k.remote(mine.at[(ALL, ALL, y2) + a], self.r1a, k.py), k.remote(mine.at[(ALL, x2, ALL) + b], self.r1b, k.px)]
        self.c2 = [k.remote(mine.at[(ALL, x2, y) + a], self.r2a, k.px), k.remote(mine.at[(ALL, x, y2) + b], self.r2b, k.py)]
        self.c3 = [k.remote(mine.at[(k.zs[d], x, y) + ab], self.r3.at[d], k.pz[d]) for d in range(3)]
        if f:
            self.rf1, self.rf2, self.rf3 = [next(work) for _ in range(3)]
            self.c1 += [k.remote(mine.at[(k.zs[d], ALL, ALL) + f], self.rf1.at[d], k.pz[d]) for d in range(3)]
            self.c2.append(k.remote(mine.at[(z, x2, ALL) + f], self.rf2, k.px))
            self.c3.append(k.remote(mine.at[(z, x, y2) + f], self.rf3, k.py))
        self.tot, self.fin = next(work), next(work)
        self.c4 = [k.remote(self.tot.at[k.c2], self.fin, k.pc)]

    def at(self, place):
        return self.prefix + place

    def s0(self):
        start(self.c0)

    def s1(self):
        if self.whole:
            arrive(self.c0)

            def add(i, carry):
                where = (i // 4, lax.rem(i // 2, 2), lax.rem(i, 2))
                add_into(self.grad, self.at(where), self.r0[where])
                return carry

            lax.fori_loop(0, 16, add, 0)
        start(self.c1)

    def s2(self):
        arrive(self.c1)
        k, cut = self.k, self.cut

        def add(i, carry):
            zz, other = i // 2, lax.rem(i, 2)
            add_into(self.grad, self.at((zz, other, k.y) + cut.a), self.r1a[zz, other])
            add_into(self.grad, self.at((zz, k.x, other) + cut.b), self.r1b[zz, other])
            return carry

        lax.fori_loop(0, 8, add, 0)
        if cut.f:
            def add_f(i, carry):
                xx, yy = i // 2, lax.rem(i, 2)
                three = self.rf1[0, xx, yy].astype(F32) + self.rf1[1, xx, yy].astype(F32) + self.rf1[2, xx, yy].astype(F32)
                add_into(self.grad, self.at((k.z, xx, yy) + cut.f), three)
                return carry

            lax.fori_loop(0, 4, add_f, 0)
        start(self.c2)

    def s3(self):
        arrive(self.c2)
        k, cut = self.k, self.cut

        def add(zz, carry):
            add_into(self.grad, self.at((zz, k.x, k.y) + cut.a), self.r2a[zz])
            add_into(self.grad, self.at((zz, k.x, k.y) + cut.b), self.r2b[zz])
            return carry

        lax.fori_loop(0, 4, add, 0)
        if cut.f:
            for yy in range(2):
                add_into(self.grad, self.at((k.z, k.x, yy) + cut.f), self.rf2[yy])
        start(self.c3)

    def s4(self):
        arrive(self.c3)
        k, cut = self.k, self.cut
        total = self.mine[(k.z, k.x, k.y) + cut.ab].astype(F32)
        for d in range(3):
            total = total + self.r3[d].astype(F32)
        if cut.f:
            rest = self.mine[(k.z, k.x, k.y) + cut.f].astype(F32) + self.rf3[...].astype(F32)
            total = jnp.concatenate([total, rest], axis=cut.axis)
        rows = total.shape[0] // 2
        self.tot[0] = total[:rows]
        self.tot[1] = total[rows:]
        start(self.c4)
        self.put(self.tot[k.c], k.c)

    def s5(self):
        arrive(self.c4)
        self.put(self.fin[...], self.k.c2)


def sign_of(value):
    return jnp.clip(value * 1e38, -1.0, 1.0)


def masked(size, seen, low):
    last = jnp.where(seen, size[low:], NEG)
    return last if low == 0 else jnp.concatenate([size[:low], last], axis=0)


def gelu_parts(value):
    rate = 0.7978845608028654
    bent = jnp.tanh(rate * (value + 0.044715 * (value * value * value)))
    result = 0.5 * value * (1.0 + bent)
    slope = 0.5 * (1.0 + bent) + 0.5 * value * (1.0 - bent * bent) * (rate * (1.0 + 0.134145 * (value * value)))
    return result, slope


def unit_rows(rows):
    centre = rows - jnp.mean(rows, axis=-1, keepdims=True)
    scale = lax.rsqrt(jnp.mean(centre * centre, axis=-1, keepdims=True) + EPS)
    return centre * scale, scale


def norm_back(grad, normed, scale):
    return scale * (grad - jnp.mean(grad, axis=-1, keepdims=True)
                    - normed * jnp.mean(grad * normed, axis=-1, keepdims=True))


def layer_kernel(
    prefix, tok, cot, v0_s, v1_s, v2_s, v3_s, v4_s, v5_s, v6_s, v7_s, wq_s, wo_s, wu_s, wd_s,
    out_bo, out_gt, out_q, out_o, out_u, out_d, out_vec,
    wq, wo, wu, wd, gv, k_qst, k_k, k_v, k_att, k_n1t,
    vec_s, wq_p, gvm, tok_all, vrows, wom, al_send, al, cotm, ga_send, ga_all, fa, fb, fc, fr, lt,
    gd, gu, go, gq,
    vs, vbq, vup, vtab, vr0, vr1, vr2, vr3,
    ssem, rsem, lsem, *work,
):
    k = Links(ssem, rsem, lsem)
    bo, gtb = al, cotm
    work = iter(work)
    z, x, y, c, x2, y2, c2 = k.z, k.x, k.y, k.c, k.x2, k.y2, k.c2
    k.greet()
    vmem = pltpu.VMEM

    vec_s[...] = jnp.zeros_like(vec_s)
    for index, (wide, ref) in enumerate(zip(WIDTHS, (v0_s, v1_s, v2_s, v3_s, v4_s, v5_s, v6_s, v7_s))):
        vec_s[index : index + 1, 0:wide] = ref[...].astype(F32).reshape(1, wide)
    for core in range(2):
        for u in range(3):
            for kind in range(3):
                first = kind * D + core * THIRD + u * 128
                wq_p[core, u, :, kind * 128 : (kind + 1) * 128] = wq_s[:, first : first + 128]
    gather_q = [Gather(k, wq_p.at[c, u], wq_p.at[c2, u], wq.at[u], wq.at[u], CUTS[f"q{u}"], False)
                for u in range(3)]

    def halves(shard, full, cut):
        half = full.shape[-1]
        return Gather(k, shard.at[:, lanes(c * half, half)], shard.at[:, lanes(c2 * half, half)], full.at[c], full.at[c2], cut)

    gather_o = halves(wo_s, wo, CUTS["out"])
    gather_d = halves(wd_s, wd, CUTS["down"])
    k.sent.pop()
    gather_d.c4 = [k.remote(wd.at[c, zz], wd.at[c, zz], k.pc) for zz in (2 * c, 2 * c + 1, 2 * c2, 2 * c2 + 1)]
    gather_u = [Gather(k, wu_s.at[:, lanes(c * 1536 + part * D, D)], wu_s.at[:, lanes(c2 * 1536 + part * D, D)],
                       wu.at[c, part], wu.at[c2, part], CUTS[f"up{part}"]) for part in range(2)]
    own_vec = k.local(vec_s, gv.at[z, x, y, c])
    own_tok = k.local(tok.at[y], tok_all.at[y, c])
    own_cot = k.local(cot.at[y], cotm.at[y])
    own_vec.start()
    start(gather_q[0].own)
    own_tok.start()
    others = [gather_q[1], gather_q[2], gather_o] + gather_u + [gather_d]
    for gather in others:
        start(gather.own)
    own_cot.start()
    k.greeted()

    vec_c = k.remote(vec_s, gv.at[z, x, y, c], k.pc)
    tok_y = k.remote(tok.at[y2], tok_all.at[y, c], k.py)
    cot_y = k.remote(cot.at[y2], cotm.at[y], k.py)
    vec_c.start()
    gather_q[0].s0()
    tok_y.start()
    for gather in others:
        gather.s0()
    own_vec.wait()
    vec_c.wait_recv()
    vec_z = [k.remote(gv.at[z, x, y], gv.at[z, x, y], dev) for dev in k.pz]
    start(vec_z)
    gather_q[0].s1()
    gather_q[1].s1()
    own_tok.wait()
    arrive(vec_z)
    vec_x = k.remote(gv.at[:, x, y], gv.at[:, x, y], k.px)
    vec_x.start()
    gather_q[0].s2()
    gather_q[2].s1()
    vec_x.wait_recv()
    vec_y = k.remote(gv.at[:, :, y], gv.at[:, :, y], k.py)
    vec_y.start()
    gather_q[1].s2()
    gather_o.s1()
    gather_q[0].s3()
    tok_y.wait_recv()
    tok_c = k.remote(tok_all.at[:, c], tok_all.at[:, c], k.pc)
    tok_c.start()
    gather_q[2].s2()
    gather_u[0].s1()
    vec_y.wait_recv()
    table = k.local(gv, gvm)
    table.start()
    table.wait()
    table = gvm[...].reshape(256, 128).astype(BF)
    for index, wide in enumerate(WIDTHS):
        vrows[index : index + 1, 0 : 32 * wide] = spread_row(table, index, wide)
    gather_q[1].s3()
    tok_c.wait_recv()

    mine_cols = lanes(c * THIRD, THIRD)
    peer_cols = lanes(c2 * THIRD, THIRD)
    al_own = k.local(al_send.at[:, c], al.at[:, :, mine_cols])
    al_c = k.remote(al_send.at[:, c2], al.at[:, :, mine_cols], k.pc)
    gathered = len(k.sent)
    limit = prefix[y] - 1
    sub = lax.broadcasted_iota(jnp.int32, (128, 256), 0)
    wq3 = wq.reshape(3, D, THIRD)

    def forward(n1, n1t, vt, qst, keys_ref, values_ref, att, wqm):
        gain = vrows[0:1, 0:D]
        shift = vrows[1:2, 0:D]

        def norm_block(b, carry):
            normed, _ = unit_rows(tok_all[b // 2, lax.rem(b, 2)].astype(F32))
            normed = (normed * gain + shift).astype(BF)
            at = rows_at(b * 256, 256)
            n1[at, :] = normed
            n1t[:, at] = normed.astype(F32).T.astype(BF)
            return carry

        lax.fori_loop(0, 4, norm_block, 0)
        keep = [k.local(n1t, k_n1t), k.local(qst, k_qst), k.local(keys_ref, k_k),
                k.local(values_ref, k_v), k.local(att, k_att)]
        keep[0].start()
        load_q = [k.local(wq3.at[u], wqm.at[u]) for u in range(3)]
        load_o = k.local(wo.reshape(2, D, THIRD), wom)

        def head(u):
            gather_q[u].s4()
            load_q[u].start()
            load_q[u].wait()

        slots = {
            (0, 3): [gather_q[2].s3, gather_o.s2, gather_u[1].s1], (0, 2): [gather_u[0].s2],
            (0, 1): [gather_o.s3, gather_d.s1], (0, 0): [gather_u[1].s2],
            (1, 3): [gather_u[0].s3], (1, 2): [gather_o.s4], (1, 1): [gather_d.s2], (1, 0): [gather_u[1].s3],
            (2, 3): [gather_o.done, load_o.start, gather_u[0].s4], (2, 2): [cot_y.start], (2, 1): [gather_d.s3], (2, 0): [],
        }

        def unit(u, carry):
            cols = lanes(u * 128)
            for which in range(3):
                @pl.when(u == which)
                def _():
                    head(which)

            def project(b, inner):
                rows = rows_at(b * 512, 512)
                value = jnp.dot(n1[rows, :], wqm[u], preferred_element_type=F32)
                parts = []
                for kind in range(3):
                    bias = vrows[2:3, lanes(kind * D + c * THIRD + u * 128)]
                    parts.append((value[:, kind * 128 : (kind + 1) * 128] + bias).astype(BF))
                queries = parts[0].astype(F32) * 0.125
                qst[cols, rows] = queries.T.astype(BF)
                keys_ref[rows, cols] = parts[1]
                values_ref[rows, cols] = parts[2]
                vt[cols, rows] = parts[2].astype(F32).T.astype(BF)
                return inner

            lax.fori_loop(0, 2, project, 0)
            for block in (3, 2, 1, 0):
                attend(u, block)
                for which in range(3):
                    if slots[which, block]:
                        @pl.when(u == which)
                        def _():
                            for step in slots[which, block]:
                                step()
            return carry

        def attend(u, block):
            rows = min(4, max(block + 1, 2)) * 256
            qcols = slice(block * 256, (block + 1) * 256)
            cols = lanes(u * 128)
            keys = keys_ref[0:rows, cols]
            queries = qst[cols, qcols]
            qpos = block * 256 + lax.broadcasted_iota(jnp.int32, (1, 256), 1)
            low = block * 256
            seen = low + lax.broadcasted_iota(jnp.int32, (rows - low, 256), 0) <= jnp.maximum(qpos, limit)
            for half in range(2):
                chosen = jnp.where(sub // 64 == half, queries, jnp.zeros_like(queries))
                scores = jnp.dot(keys, chosen, preferred_element_type=F32)
                size = jnp.abs(scores)
                size = masked(size, seen, low)
                top = jnp.max(size, axis=0, keepdims=True)
                exponent = jnp.exp(size - top)
                total = jnp.sum(exponent, axis=0, keepdims=True)
                weights = (sign_of(scores) * exponent).astype(BF)
                at = pl.ds(pl.multiple_of(u * 128 + half * 64, 64), 64)
                att[at, qcols] = jnp.dot(vt[at, 0:rows], weights, preferred_element_type=F32) / total
                lt[pl.ds(u * 2 + half, 1), qcols] = top + jnp.log(total)
            al_send[block // 2, block % 2, :, cols] = att[cols, qcols].T.astype(BF)

        lax.fori_loop(0, 3, unit, 0)
        al_own.start()
        al_c.start()
        start(keep[1:])
        load_o.wait()
        al_own.wait()
        al_c.wait_recv()
        landed(keep)

    pl.run_scoped(
        forward, vmem((1024, D), BF), vmem((D, 1024), BF), vmem((THIRD, 1024), BF),
        vmem((THIRD, 1024), BF), vmem((1024, THIRD), BF), vmem((1024, THIRD), BF), vmem((THIRD, 1024), F32),
        vmem((3, D, THIRD), BF))

    def put_to(out, half):
        def put(value, core):
            out[:, lanes(core * half, half)] = value
        return put

    down = Scatter(k, gd, (c,), (c2,), CUTS["down"], work, put_to(out_d, THIRD))

    def put_up(part):
        def put(value, core):
            out_u[:, lanes(core * 1536 + part * D, D)] = value
        return put

    up = [Scatter(k, gu, (c, part), (c2, part), CUTS[f"up{part}"], work, put_up(part)) for part in range(2)]
    outp = Scatter(k, go, (c,), (c2,), CUTS["out"], work, put_to(out_o, THIRD))

    def feed(wbuf, wdb, hid, slope, n2, n2t, alt, gpc):
        b_out, gain, shift = vrows[3:4, 0:D], vrows[4:5, 0:D], vrows[5:6, 0:D]

        def begin(yy, carry):
            rows = rows_at(yy * 256, 256)
            branch = jnp.concatenate([jnp.dot(al[yy], wom[h], preferred_element_type=F32) for h in range(2)], axis=1)
            residual = tok_all[yy, c].astype(F32) + branch + b_out
            fa[yy] = residual
            normed, _ = unit_rows(residual)
            normed = (normed * gain + shift).astype(BF)
            n2[rows, :] = normed
            n2t[:, rows] = normed.astype(F32).T.astype(BF)
            alt[:, rows] = al[yy].astype(F32).T.astype(BF)
            return carry

        lax.fori_loop(0, 2, begin, 0)
        own_cot.wait()
        cot_y.wait_recv()

        wu2 = wu.reshape(2, 2, D, D)
        wd2 = wd.reshape(2, FF, THIRD)

        def chunk(j, first, second):
            h = first if j < 2 else second
            return h, j % 2

        def up_load(j, slot, order):
            h, part = chunk(j, *order)
            return k.local(wu2.at[h, part], wbuf.at[slot])

        def down_load(j, slot, order):
            h, part = chunk(j, *order)
            rows = rows_at(h * 1536 + part * D, D)
            return [k.local(wd2.at[side, rows, :], wdb.at[slot, :, side * THIRD : (side + 1) * THIRD]) for side in range(2)]

        forth = (c, c2)
        loads = [up_load(j, j % 2, forth) for j in range(4)]
        loads[0].start()
        gather_u[1].s4()
        for j in range(4):
            loads[j].wait()
            if j == 0:
                loads[1].start()
            if j == 1:
                gather_u[0].done()
                loads[2].start()
            if j == 2:
                gather_u[1].done()
                loads[3].start()
            h, part = chunk(j, *forth)

            cols = lanes(h * 1536 + part * D, D)
            value = jnp.dot(n2[...], wbuf[j % 2], preferred_element_type=F32) + vrows[6:7, cols]
            result, bend = gelu_parts(value)
            hid[:, cols] = result.astype(BF)
            slope[:, cols] = bend

        vs[7:8, :] = jnp.sum(cotm[0].astype(F32), axis=0, keepdims=True) + jnp.sum(
            cotm[1].astype(F32), axis=0, keepdims=True)

        def down_grad(i, carry):
            total = lax.dot_general(hid[:, lanes(i * THIRD, THIRD)], cotm[...].reshape(512, D), FIRST,
                                    preferred_element_type=F32)
            zz, xx = i // 2, lax.rem(i, 2)
            for yy in range(2):
                for h in range(2):
                    gd[h, zz, xx, yy] = total[yy * 192 : (yy + 1) * 192, h * THIRD : (h + 1) * THIRD].astype(BF)
            return carry

        lax.fori_loop(0, 8, down_grad, 0)
        down.s0()
        fb[...] = jnp.zeros_like(fb)
        fc[...] = jnp.zeros_like(fc)
        gather_d.s4()
        back = (c2, c)
        again = [up_load(j, j % 2, back) for j in range(4)]
        lower = [down_load(j, j % 2, back) for j in range(4)]
        again[0].start()
        down.s1()
        gather_d.c4[0].wait_recv()
        start(lower[0])
        for j in range(4):
            slot = j % 2
            if j < 3:
                again[j + 1].start()
                gather_d.c4[j + 1].wait_recv()
                start(lower[j + 1])
            again[j].wait()
            landed(lower[j])
            h, part = chunk(j, *back)
            cols = lanes(h * 1536 + part * D, D)
            fc[...] += jnp.dot(hid[:, cols], wdb[slot], preferred_element_type=F32).reshape(2, 256, D)
            grad = lax.dot_general(cotm[...].reshape(512, D), wdb[slot], LAST, preferred_element_type=F32)
            grad = (grad * slope[:, cols]).astype(BF)
            gpc[...] = grad
            vup[0:1, cols] = jnp.sum(grad.astype(F32), axis=0, keepdims=True)
            fb[...] += lax.dot_general(gpc[...], wbuf[slot], LAST, preferred_element_type=F32).reshape(2, 256, D)

            def up_grad(zz, carry):
                total = jnp.dot(n2t[rows_at(zz * THIRD, THIRD, 128), :], gpc[...], preferred_element_type=F32)
                for i in range(8):
                    gu[h, part, zz * 2 + i // 4, i // 2 % 2, i % 2] = total[i * 48 : (i + 1) * 48].astype(BF)
                return carry

            lax.fori_loop(0, 2, up_grad, 0)
            if j < 2:
                up[j].s0()
            if j == 2:
                up[0].s1()
                down.s2()
        bo[...] = (fa[...] + fc[...] + vrows[7:8, 0:D].reshape(1, 1, D)).astype(BF)
        up[1].s1()

    ga_c = k.remote(ga_send.at[:, :, peer_cols], ga_all.at[:, c], k.pc)
    def turn(alt, gpc):
        gain = vrows[4:5, 0:D]
        vs[3:6, :] = jnp.zeros((3, D), F32)

        def mid_back(yy, carry):
            rows = rows_at(yy * 256, 256)
            normed, scale = unit_rows(fa[yy])
            grad = fb[yy]
            vs[4:5, :] += jnp.sum(grad * normed, axis=0, keepdims=True)
            vs[5:6, :] += jnp.sum(grad, axis=0, keepdims=True)
            total = cotm[yy].astype(F32) + norm_back(grad * gain, normed, scale)
            fa[yy] = total
            low = total.astype(BF)
            vs[3:4, :] += jnp.sum(low.astype(F32), axis=0, keepdims=True)
            gpc[rows, :] = low
            heads = None
            for side in range(2):
                term = lax.dot_general(low[:, side * THIRD : (side + 1) * THIRD], wom[side], LAST,
                                       preferred_element_type=F32)
                heads = term if heads is None else heads + term
            ga_send[yy] = heads.astype(BF)
            ga_all[yy, c] = ga_send[yy, :, mine_cols]
            return carry

        lax.fori_loop(0, 2, mid_back, 0)
        ga_c.start()

        def out_grad(zz, carry):
            total = jnp.dot(alt[rows_at(zz * THIRD, THIRD, 128), :], gpc[...], preferred_element_type=F32)
            for i in range(8):
                for h in range(2):
                    go[h, zz * 2 + i // 4, i // 2 % 2, i % 2] = total[i * 48 : (i + 1) * 48, h * THIRD : (h + 1) * THIRD].astype(BF)
            return carry

        lax.fori_loop(0, 2, out_grad, 0)
        outp.s0()

    def put_q(u):
        def put(value, core):
            for kind in range(3):
                out_q[:, lanes(kind * D + core * THIRD + u * 128)] = value[:, kind * 128 : (kind + 1) * 128]
        return put

    queue = [Scatter(k, gq, (u,), None, CUTS[f"q{u}"], work, put_q(u)) for u in range(3)]
    bo_own = k.local(bo.at[y], out_bo.at[y])
    bo_y = k.remote(bo.at[y2], out_bo.at[y], k.py)

    def collect(index):
        row = vbq[...] if index == 2 else vup[...] if index == 6 else vs[index : index + 1, :]
        vtab[pl.ds(index, 32, stride=8), :] = collect_rows(row, WIDTHS[index])

    def early():
        for index in (3, 4, 5, 6, 7):
            collect(index)

    def send_out():
        bo_own.start()
        bo_y.start()

    def backward(alt, gpc, qst, keys_ref, values_ref, att, n1t, gt, kt, dk, dv, gpu, wqm, gp):
        loads = [k.local(k_qst, qst), k.local(k_k, keys_ref), k.local(k_v, values_ref),
                 k.local(k_att, att), k.local(k_n1t, n1t), ]
        loads += [k.local(wq3.at[u], wqm.at[:, u * THIRD : (u + 1) * THIRD]) for u in range(3)]
        start(loads)
        turn(alt, gpc)
        ga_c.wait_recv()
        landed(loads)
        vbq[...] = jnp.zeros_like(vbq)
        slots = {
            (0, 3): [outp.s1], (0, 2): [], (0, 1): [down.s3], (0, 0): [up[0].s2, send_out],
            (1, 3): [], (1, 2): [up[1].s2], (1, 1): [outp.s2], (1, 0): [down.s4, up[0].s3, early],
            (2, 3): [up[1].s3], (2, 2): [queue[0].s2, down.s5], (2, 1): [outp.s3], (2, 0): [queue[0].s3, up[0].s4],
        }

        def unit(u, carry):
            cols = lanes(u * 128)
            for b in range(4):
                rows = slice(b * 256, (b + 1) * 256)
                gt[:, rows] = ga_all[b // 2, b % 2, :, cols].astype(F32).T.astype(BF)
                kt[:, rows] = keys_ref[rows, cols].astype(F32).T.astype(BF)
            dk[...] = jnp.zeros_like(dk)
            dv[...] = jnp.zeros_like(dv)
            for block in (3, 2, 1, 0):
                rows = min(4, max(block + 1, 2)) * 256
                qrange = slice(block * 256, (block + 1) * 256)
                keys = keys_ref[0:rows, cols]
                values = values_ref[0:rows, cols]
                queries_t = qst[cols, qrange]
                grads_t = gt[:, qrange]
                qpos = block * 256 + lax.broadcasted_iota(jnp.int32, (1, 256), 1)
                low = block * 256
                seen = low + lax.broadcasted_iota(jnp.int32, (rows - low, 256), 0) <= jnp.maximum(qpos, limit)
                prod = grads_t.astype(F32) * att[cols, qrange]
                dqs = []
                for half in range(2):
                    part = slice(half * 64, half * 64 + 64)
                    in_sub = sub // 64 == half
                    delta = jnp.sum(prod[part], axis=0, keepdims=True)
                    total = lt[pl.ds(u * 2 + half, 1), qrange]
                    zero = jnp.zeros((), BF)
                    scores = jnp.dot(keys, jnp.where(in_sub, queries_t, zero), preferred_element_type=F32)
                    pull = jnp.dot(values, jnp.where(in_sub, grads_t, zero), preferred_element_type=F32)
                    share = jnp.exp(masked(jnp.abs(scores) - total, seen, low))
                    signed = sign_of(scores) * share
                    grad_scores = (share * pull - signed * delta).astype(BF)
                    signed = signed.astype(BF)
                    dv[part, 0:rows] += lax.dot_general(grads_t[part], signed, LAST, preferred_element_type=F32)
                    dk[part, 0:rows] += lax.dot_general(queries_t[part], grad_scores, LAST, preferred_element_type=F32)
                    dqs.append(jnp.dot(kt[part, 0:rows], grad_scores, preferred_element_type=F32))
                gpu[qrange, 0:128] = (jnp.concatenate(dqs, axis=0).T * 0.125).astype(BF)
                for which in range(3):
                    if slots[which, block]:
                        @pl.when(u == which)
                        def _():
                            for step in slots[which, block]:
                                step()
            for b in range(4):
                rows = slice(b * 256, (b + 1) * 256)
                gpu[rows, 128:256] = dk[:, rows].T.astype(BF)
                gpu[rows, 256:384] = dv[:, rows].T.astype(BF)
            sums = jnp.sum(gpu[...].astype(F32), axis=0, keepdims=True)
            for kind in range(3):
                part = slice(kind * 128, (kind + 1) * 128)
                vbq[0:1, lanes(kind * D + c * THIRD + u * 128)] = sums[:, part]
                gp[:, lanes(u * THIRD + kind * 128)] = gpu[:, part]

            def weights(zz, inner):
                block = jnp.dot(n1t[rows_at(zz * THIRD, THIRD, 128), :], gpu[...], preferred_element_type=F32)
                for i in range(8):
                    gq[u, zz * 2 + i // 4, i // 2 % 2, i % 2] = block[i * 48 : (i + 1) * 48].astype(BF)
                return inner

            lax.fori_loop(0, 2, weights, 0)
            for which in range(3):
                @pl.when(u == which)
                def _():
                    queue[which].s1()
            return carry

        lax.fori_loop(0, 3, unit, 0)

        def back_rows(b):
            return lax.dot_general(gp[rows_at(b * 256, 256), :], wqm[...], LAST, preferred_element_type=F32)

        def back_peer(yy, carry):
            fb[yy] = back_rows(yy * 2 + c2)
            return carry

        def back_own(yy, carry):
            fc[yy] = back_rows(yy * 2 + c)
            return carry

        lax.fori_loop(0, 2, back_peer, 0)
        part_c.start()
        queue[1].s2()
        lax.fori_loop(0, 2, back_own, 0)
        queue[2].s2()

    part_c = k.remote(fb, fr, k.pc)

    def both(alt, gpc):
        pl.run_scoped(
            functools.partial(feed, alt=alt, gpc=gpc), vmem((2, D, D), BF), vmem((2, D, D), BF),
            vmem((512, FF), BF), vmem((512, FF), F32), vmem((512, D), BF), vmem((D, 512), BF))
        pl.run_scoped(
            functools.partial(backward, alt, gpc), vmem((THIRD, 1024), BF), vmem((1024, THIRD), BF),
            vmem((1024, THIRD), BF), vmem((THIRD, 1024), F32), vmem((D, 1024), BF), vmem((128, 1024), BF),
            vmem((128, 1024), BF), vmem((128, 1024), F32), vmem((128, 1024), F32), vmem((1024, THIRD), BF),
            vmem((D, 3 * THIRD), BF), vmem((1024, 3 * THIRD), BF))

    pl.run_scoped(both, vmem((D, 512), BF), vmem((512, D), BF))

    gain = vrows[0:1, 0:D]
    vs[0:2, :] = jnp.zeros((2, D), F32)
    part_c.wait_recv()

    def last_back(yy):
        normed, scale = unit_rows(tok_all[yy, c].astype(F32))
        grad = fc[yy] + fr[yy]
        vs[0:1, :] += jnp.sum(grad * normed, axis=0, keepdims=True)
        vs[1:2, :] += jnp.sum(grad, axis=0, keepdims=True)
        gtb[yy] = (fa[yy] + norm_back(grad * gain, normed, scale)).astype(BF)

    gt_own = k.local(gtb.at[y], out_gt.at[y])
    gt_y = k.remote(gtb.at[y2], out_gt.at[y], k.py)
    last_back(y2)
    gt_y.start()
    queue[1].s3()
    last_back(y)
    gt_own.start()
    queue[2].s3()
    for index in range(3):
        collect(index)
    table = vtab.reshape(4, 2, 2, 2, 8, 128)
    v0 = k.remote(table.at[:, :, :, c2], vr0, k.pc)
    v1 = k.remote(table.at[:, :, y2, c], vr1, k.py)
    v2 = k.remote(table.at[:, x2, y, c], vr2, k.px)
    v3 = [k.remote(table.at[k.zs[d], x, y, c], vr3.at[d], k.pz[d]) for d in range(3)]

    def tile(zz, xx, yy):
        return rows_at((((zz * 2 + xx) * 2 + yy) * 2 + c) * 8, 8, 8)

    v0.start()
    queue[0].s4()
    v0.wait_recv()

    def add_core(i, carry):
        zz, xx, yy = i // 4, lax.rem(i // 2, 2), lax.rem(i, 2)
        vtab[tile(zz, xx, yy), :] += vr0[zz, xx, yy]
        return carry

    lax.fori_loop(0, 16, add_core, 0)
    v1.start()
    for copy in k.sent[:gathered]:
        copy.wait_send()
    up[1].s4()
    queue[1].s4()
    v1.wait_recv()

    def add_y(i, carry):
        vtab[tile(i // 2, lax.rem(i, 2), y), :] += vr1[i // 2, lax.rem(i, 2)]
        return carry

    lax.fori_loop(0, 8, add_y, 0)
    v2.start()
    outp.s4()
    up[0].s5()
    queue[0].s5()
    v2.wait_recv()

    def add_x(zz, carry):
        vtab[tile(zz, x, y), :] += vr2[zz]
        return carry

    lax.fori_loop(0, 4, add_x, 0)
    start(v3)
    queue[2].s4()
    up[1].s5()
    outp.s5()
    queue[1].s5()
    queue[2].s5()
    arrive(v3)
    out_vec[...] = vtab[tile(z, x, y), :] + vr3[0] + vr3[1] + vr3[2]
    landed([gt_own, bo_own])
    arrive([gt_y, bo_y])
    for copy in k.sent[gathered:]:
        copy.wait_send()
    assert k.remotes <= REMOTES and k.locals <= LOCALS


def layer_call(*operands):
    sds = jax.ShapeDtypeStruct
    vmem = pltpu.VMEM
    dma = pltpu.SemaphoreType.DMA
    results = (
        sds((2, 256, D), BF), sds((2, 256, D), BF), sds((24, 3 * D), F32), sds((24, D), F32), sds((24, FF), F32),
        sds((96, D), F32), sds((8, 128), F32),
    )
    held = (
        sds((3, 4, 2, 2, 48, 384), BF), sds((2, 4, 2, 2, 48, 384), BF), sds((2, 2, 4, 2, 2, 48, 768), BF),
        sds((2, 4, 2, 2, 192, 384), BF), sds((4, 2, 2, 2, 8, 128), F32), sds((THIRD, 1024), BF),
        sds((1024, THIRD), BF), sds((1024, THIRD), BF), sds((THIRD, 1024), F32), sds((D, 1024), BF),
    )
    scratch = [
        vmem((8, 128), F32), vmem((2, 3, 24, THIRD), BF), vmem((4, 2, 2, 2, 8, 128), F32), vmem((2, 2, 256, D), BF), vmem((8, FF), F32),
        vmem((2, D, THIRD), BF), vmem((2, 2, 256, THIRD), BF), vmem((2, 256, D), BF), vmem((2, 256, D), BF),
        vmem((2, 256, D), BF), vmem((2, 2, 256, THIRD), BF), vmem((2, 256, D), F32), vmem((2, 256, D), F32),
        vmem((2, 256, D), F32), vmem((2, 256, D), F32), vmem((8, 1024), F32),
    ]
    scratch += [
        vmem((2, 4, 2, 2, 192, 384), BF), vmem((2, 2, 4, 2, 2, 48, 768), BF), vmem((2, 4, 2, 2, 48, 384), BF),
        vmem((3, 4, 2, 2, 48, 384), BF),
        vmem((8, D), F32), vmem((1, 3 * D), F32), vmem((1, FF), F32), vmem((256, 128), F32), vmem((4, 2, 2, 8, 128), F32),
        vmem((4, 2, 8, 128), F32), vmem((4, 8, 128), F32), vmem((3, 8, 128), F32),
        dma((REMOTES,)), dma((REMOTES,)), dma((LOCALS,)),
    ]
    for name in ("down", "up0", "up1", "out", "q0", "q1", "q2"):
        scratch += Scatter.buffers(CUTS[name], not name.startswith("q"))
    return pl.pallas_call(
        layer_kernel,
        out_shape=results + held,
        in_specs=[SM] + [ANY] * 2 + [VM] * 12,
        out_specs=(ANY, ANY) + (VM,) * 5 + (ANY,) * len(held),
        scratch_shapes=scratch,
        compiler_params=pltpu.CompilerParams(
            collective_id=0, has_side_effects=True, vmem_limit_bytes=63 * 2**20),
    )(*operands)[: len(results)]


def finish_kernel(*refs):
    sources, results, (table, sems) = refs[:7], refs[7:21], refs[21:]
    copies = [pltpu.make_async_copy(source, result, sems.at[i])
              for i, (source, result) in enumerate(zip(sources, results[:6] + (table,)))]
    start(copies)
    landed(copies)
    for index, wide in enumerate(WIDTHS):
        results[6 + index][...] = table[index, 0:wide]


def finish_call(*operands):
    sds = jax.ShapeDtypeStruct
    shapes = tuple(sds(o.shape, o.dtype) for o in operands[:6]) + tuple(sds((wide,), F32) for wide in WIDTHS)
    return pl.pallas_call(
        finish_kernel, out_shape=shapes, in_specs=[ANY] * 7, out_specs=(VM,) * 14,
        scratch_shapes=[pltpu.VMEM((8, 128), F32), pltpu.SemaphoreType.DMA((7,))],
        compiler_params=pltpu.CompilerParams(vmem_limit_bytes=60 * 2**20),
    )(*operands)


def body(
    tokens, cotangent, prefix, ln1_gain, ln1_bias, w_qkv, b_qkv, w_out, b_out,
    ln2_gain, ln2_bias, w_up, b_up, w_down, b_down,
):
    results = layer_call(
        prefix, tokens, cotangent, ln1_gain, ln1_bias, b_qkv, b_out, ln2_gain, ln2_bias, b_up, b_down,
        w_qkv, w_out, w_up, w_down)
    block_out, grad_tokens, gq, go, gu, gd, *rows = finish_call(*results)
    return (
        block_out, grad_tokens, rows[0], rows[1], gq, rows[2], go, rows[3], rows[4], rows[5], gu, rows[6], gd, rows[7],
    )


def fits(mesh):
    return dict(mesh.shape) == {"dp": 8, "seq": 4}


norm_eps = 1e-05
block_rows = 512


def layer_norm(features, gain, shift):
    centre = features - jnp.mean(features, axis=-1, keepdims=True)
    spread = jnp.mean(centre * centre, axis=-1, keepdims=True)
    return centre * lax.rsqrt(spread + norm_eps) * gain + shift


def gelu_tanh(values):
    return jax.nn.gelu(values, approximate=True)


def in_blocks(update, running, pieces):
    length = pieces[0].shape[1]
    blocks = length // block_rows
    blocked_pieces = tuple(
        (
            jnp.swapaxes(
                member.reshape((member.shape[0], blocks, block_rows) + member.shape[2:]), 0, 1
            )
            for member in pieces
        )
    )

    def advance(carried, element):
        return (update(carried, element[0], element[1] * block_rows), None)

    running, unused = lax.scan(
        advance, running, (blocked_pieces, jnp.arange(blocks, dtype=jnp.int32))
    )
    return running


def to_heads(flat_rows):
    return flat_rows.reshape(flat_rows.shape[0], flat_rows.shape[1], HEADS, HEAD_DIM)


def visible_mask(query_places, key_places, prefix_len):
    earlier = key_places[None, None, :] <= query_places[None, :, None]
    in_prefix = key_places[None, None, :] < prefix_len[:, None, None]
    return (earlier | in_prefix)[:, :, None, :]


def head_scores(query_heads, key_flat):
    return jnp.einsum(
        "bqhd,bkhd->bqhk", query_heads, to_heads(key_flat), preferred_element_type=jnp.float32
    ) * HEAD_DIM ** (-0.5)


def attend(query_heads, key_flat, value_flat, prefix_len):
    local_len = query_heads.shape[1]
    query_places = lax.axis_index("seq") * local_len + jnp.arange(local_len, dtype=jnp.int32)
    starting = (
        jnp.zeros(query_heads.shape, jnp.float32),
        jnp.zeros(query_heads.shape[:3], jnp.float32),
        jnp.zeros(query_heads.shape[:3], jnp.float32),
    )

    def update(running, pieces, offset):
        weighted, normaliser, ceiling = running
        key_piece, value_piece = pieces
        key_places = offset + jnp.arange(key_piece.shape[1], dtype=jnp.int32)
        scores = head_scores(query_heads, key_piece)
        visible = visible_mask(query_places, key_places, prefix_len)
        magnitude = jnp.where(visible, jnp.abs(scores), 0.0)
        new_ceiling = jnp.maximum(ceiling, jnp.max(magnitude, axis=-1))
        exponent = jnp.where(visible, jnp.exp(magnitude - new_ceiling[..., None]), 0.0)
        factor = jnp.exp(ceiling - new_ceiling)
        weights = (jnp.sign(scores) * exponent).astype(jnp.bfloat16)
        weighted = weighted * factor[..., None] + jnp.einsum(
            "bqhk,bkhd->bqhd", weights, to_heads(value_piece), preferred_element_type=jnp.float32
        )
        normaliser = normaliser * factor + jnp.sum(exponent, axis=-1)
        return (weighted, normaliser, new_ceiling)

    weighted, normaliser, ceiling = in_blocks(
        update,
        starting,
        (
            lax.all_gather(key_flat, "seq", axis=1, tiled=True),
            lax.all_gather(value_flat, "seq", axis=1, tiled=True),
        ),
    )
    return (weighted / normaliser[..., None], ceiling + jnp.log(normaliser))


def grad_terms(
    query_heads,
    grad_heads,
    key_flat,
    value_flat,
    log_total,
    delta_sum,
    query_places,
    key_places,
    prefix_len,
):
    scores = head_scores(query_heads, key_flat)
    sign_of = jnp.sign(scores)
    visible = visible_mask(query_places, key_places, prefix_len)
    shares = jnp.where(visible, jnp.exp(jnp.abs(scores) - log_total[..., None]), 0.0)
    grad_weights = jnp.einsum(
        "bqhd,bkhd->bqhk", grad_heads, to_heads(value_flat), preferred_element_type=jnp.float32
    )
    grad_scores = (shares * (grad_weights - sign_of * delta_sum[..., None])).astype(jnp.bfloat16)
    return ((sign_of * shares).astype(jnp.bfloat16), grad_scores)


def query_term(grad_scores, key_flat):
    return jnp.einsum(
        "bqhk,bkhd->bqhd", grad_scores, to_heads(key_flat), preferred_element_type=jnp.float32
    ) * HEAD_DIM ** (-0.5)


def key_value_terms(query_heads, grad_heads, shares_low, grad_scores):
    key_term = jnp.einsum(
        "bqhk,bqhd->bkhd", grad_scores, query_heads, preferred_element_type=jnp.float32
    ) * HEAD_DIM ** (-0.5)
    value_term = jnp.einsum(
        "bqhk,bqhd->bkhd", shares_low, grad_heads, preferred_element_type=jnp.float32
    )
    flat_shape = (key_term.shape[0], key_term.shape[1], key_term.shape[2] * key_term.shape[3])
    return jnp.concatenate([key_term.reshape(flat_shape), value_term.reshape(flat_shape)], axis=-1)


def attend_back(query_heads, key_flat, value_flat, grad_heads, log_total, delta_sum, prefix_len):
    seq_block, local_len = (query_heads.shape[0], query_heads.shape[1])
    width = key_flat.shape[2]
    local_places = lax.axis_index("seq") * local_len + jnp.arange(local_len, dtype=jnp.int32)
    starting = (
        jnp.zeros(query_heads.shape, jnp.float32),
        jnp.zeros((seq_block, lax.axis_size("seq") * local_len, 2 * width), jnp.float32),
    )

    def update_both(running, pieces, offset):
        grad_query, grad_keys = running
        key_piece, value_piece = pieces
        piece_len = key_piece.shape[1]
        key_places = offset + jnp.arange(piece_len, dtype=jnp.int32)
        shares_low, grad_scores = grad_terms(
            query_heads,
            grad_heads,
            key_piece,
            value_piece,
            log_total,
            delta_sum,
            local_places,
            key_places,
            prefix_len,
        )
        grad_query = grad_query + query_term(grad_scores, key_piece)
        current = lax.dynamic_slice_in_dim(grad_keys, offset, piece_len, 1)
        updated = current + key_value_terms(query_heads, grad_heads, shares_low, grad_scores)
        return (grad_query, lax.dynamic_update_slice_in_dim(grad_keys, updated, offset, 1))

    grad_query, grad_keys = in_blocks(
        update_both,
        starting,
        (
            lax.all_gather(key_flat, "seq", axis=1, tiled=True),
            lax.all_gather(value_flat, "seq", axis=1, tiled=True),
        ),
    )
    key_local = lax.psum_scatter(
        grad_keys.astype(jnp.bfloat16), "seq", scatter_dimension=1, tiled=True
    ).astype(jnp.float32)
    return (grad_query, key_local)


def forward_block(weights_in, token_part, prefix_len):
    (
        gain_one,
        shift_one,
        w_qkv,
        b_qkv,
        w_out,
        b_out,
        gain_two,
        shift_two,
        w_up,
        b_up,
        w_down,
        b_down,
    ) = weights_in
    seq_block, local_len, width = token_part.shape
    residual_in = token_part.reshape(-1, width).astype(jnp.float32)
    normed_one = layer_norm(
        residual_in, gain_one.astype(jnp.float32), shift_one.astype(jnp.float32)
    ).astype(jnp.bfloat16)
    projected = jnp.dot(normed_one, w_qkv, preferred_element_type=jnp.float32) + b_qkv.astype(
        jnp.float32
    )
    query_heads = (
        projected[:, :width].astype(jnp.bfloat16).reshape(seq_block, local_len, HEADS, HEAD_DIM)
    )
    key_flat = (
        projected[:, width : 2 * width].astype(jnp.bfloat16).reshape(seq_block, local_len, width)
    )
    value_flat = projected[:, 2 * width :].astype(jnp.bfloat16).reshape(seq_block, local_len, width)
    attended, log_total = attend(query_heads, key_flat, value_flat, prefix_len)
    attended_low = attended.reshape(-1, width).astype(jnp.bfloat16)
    residual_mid = (
        residual_in
        + jnp.dot(attended_low, w_out, preferred_element_type=jnp.float32)
        + b_out.astype(jnp.float32)
    )
    normed_two = layer_norm(
        residual_mid, gain_two.astype(jnp.float32), shift_two.astype(jnp.float32)
    ).astype(jnp.bfloat16)
    pre_gelu = jnp.dot(normed_two, w_up, preferred_element_type=jnp.float32) + b_up.astype(
        jnp.float32
    )
    hidden = gelu_tanh(pre_gelu).astype(jnp.bfloat16)
    result = (
        residual_mid
        + jnp.dot(hidden, w_down, preferred_element_type=jnp.float32)
        + b_down.astype(jnp.float32)
    )
    saved = (
        residual_in,
        normed_one,
        query_heads,
        key_flat,
        value_flat,
        attended,
        log_total,
        attended_low,
        residual_mid,
        normed_two,
        pre_gelu,
        hidden,
    )
    return (result.astype(jnp.bfloat16).reshape(token_part.shape), saved)


def backward_block(weights_in, saved, grad_part, prefix_len):
    (
        gain_one,
        shift_one,
        w_qkv,
        b_qkv,
        w_out,
        b_out,
        gain_two,
        shift_two,
        w_up,
        b_up,
        w_down,
        b_down,
    ) = weights_in
    (
        residual_in,
        normed_one,
        query_heads,
        key_flat,
        value_flat,
        attended,
        log_total,
        attended_low,
        residual_mid,
        normed_two,
        pre_gelu,
        hidden,
    ) = saved
    seq_block, local_len, width = grad_part.shape
    grad_result = grad_part.reshape(-1, width).astype(jnp.float32)
    grad_branch = grad_part.reshape(-1, width)
    grads_down = jnp.einsum("rf,rd->fd", hidden, grad_branch, preferred_element_type=jnp.float32)
    bias_down = jnp.sum(grad_branch, axis=0, dtype=jnp.float32)
    grad_hidden = jnp.einsum("rd,fd->rf", grad_branch, w_down, preferred_element_type=jnp.float32)
    gelu_pull = jax.vjp(gelu_tanh, pre_gelu)[1]
    grad_pre = gelu_pull(grad_hidden)[0].astype(jnp.bfloat16)
    grads_up = jnp.einsum("rd,rf->df", normed_two, grad_pre, preferred_element_type=jnp.float32)
    bias_up = jnp.sum(grad_pre, axis=0, dtype=jnp.float32)
    grad_normed_two = jnp.einsum("rf,df->rd", grad_pre, w_up, preferred_element_type=jnp.float32)
    norm_two_pull = jax.vjp(
        layer_norm, residual_mid, gain_two.astype(jnp.float32), shift_two.astype(jnp.float32)
    )[1]
    grad_mid, grads_gain_two, grads_shift_two = norm_two_pull(grad_normed_two)
    grad_mid = grad_mid + grad_result
    grad_attn = grad_mid.astype(jnp.bfloat16)
    grads_out = jnp.einsum("rd,re->de", attended_low, grad_attn, preferred_element_type=jnp.float32)
    bias_out = jnp.sum(grad_attn, axis=0, dtype=jnp.float32)
    grad_heads = (
        jnp.einsum("re,de->rd", grad_attn, w_out, preferred_element_type=jnp.float32)
        .astype(jnp.bfloat16)
        .reshape(seq_block, local_len, HEADS, HEAD_DIM)
    )
    delta_sum = jnp.sum(grad_heads.astype(jnp.float32) * attended, axis=-1)
    grad_query, key_local = attend_back(
        query_heads, key_flat, value_flat, grad_heads, log_total, delta_sum, prefix_len
    )
    grad_proj = jnp.concatenate(
        [grad_query.reshape(-1, width), key_local.reshape(-1, 2 * width)], axis=1
    ).astype(jnp.bfloat16)
    grads_qkv = jnp.einsum("rd,re->de", normed_one, grad_proj, preferred_element_type=jnp.float32)
    bias_qkv = jnp.sum(grad_proj, axis=0, dtype=jnp.float32)
    grad_normed_one = jnp.einsum("re,de->rd", grad_proj, w_qkv, preferred_element_type=jnp.float32)
    norm_one_pull = jax.vjp(
        layer_norm, residual_in, gain_one.astype(jnp.float32), shift_one.astype(jnp.float32)
    )[1]
    grad_in, grads_gain_one, grads_shift_one = norm_one_pull(grad_normed_one)
    grad_in = grad_in + grad_mid
    weight_grads = (
        grads_gain_one,
        grads_shift_one,
        grads_qkv,
        bias_qkv,
        grads_out,
        bias_out,
        grads_gain_two,
        grads_shift_two,
        grads_up,
        bias_up,
        grads_down,
        bias_down,
    )
    return (grad_in.astype(jnp.bfloat16).reshape(grad_part.shape), weight_grads)


def general_body(
    tokens,
    cotangent,
    prefix,
    ln1_gain,
    ln1_bias,
    w_qkv,
    b_qkv,
    w_out,
    b_out,
    ln2_gain,
    ln2_bias,
    w_up,
    b_up,
    w_down,
    b_down,
):
    shards = (
        ln1_gain,
        ln1_bias,
        w_qkv,
        b_qkv,
        w_out,
        b_out,
        ln2_gain,
        ln2_bias,
        w_up,
        b_up,
        w_down,
        b_down,
    )
    spread_count = lax.axis_size(("dp", "seq"))
    totals = tuple(
        (
            jnp.zeros((member.shape[0] * spread_count,) + member.shape[1:], jnp.float32)
            for member in shards
        )
    )
    seq_block = tokens.shape[0] // MB
    outputs = []
    grad_inputs = []
    for batch_index in range(MB):
        first_row = batch_index * seq_block
        token_part = tokens[first_row : first_row + seq_block]
        cotangent_part = cotangent[first_row : first_row + seq_block]
        prefix_part = prefix[first_row : first_row + seq_block]
        forward_weights = (
            lax.all_gather(shards[0], ("dp", "seq"), axis=0, tiled=True),
            lax.all_gather(shards[1], ("dp", "seq"), axis=0, tiled=True),
            lax.all_gather(shards[2], ("dp", "seq"), axis=0, tiled=True),
            lax.all_gather(shards[3], ("dp", "seq"), axis=0, tiled=True),
            lax.all_gather(shards[4], ("dp", "seq"), axis=0, tiled=True),
            lax.all_gather(shards[5], ("dp", "seq"), axis=0, tiled=True),
            lax.all_gather(shards[6], ("dp", "seq"), axis=0, tiled=True),
            lax.all_gather(shards[7], ("dp", "seq"), axis=0, tiled=True),
            lax.all_gather(shards[8], ("dp", "seq"), axis=0, tiled=True),
            lax.all_gather(shards[9], ("dp", "seq"), axis=0, tiled=True),
            lax.all_gather(shards[10], ("dp", "seq"), axis=0, tiled=True),
            lax.all_gather(shards[11], ("dp", "seq"), axis=0, tiled=True),
        )
        result, saved = forward_block(forward_weights, token_part, prefix_part)
        back_weights = (
            lax.all_gather(shards[0], ("dp", "seq"), axis=0, tiled=True),
            lax.all_gather(shards[1], ("dp", "seq"), axis=0, tiled=True),
            lax.all_gather(shards[2], ("dp", "seq"), axis=0, tiled=True),
            lax.all_gather(shards[3], ("dp", "seq"), axis=0, tiled=True),
            lax.all_gather(shards[4], ("dp", "seq"), axis=0, tiled=True),
            lax.all_gather(shards[5], ("dp", "seq"), axis=0, tiled=True),
            lax.all_gather(shards[6], ("dp", "seq"), axis=0, tiled=True),
            lax.all_gather(shards[7], ("dp", "seq"), axis=0, tiled=True),
            lax.all_gather(shards[8], ("dp", "seq"), axis=0, tiled=True),
            lax.all_gather(shards[9], ("dp", "seq"), axis=0, tiled=True),
            lax.all_gather(shards[10], ("dp", "seq"), axis=0, tiled=True),
            lax.all_gather(shards[11], ("dp", "seq"), axis=0, tiled=True),
        )
        grad_piece, weight_grads = backward_block(back_weights, saved, cotangent_part, prefix_part)
        totals = tuple(
            (running_sum + new_term for running_sum, new_term in zip(totals, weight_grads))
        )
        outputs.append(result)
        grad_inputs.append(grad_piece)
    reduced = (
        lax.psum_scatter(totals[0], ("dp", "seq"), scatter_dimension=0, tiled=True),
        lax.psum_scatter(totals[1], ("dp", "seq"), scatter_dimension=0, tiled=True),
        lax.psum_scatter(totals[2], ("dp", "seq"), scatter_dimension=0, tiled=True),
        lax.psum_scatter(totals[3], ("dp", "seq"), scatter_dimension=0, tiled=True),
        lax.psum_scatter(totals[4], ("dp", "seq"), scatter_dimension=0, tiled=True),
        lax.psum_scatter(totals[5], ("dp", "seq"), scatter_dimension=0, tiled=True),
        lax.psum_scatter(totals[6], ("dp", "seq"), scatter_dimension=0, tiled=True),
        lax.psum_scatter(totals[7], ("dp", "seq"), scatter_dimension=0, tiled=True),
        lax.psum_scatter(totals[8], ("dp", "seq"), scatter_dimension=0, tiled=True),
        lax.psum_scatter(totals[9], ("dp", "seq"), scatter_dimension=0, tiled=True),
        lax.psum_scatter(totals[10], ("dp", "seq"), scatter_dimension=0, tiled=True),
        lax.psum_scatter(totals[11], ("dp", "seq"), scatter_dimension=0, tiled=True),
    )
    return (
        jnp.concatenate(outputs, axis=0),
        jnp.concatenate(grad_inputs, axis=0),
        reduced[0],
        reduced[1],
        reduced[2],
        reduced[3],
        reduced[4],
        reduced[5],
        reduced[6],
        reduced[7],
        reduced[8],
        reduced[9],
        reduced[10],
        reduced[11],
    )


def solution(mesh):
    in_specs = (
        P("dp", "seq", None),
        P("dp", "seq", None),
        P("dp"),
        P(("dp", "seq")),
        P(("dp", "seq")),
        P(("dp", "seq"), None),
        P(("dp", "seq")),
        P(("dp", "seq"), None),
        P(("dp", "seq")),
        P(("dp", "seq")),
        P(("dp", "seq")),
        P(("dp", "seq"), None),
        P(("dp", "seq")),
        P(("dp", "seq"), None),
        P(("dp", "seq")),
    )
    out_specs = (
        P("dp", "seq", None),
        P("dp", "seq", None),
        P(("dp", "seq")),
        P(("dp", "seq")),
        P(("dp", "seq"), None),
        P(("dp", "seq")),
        P(("dp", "seq"), None),
        P(("dp", "seq")),
        P(("dp", "seq")),
        P(("dp", "seq")),
        P(("dp", "seq"), None),
        P(("dp", "seq")),
        P(("dp", "seq"), None),
        P(("dp", "seq")),
    )
    chosen = body if fits(mesh) else general_body
    return jax.shard_map(chosen, mesh=mesh, in_specs=in_specs, out_specs=out_specs, check_vma=False)
```

```python
import functools

import jax
import jax.numpy as jnp
from jax import lax
from jax.experimental import pallas as pl
from jax.experimental.pallas import tpu as pltpu
from jax.sharding import PartitionSpec as P

HEADS = 12
HEAD_DIM = 64
MB = 2

F32 = jnp.float32
BF = jnp.bfloat16
EPS = 1e-05
MESH = pl.DeviceIdType.MESH
NEG = -1e30
ANY = pl.BlockSpec(memory_space=pl.ANY)
VM = pl.BlockSpec(memory_space=pltpu.VMEM)
SM = pl.BlockSpec(memory_space=pltpu.SMEM)
WIDTHS = (24, 24, 72, 24, 24, 24, 96, 24)
D = 768
FF = 3072
THIRD = 384
LAST = (((1,), (1,)), ((), ()))
FIRST = (((0,), (0,)), ((), ()))
ALL = slice(None)
REMOTES = 224
LOCALS = 64


def places():
    dp = lax.axis_index("dp")
    sq = lax.axis_index("seq")
    return dp // 2, dp % 2, sq // 2, sq % 2


def device(z, x, y, c):
    return (z * 2 + x, y * 2 + c)


def owner_of(wide):
    column = lax.broadcasted_iota(jnp.int32, (1, 32 * wide), 1).astype(F32)
    owner = jnp.floor((column + 0.5) * (1.0 / wide))
    return owner.astype(jnp.int32), (column - owner * wide).astype(jnp.int32)


def spread_row(gathered, index, wide):
    total = 32 * wide
    row = lax.broadcasted_iota(jnp.int32, (32, 256), 0)
    place = lax.broadcasted_iota(jnp.int32, (32, 256), 1)
    pick = jnp.where(place == row * 8 + index, 1.0, 0.0).astype(BF)
    mine = jnp.dot(pick, gathered, preferred_element_type=F32).astype(BF)
    owner, rest = owner_of(wide)
    spread = jnp.where(lax.broadcasted_iota(jnp.int32, (128, total), 0) == rest, 1.0, 0.0).astype(BF)
    full = jnp.dot(mine, spread, preferred_element_type=F32)
    keep = lax.broadcasted_iota(jnp.int32, (32, total), 0) == owner
    return jnp.sum(jnp.where(keep, full, 0.0), axis=0, keepdims=True)


def collect_rows(vector, wide):
    total = 32 * wide
    owner, rest = owner_of(wide)
    gather = jnp.where(lax.broadcasted_iota(jnp.int32, (128, total), 0) == rest, 1.0, 0.0).astype(BF)
    keep = lax.broadcasted_iota(jnp.int32, (32, total), 0) == owner
    high = vector.astype(BF).astype(F32)
    out = None
    for part in (high, vector - high):
        placed = jnp.where(keep, part, 0.0).astype(BF)
        term = lax.dot_general(placed, gather, LAST, preferred_element_type=F32)
        out = term if out is None else out + term
    return out


def add_into(ref, at, other):
    ref[at] = (ref[at].astype(F32) + other.astype(F32)).astype(BF)


def start(copies):
    for copy in copies:
        copy.start()


def arrive(copies):
    for copy in copies:
        copy.wait_recv()


def landed(copies):
    for copy in copies:
        copy.wait()


def lanes(first, count=128):
    return pl.ds(pl.multiple_of(first, 128), count)


def rows_at(first, count, step=256):
    return pl.ds(pl.multiple_of(first, step), count)


class Cut:
    def __init__(self, rows, columns, a, upto=None, upto_row=None):
        first = slice(0, upto_row or rows)
        end = upto or columns
        self.rows, self.columns = rows, columns
        self.a = (first, slice(0, a))
        self.b = (first, slice(a, end))
        self.ab = (first, slice(0, end))
        self.f = None
        self.axis = 0 if upto_row else 1
        if upto:
            self.f = (slice(0, rows), slice(upto, columns))
        if upto_row:
            self.a = (slice(0, upto_row // 2), slice(0, columns))
            self.b = (slice(upto_row // 2, upto_row), slice(0, columns))
            self.f = (slice(upto_row, rows), slice(0, columns))

    def shape(self, part):
        return tuple(side.stop - side.start for side in part)


CUTS = {
    "down": Cut(192, 384, 128, upto_row=160), "up0": Cut(48, 768, 256, upto=640), "up1": Cut(48, 768, 128, upto=640),
    "out": Cut(48, 384, 128), "q0": Cut(48, 384, 128), "q1": Cut(48, 384, 128), "q2": Cut(48, 384, 128),
}


class Links:
    def __init__(self, ssem, rsem, lsem):
        self.ssem, self.rsem, self.lsem = ssem, rsem, lsem
        self.remotes = self.locals = 0
        self.sent = []
        z, x, y, c = places()
        self.z, self.x, self.y, self.c = z, x, y, c
        self.x2, self.y2, self.c2 = 1 - x, 1 - y, 1 - c
        self.px, self.py, self.pc = device(z, 1 - x, y, c), device(z, x, 1 - y, c), device(z, x, y, 1 - c)
        self.zs = [lax.rem(z + d, 4) for d in (1, 2, 3)]
        self.pz = [device(zz, x, y, c) for zz in self.zs]

    def remote(self, src, dst, dev):
        i = self.remotes
        self.remotes += 1
        copy = pltpu.make_async_remote_copy(
            src_ref=src, dst_ref=dst, send_sem=self.ssem.at[i], recv_sem=self.rsem.at[i],
            device_id=dev, device_id_type=MESH)
        self.sent.append(copy)
        return copy

    def local(self, src, dst):
        i = self.locals
        self.locals += 1
        return pltpu.make_async_copy(src, dst, self.lsem.at[i])

    def greet(self):
        barrier = pltpu.get_barrier_semaphore()
        for dev in [self.px, self.py, self.pc] + self.pz:
            pl.semaphore_signal(barrier, inc=1, device_id=dev, device_id_type=MESH)

    def greeted(self):
        pl.semaphore_wait(pltpu.get_barrier_semaphore(), 6)


class Gather:
    def __init__(self, links, own, other, mine, theirs, cut, whole=True):
        k = links
        rows = own.shape[0]
        at = pl.ds(pl.multiple_of(k.c * rows, 8), rows)
        z, x, y = k.z, k.x, k.y
        self.own = [k.local(own, mine.at[z, x, y, at])]
        self.c0 = [k.remote(other, theirs.at[z, x, y, at], k.pc)]
        a, b, ab, f = cut.a, cut.b, cut.ab, cut.f

        def send(place, dev):
            return k.remote(mine.at[place], mine.at[place], dev)

        self.c1 = [send((z, x, y) + ab, dev) for dev in k.pz]
        self.c2 = [send((ALL, x, y) + a, k.px), send((ALL, x, y) + b, k.py)]
        self.c3 = [send((ALL, ALL, y) + a, k.py), send((ALL, x, ALL) + b, k.px)]
        if f:
            self.c1.append(send((z, x, y) + f, k.py))
            self.c2.append(send((z, x, ALL) + f, k.px))
            self.c3 += [send((z, ALL, ALL) + f, dev) for dev in k.pz]
        self.c4 = [k.remote(mine, mine, k.pc)] if whole else []

    def s0(self):
        start(self.c0)

    def s1(self):
        landed(self.own)
        arrive(self.c0)
        start(self.c1)

    def s2(self):
        arrive(self.c1)
        start(self.c2)

    def s3(self):
        arrive(self.c2)
        start(self.c3)

    def s4(self):
        arrive(self.c3)
        start(self.c4)

    def done(self):
        arrive(self.c4)


class Scatter:
    @staticmethod
    def buffers(cut, whole):
        block = (cut.rows, cut.columns)
        a, b, ab = cut.shape(cut.a), cut.shape(cut.b), cut.shape(cut.ab)
        low = [(4, 2, 2) + block] if whole else []
        low += [(4, 2) + a, (4, 2) + b, (4,) + a, (4,) + b, (3,) + ab]
        if cut.f:
            f = cut.shape(cut.f)
            low += [(3, 2, 2) + f, (2,) + f, f]
        half = (cut.rows // 2, cut.columns)
        return [pltpu.VMEM(shape, BF) for shape in low] + [pltpu.VMEM((2,) + half, F32), pltpu.VMEM(half, F32)]

    def __init__(self, links, grad, prefix, other, cut, work, put):
        k = links
        self.k, self.grad, self.prefix, self.cut, self.put = k, grad, prefix, cut, put
        self.whole = other is not None
        mine = self.mine = grad.at[prefix]
        if self.whole:
            self.r0 = next(work)
            self.c0 = [k.remote(grad.at[other], self.r0, k.pc)]
        else:
            self.c0 = []
        self.r1a, self.r1b, self.r2a, self.r2b, self.r3 = [next(work) for _ in range(5)]
        z, x, y, x2, y2 = k.z, k.x, k.y, k.x2, k.y2
        a, b, ab, f = cut.a, cut.b, cut.ab, cut.f
        self.c1 = [k.remote(mine.at[(ALL, ALL, y2) + a], self.r1a, k.py), k.remote(mine.at[(ALL, x2, ALL) + b], self.r1b, k.px)]
        self.c2 = [k.remote(mine.at[(ALL, x2, y) + a], self.r2a, k.px), k.remote(mine.at[(ALL, x, y2) + b], self.r2b, k.py)]
        self.c3 = [k.remote(mine.at[(k.zs[d], x, y) + ab], self.r3.at[d], k.pz[d]) for d in range(3)]
        if f:
            self.rf1, self.rf2, self.rf3 = [next(work) for _ in range(3)]
            self.c1 += [k.remote(mine.at[(k.zs[d], ALL, ALL) + f], self.rf1.at[d], k.pz[d]) for d in range(3)]
            self.c2.append(k.remote(mine.at[(z, x2, ALL) + f], self.rf2, k.px))
            self.c3.append(k.remote(mine.at[(z, x, y2) + f], self.rf3, k.py))
        self.tot, self.fin = next(work), next(work)
        self.c4 = [k.remote(self.tot.at[k.c2], self.fin, k.pc)]

    def at(self, place):
        return self.prefix + place

    def s0(self):
        start(self.c0)

    def s1(self):
        if self.whole:
            arrive(self.c0)

            def add(i, carry):
                where = (i // 4, lax.rem(i // 2, 2), lax.rem(i, 2))
                add_into(self.grad, self.at(where), self.r0[where])
                return carry

            lax.fori_loop(0, 16, add, 0)
        start(self.c1)

    def s2(self):
        arrive(self.c1)
        k, cut = self.k, self.cut

        def add(i, carry):
            zz, other = i // 2, lax.rem(i, 2)
            add_into(self.grad, self.at((zz, other, k.y) + cut.a), self.r1a[zz, other])
            add_into(self.grad, self.at((zz, k.x, other) + cut.b), self.r1b[zz, other])
            return carry

        lax.fori_loop(0, 8, add, 0)
        if cut.f:
            def add_f(i, carry):
                xx, yy = i // 2, lax.rem(i, 2)
                three = self.rf1[0, xx, yy].astype(F32) + self.rf1[1, xx, yy].astype(F32) + self.rf1[2, xx, yy].astype(F32)
                add_into(self.grad, self.at((k.z, xx, yy) + cut.f), three)
                return carry

            lax.fori_loop(0, 4, add_f, 0)
        start(self.c2)

    def s3(self):
        arrive(self.c2)
        k, cut = self.k, self.cut

        def add(zz, carry):
            add_into(self.grad, self.at((zz, k.x, k.y) + cut.a), self.r2a[zz])
            add_into(self.grad, self.at((zz, k.x, k.y) + cut.b), self.r2b[zz])
            return carry

        lax.fori_loop(0, 4, add, 0)
        if cut.f:
            for yy in range(2):
                add_into(self.grad, self.at((k.z, k.x, yy) + cut.f), self.rf2[yy])
        start(self.c3)

    def s4(self):
        arrive(self.c3)
        k, cut = self.k, self.cut
        total = self.mine[(k.z, k.x, k.y) + cut.ab].astype(F32)
        for d in range(3):
            total = total + self.r3[d].astype(F32)
        if cut.f:
            rest = self.mine[(k.z, k.x, k.y) + cut.f].astype(F32) + self.rf3[...].astype(F32)
            total = jnp.concatenate([total, rest], axis=cut.axis)
        rows = total.shape[0] // 2
        self.tot[0] = total[:rows]
        self.tot[1] = total[rows:]
        start(self.c4)
        self.put(self.tot[k.c], k.c)

    def s5(self):
        arrive(self.c4)
        self.put(self.fin[...], self.k.c2)


def sign_of(value):
    return jnp.clip(value * 1e38, -1.0, 1.0)


def masked(size, seen, low):
    last = jnp.where(seen, size[low:], NEG)
    return last if low == 0 else jnp.concatenate([size[:low], last], axis=0)


def gelu_parts(value):
    rate = 0.7978845608028654
    bent = jnp.tanh(rate * (value + 0.044715 * (value * value * value)))
    result = 0.5 * value * (1.0 + bent)
    slope = 0.5 * (1.0 + bent) + 0.5 * value * (1.0 - bent * bent) * (rate * (1.0 + 0.134145 * (value * value)))
    return result, slope


def unit_rows(rows):
    centre = rows - jnp.mean(rows, axis=-1, keepdims=True)
    scale = lax.rsqrt(jnp.mean(centre * centre, axis=-1, keepdims=True) + EPS)
    return centre * scale, scale


def norm_back(grad, normed, scale):
    return scale * (grad - jnp.mean(grad, axis=-1, keepdims=True)
                    - normed * jnp.mean(grad * normed, axis=-1, keepdims=True))


def layer_kernel(
    prefix, tok, cot, v0_s, v1_s, v2_s, v3_s, v4_s, v5_s, v6_s, v7_s, wq_s, wo_s, wu_s, wd_s,
    out_bo, out_gt, out_q, out_o, out_u, out_d, out_vec,
    wq, wo, wu, wd, gv, k_qst, k_k, k_v, k_att, k_n1t,
    vec_s, wq_p, gvm, tok_all, vrows, wom, al_send, al, cotm, ga_send, ga_all, fa, fb, fc, fr, lt,
    gd, gu, go, gq,
    vs, vbq, vup, vtab, vr0, vr1, vr2, vr3,
    ssem, rsem, lsem, *work,
):
    k = Links(ssem, rsem, lsem)
    bo, gtb = al, cotm
    work = iter(work)
    z, x, y, c, x2, y2, c2 = k.z, k.x, k.y, k.c, k.x2, k.y2, k.c2
    k.greet()
    vmem = pltpu.VMEM

    vec_s[...] = jnp.zeros_like(vec_s)
    for index, (wide, ref) in enumerate(zip(WIDTHS, (v0_s, v1_s, v2_s, v3_s, v4_s, v5_s, v6_s, v7_s))):
        vec_s[index : index + 1, 0:wide] = ref[...].astype(F32).reshape(1, wide)
    for core in range(2):
        for u in range(3):
            for kind in range(3):
                first = kind * D + core * THIRD + u * 128
                wq_p[core, u, :, kind * 128 : (kind + 1) * 128] = wq_s[:, first : first + 128]
    gather_q = [Gather(k, wq_p.at[c, u], wq_p.at[c2, u], wq.at[u], wq.at[u], CUTS[f"q{u}"], False)
                for u in range(3)]

    def halves(shard, full, cut):
        half = full.shape[-1]
        return Gather(k, shard.at[:, lanes(c * half, half)], shard.at[:, lanes(c2 * half, half)], full.at[c], full.at[c2], cut)

    gather_o = halves(wo_s, wo, CUTS["out"])
    gather_d = halves(wd_s, wd, CUTS["down"])
    k.sent.pop()
    gather_d.c4 = [k.remote(wd.at[c, zz], wd.at[c, zz], k.pc) for zz in (2 * c, 2 * c + 1, 2 * c2, 2 * c2 + 1)]
    gather_u = [Gather(k, wu_s.at[:, lanes(c * 1536 + part * D, D)], wu_s.at[:, lanes(c2 * 1536 + part * D, D)],
                       wu.at[c, part], wu.at[c2, part], CUTS[f"up{part}"]) for part in range(2)]
    own_vec = k.local(vec_s, gv.at[z, x, y, c])
    own_tok = k.local(tok.at[y], tok_all.at[y, c])
    own_cot = k.local(cot.at[y], cotm.at[y])
    own_vec.start()
    start(gather_q[0].own)
    own_tok.start()
    others = [gather_q[1], gather_q[2], gather_o] + gather_u + [gather_d]
    for gather in others:
        start(gather.own)
    own_cot.start()
    k.greeted()

    vec_c = k.remote(vec_s, gv.at[z, x, y, c], k.pc)
    tok_y = k.remote(tok.at[y2], tok_all.at[y, c], k.py)
    cot_y = k.remote(cot.at[y2], cotm.at[y], k.py)
    vec_c.start()
    gather_q[0].s0()
    tok_y.start()
    for gather in others:
        gather.s0()
    own_vec.wait()
    vec_c.wait_recv()
    vec_z = [k.remote(gv.at[z, x, y], gv.at[z, x, y], dev) for dev in k.pz]
    start(vec_z)
    gather_q[0].s1()
    gather_q[1].s1()
    own_tok.wait()
    arrive(vec_z)
    vec_x = k.remote(gv.at[:, x, y], gv.at[:, x, y], k.px)
    vec_x.start()
    gather_q[0].s2()
    gather_q[2].s1()
    vec_x.wait_recv()
    vec_y = k.remote(gv.at[:, :, y], gv.at[:, :, y], k.py)
    vec_y.start()
    gather_q[1].s2()
    gather_o.s1()
    gather_q[0].s3()
    tok_y.wait_recv()
    tok_c = k.remote(tok_all.at[:, c], tok_all.at[:, c], k.pc)
    tok_c.start()
    gather_q[2].s2()
    gather_u[0].s1()
    vec_y.wait_recv()
    table = k.local(gv, gvm)
    table.start()
    table.wait()
    table = gvm[...].reshape(256, 128).astype(BF)
    for index, wide in enumerate(WIDTHS):
        vrows[index : index + 1, 0 : 32 * wide] = spread_row(table, index, wide)
    gather_q[1].s3()
    tok_c.wait_recv()

    mine_cols = lanes(c * THIRD, THIRD)
    peer_cols = lanes(c2 * THIRD, THIRD)
    al_own = k.local(al_send.at[:, c], al.at[:, :, mine_cols])
    al_c = k.remote(al_send.at[:, c2], al.at[:, :, mine_cols], k.pc)
    gathered = len(k.sent)
    limit = prefix[y] - 1
    sub = lax.broadcasted_iota(jnp.int32, (128, 256), 0)
    wq3 = wq.reshape(3, D, THIRD)

    def forward(n1, n1t, vt, qst, keys_ref, values_ref, att, wqm):
        gain = vrows[0:1, 0:D]
        shift = vrows[1:2, 0:D]

        def norm_block(b, carry):
            normed, _ = unit_rows(tok_all[b // 2, lax.rem(b, 2)].astype(F32))
            normed = (normed * gain + shift).astype(BF)
            at = rows_at(b * 256, 256)
            n1[at, :] = normed
            n1t[:, at] = normed.astype(F32).T.astype(BF)
            return carry

        lax.fori_loop(0, 4, norm_block, 0)
        keep = [k.local(n1t, k_n1t), k.local(qst, k_qst), k.local(keys_ref, k_k),
                k.local(values_ref, k_v), k.local(att, k_att)]
        keep[0].start()
        load_q = [k.local(wq3.at[u], wqm.at[u]) for u in range(3)]
        load_o = k.local(wo.reshape(2, D, THIRD), wom)

        def head(u):
            gather_q[u].s4()
            load_q[u].start()
            load_q[u].wait()

        slots = {
            (0, 3): [gather_q[2].s3, gather_o.s2, gather_u[1].s1], (0, 2): [gather_u[0].s2],
            (0, 1): [gather_o.s3, gather_d.s1], (0, 0): [gather_u[1].s2],
            (1, 3): [gather_u[0].s3], (1, 2): [gather_o.s4], (1, 1): [gather_d.s2], (1, 0): [gather_u[1].s3],
            (2, 3): [gather_o.done, load_o.start, gather_u[0].s4], (2, 2): [cot_y.start], (2, 1): [gather_d.s3], (2, 0): [],
        }

        def unit(u, carry):
            cols = lanes(u * 128)
            for which in range(3):
                @pl.when(u == which)
                def _():
                    head(which)

            def project(b, inner):
                rows = rows_at(b * 512, 512)
                value = jnp.dot(n1[rows, :], wqm[u], preferred_element_type=F32)
                parts = []
                for kind in range(3):
                    bias = vrows[2:3, lanes(kind * D + c * THIRD + u * 128)]
                    parts.append((value[:, kind * 128 : (kind + 1) * 128] + bias).astype(BF))
                queries = parts[0].astype(F32) * 0.125
                qst[cols, rows] = queries.T.astype(BF)
                keys_ref[rows, cols] = parts[1]
                values_ref[rows, cols] = parts[2]
                vt[cols, rows] = parts[2].astype(F32).T.astype(BF)
                return inner

            lax.fori_loop(0, 2, project, 0)
            for block in (3, 2, 1, 0):
                attend(u, block)
                for which in range(3):
                    if slots[which, block]:
                        @pl.when(u == which)
                        def _():
                            for step in slots[which, block]:
                                step()
            return carry

        def attend(u, block):
            rows = min(4, max(block + 1, 2)) * 256
            qcols = slice(block * 256, (block + 1) * 256)
            cols = lanes(u * 128)
            keys = keys_ref[0:rows, cols]
            queries = qst[cols, qcols]
            qpos = block * 256 + lax.broadcasted_iota(jnp.int32, (1, 256), 1)
            low = block * 256
            seen = low + lax.broadcasted_iota(jnp.int32, (rows - low, 256), 0) <= jnp.maximum(qpos, limit)
            for half in range(2):
                chosen = jnp.where(sub // 64 == half, queries, jnp.zeros_like(queries))
                scores = jnp.dot(keys, chosen, preferred_element_type=F32)
                size = jnp.abs(scores)
                size = masked(size, seen, low)
                top = jnp.max(size, axis=0, keepdims=True)
                exponent = jnp.exp(size - top)
                total = jnp.sum(exponent, axis=0, keepdims=True)
                weights = (sign_of(scores) * exponent).astype(BF)
                at = pl.ds(pl.multiple_of(u * 128 + half * 64, 64), 64)
                att[at, qcols] = jnp.dot(vt[at, 0:rows], weights, preferred_element_type=F32) / total
                lt[pl.ds(u * 2 + half, 1), qcols] = top + jnp.log(total)
            al_send[block // 2, block % 2, :, cols] = att[cols, qcols].T.astype(BF)

        lax.fori_loop(0, 3, unit, 0)
        al_own.start()
        al_c.start()
        start(keep[1:])
        load_o.wait()
        al_own.wait()
        al_c.wait_recv()
        landed(keep)

    pl.run_scoped(
        forward, vmem((1024, D), BF), vmem((D, 1024), BF), vmem((THIRD, 1024), BF),
        vmem((THIRD, 1024), BF), vmem((1024, THIRD), BF), vmem((1024, THIRD), BF), vmem((THIRD, 1024), F32),
        vmem((3, D, THIRD), BF))

    def put_to(out, half):
        def put(value, core):
            out[:, lanes(core * half, half)] = value
        return put

    down = Scatter(k, gd, (c,), (c2,), CUTS["down"], work, put_to(out_d, THIRD))

    def put_up(part):
        def put(value, core):
            out_u[:, lanes(core * 1536 + part * D, D)] = value
        return put

    up = [Scatter(k, gu, (c, part), (c2, part), CUTS[f"up{part}"], work, put_up(part)) for part in range(2)]
    outp = Scatter(k, go, (c,), (c2,), CUTS["out"], work, put_to(out_o, THIRD))

    def feed(wbuf, wdb, hid, slope, n2, n2t, alt, gpc):
        b_out, gain, shift = vrows[3:4, 0:D], vrows[4:5, 0:D], vrows[5:6, 0:D]

        def begin(yy, carry):
            rows = rows_at(yy * 256, 256)
            branch = jnp.concatenate([jnp.dot(al[yy], wom[h], preferred_element_type=F32) for h in range(2)], axis=1)
            residual = tok_all[yy, c].astype(F32) + branch + b_out
            fa[yy] = residual
            normed, _ = unit_rows(residual)
            normed = (normed * gain + shift).astype(BF)
            n2[rows, :] = normed
            n2t[:, rows] = normed.astype(F32).T.astype(BF)
            alt[:, rows] = al[yy].astype(F32).T.astype(BF)
            return carry

        lax.fori_loop(0, 2, begin, 0)
        own_cot.wait()
        cot_y.wait_recv()

        wu2 = wu.reshape(2, 2, D, D)
        wd2 = wd.reshape(2, FF, THIRD)

        def chunk(j, first, second):
            h = first if j < 2 else second
            return h, j % 2

        def up_load(j, slot, order):
            h, part = chunk(j, *order)
            return k.local(wu2.at[h, part], wbuf.at[slot])

        def down_load(j, slot, order):
            h, part = chunk(j, *order)
            rows = rows_at(h * 1536 + part * D, D)
            return [k.local(wd2.at[side, rows, :], wdb.at[slot, :, side * THIRD : (side + 1) * THIRD]) for side in range(2)]

        forth = (c, c2)
        loads = [up_load(j, j % 2, forth) for j in range(4)]
        loads[0].start()
        gather_u[1].s4()
        for j in range(4):
            loads[j].wait()
            if j == 0:
                loads[1].start()
            if j == 1:
                gather_u[0].done()
                loads[2].start()
            if j == 2:
                gather_u[1].done()
                loads[3].start()
            h, part = chunk(j, *forth)

            cols = lanes(h * 1536 + part * D, D)
            value = jnp.dot(n2[...], wbuf[j % 2], preferred_element_type=F32) + vrows[6:7, cols]
            result, bend = gelu_parts(value)
            hid[:, cols] = result.astype(BF)
            slope[:, cols] = bend

        vs[7:8, :] = jnp.sum(cotm[0].astype(F32), axis=0, keepdims=True) + jnp.sum(
            cotm[1].astype(F32), axis=0, keepdims=True)

        def down_grad(i, carry):
            total = lax.dot_general(hid[:, lanes(i * THIRD, THIRD)], cotm[...].reshape(512, D), FIRST,
                                    preferred_element_type=F32)
            zz, xx = i // 2, lax.rem(i, 2)
            for yy in range(2):
                for h in range(2):
                    gd[h, zz, xx, yy] = total[yy * 192 : (yy + 1) * 192, h * THIRD : (h + 1) * THIRD].astype(BF)
            return carry

        lax.fori_loop(0, 8, down_grad, 0)
        down.s0()
        fb[...] = jnp.zeros_like(fb)
        fc[...] = jnp.zeros_like(fc)
        gather_d.s4()
        back = (c2, c)
        again = [up_load(j, j % 2, back) for j in range(4)]
        lower = [down_load(j, j % 2, back) for j in range(4)]
        again[0].start()
        down.s1()
        gather_d.c4[0].wait_recv()
        start(lower[0])
        for j in range(4):
            slot = j % 2
            if j < 3:
                again[j + 1].start()
                gather_d.c4[j + 1].wait_recv()
                start(lower[j + 1])
            again[j].wait()
            landed(lower[j])
            h, part = chunk(j, *back)
            cols = lanes(h * 1536 + part * D, D)
            fc[...] += jnp.dot(hid[:, cols], wdb[slot], preferred_element_type=F32).reshape(2, 256, D)
            grad = lax.dot_general(cotm[...].reshape(512, D), wdb[slot], LAST, preferred_element_type=F32)
            grad = (grad * slope[:, cols]).astype(BF)
            gpc[...] = grad
            vup[0:1, cols] = jnp.sum(grad.astype(F32), axis=0, keepdims=True)
            fb[...] += lax.dot_general(gpc[...], wbuf[slot], LAST, preferred_element_type=F32).reshape(2, 256, D)

            def up_grad(zz, carry):
                total = jnp.dot(n2t[rows_at(zz * THIRD, THIRD, 128), :], gpc[...], preferred_element_type=F32)
                for i in range(8):
                    gu[h, part, zz * 2 + i // 4, i // 2 % 2, i % 2] = total[i * 48 : (i + 1) * 48].astype(BF)
                return carry

            lax.fori_loop(0, 2, up_grad, 0)
            if j < 2:
                up[j].s0()
            if j == 2:
                up[0].s1()
                down.s2()
        bo[...] = (fa[...] + fc[...] + vrows[7:8, 0:D].reshape(1, 1, D)).astype(BF)
        up[1].s1()

    ga_c = k.remote(ga_send.at[:, :, peer_cols], ga_all.at[:, c], k.pc)
    def turn(alt, gpc):
        gain = vrows[4:5, 0:D]
        vs[3:6, :] = jnp.zeros((3, D), F32)

        def mid_back(yy, carry):
            rows = rows_at(yy * 256, 256)
            normed, scale = unit_rows(fa[yy])
            grad = fb[yy]
            vs[4:5, :] += jnp.sum(grad * normed, axis=0, keepdims=True)
            vs[5:6, :] += jnp.sum(grad, axis=0, keepdims=True)
            total = cotm[yy].astype(F32) + norm_back(grad * gain, normed, scale)
            fa[yy] = total
            low = total.astype(BF)
            vs[3:4, :] += jnp.sum(low.astype(F32), axis=0, keepdims=True)
            gpc[rows, :] = low
            heads = None
            for side in range(2):
                term = lax.dot_general(low[:, side * THIRD : (side + 1) * THIRD], wom[side], LAST,
                                       preferred_element_type=F32)
                heads = term if heads is None else heads + term
            ga_send[yy] = heads.astype(BF)
            ga_all[yy, c] = ga_send[yy, :, mine_cols]
            return carry

        lax.fori_loop(0, 2, mid_back, 0)
        ga_c.start()

        def out_grad(zz, carry):
            total = jnp.dot(alt[rows_at(zz * THIRD, THIRD, 128), :], gpc[...], preferred_element_type=F32)
            for i in range(8):
                for h in range(2):
                    go[h, zz * 2 + i // 4, i // 2 % 2, i % 2] = total[i * 48 : (i + 1) * 48, h * THIRD : (h + 1) * THIRD].astype(BF)
            return carry

        lax.fori_loop(0, 2, out_grad, 0)
        outp.s0()

    def put_q(u):
        def put(value, core):
            for kind in range(3):
                out_q[:, lanes(kind * D + core * THIRD + u * 128)] = value[:, kind * 128 : (kind + 1) * 128]
        return put

    queue = [Scatter(k, gq, (u,), None, CUTS[f"q{u}"], work, put_q(u)) for u in range(3)]
    bo_own = k.local(bo.at[y], out_bo.at[y])
    bo_y = k.remote(bo.at[y2], out_bo.at[y], k.py)

    def collect(index):
        row = vbq[...] if index == 2 else vup[...] if index == 6 else vs[index : index + 1, :]
        vtab[pl.ds(index, 32, stride=8), :] = collect_rows(row, WIDTHS[index])

    def early():
        for index in (3, 4, 5, 6, 7):
            collect(index)

    def send_out():
        bo_own.start()
        bo_y.start()

    def backward(alt, gpc, qst, keys_ref, values_ref, att, n1t, gt, kt, dk, dv, gpu, wqm, gp):
        loads = [k.local(k_qst, qst), k.local(k_k, keys_ref), k.local(k_v, values_ref),
                 k.local(k_att, att), k.local(k_n1t, n1t), ]
        loads += [k.local(wq3.at[u], wqm.at[:, u * THIRD : (u + 1) * THIRD]) for u in range(3)]
        start(loads)
        turn(alt, gpc)
        ga_c.wait_recv()
        landed(loads)
        vbq[...] = jnp.zeros_like(vbq)
        slots = {
            (0, 3): [outp.s1], (0, 2): [], (0, 1): [down.s3], (0, 0): [up[0].s2, send_out],
            (1, 3): [], (1, 2): [up[1].s2], (1, 1): [outp.s2], (1, 0): [down.s4, up[0].s3, early],
            (2, 3): [up[1].s3], (2, 2): [queue[0].s2, down.s5], (2, 1): [outp.s3], (2, 0): [queue[0].s3, up[0].s4],
        }

        def unit(u, carry):
            cols = lanes(u * 128)
            for b in range(4):
                rows = slice(b * 256, (b + 1) * 256)
                gt[:, rows] = ga_all[b // 2, b % 2, :, cols].astype(F32).T.astype(BF)
                kt[:, rows] = keys_ref[rows, cols].astype(F32).T.astype(BF)
            dk[...] = jnp.zeros_like(dk)
            dv[...] = jnp.zeros_like(dv)
            for block in (3, 2, 1, 0):
                rows = min(4, max(block + 1, 2)) * 256
                qrange = slice(block * 256, (block + 1) * 256)
                keys = keys_ref[0:rows, cols]
                values = values_ref[0:rows, cols]
                queries_t = qst[cols, qrange]
                grads_t = gt[:, qrange]
                qpos = block * 256 + lax.broadcasted_iota(jnp.int32, (1, 256), 1)
                low = block * 256
                seen = low + lax.broadcasted_iota(jnp.int32, (rows - low, 256), 0) <= jnp.maximum(qpos, limit)
                prod = grads_t.astype(F32) * att[cols, qrange]
                dqs = []
                for half in range(2):
                    part = slice(half * 64, half * 64 + 64)
                    in_sub = sub // 64 == half
                    delta = jnp.sum(prod[part], axis=0, keepdims=True)
                    total = lt[pl.ds(u * 2 + half, 1), qrange]
                    zero = jnp.zeros((), BF)
                    scores = jnp.dot(keys, jnp.where(in_sub, queries_t, zero), preferred_element_type=F32)
                    pull = jnp.dot(values, jnp.where(in_sub, grads_t, zero), preferred_element_type=F32)
                    share = jnp.exp(masked(jnp.abs(scores) - total, seen, low))
                    signed = sign_of(scores) * share
                    grad_scores = (share * pull - signed * delta).astype(BF)
                    signed = signed.astype(BF)
                    dv[part, 0:rows] += lax.dot_general(grads_t[part], signed, LAST, preferred_element_type=F32)
                    dk[part, 0:rows] += lax.dot_general(queries_t[part], grad_scores, LAST, preferred_element_type=F32)
                    dqs.append(jnp.dot(kt[part, 0:rows], grad_scores, preferred_element_type=F32))
                gpu[qrange, 0:128] = (jnp.concatenate(dqs, axis=0).T * 0.125).astype(BF)
                for which in range(3):
                    if slots[which, block]:
                        @pl.when(u == which)
                        def _():
                            for step in slots[which, block]:
                                step()
            for b in range(4):
                rows = slice(b * 256, (b + 1) * 256)
                gpu[rows, 128:256] = dk[:, rows].T.astype(BF)
                gpu[rows, 256:384] = dv[:, rows].T.astype(BF)
            sums = jnp.sum(gpu[...].astype(F32), axis=0, keepdims=True)
            for kind in range(3):
                part = slice(kind * 128, (kind + 1) * 128)
                vbq[0:1, lanes(kind * D + c * THIRD + u * 128)] = sums[:, part]
                gp[:, lanes(u * THIRD + kind * 128)] = gpu[:, part]

            def weights(zz, inner):
                block = jnp.dot(n1t[rows_at(zz * THIRD, THIRD, 128), :], gpu[...], preferred_element_type=F32)
                for i in range(8):
                    gq[u, zz * 2 + i // 4, i // 2 % 2, i % 2] = block[i * 48 : (i + 1) * 48].astype(BF)
                return inner

            lax.fori_loop(0, 2, weights, 0)
            for which in range(3):
                @pl.when(u == which)
                def _():
                    queue[which].s1()
            return carry

        lax.fori_loop(0, 3, unit, 0)

        def back_rows(b):
            return lax.dot_general(gp[rows_at(b * 256, 256), :], wqm[...], LAST, preferred_element_type=F32)

        def back_peer(yy, carry):
            fb[yy] = back_rows(yy * 2 + c2)
            return carry

        def back_own(yy, carry):
            fc[yy] = back_rows(yy * 2 + c)
            return carry

        lax.fori_loop(0, 2, back_peer, 0)
        part_c.start()
        queue[1].s2()
        lax.fori_loop(0, 2, back_own, 0)
        queue[2].s2()

    part_c = k.remote(fb, fr, k.pc)

    def both(alt, gpc):
        pl.run_scoped(
            functools.partial(feed, alt=alt, gpc=gpc), vmem((2, D, D), BF), vmem((2, D, D), BF),
            vmem((512, FF), BF), vmem((512, FF), F32), vmem((512, D), BF), vmem((D, 512), BF))
        pl.run_scoped(
            functools.partial(backward, alt, gpc), vmem((THIRD, 1024), BF), vmem((1024, THIRD), BF),
            vmem((1024, THIRD), BF), vmem((THIRD, 1024), F32), vmem((D, 1024), BF), vmem((128, 1024), BF),
            vmem((128, 1024), BF), vmem((128, 1024), F32), vmem((128, 1024), F32), vmem((1024, THIRD), BF),
            vmem((D, 3 * THIRD), BF), vmem((1024, 3 * THIRD), BF))

    pl.run_scoped(both, vmem((D, 512), BF), vmem((512, D), BF))

    gain = vrows[0:1, 0:D]
    vs[0:2, :] = jnp.zeros((2, D), F32)
    part_c.wait_recv()

    def last_back(yy):
        normed, scale = unit_rows(tok_all[yy, c].astype(F32))
        grad = fc[yy] + fr[yy]
        vs[0:1, :] += jnp.sum(grad * normed, axis=0, keepdims=True)
        vs[1:2, :] += jnp.sum(grad, axis=0, keepdims=True)
        gtb[yy] = (fa[yy] + norm_back(grad * gain, normed, scale)).astype(BF)

    gt_own = k.local(gtb.at[y], out_gt.at[y])
    gt_y = k.remote(gtb.at[y2], out_gt.at[y], k.py)
    last_back(y2)
    gt_y.start()
    queue[1].s3()
    last_back(y)
    gt_own.start()
    queue[2].s3()
    for index in range(3):
        collect(index)
    table = vtab.reshape(4, 2, 2, 2, 8, 128)
    v0 = k.remote(table.at[:, :, :, c2], vr0, k.pc)
    v1 = k.remote(table.at[:, :, y2, c], vr1, k.py)
    v2 = k.remote(table.at[:, x2, y, c], vr2, k.px)
    v3 = [k.remote(table.at[k.zs[d], x, y, c], vr3.at[d], k.pz[d]) for d in range(3)]

    def tile(zz, xx, yy):
        return rows_at((((zz * 2 + xx) * 2 + yy) * 2 + c) * 8, 8, 8)

    v0.start()
    queue[0].s4()
    v0.wait_recv()

    def add_core(i, carry):
        zz, xx, yy = i // 4, lax.rem(i // 2, 2), lax.rem(i, 2)
        vtab[tile(zz, xx, yy), :] += vr0[zz, xx, yy]
        return carry

    lax.fori_loop(0, 16, add_core, 0)
    v1.start()
    for copy in k.sent[:gathered]:
        copy.wait_send()
    up[1].s4()
    queue[1].s4()
    v1.wait_recv()

    def add_y(i, carry):
        vtab[tile(i // 2, lax.rem(i, 2), y), :] += vr1[i // 2, lax.rem(i, 2)]
        return carry

    lax.fori_loop(0, 8, add_y, 0)
    v2.start()
    outp.s4()
    up[0].s5()
    queue[0].s5()
    v2.wait_recv()

    def add_x(zz, carry):
        vtab[tile(zz, x, y), :] += vr2[zz]
        return carry

    lax.fori_loop(0, 4, add_x, 0)
    start(v3)
    queue[2].s4()
    up[1].s5()
    outp.s5()
    queue[1].s5()
    queue[2].s5()
    arrive(v3)
    out_vec[...] = vtab[tile(z, x, y), :] + vr3[0] + vr3[1] + vr3[2]
    landed([gt_own, bo_own])
    arrive([gt_y, bo_y])
    for copy in k.sent[gathered:]:
        copy.wait_send()
    assert k.remotes <= REMOTES and k.locals <= LOCALS


def layer_call(*operands):
    sds = jax.ShapeDtypeStruct
    vmem = pltpu.VMEM
    dma = pltpu.SemaphoreType.DMA
    results = (
        sds((2, 256, D), BF), sds((2, 256, D), BF), sds((24, 3 * D), F32), sds((24, D), F32), sds((24, FF), F32),
        sds((96, D), F32), sds((8, 128), F32),
    )
    held = (
        sds((3, 4, 2, 2, 48, 384), BF), sds((2, 4, 2, 2, 48, 384), BF), sds((2, 2, 4, 2, 2, 48, 768), BF),
        sds((2, 4, 2, 2, 192, 384), BF), sds((4, 2, 2, 2, 8, 128), F32), sds((THIRD, 1024), BF),
        sds((1024, THIRD), BF), sds((1024, THIRD), BF), sds((THIRD, 1024), F32), sds((D, 1024), BF),
    )
    scratch = [
        vmem((8, 128), F32), vmem((2, 3, 24, THIRD), BF), vmem((4, 2, 2, 2, 8, 128), F32), vmem((2, 2, 256, D), BF), vmem((8, FF), F32),
        vmem((2, D, THIRD), BF), vmem((2, 2, 256, THIRD), BF), vmem((2, 256, D), BF), vmem((2, 256, D), BF),
        vmem((2, 256, D), BF), vmem((2, 2, 256, THIRD), BF), vmem((2, 256, D), F32), vmem((2, 256, D), F32),
        vmem((2, 256, D), F32), vmem((2, 256, D), F32), vmem((8, 1024), F32),
    ]
    scratch += [
        vmem((2, 4, 2, 2, 192, 384), BF), vmem((2, 2, 4, 2, 2, 48, 768), BF), vmem((2, 4, 2, 2, 48, 384), BF),
        vmem((3, 4, 2, 2, 48, 384), BF),
        vmem((8, D), F32), vmem((1, 3 * D), F32), vmem((1, FF), F32), vmem((256, 128), F32), vmem((4, 2, 2, 8, 128), F32),
        vmem((4, 2, 8, 128), F32), vmem((4, 8, 128), F32), vmem((3, 8, 128), F32),
        dma((REMOTES,)), dma((REMOTES,)), dma((LOCALS,)),
    ]
    for name in ("down", "up0", "up1", "out", "q0", "q1", "q2"):
        scratch += Scatter.buffers(CUTS[name], not name.startswith("q"))
    return pl.pallas_call(
        layer_kernel,
        out_shape=results + held,
        in_specs=[SM] + [ANY] * 2 + [VM] * 12,
        out_specs=(ANY, ANY) + (VM,) * 5 + (ANY,) * len(held),
        scratch_shapes=scratch,
        compiler_params=pltpu.CompilerParams(
            collective_id=0, has_side_effects=True, vmem_limit_bytes=63 * 2**20),
    )(*operands)[: len(results)]


def finish_kernel(*refs):
    sources, results, (table, sems) = refs[:7], refs[7:21], refs[21:]
    copies = [pltpu.make_async_copy(source, result, sems.at[i])
              for i, (source, result) in enumerate(zip(sources, results[:6] + (table,)))]
    start(copies)
    landed(copies)
    for index, wide in enumerate(WIDTHS):
        results[6 + index][...] = table[index, 0:wide]


def finish_call(*operands):
    sds = jax.ShapeDtypeStruct
    shapes = tuple(sds(o.shape, o.dtype) for o in operands[:6]) + tuple(sds((wide,), F32) for wide in WIDTHS)
    return pl.pallas_call(
        finish_kernel, out_shape=shapes, in_specs=[ANY] * 7, out_specs=(VM,) * 14,
        scratch_shapes=[pltpu.VMEM((8, 128), F32), pltpu.SemaphoreType.DMA((7,))],
        compiler_params=pltpu.CompilerParams(vmem_limit_bytes=60 * 2**20),
    )(*operands)


def body(
    tokens, cotangent, prefix, ln1_gain, ln1_bias, w_qkv, b_qkv, w_out, b_out,
    ln2_gain, ln2_bias, w_up, b_up, w_down, b_down,
):
    results = layer_call(
        prefix, tokens, cotangent, ln1_gain, ln1_bias, b_qkv, b_out, ln2_gain, ln2_bias, b_up, b_down,
        w_qkv, w_out, w_up, w_down)
    block_out, grad_tokens, gq, go, gu, gd, *rows = finish_call(*results)
    return (
        block_out, grad_tokens, rows[0], rows[1], gq, rows[2], go, rows[3], rows[4], rows[5], gu, rows[6], gd, rows[7],
    )


def fits(mesh):
    return dict(mesh.shape) == {"dp": 8, "seq": 4}


norm_eps = 1e-05
block_rows = 512


def layer_norm(features, gain, shift):
    centre = features - jnp.mean(features, axis=-1, keepdims=True)
    spread = jnp.mean(centre * centre, axis=-1, keepdims=True)
    return centre * lax.rsqrt(spread + norm_eps) * gain + shift


def gelu_tanh(values):
    return jax.nn.gelu(values, approximate=True)


def in_blocks(update, running, pieces):
    length = pieces[0].shape[1]
    blocks = length // block_rows
    blocked_pieces = tuple(
        (
            jnp.swapaxes(
                member.reshape((member.shape[0], blocks, block_rows) + member.shape[2:]), 0, 1
            )
            for member in pieces
        )
    )

    def advance(carried, element):
        return (update(carried, element[0], element[1] * block_rows), None)

    running, unused = lax.scan(
        advance, running, (blocked_pieces, jnp.arange(blocks, dtype=jnp.int32))
    )
    return running


def to_heads(flat_rows):
    return flat_rows.reshape(flat_rows.shape[0], flat_rows.shape[1], HEADS, HEAD_DIM)


def visible_mask(query_places, key_places, prefix_len):
    earlier = key_places[None, None, :] <= query_places[None, :, None]
    in_prefix = key_places[None, None, :] < prefix_len[:, None, None]
    return (earlier | in_prefix)[:, :, None, :]


def head_scores(query_heads, key_flat):
    return jnp.einsum(
        "bqhd,bkhd->bqhk", query_heads, to_heads(key_flat), preferred_element_type=jnp.float32
    ) * HEAD_DIM ** (-0.5)


def attend(query_heads, key_flat, value_flat, prefix_len):
    local_len = query_heads.shape[1]
    query_places = lax.axis_index("seq") * local_len + jnp.arange(local_len, dtype=jnp.int32)
    starting = (
        jnp.zeros(query_heads.shape, jnp.float32),
        jnp.zeros(query_heads.shape[:3], jnp.float32),
        jnp.zeros(query_heads.shape[:3], jnp.float32),
    )

    def update(running, pieces, offset):
        weighted, normaliser, ceiling = running
        key_piece, value_piece = pieces
        key_places = offset + jnp.arange(key_piece.shape[1], dtype=jnp.int32)
        scores = head_scores(query_heads, key_piece)
        visible = visible_mask(query_places, key_places, prefix_len)
        magnitude = jnp.where(visible, jnp.abs(scores), 0.0)
        new_ceiling = jnp.maximum(ceiling, jnp.max(magnitude, axis=-1))
        exponent = jnp.where(visible, jnp.exp(magnitude - new_ceiling[..., None]), 0.0)
        factor = jnp.exp(ceiling - new_ceiling)
        weights = (jnp.sign(scores) * exponent).astype(jnp.bfloat16)
        weighted = weighted * factor[..., None] + jnp.einsum(
            "bqhk,bkhd->bqhd", weights, to_heads(value_piece), preferred_element_type=jnp.float32
        )
        normaliser = normaliser * factor + jnp.sum(exponent, axis=-1)
        return (weighted, normaliser, new_ceiling)

    weighted, normaliser, ceiling = in_blocks(
        update,
        starting,
        (
            lax.all_gather(key_flat, "seq", axis=1, tiled=True),
            lax.all_gather(value_flat, "seq", axis=1, tiled=True),
        ),
    )
    return (weighted / normaliser[..., None], ceiling + jnp.log(normaliser))


def grad_terms(
    query_heads,
    grad_heads,
    key_flat,
    value_flat,
    log_total,
    delta_sum,
    query_places,
    key_places,
    prefix_len,
):
    scores = head_scores(query_heads, key_flat)
    sign_of = jnp.sign(scores)
    visible = visible_mask(query_places, key_places, prefix_len)
    shares = jnp.where(visible, jnp.exp(jnp.abs(scores) - log_total[..., None]), 0.0)
    grad_weights = jnp.einsum(
        "bqhd,bkhd->bqhk", grad_heads, to_heads(value_flat), preferred_element_type=jnp.float32
    )
    grad_scores = (shares * (grad_weights - sign_of * delta_sum[..., None])).astype(jnp.bfloat16)
    return ((sign_of * shares).astype(jnp.bfloat16), grad_scores)


def query_term(grad_scores, key_flat):
    return jnp.einsum(
        "bqhk,bkhd->bqhd", grad_scores, to_heads(key_flat), preferred_element_type=jnp.float32
    ) * HEAD_DIM ** (-0.5)


def key_value_terms(query_heads, grad_heads, shares_low, grad_scores):
    key_term = jnp.einsum(
        "bqhk,bqhd->bkhd", grad_scores, query_heads, preferred_element_type=jnp.float32
    ) * HEAD_DIM ** (-0.5)
    value_term = jnp.einsum(
        "bqhk,bqhd->bkhd", shares_low, grad_heads, preferred_element_type=jnp.float32
    )
    flat_shape = (key_term.shape[0], key_term.shape[1], key_term.shape[2] * key_term.shape[3])
    return jnp.concatenate([key_term.reshape(flat_shape), value_term.reshape(flat_shape)], axis=-1)


def attend_back(query_heads, key_flat, value_flat, grad_heads, log_total, delta_sum, prefix_len):
    seq_block, local_len = (query_heads.shape[0], query_heads.shape[1])
    width = key_flat.shape[2]
    local_places = lax.axis_index("seq") * local_len + jnp.arange(local_len, dtype=jnp.int32)
    starting = (
        jnp.zeros(query_heads.shape, jnp.float32),
        jnp.zeros((seq_block, lax.axis_size("seq") * local_len, 2 * width), jnp.float32),
    )

    def update_both(running, pieces, offset):
        grad_query, grad_keys = running
        key_piece, value_piece = pieces
        piece_len = key_piece.shape[1]
        key_places = offset + jnp.arange(piece_len, dtype=jnp.int32)
        shares_low, grad_scores = grad_terms(
            query_heads,
            grad_heads,
            key_piece,
            value_piece,
            log_total,
            delta_sum,
            local_places,
            key_places,
            prefix_len,
        )
        grad_query = grad_query + query_term(grad_scores, key_piece)
        current = lax.dynamic_slice_in_dim(grad_keys, offset, piece_len, 1)
        updated = current + key_value_terms(query_heads, grad_heads, shares_low, grad_scores)
        return (grad_query, lax.dynamic_update_slice_in_dim(grad_keys, updated, offset, 1))

    grad_query, grad_keys = in_blocks(
        update_both,
        starting,
        (
            lax.all_gather(key_flat, "seq", axis=1, tiled=True),
            lax.all_gather(value_flat, "seq", axis=1, tiled=True),
        ),
    )
    key_local = lax.psum_scatter(
        grad_keys.astype(jnp.bfloat16), "seq", scatter_dimension=1, tiled=True
    ).astype(jnp.float32)
    return (grad_query, key_local)


def forward_block(weights_in, token_part, prefix_len):
    (
        gain_one,
        shift_one,
        w_qkv,
        b_qkv,
        w_out,
        b_out,
        gain_two,
        shift_two,
        w_up,
        b_up,
        w_down,
        b_down,
    ) = weights_in
    seq_block, local_len, width = token_part.shape
    residual_in = token_part.reshape(-1, width).astype(jnp.float32)
    normed_one = layer_norm(
        residual_in, gain_one.astype(jnp.float32), shift_one.astype(jnp.float32)
    ).astype(jnp.bfloat16)
    projected = jnp.dot(normed_one, w_qkv, preferred_element_type=jnp.float32) + b_qkv.astype(
        jnp.float32
    )
    query_heads = (
        projected[:, :width].astype(jnp.bfloat16).reshape(seq_block, local_len, HEADS, HEAD_DIM)
    )
    key_flat = (
        projected[:, width : 2 * width].astype(jnp.bfloat16).reshape(seq_block, local_len, width)
    )
    value_flat = projected[:, 2 * width :].astype(jnp.bfloat16).reshape(seq_block, local_len, width)
    attended, log_total = attend(query_heads, key_flat, value_flat, prefix_len)
    attended_low = attended.reshape(-1, width).astype(jnp.bfloat16)
    residual_mid = (
        residual_in
        + jnp.dot(attended_low, w_out, preferred_element_type=jnp.float32)
        + b_out.astype(jnp.float32)
    )
    normed_two = layer_norm(
        residual_mid, gain_two.astype(jnp.float32), shift_two.astype(jnp.float32)
    ).astype(jnp.bfloat16)
    pre_gelu = jnp.dot(normed_two, w_up, preferred_element_type=jnp.float32) + b_up.astype(
        jnp.float32
    )
    hidden = gelu_tanh(pre_gelu).astype(jnp.bfloat16)
    result = (
        residual_mid
        + jnp.dot(hidden, w_down, preferred_element_type=jnp.float32)
        + b_down.astype(jnp.float32)
    )
    saved = (
        residual_in,
        normed_one,
        query_heads,
        key_flat,
        value_flat,
        attended,
        log_total,
        attended_low,
        residual_mid,
        normed_two,
        pre_gelu,
        hidden,
    )
    return (result.astype(jnp.bfloat16).reshape(token_part.shape), saved)


def backward_block(weights_in, saved, grad_part, prefix_len):
    (
        gain_one,
        shift_one,
        w_qkv,
        b_qkv,
        w_out,
        b_out,
        gain_two,
        shift_two,
        w_up,
        b_up,
        w_down,
        b_down,
    ) = weights_in
    (
        residual_in,
        normed_one,
        query_heads,
        key_flat,
        value_flat,
        attended,
        log_total,
        attended_low,
        residual_mid,
        normed_two,
        pre_gelu,
        hidden,
    ) = saved
    seq_block, local_len, width = grad_part.shape
    grad_result = grad_part.reshape(-1, width).astype(jnp.float32)
    grad_branch = grad_part.reshape(-1, width)
    grads_down = jnp.einsum("rf,rd->fd", hidden, grad_branch, preferred_element_type=jnp.float32)
    bias_down = jnp.sum(grad_branch, axis=0, dtype=jnp.float32)
    grad_hidden = jnp.einsum("rd,fd->rf", grad_branch, w_down, preferred_element_type=jnp.float32)
    gelu_pull = jax.vjp(gelu_tanh, pre_gelu)[1]
    grad_pre = gelu_pull(grad_hidden)[0].astype(jnp.bfloat16)
    grads_up = jnp.einsum("rd,rf->df", normed_two, grad_pre, preferred_element_type=jnp.float32)
    bias_up = jnp.sum(grad_pre, axis=0, dtype=jnp.float32)
    grad_normed_two = jnp.einsum("rf,df->rd", grad_pre, w_up, preferred_element_type=jnp.float32)
    norm_two_pull = jax.vjp(
        layer_norm, residual_mid, gain_two.astype(jnp.float32), shift_two.astype(jnp.float32)
    )[1]
    grad_mid, grads_gain_two, grads_shift_two = norm_two_pull(grad_normed_two)
    grad_mid = grad_mid + grad_result
    grad_attn = grad_mid.astype(jnp.bfloat16)
    grads_out = jnp.einsum("rd,re->de", attended_low, grad_attn, preferred_element_type=jnp.float32)
    bias_out = jnp.sum(grad_attn, axis=0, dtype=jnp.float32)
    grad_heads = (
        jnp.einsum("re,de->rd", grad_attn, w_out, preferred_element_type=jnp.float32)
        .astype(jnp.bfloat16)
        .reshape(seq_block, local_len, HEADS, HEAD_DIM)
    )
    delta_sum = jnp.sum(grad_heads.astype(jnp.float32) * attended, axis=-1)
    grad_query, key_local = attend_back(
        query_heads, key_flat, value_flat, grad_heads, log_total, delta_sum, prefix_len
    )
    grad_proj = jnp.concatenate(
        [grad_query.reshape(-1, width), key_local.reshape(-1, 2 * width)], axis=1
    ).astype(jnp.bfloat16)
    grads_qkv = jnp.einsum("rd,re->de", normed_one, grad_proj, preferred_element_type=jnp.float32)
    bias_qkv = jnp.sum(grad_proj, axis=0, dtype=jnp.float32)
    grad_normed_one = jnp.einsum("re,de->rd", grad_proj, w_qkv, preferred_element_type=jnp.float32)
    norm_one_pull = jax.vjp(
        layer_norm, residual_in, gain_one.astype(jnp.float32), shift_one.astype(jnp.float32)
    )[1]
    grad_in, grads_gain_one, grads_shift_one = norm_one_pull(grad_normed_one)
    grad_in = grad_in + grad_mid
    weight_grads = (
        grads_gain_one,
        grads_shift_one,
        grads_qkv,
        bias_qkv,
        grads_out,
        bias_out,
        grads_gain_two,
        grads_shift_two,
        grads_up,
        bias_up,
        grads_down,
        bias_down,
    )
    return (grad_in.astype(jnp.bfloat16).reshape(grad_part.shape), weight_grads)


def general_body(
    tokens,
    cotangent,
    prefix,
    ln1_gain,
    ln1_bias,
    w_qkv,
    b_qkv,
    w_out,
    b_out,
    ln2_gain,
    ln2_bias,
    w_up,
    b_up,
    w_down,
    b_down,
):
    shards = (
        ln1_gain,
        ln1_bias,
        w_qkv,
        b_qkv,
        w_out,
        b_out,
        ln2_gain,
        ln2_bias,
        w_up,
        b_up,
        w_down,
        b_down,
    )
    spread_count = lax.axis_size(("dp", "seq"))
    totals = tuple(
        (
            jnp.zeros((member.shape[0] * spread_count,) + member.shape[1:], jnp.float32)
            for member in shards
        )
    )
    seq_block = tokens.shape[0] // MB
    outputs = []
    grad_inputs = []
    for batch_index in range(MB):
        first_row = batch_index * seq_block
        token_part = tokens[first_row : first_row + seq_block]
        cotangent_part = cotangent[first_row : first_row + seq_block]
        prefix_part = prefix[first_row : first_row + seq_block]
        forward_weights = (
            lax.all_gather(shards[0], ("dp", "seq"), axis=0, tiled=True),
            lax.all_gather(shards[1], ("dp", "seq"), axis=0, tiled=True),
            lax.all_gather(shards[2], ("dp", "seq"), axis=0, tiled=True),
            lax.all_gather(shards[3], ("dp", "seq"), axis=0, tiled=True),
            lax.all_gather(shards[4], ("dp", "seq"), axis=0, tiled=True),
            lax.all_gather(shards[5], ("dp", "seq"), axis=0, tiled=True),
            lax.all_gather(shards[6], ("dp", "seq"), axis=0, tiled=True),
            lax.all_gather(shards[7], ("dp", "seq"), axis=0, tiled=True),
            lax.all_gather(shards[8], ("dp", "seq"), axis=0, tiled=True),
            lax.all_gather(shards[9], ("dp", "seq"), axis=0, tiled=True),
            lax.all_gather(shards[10], ("dp", "seq"), axis=0, tiled=True),
            lax.all_gather(shards[11], ("dp", "seq"), axis=0, tiled=True),
        )
        result, saved = forward_block(forward_weights, token_part, prefix_part)
        back_weights = (
            lax.all_gather(shards[0], ("dp", "seq"), axis=0, tiled=True),
            lax.all_gather(shards[1], ("dp", "seq"), axis=0, tiled=True),
            lax.all_gather(shards[2], ("dp", "seq"), axis=0, tiled=True),
            lax.all_gather(shards[3], ("dp", "seq"), axis=0, tiled=True),
            lax.all_gather(shards[4], ("dp", "seq"), axis=0, tiled=True),
            lax.all_gather(shards[5], ("dp", "seq"), axis=0, tiled=True),
            lax.all_gather(shards[6], ("dp", "seq"), axis=0, tiled=True),
            lax.all_gather(shards[7], ("dp", "seq"), axis=0, tiled=True),
            lax.all_gather(shards[8], ("dp", "seq"), axis=0, tiled=True),
            lax.all_gather(shards[9], ("dp", "seq"), axis=0, tiled=True),
            lax.all_gather(shards[10], ("dp", "seq"), axis=0, tiled=True),
            lax.all_gather(shards[11], ("dp", "seq"), axis=0, tiled=True),
        )
        grad_piece, weight_grads = backward_block(back_weights, saved, cotangent_part, prefix_part)
        totals = tuple(
            (running_sum + new_term for running_sum, new_term in zip(totals, weight_grads))
        )
        outputs.append(result)
        grad_inputs.append(grad_piece)
    reduced = (
        lax.psum_scatter(totals[0], ("dp", "seq"), scatter_dimension=0, tiled=True),
        lax.psum_scatter(totals[1], ("dp", "seq"), scatter_dimension=0, tiled=True),
        lax.psum_scatter(totals[2], ("dp", "seq"), scatter_dimension=0, tiled=True),
        lax.psum_scatter(totals[3], ("dp", "seq"), scatter_dimension=0, tiled=True),
        lax.psum_scatter(totals[4], ("dp", "seq"), scatter_dimension=0, tiled=True),
        lax.psum_scatter(totals[5], ("dp", "seq"), scatter_dimension=0, tiled=True),
        lax.psum_scatter(totals[6], ("dp", "seq"), scatter_dimension=0, tiled=True),
        lax.psum_scatter(totals[7], ("dp", "seq"), scatter_dimension=0, tiled=True),
        lax.psum_scatter(totals[8], ("dp", "seq"), scatter_dimension=0, tiled=True),
        lax.psum_scatter(totals[9], ("dp", "seq"), scatter_dimension=0, tiled=True),
        lax.psum_scatter(totals[10], ("dp", "seq"), scatter_dimension=0, tiled=True),
        lax.psum_scatter(totals[11], ("dp", "seq"), scatter_dimension=0, tiled=True),
    )
    return (
        jnp.concatenate(outputs, axis=0),
        jnp.concatenate(grad_inputs, axis=0),
        reduced[0],
        reduced[1],
        reduced[2],
        reduced[3],
        reduced[4],
        reduced[5],
        reduced[6],
        reduced[7],
        reduced[8],
        reduced[9],
        reduced[10],
        reduced[11],
    )


def solution(mesh):
    in_specs = (
        P("dp", "seq", None),
        P("dp", "seq", None),
        P("dp"),
        P(("dp", "seq")),
        P(("dp", "seq")),
        P(("dp", "seq"), None),
        P(("dp", "seq")),
        P(("dp", "seq"), None),
        P(("dp", "seq")),
        P(("dp", "seq")),
        P(("dp", "seq")),
        P(("dp", "seq"), None),
        P(("dp", "seq")),
        P(("dp", "seq"), None),
        P(("dp", "seq")),
    )
    out_specs = (
        P("dp", "seq", None),
        P("dp", "seq", None),
        P(("dp", "seq")),
        P(("dp", "seq")),
        P(("dp", "seq"), None),
        P(("dp", "seq")),
        P(("dp", "seq"), None),
        P(("dp", "seq")),
        P(("dp", "seq")),
        P(("dp", "seq")),
        P(("dp", "seq"), None),
        P(("dp", "seq")),
        P(("dp", "seq"), None),
        P(("dp", "seq")),
    )
    chosen = body if fits(mesh) else general_body
    return jax.shard_map(chosen, mesh=mesh, in_specs=in_specs, out_specs=out_specs, check_vma=False)
```

```python
import functools

import jax
import jax.numpy as jnp
from jax import lax
from jax.experimental import pallas as pl
from jax.experimental.pallas import tpu as pltpu
from jax.sharding import PartitionSpec as P

HEADS = 12
HEAD_DIM = 64
MB = 2

F32 = jnp.float32
BF = jnp.bfloat16
EPS = 1e-05
MESH = pl.DeviceIdType.MESH
NEG = -1e30
ANY = pl.BlockSpec(memory_space=pl.ANY)
VM = pl.BlockSpec(memory_space=pltpu.VMEM)
SM = pl.BlockSpec(memory_space=pltpu.SMEM)
WIDTHS = (24, 24, 72, 24, 24, 24, 96, 24)
D = 768
FF = 3072
THIRD = 384
LAST = (((1,), (1,)), ((), ()))
FIRST = (((0,), (0,)), ((), ()))
ALL = slice(None)
REMOTES = 224
LOCALS = 64


def places():
    dp = lax.axis_index("dp")
    sq = lax.axis_index("seq")
    return dp // 2, dp % 2, sq // 2, sq % 2


def device(z, x, y, c):
    return (z * 2 + x, y * 2 + c)


def owner_of(wide):
    column = lax.broadcasted_iota(jnp.int32, (1, 32 * wide), 1).astype(F32)
    owner = jnp.floor((column + 0.5) * (1.0 / wide))
    return owner.astype(jnp.int32), (column - owner * wide).astype(jnp.int32)


def spread_row(gathered, index, wide):
    total = 32 * wide
    row = lax.broadcasted_iota(jnp.int32, (32, 256), 0)
    place = lax.broadcasted_iota(jnp.int32, (32, 256), 1)
    pick = jnp.where(place == row * 8 + index, 1.0, 0.0).astype(BF)
    mine = jnp.dot(pick, gathered, preferred_element_type=F32).astype(BF)
    owner, rest = owner_of(wide)
    spread = jnp.where(lax.broadcasted_iota(jnp.int32, (128, total), 0) == rest, 1.0, 0.0).astype(BF)
    full = jnp.dot(mine, spread, preferred_element_type=F32)
    keep = lax.broadcasted_iota(jnp.int32, (32, total), 0) == owner
    return jnp.sum(jnp.where(keep, full, 0.0), axis=0, keepdims=True)


def collect_rows(vector, wide):
    total = 32 * wide
    owner, rest = owner_of(wide)
    gather = jnp.where(lax.broadcasted_iota(jnp.int32, (128, total), 0) == rest, 1.0, 0.0).astype(BF)
    keep = lax.broadcasted_iota(jnp.int32, (32, total), 0) == owner
    high = vector.astype(BF).astype(F32)
    out = None
    for part in (high, vector - high):
        placed = jnp.where(keep, part, 0.0).astype(BF)
        term = lax.dot_general(placed, gather, LAST, preferred_element_type=F32)
        out = term if out is None else out + term
    return out


def add_into(ref, at, other):
    ref[at] = (ref[at].astype(F32) + other.astype(F32)).astype(BF)


def start(copies):
    for copy in copies:
        copy.start()


def arrive(copies):
    for copy in copies:
        copy.wait_recv()


def landed(copies):
    for copy in copies:
        copy.wait()


def lanes(first, count=128):
    return pl.ds(pl.multiple_of(first, 128), count)


def rows_at(first, count, step=256):
    return pl.ds(pl.multiple_of(first, step), count)


class Cut:
    def __init__(self, rows, columns, a, upto=None, upto_row=None):
        first = slice(0, upto_row or rows)
        end = upto or columns
        self.rows, self.columns = rows, columns
        self.a = (first, slice(0, a))
        self.b = (first, slice(a, end))
        self.ab = (first, slice(0, end))
        self.f = None
        self.axis = 0 if upto_row else 1
        if upto:
            self.f = (slice(0, rows), slice(upto, columns))
        if upto_row:
            self.a = (slice(0, upto_row // 2), slice(0, columns))
            self.b = (slice(upto_row // 2, upto_row), slice(0, columns))
            self.f = (slice(upto_row, rows), slice(0, columns))

    def shape(self, part):
        return tuple(side.stop - side.start for side in part)


CUTS = {
    "down": Cut(192, 384, 128, upto_row=160), "up0": Cut(48, 768, 256, upto=640), "up1": Cut(48, 768, 128, upto=640),
    "out": Cut(48, 384, 128), "q0": Cut(48, 384, 128), "q1": Cut(48, 384, 128), "q2": Cut(48, 384, 128),
}


class Links:
    def __init__(self, ssem, rsem, lsem):
        self.ssem, self.rsem, self.lsem = ssem, rsem, lsem
        self.remotes = self.locals = 0
        self.sent = []
        z, x, y, c = places()
        self.z, self.x, self.y, self.c = z, x, y, c
        self.x2, self.y2, self.c2 = 1 - x, 1 - y, 1 - c
        self.px, self.py, self.pc = device(z, 1 - x, y, c), device(z, x, 1 - y, c), device(z, x, y, 1 - c)
        self.zs = [lax.rem(z + d, 4) for d in (1, 2, 3)]
        self.pz = [device(zz, x, y, c) for zz in self.zs]

    def remote(self, src, dst, dev):
        i = self.remotes
        self.remotes += 1
        copy = pltpu.make_async_remote_copy(
            src_ref=src, dst_ref=dst, send_sem=self.ssem.at[i], recv_sem=self.rsem.at[i],
            device_id=dev, device_id_type=MESH)
        self.sent.append(copy)
        return copy

    def local(self, src, dst):
        i = self.locals
        self.locals += 1
        return pltpu.make_async_copy(src, dst, self.lsem.at[i])

    def greet(self):
        barrier = pltpu.get_barrier_semaphore()
        for dev in [self.px, self.py, self.pc] + self.pz:
            pl.semaphore_signal(barrier, inc=1, device_id=dev, device_id_type=MESH)

    def greeted(self):
        pl.semaphore_wait(pltpu.get_barrier_semaphore(), 6)


class Gather:
    def __init__(self, links, own, other, mine, theirs, cut, whole=True):
        k = links
        rows = own.shape[0]
        at = pl.ds(pl.multiple_of(k.c * rows, 8), rows)
        z, x, y = k.z, k.x, k.y
        self.own = [k.local(own, mine.at[z, x, y, at])]
        self.c0 = [k.remote(other, theirs.at[z, x, y, at], k.pc)]
        a, b, ab, f = cut.a, cut.b, cut.ab, cut.f

        def send(place, dev):
            return k.remote(mine.at[place], mine.at[place], dev)

        self.c1 = [send((z, x, y) + ab, dev) for dev in k.pz]
        self.c2 = [send((ALL, x, y) + a, k.px), send((ALL, x, y) + b, k.py)]
        self.c3 = [send((ALL, ALL, y) + a, k.py), send((ALL, x, ALL) + b, k.px)]
        if f:
            self.c1.append(send((z, x, y) + f, k.py))
            self.c2.append(send((z, x, ALL) + f, k.px))
            self.c3 += [send((z, ALL, ALL) + f, dev) for dev in k.pz]
        self.c4 = [k.remote(mine, mine, k.pc)] if whole else []

    def s0(self):
        start(self.c0)

    def s1(self):
        landed(self.own)
        arrive(self.c0)
        start(self.c1)

    def s2(self):
        arrive(self.c1)
        start(self.c2)

    def s3(self):
        arrive(self.c2)
        start(self.c3)

    def s4(self):
        arrive(self.c3)
        start(self.c4)

    def done(self):
        arrive(self.c4)


class Scatter:
    @staticmethod
    def buffers(cut, whole):
        block = (cut.rows, cut.columns)
        a, b, ab = cut.shape(cut.a), cut.shape(cut.b), cut.shape(cut.ab)
        low = [(4, 2, 2) + block] if whole else []
        low += [(4, 2) + a, (4, 2) + b, (4,) + a, (4,) + b, (3,) + ab]
        if cut.f:
            f = cut.shape(cut.f)
            low += [(3, 2, 2) + f, (2,) + f, f]
        half = (cut.rows // 2, cut.columns)
        return [pltpu.VMEM(shape, BF) for shape in low] + [pltpu.VMEM((2,) + half, F32), pltpu.VMEM(half, F32)]

    def __init__(self, links, grad, prefix, other, cut, work, put):
        k = links
        self.k, self.grad, self.prefix, self.cut, self.put = k, grad, prefix, cut, put
        self.whole = other is not None
        mine = self.mine = grad.at[prefix]
        if self.whole:
            self.r0 = next(work)
            self.c0 = [k.remote(grad.at[other], self.r0, k.pc)]
        else:
            self.c0 = []
        self.r1a, self.r1b, self.r2a, self.r2b, self.r3 = [next(work) for _ in range(5)]
        z, x, y, x2, y2 = k.z, k.x, k.y, k.x2, k.y2
        a, b, ab, f = cut.a, cut.b, cut.ab, cut.f
        self.c1 = [k.remote(mine.at[(ALL, ALL, y2) + a], self.r1a, k.py), k.remote(mine.at[(ALL, x2, ALL) + b], self.r1b, k.px)]
        self.c2 = [k.remote(mine.at[(ALL, x2, y) + a], self.r2a, k.px), k.remote(mine.at[(ALL, x, y2) + b], self.r2b, k.py)]
        self.c3 = [k.remote(mine.at[(k.zs[d], x, y) + ab], self.r3.at[d], k.pz[d]) for d in range(3)]
        if f:
            self.rf1, self.rf2, self.rf3 = [next(work) for _ in range(3)]
            self.c1 += [k.remote(mine.at[(k.zs[d], ALL, ALL) + f], self.rf1.at[d], k.pz[d]) for d in range(3)]
            self.c2.append(k.remote(mine.at[(z, x2, ALL) + f], self.rf2, k.px))
            self.c3.append(k.remote(mine.at[(z, x, y2) + f], self.rf3, k.py))
        self.tot, self.fin = next(work), next(work)
        self.c4 = [k.remote(self.tot.at[k.c2], self.fin, k.pc)]

    def at(self, place):
        return self.prefix + place

    def s0(self):
        start(self.c0)

    def s1(self):
        if self.whole:
            arrive(self.c0)

            def add(i, carry):
                where = (i // 4, lax.rem(i // 2, 2), lax.rem(i, 2))
                add_into(self.grad, self.at(where), self.r0[where])
                return carry

            lax.fori_loop(0, 16, add, 0)
        start(self.c1)

    def s2(self):
        arrive(self.c1)
        k, cut = self.k, self.cut

        def add(i, carry):
            zz, other = i // 2, lax.rem(i, 2)
            add_into(self.grad, self.at((zz, other, k.y) + cut.a), self.r1a[zz, other])
            add_into(self.grad, self.at((zz, k.x, other) + cut.b), self.r1b[zz, other])
            return carry

        lax.fori_loop(0, 8, add, 0)
        if cut.f:
            def add_f(i, carry):
                xx, yy = i // 2, lax.rem(i, 2)
                three = self.rf1[0, xx, yy].astype(F32) + self.rf1[1, xx, yy].astype(F32) + self.rf1[2, xx, yy].astype(F32)
                add_into(self.grad, self.at((k.z, xx, yy) + cut.f), three)
                return carry

            lax.fori_loop(0, 4, add_f, 0)
        start(self.c2)

    def s3(self):
        arrive(self.c2)
        k, cut = self.k, self.cut

        def add(zz, carry):
            add_into(self.grad, self.at((zz, k.x, k.y) + cut.a), self.r2a[zz])
            add_into(self.grad, self.at((zz, k.x, k.y) + cut.b), self.r2b[zz])
            return carry

        lax.fori_loop(0, 4, add, 0)
        if cut.f:
            for yy in range(2):
                add_into(self.grad, self.at((k.z, k.x, yy) + cut.f), self.rf2[yy])
        start(self.c3)

    def s4(self):
        arrive(self.c3)
        k, cut = self.k, self.cut
        total = self.mine[(k.z, k.x, k.y) + cut.ab].astype(F32)
        for d in range(3):
            total = total + self.r3[d].astype(F32)
        if cut.f:
            rest = self.mine[(k.z, k.x, k.y) + cut.f].astype(F32) + self.rf3[...].astype(F32)
            total = jnp.concatenate([total, rest], axis=cut.axis)
        rows = total.shape[0] // 2
        self.tot[0] = total[:rows]
        self.tot[1] = total[rows:]
        start(self.c4)
        self.put(self.tot[k.c], k.c)

    def s5(self):
        arrive(self.c4)
        self.put(self.fin[...], self.k.c2)


def sign_of(value):
    return jnp.clip(value * 1e38, -1.0, 1.0)


def masked(size, seen, low):
    last = jnp.where(seen, size[low:], NEG)
    return last if low == 0 else jnp.concatenate([size[:low], last], axis=0)


def gelu_parts(value):
    rate = 0.7978845608028654
    bent = jnp.tanh(rate * (value + 0.044715 * (value * value * value)))
    result = 0.5 * value * (1.0 + bent)
    slope = 0.5 * (1.0 + bent) + 0.5 * value * (1.0 - bent * bent) * (rate * (1.0 + 0.134145 * (value * value)))
    return result, slope


def unit_rows(rows):
    centre = rows - jnp.mean(rows, axis=-1, keepdims=True)
    scale = lax.rsqrt(jnp.mean(centre * centre, axis=-1, keepdims=True) + EPS)
    return centre * scale, scale


def norm_back(grad, normed, scale):
    return scale * (grad - jnp.mean(grad, axis=-1, keepdims=True)
                    - normed * jnp.mean(grad * normed, axis=-1, keepdims=True))


def layer_kernel(
    prefix, tok, cot, v0_s, v1_s, v2_s, v3_s, v4_s, v5_s, v6_s, v7_s, wq_s, wo_s, wu_s, wd_s,
    out_bo, out_gt, out_q, out_o, out_u, out_d, out_vec,
    wq, wo, wu, wd, gv, k_qst, k_k, k_v, k_att, k_n1t,
    vec_s, wq_p, gvm, tok_all, vrows, wom, al_send, al, cotm, ga_send, ga_all, fa, fb, fc, fr, lt,
    gd, gu, go, gq,
    vs, vbq, vup, vtab, vr0, vr1, vr2, vr3,
    ssem, rsem, lsem, *work,
):
    k = Links(ssem, rsem, lsem)
    bo, gtb = al, cotm
    work = iter(work)
    z, x, y, c, x2, y2, c2 = k.z, k.x, k.y, k.c, k.x2, k.y2, k.c2
    k.greet()
    vmem = pltpu.VMEM

    vec_s[...] = jnp.zeros_like(vec_s)
    for index, (wide, ref) in enumerate(zip(WIDTHS, (v0_s, v1_s, v2_s, v3_s, v4_s, v5_s, v6_s, v7_s))):
        vec_s[index : index + 1, 0:wide] = ref[...].astype(F32).reshape(1, wide)
    for core in range(2):
        for u in range(3):
            for kind in range(3):
                first = kind * D + core * THIRD + u * 128
                wq_p[core, u, :, kind * 128 : (kind + 1) * 128] = wq_s[:, first : first + 128]
    gather_q = [Gather(k, wq_p.at[c, u], wq_p.at[c2, u], wq.at[u], wq.at[u], CUTS[f"q{u}"], False)
                for u in range(3)]

    def halves(shard, full, cut):
        half = full.shape[-1]
        return Gather(k, shard.at[:, lanes(c * half, half)], shard.at[:, lanes(c2 * half, half)], full.at[c], full.at[c2], cut)

    gather_o = halves(wo_s, wo, CUTS["out"])
    gather_d = halves(wd_s, wd, CUTS["down"])
    k.sent.pop()
    gather_d.c4 = [k.remote(wd.at[c, zz], wd.at[c, zz], k.pc) for zz in (2 * c, 2 * c + 1, 2 * c2, 2 * c2 + 1)]
    gather_u = [Gather(k, wu_s.at[:, lanes(c * 1536 + part * D, D)], wu_s.at[:, lanes(c2 * 1536 + part * D, D)],
                       wu.at[c, part], wu.at[c2, part], CUTS[f"up{part}"]) for part in range(2)]
    own_vec = k.local(vec_s, gv.at[z, x, y, c])
    own_tok = k.local(tok.at[y], tok_all.at[y, c])
    own_cot = k.local(cot.at[y], cotm.at[y])
    own_vec.start()
    start(gather_q[0].own)
    own_tok.start()
    others = [gather_q[1], gather_q[2], gather_o] + gather_u + [gather_d]
    for gather in others:
        start(gather.own)
    own_cot.start()
    k.greeted()

    vec_c = k.remote(vec_s, gv.at[z, x, y, c], k.pc)
    tok_y = k.remote(tok.at[y2], tok_all.at[y, c], k.py)
    cot_y = k.remote(cot.at[y2], cotm.at[y], k.py)
    vec_c.start()
    gather_q[0].s0()
    tok_y.start()
    for gather in others:
        gather.s0()
    own_vec.wait()
    vec_c.wait_recv()
    vec_z = [k.remote(gv.at[z, x, y], gv.at[z, x, y], dev) for dev in k.pz]
    start(vec_z)
    gather_q[0].s1()
    gather_q[1].s1()
    own_tok.wait()
    arrive(vec_z)
    vec_x = k.remote(gv.at[:, x, y], gv.at[:, x, y], k.px)
    vec_x.start()
    gather_q[0].s2()
    gather_q[2].s1()
    vec_x.wait_recv()
    vec_y = k.remote(gv.at[:, :, y], gv.at[:, :, y], k.py)
    vec_y.start()
    gather_q[1].s2()
    gather_o.s1()
    gather_q[0].s3()
    tok_y.wait_recv()
    tok_c = k.remote(tok_all.at[:, c], tok_all.at[:, c], k.pc)
    tok_c.start()
    gather_q[2].s2()
    gather_u[0].s1()
    vec_y.wait_recv()
    table = k.local(gv, gvm)
    table.start()
    table.wait()
    table = gvm[...].reshape(256, 128).astype(BF)
    for index, wide in enumerate(WIDTHS):
        vrows[index : index + 1, 0 : 32 * wide] = spread_row(table, index, wide)
    gather_q[1].s3()
    tok_c.wait_recv()

    mine_cols = lanes(c * THIRD, THIRD)
    peer_cols = lanes(c2 * THIRD, THIRD)
    al_own = k.local(al_send.at[:, c], al.at[:, :, mine_cols])
    al_c = k.remote(al_send.at[:, c2], al.at[:, :, mine_cols], k.pc)
    gathered = len(k.sent)
    limit = prefix[y] - 1
    sub = lax.broadcasted_iota(jnp.int32, (128, 256), 0)
    wq3 = wq.reshape(3, D, THIRD)

    def forward(n1, n1t, vt, qst, keys_ref, values_ref, att, wqm):
        gain = vrows[0:1, 0:D]
        shift = vrows[1:2, 0:D]

        def norm_block(b, carry):
            normed, _ = unit_rows(tok_all[b // 2, lax.rem(b, 2)].astype(F32))
            normed = (normed * gain + shift).astype(BF)
            at = rows_at(b * 256, 256)
            n1[at, :] = normed
            n1t[:, at] = normed.astype(F32).T.astype(BF)
            return carry

        lax.fori_loop(0, 4, norm_block, 0)
        keep = [k.local(n1t, k_n1t), k.local(qst, k_qst), k.local(keys_ref, k_k),
                k.local(values_ref, k_v), k.local(att, k_att)]
        keep[0].start()
        load_q = [k.local(wq3.at[u], wqm.at[u]) for u in range(3)]
        load_o = k.local(wo.reshape(2, D, THIRD), wom)

        def head(u):
            gather_q[u].s4()
            load_q[u].start()
            load_q[u].wait()

        slots = {
            (0, 3): [gather_q[2].s3, gather_o.s2, gather_u[1].s1], (0, 2): [gather_u[0].s2],
            (0, 1): [gather_o.s3, gather_d.s1], (0, 0): [gather_u[1].s2],
            (1, 3): [gather_u[0].s3], (1, 2): [gather_o.s4], (1, 1): [gather_d.s2], (1, 0): [gather_u[1].s3],
            (2, 3): [gather_o.done, load_o.start, gather_u[0].s4], (2, 2): [cot_y.start], (2, 1): [gather_d.s3], (2, 0): [],
        }

        def unit(u, carry):
            cols = lanes(u * 128)
            for which in range(3):
                @pl.when(u == which)
                def _():
                    head(which)

            def project(b, inner):
                rows = rows_at(b * 512, 512)
                value = jnp.dot(n1[rows, :], wqm[u], preferred_element_type=F32)
                parts = []
                for kind in range(3):
                    bias = vrows[2:3, lanes(kind * D + c * THIRD + u * 128)]
                    parts.append((value[:, kind * 128 : (kind + 1) * 128] + bias).astype(BF))
                queries = parts[0].astype(F32) * 0.125
                qst[cols, rows] = queries.T.astype(BF)
                keys_ref[rows, cols] = parts[1]
                values_ref[rows, cols] = parts[2]
                vt[cols, rows] = parts[2].astype(F32).T.astype(BF)
                return inner

            lax.fori_loop(0, 2, project, 0)
            for block in (3, 2, 1, 0):
                attend(u, block)
                for which in range(3):
                    if slots[which, block]:
                        @pl.when(u == which)
                        def _():
                            for step in slots[which, block]:
                                step()
            return carry

        def attend(u, block):
            rows = min(4, max(block + 1, 2)) * 256
            qcols = slice(block * 256, (block + 1) * 256)
            cols = lanes(u * 128)
            keys = keys_ref[0:rows, cols]
            queries = qst[cols, qcols]
            qpos = block * 256 + lax.broadcasted_iota(jnp.int32, (1, 256), 1)
            low = block * 256
            seen = low + lax.broadcasted_iota(jnp.int32, (rows - low, 256), 0) <= jnp.maximum(qpos, limit)
            for half in range(2):
                chosen = jnp.where(sub // 64 == half, queries, jnp.zeros_like(queries))
                scores = jnp.dot(keys, chosen, preferred_element_type=F32)
                size = jnp.abs(scores)
                size = masked(size, seen, low)
                top = jnp.max(size, axis=0, keepdims=True)
                exponent = jnp.exp(size - top)
                total = jnp.sum(exponent, axis=0, keepdims=True)
                weights = (sign_of(scores) * exponent).astype(BF)
                at = pl.ds(pl.multiple_of(u * 128 + half * 64, 64), 64)
                att[at, qcols] = jnp.dot(vt[at, 0:rows], weights, preferred_element_type=F32) / total
                lt[pl.ds(u * 2 + half, 1), qcols] = top + jnp.log(total)
            al_send[block // 2, block % 2, :, cols] = att[cols, qcols].T.astype(BF)

        lax.fori_loop(0, 3, unit, 0)
        al_own.start()
        al_c.start()
        start(keep[1:])
        load_o.wait()
        al_own.wait()
        al_c.wait_recv()
        landed(keep)

    pl.run_scoped(
        forward, vmem((1024, D), BF), vmem((D, 1024), BF), vmem((THIRD, 1024), BF),
        vmem((THIRD, 1024), BF), vmem((1024, THIRD), BF), vmem((1024, THIRD), BF), vmem((THIRD, 1024), F32),
        vmem((3, D, THIRD), BF))

    def put_to(out, half):
        def put(value, core):
            out[:, lanes(core * half, half)] = value
        return put

    down = Scatter(k, gd, (c,), (c2,), CUTS["down"], work, put_to(out_d, THIRD))

    def put_up(part):
        def put(value, core):
            out_u[:, lanes(core * 1536 + part * D, D)] = value
        return put

    up = [Scatter(k, gu, (c, part), (c2, part), CUTS[f"up{part}"], work, put_up(part)) for part in range(2)]
    outp = Scatter(k, go, (c,), (c2,), CUTS["out"], work, put_to(out_o, THIRD))

    def feed(wbuf, wdb, hid, slope, n2, n2t, alt, gpc):
        b_out, gain, shift = vrows[3:4, 0:D], vrows[4:5, 0:D], vrows[5:6, 0:D]

        def begin(yy, carry):
            rows = rows_at(yy * 256, 256)
            branch = jnp.concatenate([jnp.dot(al[yy], wom[h], preferred_element_type=F32) for h in range(2)], axis=1)
            residual = tok_all[yy, c].astype(F32) + branch + b_out
            fa[yy] = residual
            normed, _ = unit_rows(residual)
            normed = (normed * gain + shift).astype(BF)
            n2[rows, :] = normed
            n2t[:, rows] = normed.astype(F32).T.astype(BF)
            alt[:, rows] = al[yy].astype(F32).T.astype(BF)
            return carry

        lax.fori_loop(0, 2, begin, 0)
        own_cot.wait()
        cot_y.wait_recv()

        wu2 = wu.reshape(2, 2, D, D)
        wd2 = wd.reshape(2, FF, THIRD)

        def chunk(j, first, second):
            h = first if j < 2 else second
            return h, j % 2

        def up_load(j, slot, order):
            h, part = chunk(j, *order)
            return k.local(wu2.at[h, part], wbuf.at[slot])

        def down_load(j, slot, order):
            h, part = chunk(j, *order)
            rows = rows_at(h * 1536 + part * D, D)
            return [k.local(wd2.at[side, rows, :], wdb.at[slot, :, side * THIRD : (side + 1) * THIRD]) for side in range(2)]

        forth = (c, c2)
        loads = [up_load(j, j % 2, forth) for j in range(4)]
        loads[0].start()
        gather_u[1].s4()
        for j in range(4):
            loads[j].wait()
            if j == 0:
                loads[1].start()
            if j == 1:
                gather_u[0].done()
                loads[2].start()
            if j == 2:
                gather_u[1].done()
                loads[3].start()
            h, part = chunk(j, *forth)

            cols = lanes(h * 1536 + part * D, D)
            value = jnp.dot(n2[...], wbuf[j % 2], preferred_element_type=F32) + vrows[6:7, cols]
            result, bend = gelu_parts(value)
            hid[:, cols] = result.astype(BF)
            slope[:, cols] = bend

        vs[7:8, :] = jnp.sum(cotm[0].astype(F32), axis=0, keepdims=True) + jnp.sum(
            cotm[1].astype(F32), axis=0, keepdims=True)

        def down_grad(i, carry):
            total = lax.dot_general(hid[:, lanes(i * THIRD, THIRD)], cotm[...].reshape(512, D), FIRST,
                                    preferred_element_type=F32)
            zz, xx = i // 2, lax.rem(i, 2)
            for yy in range(2):
                for h in range(2):
                    gd[h, zz, xx, yy] = total[yy * 192 : (yy + 1) * 192, h * THIRD : (h + 1) * THIRD].astype(BF)
            return carry

        lax.fori_loop(0, 8, down_grad, 0)
        down.s0()
        gather_d.s4()
        back = (c2, c)
        again = [up_load(j, j % 2, back) for j in range(4)]
        lower = [down_load(j, j % 2, back) for j in range(4)]
        again[0].start()
        down.s1()
        gather_d.c4[0].wait_recv()
        start(lower[0])
        for j in range(4):
            slot = j % 2
            if j < 3:
                again[j + 1].start()
                gather_d.c4[j + 1].wait_recv()
                start(lower[j + 1])
            again[j].wait()
            landed(lower[j])
            h, part = chunk(j, *back)
            cols = lanes(h * 1536 + part * D, D)
            term = jnp.dot(hid[:, cols], wdb[slot], preferred_element_type=F32).reshape(2, 256, D)
            fc[...] = term if j == 0 else fc[...] + term
            grad = lax.dot_general(cotm[...].reshape(512, D), wdb[slot], LAST, preferred_element_type=F32)
            grad = (grad * slope[:, cols]).astype(BF)
            gpc[...] = grad
            vup[0:1, cols] = jnp.sum(grad.astype(F32), axis=0, keepdims=True)
            term = lax.dot_general(gpc[...], wbuf[slot], LAST, preferred_element_type=F32).reshape(2, 256, D)
            fb[...] = term if j == 0 else fb[...] + term

            def up_grad(zz, carry):
                total = jnp.dot(n2t[rows_at(zz * THIRD, THIRD, 128), :], gpc[...], preferred_element_type=F32)
                for i in range(8):
                    gu[h, part, zz * 2 + i // 4, i // 2 % 2, i % 2] = total[i * 48 : (i + 1) * 48].astype(BF)
                return carry

            lax.fori_loop(0, 2, up_grad, 0)
            if j < 2:
                up[j].s0()
            if j == 2:
                up[0].s1()
                down.s2()
        bo[...] = (fa[...] + fc[...] + vrows[7:8, 0:D].reshape(1, 1, D)).astype(BF)
        up[1].s1()

    ga_c = k.remote(ga_send.at[:, :, peer_cols], ga_all.at[:, c], k.pc)
    def turn(alt, gpc):
        gain = vrows[4:5, 0:D]
        vs[3:6, :] = jnp.zeros((3, D), F32)

        def mid_back(yy, carry):
            rows = rows_at(yy * 256, 256)
            normed, scale = unit_rows(fa[yy])
            grad = fb[yy]
            vs[4:5, :] += jnp.sum(grad * normed, axis=0, keepdims=True)
            vs[5:6, :] += jnp.sum(grad, axis=0, keepdims=True)
            total = cotm[yy].astype(F32) + norm_back(grad * gain, normed, scale)
            fa[yy] = total
            low = total.astype(BF)
            vs[3:4, :] += jnp.sum(low.astype(F32), axis=0, keepdims=True)
            gpc[rows, :] = low
            heads = None
            for side in range(2):
                term = lax.dot_general(low[:, side * THIRD : (side + 1) * THIRD], wom[side], LAST,
                                       preferred_element_type=F32)
                heads = term if heads is None else heads + term
            ga_send[yy] = heads.astype(BF)
            ga_all[yy, c] = ga_send[yy, :, mine_cols]
            return carry

        lax.fori_loop(0, 2, mid_back, 0)
        ga_c.start()

        def out_grad(zz, carry):
            total = jnp.dot(alt[rows_at(zz * THIRD, THIRD, 128), :], gpc[...], preferred_element_type=F32)
            for i in range(8):
                for h in range(2):
                    go[h, zz * 2 + i // 4, i // 2 % 2, i % 2] = total[i * 48 : (i + 1) * 48, h * THIRD : (h + 1) * THIRD].astype(BF)
            return carry

        lax.fori_loop(0, 2, out_grad, 0)
        outp.s0()

    def put_q(u):
        def put(value, core):
            for kind in range(3):
                out_q[:, lanes(kind * D + core * THIRD + u * 128)] = value[:, kind * 128 : (kind + 1) * 128]
        return put

    queue = [Scatter(k, gq, (u,), None, CUTS[f"q{u}"], work, put_q(u)) for u in range(3)]
    bo_own = k.local(bo.at[y], out_bo.at[y])
    bo_y = k.remote(bo.at[y2], out_bo.at[y], k.py)

    def collect(index):
        row = vbq[...] if index == 2 else vup[...] if index == 6 else vs[index : index + 1, :]
        vtab[pl.ds(index, 32, stride=8), :] = collect_rows(row, WIDTHS[index])

    def early():
        for index in (3, 4, 5, 6, 7):
            collect(index)

    def send_out():
        bo_own.start()
        bo_y.start()

    def backward(alt, gpc, qst, keys_ref, values_ref, att, n1t, gt, kt, dk, dv, gpu, wqm, gp):
        loads = [k.local(k_qst, qst), k.local(k_k, keys_ref), k.local(k_v, values_ref),
                 k.local(k_att, att), k.local(k_n1t, n1t), ]
        loads += [k.local(wq3.at[u], wqm.at[:, u * THIRD : (u + 1) * THIRD]) for u in range(3)]
        start(loads)
        turn(alt, gpc)
        ga_c.wait_recv()
        landed(loads)
        vbq[...] = jnp.zeros_like(vbq)
        slots = {
            (0, 3): [outp.s1], (0, 2): [], (0, 1): [down.s3], (0, 0): [up[0].s2, send_out],
            (1, 3): [], (1, 2): [up[1].s2], (1, 1): [outp.s2], (1, 0): [down.s4, up[0].s3, early],
            (2, 3): [up[1].s3], (2, 2): [queue[0].s2, down.s5], (2, 1): [outp.s3], (2, 0): [queue[0].s3, up[0].s4],
        }

        def unit(u, carry):
            cols = lanes(u * 128)
            for b in range(4):
                rows = slice(b * 256, (b + 1) * 256)
                gt[:, rows] = ga_all[b // 2, b % 2, :, cols].astype(F32).T.astype(BF)
                kt[:, rows] = keys_ref[rows, cols].astype(F32).T.astype(BF)
            dk[...] = jnp.zeros_like(dk)
            dv[...] = jnp.zeros_like(dv)
            for block in (3, 2, 1, 0):
                rows = min(4, max(block + 1, 2)) * 256
                qrange = slice(block * 256, (block + 1) * 256)
                keys = keys_ref[0:rows, cols]
                values = values_ref[0:rows, cols]
                queries_t = qst[cols, qrange]
                grads_t = gt[:, qrange]
                qpos = block * 256 + lax.broadcasted_iota(jnp.int32, (1, 256), 1)
                low = block * 256
                seen = low + lax.broadcasted_iota(jnp.int32, (rows - low, 256), 0) <= jnp.maximum(qpos, limit)
                prod = grads_t.astype(F32) * att[cols, qrange]
                dqs = []
                for half in range(2):
                    part = slice(half * 64, half * 64 + 64)
                    in_sub = sub // 64 == half
                    delta = jnp.sum(prod[part], axis=0, keepdims=True)
                    total = lt[pl.ds(u * 2 + half, 1), qrange]
                    zero = jnp.zeros((), BF)
                    scores = jnp.dot(keys, jnp.where(in_sub, queries_t, zero), preferred_element_type=F32)
                    pull = jnp.dot(values, jnp.where(in_sub, grads_t, zero), preferred_element_type=F32)
                    share = jnp.exp(masked(jnp.abs(scores) - total, seen, low))
                    signed = sign_of(scores) * share
                    grad_scores = (share * pull - signed * delta).astype(BF)
                    signed = signed.astype(BF)
                    dv[part, 0:rows] += lax.dot_general(grads_t[part], signed, LAST, preferred_element_type=F32)
                    dk[part, 0:rows] += lax.dot_general(queries_t[part], grad_scores, LAST, preferred_element_type=F32)
                    dqs.append(jnp.dot(kt[part, 0:rows], grad_scores, preferred_element_type=F32))
                gpu[qrange, 0:128] = (jnp.concatenate(dqs, axis=0).T * 0.125).astype(BF)
                for which in range(3):
                    if slots[which, block]:
                        @pl.when(u == which)
                        def _():
                            for step in slots[which, block]:
                                step()
            for b in range(4):
                rows = slice(b * 256, (b + 1) * 256)
                gpu[rows, 128:256] = dk[:, rows].T.astype(BF)
                gpu[rows, 256:384] = dv[:, rows].T.astype(BF)
            sums = jnp.sum(gpu[...].astype(F32), axis=0, keepdims=True)
            for kind in range(3):
                part = slice(kind * 128, (kind + 1) * 128)
                vbq[0:1, lanes(kind * D + c * THIRD + u * 128)] = sums[:, part]
                gp[:, lanes(u * THIRD + kind * 128)] = gpu[:, part]

            def weights(zz, inner):
                block = jnp.dot(n1t[rows_at(zz * THIRD, THIRD, 128), :], gpu[...], preferred_element_type=F32)
                for i in range(8):
                    gq[u, zz * 2 + i // 4, i // 2 % 2, i % 2] = block[i * 48 : (i + 1) * 48].astype(BF)
                return inner

            lax.fori_loop(0, 2, weights, 0)
            for which in range(3):
                @pl.when(u == which)
                def _():
                    queue[which].s1()
            return carry

        lax.fori_loop(0, 3, unit, 0)

        def back_rows(b):
            return lax.dot_general(gp[rows_at(b * 256, 256), :], wqm[...], LAST, preferred_element_type=F32)

        def back_peer(yy, carry):
            fb[yy] = back_rows(yy * 2 + c2)
            return carry

        def back_own(yy, carry):
            fc[yy] = back_rows(yy * 2 + c)
            return carry

        lax.fori_loop(0, 2, back_peer, 0)
        part_c.start()
        queue[1].s2()
        lax.fori_loop(0, 2, back_own, 0)
        queue[2].s2()

    part_c = k.remote(fb, fr, k.pc)

    def both(alt, gpc):
        pl.run_scoped(
            functools.partial(feed, alt=alt, gpc=gpc), vmem((2, D, D), BF), vmem((2, D, D), BF),
            vmem((512, FF), BF), vmem((512, FF), F32), vmem((512, D), BF), vmem((D, 512), BF))
        pl.run_scoped(
            functools.partial(backward, alt, gpc), vmem((THIRD, 1024), BF), vmem((1024, THIRD), BF),
            vmem((1024, THIRD), BF), vmem((THIRD, 1024), F32), vmem((D, 1024), BF), vmem((128, 1024), BF),
            vmem((128, 1024), BF), vmem((128, 1024), F32), vmem((128, 1024), F32), vmem((1024, THIRD), BF),
            vmem((D, 3 * THIRD), BF), vmem((1024, 3 * THIRD), BF))

    pl.run_scoped(both, vmem((D, 512), BF), vmem((512, D), BF))

    gain = vrows[0:1, 0:D]
    vs[0:2, :] = jnp.zeros((2, D), F32)
    part_c.wait_recv()

    def last_back(yy):
        normed, scale = unit_rows(tok_all[yy, c].astype(F32))
        grad = fc[yy] + fr[yy]
        vs[0:1, :] += jnp.sum(grad * normed, axis=0, keepdims=True)
        vs[1:2, :] += jnp.sum(grad, axis=0, keepdims=True)
        gtb[yy] = (fa[yy] + norm_back(grad * gain, normed, scale)).astype(BF)

    gt_own = k.local(gtb.at[y], out_gt.at[y])
    gt_y = k.remote(gtb.at[y2], out_gt.at[y], k.py)
    last_back(y2)
    gt_y.start()
    queue[1].s3()
    last_back(y)
    gt_own.start()
    queue[2].s3()
    for index in range(3):
        collect(index)
    table = vtab.reshape(4, 2, 2, 2, 8, 128)
    v0 = k.remote(table.at[:, :, :, c2], vr0, k.pc)
    v1 = k.remote(table.at[:, :, y2, c], vr1, k.py)
    v2 = k.remote(table.at[:, x2, y, c], vr2, k.px)
    v3 = [k.remote(table.at[k.zs[d], x, y, c], vr3.at[d], k.pz[d]) for d in range(3)]

    def tile(zz, xx, yy):
        return rows_at((((zz * 2 + xx) * 2 + yy) * 2 + c) * 8, 8, 8)

    v0.start()
    queue[0].s4()
    v0.wait_recv()

    def add_core(i, carry):
        zz, xx, yy = i // 4, lax.rem(i // 2, 2), lax.rem(i, 2)
        vtab[tile(zz, xx, yy), :] += vr0[zz, xx, yy]
        return carry

    lax.fori_loop(0, 16, add_core, 0)
    v1.start()
    for copy in k.sent[:gathered]:
        copy.wait_send()
    up[1].s4()
    queue[1].s4()
    v1.wait_recv()

    def add_y(i, carry):
        vtab[tile(i // 2, lax.rem(i, 2), y), :] += vr1[i // 2, lax.rem(i, 2)]
        return carry

    lax.fori_loop(0, 8, add_y, 0)
    v2.start()
    outp.s4()
    up[0].s5()
    queue[0].s5()
    v2.wait_recv()

    def add_x(zz, carry):
        vtab[tile(zz, x, y), :] += vr2[zz]
        return carry

    lax.fori_loop(0, 4, add_x, 0)
    start(v3)
    queue[2].s4()
    up[1].s5()
    outp.s5()
    queue[1].s5()
    queue[2].s5()
    arrive(v3)
    out_vec[...] = vtab[tile(z, x, y), :] + vr3[0] + vr3[1] + vr3[2]
    landed([gt_own, bo_own])
    arrive([gt_y, bo_y])
    for copy in k.sent[gathered:]:
        copy.wait_send()
    assert k.remotes <= REMOTES and k.locals <= LOCALS


def layer_call(*operands):
    sds = jax.ShapeDtypeStruct
    vmem = pltpu.VMEM
    dma = pltpu.SemaphoreType.DMA
    results = (
        sds((2, 256, D), BF), sds((2, 256, D), BF), sds((24, 3 * D), F32), sds((24, D), F32), sds((24, FF), F32),
        sds((96, D), F32), sds((8, 128), F32),
    )
    held = (
        sds((3, 4, 2, 2, 48, 384), BF), sds((2, 4, 2, 2, 48, 384), BF), sds((2, 2, 4, 2, 2, 48, 768), BF),
        sds((2, 4, 2, 2, 192, 384), BF), sds((4, 2, 2, 2, 8, 128), F32), sds((THIRD, 1024), BF),
        sds((1024, THIRD), BF), sds((1024, THIRD), BF), sds((THIRD, 1024), F32), sds((D, 1024), BF),
    )
    scratch = [
        vmem((8, 128), F32), vmem((2, 3, 24, THIRD), BF), vmem((4, 2, 2, 2, 8, 128), F32), vmem((2, 2, 256, D), BF), vmem((8, FF), F32),
        vmem((2, D, THIRD), BF), vmem((2, 2, 256, THIRD), BF), vmem((2, 256, D), BF), vmem((2, 256, D), BF),
        vmem((2, 256, D), BF), vmem((2, 2, 256, THIRD), BF), vmem((2, 256, D), F32), vmem((2, 256, D), F32),
        vmem((2, 256, D), F32), vmem((2, 256, D), F32), vmem((8, 1024), F32),
    ]
    scratch += [
        vmem((2, 4, 2, 2, 192, 384), BF), vmem((2, 2, 4, 2, 2, 48, 768), BF), vmem((2, 4, 2, 2, 48, 384), BF),
        vmem((3, 4, 2, 2, 48, 384), BF),
        vmem((8, D), F32), vmem((1, 3 * D), F32), vmem((1, FF), F32), vmem((256, 128), F32), vmem((4, 2, 2, 8, 128), F32),
        vmem((4, 2, 8, 128), F32), vmem((4, 8, 128), F32), vmem((3, 8, 128), F32),
        dma((REMOTES,)), dma((REMOTES,)), dma((LOCALS,)),
    ]
    for name in ("down", "up0", "up1", "out", "q0", "q1", "q2"):
        scratch += Scatter.buffers(CUTS[name], not name.startswith("q"))
    return pl.pallas_call(
        layer_kernel,
        out_shape=results + held,
        in_specs=[SM] + [ANY] * 2 + [VM] * 12,
        out_specs=(ANY, ANY) + (VM,) * 5 + (ANY,) * len(held),
        scratch_shapes=scratch,
        compiler_params=pltpu.CompilerParams(
            collective_id=0, has_side_effects=True, vmem_limit_bytes=63 * 2**20),
    )(*operands)[: len(results)]


def finish_kernel(*refs):
    sources, results, (table, sems) = refs[:7], refs[7:21], refs[21:]
    copies = [pltpu.make_async_copy(source, result, sems.at[i])
              for i, (source, result) in enumerate(zip(sources, results[:6] + (table,)))]
    start(copies)
    landed(copies)
    for index, wide in enumerate(WIDTHS):
        results[6 + index][...] = table[index, 0:wide]


def finish_call(*operands):
    sds = jax.ShapeDtypeStruct
    shapes = tuple(sds(o.shape, o.dtype) for o in operands[:6]) + tuple(sds((wide,), F32) for wide in WIDTHS)
    return pl.pallas_call(
        finish_kernel, out_shape=shapes, in_specs=[ANY] * 7, out_specs=(VM,) * 14,
        scratch_shapes=[pltpu.VMEM((8, 128), F32), pltpu.SemaphoreType.DMA((7,))],
        compiler_params=pltpu.CompilerParams(vmem_limit_bytes=60 * 2**20),
    )(*operands)


def body(
    tokens, cotangent, prefix, ln1_gain, ln1_bias, w_qkv, b_qkv, w_out, b_out,
    ln2_gain, ln2_bias, w_up, b_up, w_down, b_down,
):
    results = layer_call(
        prefix, tokens, cotangent, ln1_gain, ln1_bias, b_qkv, b_out, ln2_gain, ln2_bias, b_up, b_down,
        w_qkv, w_out, w_up, w_down)
    block_out, grad_tokens, gq, go, gu, gd, *rows = finish_call(*results)
    return (
        block_out, grad_tokens, rows[0], rows[1], gq, rows[2], go, rows[3], rows[4], rows[5], gu, rows[6], gd, rows[7],
    )


def fits(mesh):
    return dict(mesh.shape) == {"dp": 8, "seq": 4}


norm_eps = 1e-05
block_rows = 512


def layer_norm(features, gain, shift):
    centre = features - jnp.mean(features, axis=-1, keepdims=True)
    spread = jnp.mean(centre * centre, axis=-1, keepdims=True)
    return centre * lax.rsqrt(spread + norm_eps) * gain + shift


def gelu_tanh(values):
    return jax.nn.gelu(values, approximate=True)


def in_blocks(update, running, pieces):
    length = pieces[0].shape[1]
    blocks = length // block_rows
    blocked_pieces = tuple(
        (
            jnp.swapaxes(
                member.reshape((member.shape[0], blocks, block_rows) + member.shape[2:]), 0, 1
            )
            for member in pieces
        )
    )

    def advance(carried, element):
        return (update(carried, element[0], element[1] * block_rows), None)

    running, unused = lax.scan(
        advance, running, (blocked_pieces, jnp.arange(blocks, dtype=jnp.int32))
    )
    return running


def to_heads(flat_rows):
    return flat_rows.reshape(flat_rows.shape[0], flat_rows.shape[1], HEADS, HEAD_DIM)


def visible_mask(query_places, key_places, prefix_len):
    earlier = key_places[None, None, :] <= query_places[None, :, None]
    in_prefix = key_places[None, None, :] < prefix_len[:, None, None]
    return (earlier | in_prefix)[:, :, None, :]


def head_scores(query_heads, key_flat):
    return jnp.einsum(
        "bqhd,bkhd->bqhk", query_heads, to_heads(key_flat), preferred_element_type=jnp.float32
    ) * HEAD_DIM ** (-0.5)


def attend(query_heads, key_flat, value_flat, prefix_len):
    local_len = query_heads.shape[1]
    query_places = lax.axis_index("seq") * local_len + jnp.arange(local_len, dtype=jnp.int32)
    starting = (
        jnp.zeros(query_heads.shape, jnp.float32),
        jnp.zeros(query_heads.shape[:3], jnp.float32),
        jnp.zeros(query_heads.shape[:3], jnp.float32),
    )

    def update(running, pieces, offset):
        weighted, normaliser, ceiling = running
        key_piece, value_piece = pieces
        key_places = offset + jnp.arange(key_piece.shape[1], dtype=jnp.int32)
        scores = head_scores(query_heads, key_piece)
        visible = visible_mask(query_places, key_places, prefix_len)
        magnitude = jnp.where(visible, jnp.abs(scores), 0.0)
        new_ceiling = jnp.maximum(ceiling, jnp.max(magnitude, axis=-1))
        exponent = jnp.where(visible, jnp.exp(magnitude - new_ceiling[..., None]), 0.0)
        factor = jnp.exp(ceiling - new_ceiling)
        weights = (jnp.sign(scores) * exponent).astype(jnp.bfloat16)
        weighted = weighted * factor[..., None] + jnp.einsum(
            "bqhk,bkhd->bqhd", weights, to_heads(value_piece), preferred_element_type=jnp.float32
        )
        normaliser = normaliser * factor + jnp.sum(exponent, axis=-1)
        return (weighted, normaliser, new_ceiling)

    weighted, normaliser, ceiling = in_blocks(
        update,
        starting,
        (
            lax.all_gather(key_flat, "seq", axis=1, tiled=True),
            lax.all_gather(value_flat, "seq", axis=1, tiled=True),
        ),
    )
    return (weighted / normaliser[..., None], ceiling + jnp.log(normaliser))


def grad_terms(
    query_heads,
    grad_heads,
    key_flat,
    value_flat,
    log_total,
    delta_sum,
    query_places,
    key_places,
    prefix_len,
):
    scores = head_scores(query_heads, key_flat)
    sign_of = jnp.sign(scores)
    visible = visible_mask(query_places, key_places, prefix_len)
    shares = jnp.where(visible, jnp.exp(jnp.abs(scores) - log_total[..., None]), 0.0)
    grad_weights = jnp.einsum(
        "bqhd,bkhd->bqhk", grad_heads, to_heads(value_flat), preferred_element_type=jnp.float32
    )
    grad_scores = (shares * (grad_weights - sign_of * delta_sum[..., None])).astype(jnp.bfloat16)
    return ((sign_of * shares).astype(jnp.bfloat16), grad_scores)


def query_term(grad_scores, key_flat):
    return jnp.einsum(
        "bqhk,bkhd->bqhd", grad_scores, to_heads(key_flat), preferred_element_type=jnp.float32
    ) * HEAD_DIM ** (-0.5)


def key_value_terms(query_heads, grad_heads, shares_low, grad_scores):
    key_term = jnp.einsum(
        "bqhk,bqhd->bkhd", grad_scores, query_heads, preferred_element_type=jnp.float32
    ) * HEAD_DIM ** (-0.5)
    value_term = jnp.einsum(
        "bqhk,bqhd->bkhd", shares_low, grad_heads, preferred_element_type=jnp.float32
    )
    flat_shape = (key_term.shape[0], key_term.shape[1], key_term.shape[2] * key_term.shape[3])
    return jnp.concatenate([key_term.reshape(flat_shape), value_term.reshape(flat_shape)], axis=-1)


def attend_back(query_heads, key_flat, value_flat, grad_heads, log_total, delta_sum, prefix_len):
    seq_block, local_len = (query_heads.shape[0], query_heads.shape[1])
    width = key_flat.shape[2]
    local_places = lax.axis_index("seq") * local_len + jnp.arange(local_len, dtype=jnp.int32)
    starting = (
        jnp.zeros(query_heads.shape, jnp.float32),
        jnp.zeros((seq_block, lax.axis_size("seq") * local_len, 2 * width), jnp.float32),
    )

    def update_both(running, pieces, offset):
        grad_query, grad_keys = running
        key_piece, value_piece = pieces
        piece_len = key_piece.shape[1]
        key_places = offset + jnp.arange(piece_len, dtype=jnp.int32)
        shares_low, grad_scores = grad_terms(
            query_heads,
            grad_heads,
            key_piece,
            value_piece,
            log_total,
            delta_sum,
            local_places,
            key_places,
            prefix_len,
        )
        grad_query = grad_query + query_term(grad_scores, key_piece)
        current = lax.dynamic_slice_in_dim(grad_keys, offset, piece_len, 1)
        updated = current + key_value_terms(query_heads, grad_heads, shares_low, grad_scores)
        return (grad_query, lax.dynamic_update_slice_in_dim(grad_keys, updated, offset, 1))

    grad_query, grad_keys = in_blocks(
        update_both,
        starting,
        (
            lax.all_gather(key_flat, "seq", axis=1, tiled=True),
            lax.all_gather(value_flat, "seq", axis=1, tiled=True),
        ),
    )
    key_local = lax.psum_scatter(
        grad_keys.astype(jnp.bfloat16), "seq", scatter_dimension=1, tiled=True
    ).astype(jnp.float32)
    return (grad_query, key_local)


def forward_block(weights_in, token_part, prefix_len):
    (
        gain_one,
        shift_one,
        w_qkv,
        b_qkv,
        w_out,
        b_out,
        gain_two,
        shift_two,
        w_up,
        b_up,
        w_down,
        b_down,
    ) = weights_in
    seq_block, local_len, width = token_part.shape
    residual_in = token_part.reshape(-1, width).astype(jnp.float32)
    normed_one = layer_norm(
        residual_in, gain_one.astype(jnp.float32), shift_one.astype(jnp.float32)
    ).astype(jnp.bfloat16)
    projected = jnp.dot(normed_one, w_qkv, preferred_element_type=jnp.float32) + b_qkv.astype(
        jnp.float32
    )
    query_heads = (
        projected[:, :width].astype(jnp.bfloat16).reshape(seq_block, local_len, HEADS, HEAD_DIM)
    )
    key_flat = (
        projected[:, width : 2 * width].astype(jnp.bfloat16).reshape(seq_block, local_len, width)
    )
    value_flat = projected[:, 2 * width :].astype(jnp.bfloat16).reshape(seq_block, local_len, width)
    attended, log_total = attend(query_heads, key_flat, value_flat, prefix_len)
    attended_low = attended.reshape(-1, width).astype(jnp.bfloat16)
    residual_mid = (
        residual_in
        + jnp.dot(attended_low, w_out, preferred_element_type=jnp.float32)
        + b_out.astype(jnp.float32)
    )
    normed_two = layer_norm(
        residual_mid, gain_two.astype(jnp.float32), shift_two.astype(jnp.float32)
    ).astype(jnp.bfloat16)
    pre_gelu = jnp.dot(normed_two, w_up, preferred_element_type=jnp.float32) + b_up.astype(
        jnp.float32
    )
    hidden = gelu_tanh(pre_gelu).astype(jnp.bfloat16)
    result = (
        residual_mid
        + jnp.dot(hidden, w_down, preferred_element_type=jnp.float32)
        + b_down.astype(jnp.float32)
    )
    saved = (
        residual_in,
        normed_one,
        query_heads,
        key_flat,
        value_flat,
        attended,
        log_total,
        attended_low,
        residual_mid,
        normed_two,
        pre_gelu,
        hidden,
    )
    return (result.astype(jnp.bfloat16).reshape(token_part.shape), saved)


def backward_block(weights_in, saved, grad_part, prefix_len):
    (
        gain_one,
        shift_one,
        w_qkv,
        b_qkv,
        w_out,
        b_out,
        gain_two,
        shift_two,
        w_up,
        b_up,
        w_down,
        b_down,
    ) = weights_in
    (
        residual_in,
        normed_one,
        query_heads,
        key_flat,
        value_flat,
        attended,
        log_total,
        attended_low,
        residual_mid,
        normed_two,
        pre_gelu,
        hidden,
    ) = saved
    seq_block, local_len, width = grad_part.shape
    grad_result = grad_part.reshape(-1, width).astype(jnp.float32)
    grad_branch = grad_part.reshape(-1, width)
    grads_down = jnp.einsum("rf,rd->fd", hidden, grad_branch, preferred_element_type=jnp.float32)
    bias_down = jnp.sum(grad_branch, axis=0, dtype=jnp.float32)
    grad_hidden = jnp.einsum("rd,fd->rf", grad_branch, w_down, preferred_element_type=jnp.float32)
    gelu_pull = jax.vjp(gelu_tanh, pre_gelu)[1]
    grad_pre = gelu_pull(grad_hidden)[0].astype(jnp.bfloat16)
    grads_up = jnp.einsum("rd,rf->df", normed_two, grad_pre, preferred_element_type=jnp.float32)
    bias_up = jnp.sum(grad_pre, axis=0, dtype=jnp.float32)
    grad_normed_two = jnp.einsum("rf,df->rd", grad_pre, w_up, preferred_element_type=jnp.float32)
    norm_two_pull = jax.vjp(
        layer_norm, residual_mid, gain_two.astype(jnp.float32), shift_two.astype(jnp.float32)
    )[1]
    grad_mid, grads_gain_two, grads_shift_two = norm_two_pull(grad_normed_two)
    grad_mid = grad_mid + grad_result
    grad_attn = grad_mid.astype(jnp.bfloat16)
    grads_out = jnp.einsum("rd,re->de", attended_low, grad_attn, preferred_element_type=jnp.float32)
    bias_out = jnp.sum(grad_attn, axis=0, dtype=jnp.float32)
    grad_heads = (
        jnp.einsum("re,de->rd", grad_attn, w_out, preferred_element_type=jnp.float32)
        .astype(jnp.bfloat16)
        .reshape(seq_block, local_len, HEADS, HEAD_DIM)
    )
    delta_sum = jnp.sum(grad_heads.astype(jnp.float32) * attended, axis=-1)
    grad_query, key_local = attend_back(
        query_heads, key_flat, value_flat, grad_heads, log_total, delta_sum, prefix_len
    )
    grad_proj = jnp.concatenate(
        [grad_query.reshape(-1, width), key_local.reshape(-1, 2 * width)], axis=1
    ).astype(jnp.bfloat16)
    grads_qkv = jnp.einsum("rd,re->de", normed_one, grad_proj, preferred_element_type=jnp.float32)
    bias_qkv = jnp.sum(grad_proj, axis=0, dtype=jnp.float32)
    grad_normed_one = jnp.einsum("re,de->rd", grad_proj, w_qkv, preferred_element_type=jnp.float32)
    norm_one_pull = jax.vjp(
        layer_norm, residual_in, gain_one.astype(jnp.float32), shift_one.astype(jnp.float32)
    )[1]
    grad_in, grads_gain_one, grads_shift_one = norm_one_pull(grad_normed_one)
    grad_in = grad_in + grad_mid
    weight_grads = (
        grads_gain_one,
        grads_shift_one,
        grads_qkv,
        bias_qkv,
        grads_out,
        bias_out,
        grads_gain_two,
        grads_shift_two,
        grads_up,
        bias_up,
        grads_down,
        bias_down,
    )
    return (grad_in.astype(jnp.bfloat16).reshape(grad_part.shape), weight_grads)


def general_body(
    tokens,
    cotangent,
    prefix,
    ln1_gain,
    ln1_bias,
    w_qkv,
    b_qkv,
    w_out,
    b_out,
    ln2_gain,
    ln2_bias,
    w_up,
    b_up,
    w_down,
    b_down,
):
    shards = (
        ln1_gain,
        ln1_bias,
        w_qkv,
        b_qkv,
        w_out,
        b_out,
        ln2_gain,
        ln2_bias,
        w_up,
        b_up,
        w_down,
        b_down,
    )
    spread_count = lax.axis_size(("dp", "seq"))
    totals = tuple(
        (
            jnp.zeros((member.shape[0] * spread_count,) + member.shape[1:], jnp.float32)
            for member in shards
        )
    )
    seq_block = tokens.shape[0] // MB
    outputs = []
    grad_inputs = []
    for batch_index in range(MB):
        first_row = batch_index * seq_block
        token_part = tokens[first_row : first_row + seq_block]
        cotangent_part = cotangent[first_row : first_row + seq_block]
        prefix_part = prefix[first_row : first_row + seq_block]
        forward_weights = (
            lax.all_gather(shards[0], ("dp", "seq"), axis=0, tiled=True),
            lax.all_gather(shards[1], ("dp", "seq"), axis=0, tiled=True),
            lax.all_gather(shards[2], ("dp", "seq"), axis=0, tiled=True),
            lax.all_gather(shards[3], ("dp", "seq"), axis=0, tiled=True),
            lax.all_gather(shards[4], ("dp", "seq"), axis=0, tiled=True),
            lax.all_gather(shards[5], ("dp", "seq"), axis=0, tiled=True),
            lax.all_gather(shards[6], ("dp", "seq"), axis=0, tiled=True),
            lax.all_gather(shards[7], ("dp", "seq"), axis=0, tiled=True),
            lax.all_gather(shards[8], ("dp", "seq"), axis=0, tiled=True),
            lax.all_gather(shards[9], ("dp", "seq"), axis=0, tiled=True),
            lax.all_gather(shards[10], ("dp", "seq"), axis=0, tiled=True),
            lax.all_gather(shards[11], ("dp", "seq"), axis=0, tiled=True),
        )
        result, saved = forward_block(forward_weights, token_part, prefix_part)
        back_weights = (
            lax.all_gather(shards[0], ("dp", "seq"), axis=0, tiled=True),
            lax.all_gather(shards[1], ("dp", "seq"), axis=0, tiled=True),
            lax.all_gather(shards[2], ("dp", "seq"), axis=0, tiled=True),
            lax.all_gather(shards[3], ("dp", "seq"), axis=0, tiled=True),
            lax.all_gather(shards[4], ("dp", "seq"), axis=0, tiled=True),
            lax.all_gather(shards[5], ("dp", "seq"), axis=0, tiled=True),
            lax.all_gather(shards[6], ("dp", "seq"), axis=0, tiled=True),
            lax.all_gather(shards[7], ("dp", "seq"), axis=0, tiled=True),
            lax.all_gather(shards[8], ("dp", "seq"), axis=0, tiled=True),
            lax.all_gather(shards[9], ("dp", "seq"), axis=0, tiled=True),
            lax.all_gather(shards[10], ("dp", "seq"), axis=0, tiled=True),
            lax.all_gather(shards[11], ("dp", "seq"), axis=0, tiled=True),
        )
        grad_piece, weight_grads = backward_block(back_weights, saved, cotangent_part, prefix_part)
        totals = tuple(
            (running_sum + new_term for running_sum, new_term in zip(totals, weight_grads))
        )
        outputs.append(result)
        grad_inputs.append(grad_piece)
    reduced = (
        lax.psum_scatter(totals[0], ("dp", "seq"), scatter_dimension=0, tiled=True),
        lax.psum_scatter(totals[1], ("dp", "seq"), scatter_dimension=0, tiled=True),
        lax.psum_scatter(totals[2], ("dp", "seq"), scatter_dimension=0, tiled=True),
        lax.psum_scatter(totals[3], ("dp", "seq"), scatter_dimension=0, tiled=True),
        lax.psum_scatter(totals[4], ("dp", "seq"), scatter_dimension=0, tiled=True),
        lax.psum_scatter(totals[5], ("dp", "seq"), scatter_dimension=0, tiled=True),
        lax.psum_scatter(totals[6], ("dp", "seq"), scatter_dimension=0, tiled=True),
        lax.psum_scatter(totals[7], ("dp", "seq"), scatter_dimension=0, tiled=True),
        lax.psum_scatter(totals[8], ("dp", "seq"), scatter_dimension=0, tiled=True),
        lax.psum_scatter(totals[9], ("dp", "seq"), scatter_dimension=0, tiled=True),
        lax.psum_scatter(totals[10], ("dp", "seq"), scatter_dimension=0, tiled=True),
        lax.psum_scatter(totals[11], ("dp", "seq"), scatter_dimension=0, tiled=True),
    )
    return (
        jnp.concatenate(outputs, axis=0),
        jnp.concatenate(grad_inputs, axis=0),
        reduced[0],
        reduced[1],
        reduced[2],
        reduced[3],
        reduced[4],
        reduced[5],
        reduced[6],
        reduced[7],
        reduced[8],
        reduced[9],
        reduced[10],
        reduced[11],
    )


def solution(mesh):
    in_specs = (
        P("dp", "seq", None),
        P("dp", "seq", None),
        P("dp"),
        P(("dp", "seq")),
        P(("dp", "seq")),
        P(("dp", "seq"), None),
        P(("dp", "seq")),
        P(("dp", "seq"), None),
        P(("dp", "seq")),
        P(("dp", "seq")),
        P(("dp", "seq")),
        P(("dp", "seq"), None),
        P(("dp", "seq")),
        P(("dp", "seq"), None),
        P(("dp", "seq")),
    )
    out_specs = (
        P("dp", "seq", None),
        P("dp", "seq", None),
        P(("dp", "seq")),
        P(("dp", "seq")),
        P(("dp", "seq"), None),
        P(("dp", "seq")),
        P(("dp", "seq"), None),
        P(("dp", "seq")),
        P(("dp", "seq")),
        P(("dp", "seq")),
        P(("dp", "seq"), None),
        P(("dp", "seq")),
        P(("dp", "seq"), None),
        P(("dp", "seq")),
    )
    chosen = body if fits(mesh) else general_body
    return jax.shard_map(chosen, mesh=mesh, in_specs=in_specs, out_specs=out_specs, check_vma=False)
```
